32 devices in a mesh: dp: 4 (over y, x), ctx: 8 (over z, core).
Axes of the slice: x: 2, y: 2, z: 4, core: 2. Of those that a mesh axis runs over, the one named last changes fastest.
Arguments:
- inputs: bfloat16 [4096, 960], P(('dp', 'ctx')), may hold values from -6 to 6
- cotangent: bfloat16 [4096, 960], P(('dp', 'ctx')), may hold values from -6 to 6
- w_query: bfloat16 [960, 960], P('dp', 'ctx'), may hold values from -1 to 1
- w_key: bfloat16 [960, 320], P('dp', 'ctx'), may hold values from -1 to 1
- w_value: bfloat16 [960, 320], P('dp', 'ctx'), may hold values from -0.1875 to 0.1875
- w_output: bfloat16 [960, 960], P('dp', 'ctx'), may hold values from -0.75 to 0.75
- w_gate: bfloat16 [960, 2560], P('dp', 'ctx'), may hold values from -0.1875 to 0.1875
- w_up: bfloat16 [960, 2560], P('dp', 'ctx'), may hold values from -0.1875 to 0.1875
- w_down: bfloat16 [2560, 960], P('dp', 'ctx'), may hold values from -0.125 to 0.125
- gain_attn: bfloat16 [960], P('ctx'), may hold values from 0.5 to 1.5
- gain_ffn: bfloat16 [960], P('ctx'), may hold values from 0.5 to 1.5
Outputs:
- out_act: bfloat16 [4096, 960], P(('dp', 'ctx'))
- grad_input: float32 [4096, 960], P(('dp', 'ctx'))
- grad_w_query: float32 [960, 960], P('dp', 'ctx')
- grad_w_key: float32 [960, 320], P('dp', 'ctx')
- grad_w_value: float32 [960, 320], P('dp', 'ctx')
- grad_w_output: float32 [960, 960], P('dp', 'ctx')
- grad_w_gate: float32 [960, 2560], P('dp', 'ctx')
- grad_w_up: float32 [960, 2560], P('dp', 'ctx')
- grad_w_down: float32 [2560, 960], P('dp', 'ctx')
- grad_gain_attn: float32 [960], P('ctx')
- grad_gain_ffn: float32 [960], P('ctx')
The draws below stay inside these ranges and needn't reach their ends.
All inputs are finite; a program needn't handle non-finite values.
Results may differ from the reference program's by a relative error of at most 0.028.
Values may be sent and summed in bfloat16 or wider, within the bound.
A program may use at most 128 MiB of HBM per device.

```python
import jax
import jax.numpy as jnp
from jax import lax

D = 960
HEADS = 15
KV_HEADS = 5
HEAD_DIM = 64
FF = 2560
TOK_DEV = 128
SEQS = 4
LENGTH = 1024
TOKENS = 4096


def draw_inputs(key, part):
    input_key = jax.random.fold_in(key, 11)
    normal_key = jax.random.fold_in(input_key, 0)
    drawn_draw = jax.random.truncated_normal(normal_key, -6.0, 6.0, (TOKENS, D), jnp.float32)
    return drawn_draw.astype(jnp.bfloat16)


def drawn_weight(key, salt, column_count):
    weight_key = jax.random.fold_in(key, salt)
    entries = jax.random.truncated_normal(weight_key, -6.0, 6.0, (D, column_count), jnp.float32) * D ** (-0.5)
    return entries.astype(jnp.bfloat16)


def draw_w_query(key, part):
    return drawn_weight(key, 23, HEADS * HEAD_DIM)


def draw_w_key(key, part):
    return drawn_weight(key, 37, KV_HEADS * HEAD_DIM)


def shard_levels(stream_key, extent, cuts, low, high):
    gain, own = 1.0, jax.random.fold_in(stream_key, 6)
    for dim, shards_of in cuts:
        steps = jnp.exp(jax.random.uniform(jax.random.fold_in(own, dim), (shards_of,), jnp.float32, low / len(cuts), high / len(cuts)))
        gain = gain * jnp.repeat(steps, extent[dim] // shards_of).reshape([-1 if axis == dim else 1 for axis in range(len(extent))])
    return gain


def noise(own_key, extent, width, reach, shards=(), held_as=jnp.bfloat16):
    values = jax.random.normal(own_key, extent, jnp.float32) * width
    if len(shards) > 0:
        values = shard_levels(own_key, extent, shards, -0.22, 0.18) * values
    return jnp.clip(values, min=-reach, max=reach).astype(held_as)


def setup_inputs(seed: int = 0) -> dict:
    key_list = jax.random.split(jax.random.key(seed), 12)
    return {
        "inputs": draw_inputs(jax.random.fold_in(key_list[11], 71), 0),
        "cotangent": noise(key_list[1], (TOKENS, D), 1.0, 6.0, ((0, 32),)),
        "w_query": draw_w_query(jax.random.fold_in(key_list[11], 71), 0),
        "w_key": draw_w_key(jax.random.fold_in(key_list[11], 71), 0),
        "w_value": noise(key_list[4], (D, KV_HEADS * HEAD_DIM), D ** -0.5, 0.1875, ((0, 4), (1, 8))),
        "w_output": noise(key_list[5], (HEADS * HEAD_DIM, D), (HEADS * HEAD_DIM // 16) ** -0.5, 0.75, ((0, 4), (1, 8))),
        "w_gate": noise(key_list[6], (D, FF), D ** -0.5, 0.1875, ((0, 4), (1, 8))),
        "w_up": noise(key_list[7], (D, FF), D ** -0.5, 0.1875, ((0, 4), (1, 8))),
        "w_down": noise(key_list[8], (FF, D), FF ** -0.5, 0.125, ((0, 4), (1, 8))),
        "gain_attn": jnp.clip(1.0 + 0.1 * jax.random.normal(key_list[9], (D,), jnp.float32), 0.5, 1.5).astype(jnp.bfloat16),
        "gain_ffn": jnp.clip(1.0 + 0.1 * jax.random.normal(key_list[10], (D,), jnp.float32), 0.5, 1.5).astype(jnp.bfloat16),
    }


epsilon = 1e-05
rope_base = 10000.0

def rope_tables(first_pos, row_count, head_width):
    half_width = head_width // 2
    frequency = rope_base ** (-jnp.arange(half_width).astype(jnp.float32) * 2.0 / head_width)
    positions = (first_pos + jnp.arange(row_count)).astype(jnp.float32)
    angles = positions[:, None] * frequency[None, :]
    return (jnp.cos(angles), jnp.sin(angles))

def rotate(vectors, cosine_t, sine_t):
    half_width = vectors.shape[-1] // 2
    lower_half = vectors[..., :half_width]
    upper_half = vectors[..., half_width:]
    cos_b = cosine_t[:, None, :]
    sin_b = sine_t[:, None, :]
    return jnp.concatenate([lower_half * cos_b - upper_half * sin_b, upper_half * cos_b + lower_half * sin_b], axis=-1)

def unrotate(vectors, cosine_t, sine_t):
    half_width = vectors.shape[-1] // 2
    lower_half = vectors[..., :half_width]
    upper_half = vectors[..., half_width:]
    cos_b = cosine_t[:, None, :]
    sin_b = sine_t[:, None, :]
    return jnp.concatenate([lower_half * cos_b + upper_half * sin_b, upper_half * cos_b - lower_half * sin_b], axis=-1)

def norm_forward(hidden, gain_vec):
    inverse = lax.rsqrt(lax.optimization_barrier(jnp.mean(hidden * hidden, axis=-1, keepdims=True)) + epsilon)
    return (hidden * inverse * gain_vec, inverse)

def norm_backward(hidden, inverse, gain_vec, upstream):
    scaled = upstream * gain_vec
    feature_count = hidden.shape[-1]
    cubed = inverse * inverse * inverse
    d_hidden = inverse * scaled - hidden * cubed * lax.optimization_barrier(jnp.sum(scaled * hidden, axis=-1, keepdims=True)) / feature_count
    d_gain = lax.optimization_barrier(jnp.sum(upstream * hidden * inverse, axis=0))
    return (d_hidden, d_gain)

def rounded(vectors):
    return lax.optimization_barrier(vectors.astype(jnp.bfloat16)).astype(jnp.float32)

def one_sequence(weights, gain_pair, inputs, cotangent):
    w_query, w_key, w_value, w_output, w_gate, w_up, w_down = weights
    gain_one = gain_pair[0].astype(jnp.float32)
    gain_two = gain_pair[1].astype(jnp.float32)
    length = inputs.shape[0]
    group_size = HEADS // KV_HEADS
    score_scale = HEAD_DIM ** (-0.5)
    block_count = length // TOK_DEV
    cosine_t, sine_t = rope_tables(0, length, HEAD_DIM)
    hidden = inputs.astype(jnp.float32)
    normed_f, inv_one = norm_forward(hidden, gain_one)
    normed_one = normed_f.astype(jnp.bfloat16)
    query_pre = jnp.dot(normed_one, w_query, preferred_element_type=jnp.float32).reshape(length, HEADS, HEAD_DIM)
    queries = rotate(query_pre, cosine_t, sine_t).astype(jnp.bfloat16).reshape(length, KV_HEADS, group_size, HEAD_DIM)
    key_pre = jnp.dot(normed_one, w_key, preferred_element_type=jnp.float32).reshape(length, KV_HEADS, HEAD_DIM)
    key_heads = rotate(key_pre, cosine_t, sine_t).astype(jnp.bfloat16)
    value_heads = jnp.dot(normed_one, w_value, preferred_element_type=jnp.float32).astype(jnp.bfloat16).reshape(length, KV_HEADS, HEAD_DIM)
    key_f = key_heads.astype(jnp.float32)
    value_f = value_heads.astype(jnp.float32)
    key_pos = jnp.arange(length).astype(jnp.int32)

    def scores_for(block_index):
        first_row = (block_index * TOK_DEV).astype(jnp.int32)
        query_block = lax.dynamic_slice_in_dim(queries, first_row, TOK_DEV, 0).astype(jnp.float32)
        raw_scores = jnp.einsum('tkgd,skd->kgts', query_block, key_f) * score_scale
        query_pos = first_row + jnp.arange(TOK_DEV).astype(jnp.int32)
        allowed = query_pos[:, None] >= key_pos[None, :]
        return (jnp.where(allowed, raw_scores, -1e+30), query_block)

    def forward_block(block_index):
        masked, query_block = scores_for(block_index)
        row_max = lax.optimization_barrier(jnp.max(masked, axis=-1))
        expo = jnp.exp(masked - row_max[..., None])
        weight_sum = lax.optimization_barrier(jnp.sum(expo, axis=-1))
        mixed_heads = jnp.einsum('kgts,skd->kgtd', rounded(expo), value_f) / weight_sum[..., None]
        return (mixed_heads.astype(jnp.bfloat16), row_max + jnp.log(weight_sum))
    block_ids = jnp.arange(block_count).astype(jnp.int32)
    attended_blocks, logsum = lax.map(forward_block, block_ids)
    attended = jnp.transpose(attended_blocks, (0, 3, 1, 2, 4)).reshape(length, HEADS * HEAD_DIM)
    middle = hidden + jnp.dot(attended, w_output, preferred_element_type=jnp.float32)
    normed_g, inv_two = norm_forward(middle, gain_two)
    normed_two = normed_g.astype(jnp.bfloat16)
    gate_pre = jnp.dot(normed_two, w_gate, preferred_element_type=jnp.float32)
    up_pre = jnp.dot(normed_two, w_up, preferred_element_type=jnp.float32)
    sigma = jax.nn.sigmoid(gate_pre)
    silu_gate = gate_pre * sigma
    mixed_act = (silu_gate * up_pre).astype(jnp.bfloat16)
    result = middle + jnp.dot(mixed_act, w_down, preferred_element_type=jnp.float32)
    out_act = result.astype(jnp.bfloat16)
    cot_f = cotangent.astype(jnp.float32)
    grad_down = jnp.dot(mixed_act.T, cotangent, preferred_element_type=jnp.float32)
    d_mixed = jnp.dot(cotangent, w_down.T, preferred_element_type=jnp.float32)
    d_gate = (d_mixed * up_pre * sigma * (1.0 + gate_pre * (1.0 - sigma))).astype(jnp.bfloat16)
    d_up = (d_mixed * silu_gate).astype(jnp.bfloat16)
    grad_gate = jnp.dot(normed_two.T, d_gate, preferred_element_type=jnp.float32)
    grad_up = jnp.dot(normed_two.T, d_up, preferred_element_type=jnp.float32)
    d_norm_two = jnp.dot(d_gate, w_gate.T, preferred_element_type=jnp.float32) + jnp.dot(d_up, w_up.T, preferred_element_type=jnp.float32)
    d_mid_norm, grad_gain_two = norm_backward(middle, inv_two, gain_two, d_norm_two)
    d_middle = cot_f + d_mid_norm
    d_middle_b = d_middle.astype(jnp.bfloat16)
    grad_output = jnp.dot(attended.T, d_middle_b, preferred_element_type=jnp.float32)
    d_attended = jnp.dot(d_middle_b, w_output.T, preferred_element_type=jnp.float32).astype(jnp.bfloat16)
    grad_heads = d_attended.reshape(length, KV_HEADS, group_size, HEAD_DIM)
    attended_heads = attended.reshape(length, KV_HEADS, group_size, HEAD_DIM)

    def backward_block(loop_carry, block_index):
        grad_keys, grad_values = loop_carry
        masked, query_block = scores_for(block_index)
        first_row = (block_index * TOK_DEV).astype(jnp.int32)
        grad_block = lax.dynamic_slice_in_dim(grad_heads, first_row, TOK_DEV, 0).astype(jnp.float32)
        att_block = lax.dynamic_slice_in_dim(attended_heads, first_row, TOK_DEV, 0).astype(jnp.float32)
        delta_rows = jnp.einsum('tkgd,tkgd->kgt', grad_block, att_block)
        probs = jnp.exp(masked - logsum[block_index][..., None])
        grad_values = grad_values + jnp.einsum('kgts,tkgd->skd', rounded(probs), grad_block)
        grad_probs = jnp.einsum('tkgd,skd->kgts', grad_block, value_f)
        d_scores = rounded(probs * (grad_probs - delta_rows[..., None]))
        grad_query = jnp.einsum('kgts,skd->tkgd', d_scores, key_f) * score_scale
        grad_keys = grad_keys + jnp.einsum('kgts,tkgd->skd', d_scores, query_block) * score_scale
        return ((grad_keys, grad_values), grad_query)
    zero_kv = jnp.zeros((length, KV_HEADS, HEAD_DIM), jnp.float32)
    (grad_keys, grad_values), grad_query = lax.scan(backward_block, (zero_kv, zero_kv), block_ids)
    grad_query = grad_query.reshape(length, HEADS, HEAD_DIM)
    dq_in = unrotate(grad_query, cosine_t, sine_t).astype(jnp.bfloat16).reshape(length, HEADS * HEAD_DIM)
    dk_in = unrotate(grad_keys, cosine_t, sine_t).astype(jnp.bfloat16).reshape(length, KV_HEADS * HEAD_DIM)
    dv_in = grad_values.astype(jnp.bfloat16).reshape(length, KV_HEADS * HEAD_DIM)
    grad_wq = jnp.dot(normed_one.T, dq_in, preferred_element_type=jnp.float32)
    grad_wk = jnp.dot(normed_one.T, dk_in, preferred_element_type=jnp.float32)
    grad_wv = jnp.dot(normed_one.T, dv_in, preferred_element_type=jnp.float32)
    d_norm_one = jnp.dot(dq_in, w_query.T, preferred_element_type=jnp.float32)
    d_norm_one = d_norm_one + jnp.dot(dk_in, w_key.T, preferred_element_type=jnp.float32)
    d_norm_one = d_norm_one + jnp.dot(dv_in, w_value.T, preferred_element_type=jnp.float32)
    d_in_norm, grad_gain_one = norm_backward(hidden, inv_one, gain_one, d_norm_one)
    grad_input = d_middle + d_in_norm
    grads = (grad_wq, grad_wk, grad_wv, grad_output, grad_gate, grad_up, grad_down, grad_gain_one, grad_gain_two)
    return (out_act, grad_input, grads)

def reference(inputs, cotangent, w_query, w_key, w_value, w_output, w_gate, w_up, w_down, gain_attn, gain_ffn):
    weights = (w_query, w_key, w_value, w_output, w_gate, w_up, w_down)
    gain_pair = (gain_attn, gain_ffn)
    seq_inputs = inputs.reshape(SEQS, LENGTH, D)
    seq_cot = cotangent.reshape(SEQS, LENGTH, D)
    zero_grads = tuple((jnp.zeros(weight.shape, jnp.float32) for weight in weights + gain_pair))

    def seq_step(loop_carry, seq_pair):
        out_act, grad_input, grads = one_sequence(weights, gain_pair, seq_pair[0], seq_pair[1])
        summed = tuple((left + right for left, right in zip(loop_carry, grads)))
        return (summed, (out_act, grad_input))
    totals, (outs, grad_ins) = lax.scan(seq_step, zero_grads, (seq_inputs, seq_cot))
    return (outs.reshape(TOKENS, D), grad_ins.reshape(TOKENS, D), totals[0], totals[1], totals[2], totals[3], totals[4], totals[5], totals[6], totals[7], totals[8])
```

```python
import functools

import jax
import jax.numpy as jnp
from jax import lax
from jax.experimental import pallas as pl
from jax.experimental.pallas import tpu as pltpu
from jax.sharding import PartitionSpec as P

HEADS = 15
KV_HEADS = 5
HEAD_DIM = 64
GROUP = HEADS // KV_HEADS

epsilon = 1e-05
rope_base = 10000.0
bf16 = jnp.bfloat16
f32 = jnp.float32


def remote(src, dst, send, recv, axis, peer):
    return pltpu.make_async_remote_copy(
        src_ref=src,
        dst_ref=dst,
        send_sem=send,
        recv_sem=recv,
        device_id={axis: peer},
        device_id_type=pl.DeviceIdType.MESH,
    )


class Gather:
    axis = "dp"

    def __init__(self, array):
        self.array = array

    def plan(self, sizes):
        self.n = sizes[self.axis]
        self.out = jax.ShapeDtypeStruct((self.n,) + self.array.shape, self.array.dtype)
        self.scratch = [pltpu.SemaphoreType.DMA((self.n,))] * 2 + [pltpu.SemaphoreType.DMA(())]

    def start(self, src, dst, send, recv, own):
        me = lax.axis_index(self.axis)
        self.local = pltpu.make_async_copy(src, dst.at[me], own)
        self.local.start()
        self.copies = []
        for k in range(1, self.n):
            peer = lax.rem(me + k, self.n)
            copy = remote(src, dst.at[me], send.at[k], recv.at[k], self.axis, peer)
            copy.start()
            self.copies.append(copy)

    def middle(self, *refs):
        pass

    def finish(self, src, dst, send, recv, own):
        me = lax.axis_index(self.axis)
        for k in range(1, self.n):
            slot = lax.rem(me + self.n - k, self.n)
            remote(src, dst.at[slot], send.at[k], recv.at[k], self.axis, slot).wait_recv()
        for copy in self.copies:
            copy.wait_send()
        self.local.wait()


class Relay:
    axis = "ctx"

    def __init__(self, array):
        self.array = array

    def plan(self, sizes):
        self.n = sizes[self.axis]
        chips = self.n // 2
        self.out = jax.ShapeDtypeStruct((self.n,) + self.array.shape, self.array.dtype)
        self.scratch = [pltpu.SemaphoreType.DMA((chips,))] * 6 + [pltpu.SemaphoreType.DMA(())]

    def at(self):
        me = lax.axis_index(self.axis)
        chip, core = me // 2, me % 2
        return me, chip, core, me + 1 - 2 * core, self.n // 2

    def start(self, src, dst, rs, rr, ls, lr, ps, pr, own):
        me, chip, core, partner, chips = self.at()

        @pl.when(chip < chips - 1)
        def _():
            remote(src, dst.at[me], rs.at[0], rr.at[0], self.axis, me + 2).start()

        @pl.when(chip > 0)
        def _():
            remote(src, dst.at[me], ls.at[0], lr.at[0], self.axis, me - 2).start()

        remote(src, dst.at[me], ps.at[chip], pr.at[chip], self.axis, partner).start()
        pltpu.make_async_copy(src, dst.at[me], own).start()

    def step(self, k, src, dst, rs, rr, ls, lr, ps, pr, own):
        me, chip, core, partner, chips = self.at()

        def arrived(slot_chip, way, send, recv):
            slot = slot_chip * 2 + core
            back = me - 2 * way
            remote(dst.at[slot], dst.at[slot], send.at[k], recv.at[k], self.axis, back).wait_recv()

            @pl.when(jnp.logical_and(chip + way >= 0, chip + way < chips))
            def _():
                remote(
                    dst.at[slot],
                    dst.at[slot],
                    send.at[k + 1],
                    recv.at[k + 1],
                    self.axis,
                    me + 2 * way,
                ).start()

            remote(
                dst.at[slot], dst.at[slot], ps.at[slot_chip], pr.at[slot_chip], self.axis, partner
            ).start()

        @pl.when(chip - 1 - k >= 0)
        def _():
            arrived(chip - 1 - k, 1, rs, rr)

        @pl.when(chip + 1 + k < chips)
        def _():
            arrived(chip + 1 + k, -1, ls, lr)

    def finish(self, src, dst, rs, rr, ls, lr, ps, pr, own):
        me, chip, core, partner, chips = self.at()
        for c in range(chips):
            slot = 2 * c + 1 - core
            remote(src, dst.at[slot], ps.at[c], pr.at[c], self.axis, partner).wait_recv()
        for c in range(chips):
            remote(src, dst.at[2 * c + core], ps.at[c], pr.at[c], self.axis, partner).wait_send()
        for k in range(chips - 1):

            @pl.when(jnp.logical_and(chip < chips - 1, k <= chip))
            def _():
                remote(src, dst.at[me], rs.at[k], rr.at[k], self.axis, me + 2).wait_send()

            @pl.when(jnp.logical_and(chip > 0, k <= chips - 1 - chip))
            def _():
                remote(src, dst.at[me], ls.at[k], lr.at[k], self.axis, me - 2).wait_send()

        pltpu.make_async_copy(src, dst.at[me], own).wait()


class Turn:
    axis = "all"

    def __init__(self, array):
        self.array = array

    def plan(self, sizes):
        self.dp, self.n = sizes["dp"], sizes["ctx"]
        self.m = self.n // self.dp
        self.out = jax.ShapeDtypeStruct(self.array.shape, self.array.dtype)
        self.scratch = [pltpu.SemaphoreType.DMA((self.m,))] * 2

    def each(self, src, dst, send, recv):
        row, col = lax.axis_index("dp"), lax.axis_index("ctx")
        put = col % self.m
        for i in range(self.m):
            to_row, to_col = col // self.m, row * self.m + i
            here = jnp.logical_and(to_row == row, to_col == col)
            far = pltpu.make_async_remote_copy(
                src_ref=src.at[i],
                dst_ref=dst.at[put],
                send_sem=send.at[i],
                recv_sem=recv.at[put],
                device_id={"dp": to_row, "ctx": to_col},
                device_id_type=pl.DeviceIdType.MESH,
            )
            local = pltpu.make_async_copy(src.at[i], dst.at[put], recv.at[put])
            yield i, here, far, local

    def start(self, *refs):
        for i, here, far, local in self.each(*refs):
            pl.when(here)(local.start)
            pl.when(jnp.logical_not(here))(far.start)

    def finish(self, src, dst, send, recv):
        row, col = lax.axis_index("dp"), lax.axis_index("ctx")
        for i, here, far, local in self.each(src, dst, send, recv):
            pl.when(jnp.logical_not(here))(far.wait_send)
        for i in range(self.m):
            own = jnp.logical_and(col // self.m == row, row * self.m + i == col)
            local = pltpu.make_async_copy(src.at[i], dst.at[i], recv.at[i])
            far = pltpu.make_async_remote_copy(
                src_ref=src.at[i],
                dst_ref=dst.at[i],
                send_sem=send.at[i],
                recv_sem=recv.at[i],
                device_id={"dp": col // self.m, "ctx": row * self.m + i},
                device_id_type=pl.DeviceIdType.MESH,
            )
            pl.when(own)(local.wait)
            pl.when(jnp.logical_not(own))(far.wait_recv)

    def middle(self, *refs):
        pass


class Swap:
    def __init__(self, axis, array):
        self.axis, self.array = axis, array

    def plan(self, sizes):
        self.n = sizes[self.axis]
        self.out = jax.ShapeDtypeStruct(self.array.shape, self.array.dtype)
        self.scratch = [pltpu.SemaphoreType.DMA((self.n,))] * 2 + [pltpu.SemaphoreType.DMA(())]

    def start(self, src, dst, send, recv, own):
        me = lax.axis_index(self.axis)
        self.local = pltpu.make_async_copy(src.at[me], dst.at[me], own)
        self.local.start()
        self.copies = []
        for k in range(1, self.n):
            peer = lax.rem(me + k, self.n)
            copy = remote(src.at[peer], dst.at[me], send.at[k], recv.at[k], self.axis, peer)
            copy.start()
            self.copies.append(copy)

    def middle(self, *refs):
        pass

    def finish(self, src, dst, send, recv, own):
        me = lax.axis_index(self.axis)
        for k in range(1, self.n):
            slot = lax.rem(me + self.n - k, self.n)
            remote(
                src.at[slot], dst.at[slot], send.at[k], recv.at[k], self.axis, slot
            ).wait_recv()
        for copy in self.copies:
            copy.wait_send()
        self.local.wait()


class Shift:
    def __init__(self, axis, array, by):
        self.axis, self.array, self.by = axis, array, by

    def plan(self, sizes):
        self.n = sizes[self.axis]
        self.out = jax.ShapeDtypeStruct(self.array.shape, self.array.dtype)
        self.scratch = [pltpu.SemaphoreType.DMA(())] * 2

    def start(self, src, dst, send, recv):
        me = lax.axis_index(self.axis)
        peer = lax.rem(me + self.n + self.by, self.n)
        self.copy = remote(src, dst, send, recv, self.axis, peer)
        self.copy.start()

    def middle(self, *refs):
        pass

    def finish(self, *refs):
        self.copy.wait_recv()
        self.copy.wait_send()


class Reduce:
    axis = "ctx"

    def __init__(self, array):
        self.array = array

    def plan(self, sizes):
        self.n = sizes[self.axis]
        block = self.array.shape[1:]
        chips = self.n // 2
        self.out = jax.ShapeDtypeStruct(block, f32)
        slots = pltpu.VMEM((chips,) + block, self.array.dtype)
        self.scratch = [pltpu.SemaphoreType.DMA((chips,))] * 4 + [slots] * 3

    def start(self, src, dst, psend, precv, send, recv, near, term, far):
        me = lax.axis_index(self.axis)
        chips = self.n // 2
        chip, core = me // 2, me % 2
        partner = me + 1 - 2 * core
        self.copies = []
        for k in list(range(1, chips)) + [0]:
            slot = lax.rem(chip + k, chips) * 2 + 1 - core
            copy = remote(
                src.at[slot], near.at[k], psend.at[k], precv.at[k], self.axis, partner
            )
            copy.start()
            self.copies.append(copy)

    def middle(self, src, dst, psend, precv, send, recv, near, term, far):
        me = lax.axis_index(self.axis)
        chips = self.n // 2
        chip, core = me // 2, me % 2
        partner = me + 1 - 2 * core
        for k in range(1, chips):
            remote(
                src.at[me], near.at[k], psend.at[k], precv.at[k], self.axis, partner
            ).wait_recv()
            peer = lax.rem(chip + k, chips) * 2 + core
            both = src[peer].astype(f32) + near[k].astype(f32)
            term[k] = both.astype(term.dtype)
            copy = remote(term.at[k], far.at[k], send.at[k], recv.at[k], self.axis, peer)
            copy.start()
            self.copies.append(copy)

    def finish(self, src, dst, psend, precv, send, recv, near, term, far):
        me = lax.axis_index(self.axis)
        chips = self.n // 2
        core = me % 2
        partner = me + 1 - 2 * core
        remote(src.at[me], near.at[0], psend.at[0], precv.at[0], self.axis, partner).wait_recv()
        dst[...] = src[me].astype(f32) + near[0].astype(f32)
        for k in range(1, chips):
            remote(
                src.at[me], far.at[k], send.at[k], recv.at[k], self.axis, partner
            ).wait_recv()
            dst[...] += far[k].astype(f32)
        for copy in self.copies:
            copy.wait_send()


def exchange(ident, *tasks):
    sizes = {axis: lax.axis_size(axis) for axis in ("dp", "ctx")}
    for task in tasks:
        task.plan(sizes)
    axes = [axis for axis in ("dp", "ctx") if any(task.axis == axis for task in tasks)]
    everyone = any(task.axis == "all" for task in tasks)
    axes = [] if everyone else axes
    count = len(tasks)

    def kernel(*refs):
        barrier = pltpu.get_barrier_semaphore()
        greeted = 0
        if everyone:
            row, col = lax.axis_index("dp"), lax.axis_index("ctx")
            for i in range(1, sizes["dp"] * sizes["ctx"]):
                other = lax.rem(row * sizes["ctx"] + col + i, sizes["dp"] * sizes["ctx"])
                pl.semaphore_signal(
                    barrier,
                    inc=1,
                    device_id={"dp": other // sizes["ctx"], "ctx": other % sizes["ctx"]},
                    device_id_type=pl.DeviceIdType.MESH,
                )
                greeted += 1
        for axis in axes:
            me, n = lax.axis_index(axis), sizes[axis]
            for k in range(1, n):
                pl.semaphore_signal(
                    barrier,
                    inc=1,
                    device_id={axis: lax.rem(me + k, n)},
                    device_id_type=pl.DeviceIdType.MESH,
                )
            greeted += n - 1
        pl.semaphore_wait(barrier, greeted)
        held, at = [], 2 * count
        for i, task in enumerate(tasks):
            held.append((refs[i], refs[count + i]) + tuple(refs[at : at + len(task.scratch)]))
            at += len(task.scratch)
        for task, own in zip(tasks, held):
            task.start(*own)
        for k in range(sizes["ctx"] // 2 - 1):
            for task, own in zip(tasks, held):
                if isinstance(task, Relay):
                    task.step(k, *own)
                elif k == 0:
                    task.middle(*own)
        for task, own in zip(tasks, held):
            task.finish(*own)

    return pl.pallas_call(
        kernel,
        out_shape=[task.out for task in tasks],
        in_specs=[pl.BlockSpec(memory_space=pltpu.VMEM)] * count,
        out_specs=[pl.BlockSpec(memory_space=pltpu.VMEM)] * count,
        scratch_shapes=[shape for task in tasks for shape in task.scratch],
        compiler_params=pltpu.CompilerParams(
            collective_id=ident, has_side_effects=True, vmem_limit_bytes=60 * 1024 * 1024
        ),
        name=f"exchange_{ident}",
    )(*[task.array for task in tasks])


def spread(axes, sizes, everyone):
    barrier = pltpu.get_barrier_semaphore()
    greeted = 0
    if everyone:
        row, col = lax.axis_index("dp"), lax.axis_index("ctx")
        total = sizes["dp"] * sizes["ctx"]

        def greet(i, carry):
            other = lax.rem(row * sizes["ctx"] + col + i, total)
            pl.semaphore_signal(
                barrier,
                inc=1,
                device_id={"dp": other // sizes["ctx"], "ctx": other % sizes["ctx"]},
                device_id_type=pl.DeviceIdType.MESH,
            )
            return carry

        lax.fori_loop(1, total, greet, 0)
        greeted = total - 1
    else:
        for axis in axes:
            me, n = lax.axis_index(axis), sizes[axis]
            for k in range(1, n):
                pl.semaphore_signal(
                    barrier,
                    inc=1,
                    device_id={axis: lax.rem(me + k, n)},
                    device_id_type=pl.DeviceIdType.MESH,
                )
            greeted += n - 1
    pl.semaphore_wait(barrier, greeted)


def entry(ident, inputs, kv_rows, q_rows, o_rows, gains, down_rows, wide, near):
    sizes = {axis: lax.axis_size(axis) for axis in ("dp", "ctx")}
    dp, ctx = sizes["dp"], sizes["ctx"]
    in_rows, o_w = o_rows.shape
    shape = jax.ShapeDtypeStruct
    x_task, gain_task = Relay(inputs), Relay(gains)
    kv_task = Relay(kv_rows)
    kv_wide = Gather(shape((ctx,) + kv_rows.shape, bf16))
    q_task = Gather(q_rows)
    q_part = shape((dp,) + q_rows.shape, bf16)
    q_more = Shift("ctx", q_part, -1) if near else Relay(q_part)
    o_task = Gather(o_rows)
    o_more = Swap("ctx", shape((ctx, wide, o_w), bf16))
    down_task = Turn(down_rows)
    tasks = [x_task, gain_task, kv_task, kv_wide, q_task, q_more, o_task, o_more, down_task]
    for task in tasks:
        task.plan(sizes)
    outs = [x_task, gain_task, kv_wide, q_task, q_more, o_more, down_task]
    steps = ctx // 2 - 1

    def kernel(*refs):
        x_in, gain_in, kv_in, q_in, o_in, down_in = refs[:6]
        x_out, gain_out, kv_out, q_out, more_out, o_out, down_out = refs[6:13]
        kv_got, o_got, o_cut = refs[13:16]
        sems, at = [], 16
        for task in tasks:
            sems.append(tuple(refs[at : at + len(task.scratch)]))
            at += len(task.scratch)
        spread(("dp", "ctx"), sizes, True)
        held = {}
        pairs = [
            (x_in, x_out),
            (gain_in, gain_out),
            (kv_in, kv_got),
            (kv_got, kv_out),
            (q_in, q_out),
            (q_out, more_out),
            (o_in, o_got),
            (o_cut, o_out),
            (down_in, down_out),
        ]
        for task, pair, sem in zip(tasks, pairs, sems):
            held[task] = pair + sem
        for task in (kv_task, q_task, gain_task, x_task, o_task, down_task):
            task.start(*held[task])
        for k in range(steps):
            kv_task.step(k, *held[kv_task])
            gain_task.step(k, *held[gain_task])
        kv_task.finish(*held[kv_task])
        kv_wide.start(*held[kv_wide])
        q_task.finish(*held[q_task])
        q_more.start(*held[q_more])
        if steps:
            x_task.step(0, *held[x_task])
        o_task.finish(*held[o_task])
        for j in range(ctx):
            for r in range(dp):
                low, high = max(r * in_rows, j * wide), min((r + 1) * in_rows, (j + 1) * wide)
                if low < high:
                    o_cut[j, low - j * wide : high - j * wide] = o_got[
                        r, low - r * in_rows : high - r * in_rows
                    ]
            used = min(max(HEADS * HEAD_DIM - j * wide, 0), wide)
            if used < wide:
                o_cut[j, used:] = jnp.zeros((wide - used, o_w), bf16)
        o_more.start(*held[o_more])
        for k in range(1, steps):
            x_task.step(k, *held[x_task])
        if not near:
            for k in range(steps):
                q_more.step(k, *held[q_more])
        for task in (gain_task, x_task, kv_wide, q_more, o_more, down_task):
            task.finish(*held[task])

    return pl.pallas_call(
        kernel,
        out_shape=[task.out for task in outs],
        in_specs=[pl.BlockSpec(memory_space=pltpu.VMEM)] * 6,
        out_specs=[pl.BlockSpec(memory_space=pltpu.VMEM)] * len(outs),
        scratch_shapes=[
            pltpu.VMEM((ctx,) + kv_rows.shape, bf16),
            pltpu.VMEM((dp, in_rows, o_w), bf16),
            pltpu.VMEM((ctx, wide, o_w), bf16),
        ]
        + [shape for task in tasks for shape in task.scratch],
        compiler_params=pltpu.CompilerParams(
            collective_id=ident, has_side_effects=True, vmem_limit_bytes=60 * 1024 * 1024
        ),
        name=f"exchange_{ident}",
    )(inputs, gains, kv_rows, q_rows, o_rows, down_rows)


def mm(a, b, dims):
    return lax.dot_general(a, b, ((dims[:1], dims[1:]), ((), ())), preferred_element_type=f32)


def nn(a, b):
    return mm(a, b, (1, 0))


def nt(a, b):
    return mm(a, b, (1, 1))


def tn(a, b):
    return mm(a, b, (0, 0))


def turned(rows):
    width = rows.shape[-1]
    parts = rows.reshape(-1, 2, HEAD_DIM // 2, width)
    return jnp.concatenate([-parts[:, 1:], parts[:, :1]], axis=1).reshape(rows.shape)


def rope_tables(row_count):
    half = HEAD_DIM // 2
    frequency = rope_base ** (-jnp.arange(half).astype(f32) * 2.0 / HEAD_DIM)
    angles = jnp.arange(row_count).astype(f32)[:, None] * frequency[None, :]
    return jnp.tile(jnp.cos(angles), (1, 2)), jnp.tile(jnp.sin(angles), (1, 2))


def norm_backward(hidden, inverse, gain_vec, upstream):
    scaled = upstream * gain_vec
    cubed = inverse * inverse * inverse
    d_hidden = (
        inverse * scaled
        - hidden
        * cubed
        * jnp.sum(scaled * hidden, axis=-1, keepdims=True)
        / hidden.shape[-1]
    )
    return d_hidden, jnp.sum(upstream * hidden * inverse, axis=0)


def inverse_rms(hidden):
    return lax.rsqrt(jnp.mean(hidden * hidden, axis=-1, keepdims=True) + epsilon)


def masked_scores(queries, keys, first):
    scores = nt(queries, keys) * HEAD_DIM ** (-0.5)
    rows = first + lax.broadcasted_iota(jnp.int32, scores.shape, 0)
    return jnp.where(rows >= lax.broadcasted_iota(jnp.int32, scores.shape, 1), scores, -1e30)


def shards(
    inputs, cotangent, w_query, w_key, w_value, w_output, w_gate, w_up, w_down, gain_attn, gain_ffn
):
    dp, ctx = lax.axis_size("dp"), lax.axis_size("ctx")
    me = lax.axis_index("ctx")
    rows, width = inputs.shape
    length = rows * ctx
    q_w, k_w, o_w, f_w = w_query.shape[1], w_key.shape[1], w_output.shape[1], w_gate.shape[1]
    in_rows = w_query.shape[0]
    held = -(-HEADS // ctx)
    wide = held * HEAD_DIM
    total = ctx * wide
    near = all(wide * j >= q_w * j and wide * (j + 1) <= q_w * (j + 2) for j in range(ctx))

    each = ctx // dp
    gains = jnp.stack([gain_attn, gain_ffn])
    kv_rows = jnp.concatenate([w_key, w_value], axis=1).T
    down_rows = w_down.reshape(each, f_w, o_w).transpose(0, 2, 1)
    w_gu = lax.all_gather(jnp.concatenate([w_gate, w_up], axis=1), "dp", tiled=True)
    all_x, all_gains, kv_all, q_part, q_next, o_mine, down_rows = entry(
        0, inputs, kv_rows, w_query.T, w_output, gains, down_rows, wide, near
    )
    w_down_t = lax.all_gather(down_rows.reshape(each * o_w, f_w), "dp", tiled=True)
    cot_late, all_x = lax.optimization_barrier((cotangent, all_x))
    cot_full = lax.all_gather(cot_late, "ctx", tiled=True)
    kv_all = kv_all.transpose(1, 2, 0, 3).reshape(ctx, 2 * k_w, width)
    if near:
        q_part = q_part.transpose(1, 0, 2).reshape(q_w, width)
        q_next = q_next.transpose(1, 0, 2).reshape(q_w, width)
        q_rows = jnp.concatenate(
            [q_part, jnp.where(me == ctx - 1, jnp.zeros_like(q_next), q_next)], axis=0
        )
        q_rows = jnp.pad(q_rows, ((0, wide), (0, 0)))
        wq = lax.dynamic_slice(q_rows, (me * (wide - q_w), 0), (wide, width))
    else:
        q_next = q_next.transpose(0, 2, 1, 3)
        q_rows = jnp.pad(q_next.reshape(-1, width), ((0, total - HEADS * HEAD_DIM), (0, 0)))
        wq = lax.dynamic_slice(q_rows, (me * wide, 0), (wide, width))
    wk_all = kv_all[:, :k_w].reshape(-1, width)
    wv_all = kv_all[:, k_w:].reshape(-1, width)
    kv_head = [jnp.minimum((me * held + h) // GROUP, KV_HEADS - 1) for h in range(held)]

    def of_heads(array):
        return jnp.concatenate(
            [lax.dynamic_slice(array, (k * HEAD_DIM, 0), (HEAD_DIM, width)) for k in kv_head]
        )

    wk, wv = of_heads(wk_all), of_heads(wv_all)
    wo = o_mine.transpose(1, 0, 2).reshape(wide, ctx * o_w)
    gain_rows = all_gains.transpose(1, 0, 2).reshape(2, width).astype(f32)
    gain_one, gain_two = gain_rows[0], gain_rows[1]

    x_full = all_x.reshape(length, width)
    hid_full = x_full.astype(f32)
    normed_one = (hid_full * inverse_rms(hid_full) * gain_one).astype(bf16)
    cosine, sine = rope_tables(length)
    cosine, sine = jnp.tile(cosine, (1, held)), jnp.tile(sine, (1, held))
    projected = nt(normed_one, jnp.concatenate([wq, turned(wq), wk, turned(wk), wv]))
    q_a, q_b, k_a, k_b, v_a = [projected[:, i * wide : (i + 1) * wide] for i in range(5)]
    queries = (q_a * cosine + q_b * sine).astype(bf16)
    q_side = (q_a * sine - q_b * cosine).astype(bf16)
    keys = (k_a * cosine + k_b * sine).astype(bf16)
    k_side = (k_a * sine - k_b * cosine).astype(bf16)
    values = v_a.astype(bf16)

    def head(array, h):
        return array[:, h * HEAD_DIM : (h + 1) * HEAD_DIM]

    chunk = min(256, length)
    firsts = list(range(0, length, chunk))
    attended, logsums = [], []
    for h in range(held):
        q_h, k_h, v_h = head(queries, h), head(keys, h), head(values, h)
        outs, logs = [], []
        for first in firsts:
            last = first + chunk
            scores = masked_scores(q_h[first:last], k_h[:last], first)
            top = jnp.max(scores, axis=-1, keepdims=True)
            expo = jnp.exp(scores - top)
            weight = jnp.sum(expo, axis=-1, keepdims=True)
            outs.append(nn(expo.astype(bf16), v_h[:last]) / weight)
            logs.append(top + jnp.log(weight))
        real = me * held + h < HEADS
        attended.append(jnp.where(real, jnp.concatenate(outs), 0.0).astype(bf16))
        logsums.append(logs)
    attended_all = jnp.concatenate(attended, axis=1)

    (mid_sum,) = exchange(2, Reduce(nn(attended_all, wo).astype(bf16).reshape(ctx, rows, width)))
    hidden = inputs.astype(f32)
    middle = hidden + mid_sum
    inv_two = inverse_rms(middle)
    normed_two_mine = (middle * inv_two * gain_two).astype(bf16)
    (normed_two,) = exchange(3, Relay(normed_two_mine))
    normed_two = normed_two.reshape(length, width)

    both = nn(normed_two, w_gu)
    gate_pre, up_pre = both[:, :f_w], both[:, f_w:]
    d_mixed = nn(cot_full, w_down_t)
    sigma = jax.nn.sigmoid(gate_pre)
    silu_gate = gate_pre * sigma
    mixed_act = (silu_gate * up_pre).astype(bf16)
    d_gate = (d_mixed * up_pre * sigma * (1.0 + gate_pre * (1.0 - sigma))).astype(bf16)
    d_up = (d_mixed * silu_gate).astype(bf16)
    d_both = jnp.concatenate([d_gate, d_up], axis=1)
    out_part = nt(mixed_act, w_down_t).astype(bf16)
    d_two_part = nt(d_both, w_gu).astype(bf16)
    g_down = tn(cot_full, mixed_act).astype(bf16)
    g_gu = tn(normed_two, d_both).astype(bf16)

    (d_norm_two,) = exchange(4, Reduce(d_two_part.reshape(ctx, rows, width)))
    g_three = lax.psum_scatter(jnp.concatenate([g_gu, g_down], axis=1), "dp", tiled=True)
    g_gu_sum = g_three[:, : 2 * f_w].astype(f32)
    g_down_part = g_three[:, 2 * f_w :].reshape(each, o_w, f_w)
    out_sum = lax.psum_scatter(out_part, "ctx", tiled=True).astype(f32)
    d_mid_norm, g_gain_two = norm_backward(middle, inv_two, gain_two, d_norm_two)
    d_middle = cotangent.astype(f32) + d_mid_norm
    (d_mid_full,) = exchange(5, Relay(d_middle.astype(bf16)))
    out_act = (middle + out_sum).astype(bf16)
    d_mid_full = d_mid_full.reshape(length, width)

    g_out = tn(d_mid_full, attended_all).astype(bf16)
    d_attended = nt(d_mid_full, wo).astype(bf16)
    dq_all, dk_all, dv_all = [], [], []
    for h in range(held):
        q_h, k_h, v_h = head(queries, h), head(keys, h), head(values, h)
        q_two = jnp.concatenate([q_h, head(q_side, h)], axis=1)
        k_two = jnp.concatenate([k_h, head(k_side, h)], axis=1)
        grad_h = head(d_attended, h)
        delta = jnp.sum(grad_h.astype(f32) * attended[h].astype(f32), axis=-1, keepdims=True)
        dq_parts = []
        dk = jnp.zeros((length, 2 * HEAD_DIM), f32)
        dv = jnp.zeros((length, HEAD_DIM), f32)
        for i, first in enumerate(firsts):
            last = first + chunk
            probs = jnp.exp(masked_scores(q_h[first:last], k_h[:last], first) - logsums[h][i])
            d_probs = nt(grad_h[first:last], v_h[:last])
            d_scores = (probs * (d_probs - delta[first:last])).astype(bf16)
            dq_parts.append(nn(d_scores, k_two[:last]))
            tail = ((0, length - last), (0, 0))
            dk = dk + jnp.pad(tn(d_scores, q_two[first:last]), tail)
            dv = dv + jnp.pad(tn(probs.astype(bf16), grad_h[first:last]), tail)
        dq = jnp.concatenate(dq_parts)
        real = me * held + h < HEADS
        cos_h, sin_h = head(cosine, 0), head(sine, 0)

        def back(two):
            turned_back = two[:, :HEAD_DIM] * cos_h + two[:, HEAD_DIM:] * sin_h
            return jnp.where(real, turned_back * HEAD_DIM ** (-0.5), 0.0).astype(bf16)

        dq_all.append(back(dq))
        dk_all.append(back(dk))
        dv_all.append(jnp.where(real, dv, 0.0).astype(bf16))
    d_qkv = jnp.concatenate(dq_all + dk_all + dv_all, axis=1)
    d_one_f = nn(d_qkv, jnp.concatenate([wq, wk, wv]))
    d_one_part = d_one_f.astype(bf16)
    g_gain_one = jnp.sum(d_one_f * hid_full * inverse_rms(hid_full), axis=0)
    g_gain = jnp.stack([g_gain_one, g_gain_two]).reshape(2, ctx, -1).transpose(1, 0, 2)
    g_qkv = tn(d_qkv, normed_one).astype(bf16)
    g_qkv = g_qkv.reshape(3 * wide, dp, in_rows).transpose(1, 0, 2)

    d_norm_one, g_out_all, g_qkv_all, g_down_mine, gain_all = exchange(
        6,
        Reduce(d_one_part.reshape(ctx, rows, width)),
        Swap("ctx", g_out.reshape(ctx, o_w, wide)),
        Swap("dp", g_qkv),
        Turn(g_down_part),
        Swap("ctx", g_gain),
    )
    inv_one = inverse_rms(hidden)
    d_in_norm, _ = norm_backward(hidden, inv_one, gain_one, d_norm_one)
    grad_input = d_middle + d_in_norm
    g_down_sum = g_down_mine.astype(f32).transpose(0, 2, 1).reshape(each * f_w, o_w)
    g_qkv_sum = jnp.sum(g_qkv_all.astype(f32), axis=0)
    gq_part = g_qkv_sum[:wide].astype(bf16)
    g_kv = jnp.zeros((2, KV_HEADS * HEAD_DIM, in_rows), f32)
    for kind in range(2):
        for h in range(held):
            at = (kind, kv_head[h] * HEAD_DIM, 0)
            base = (1 + kind) * wide + h * HEAD_DIM
            block = lax.dynamic_slice(g_kv, at, (1, HEAD_DIM, in_rows))
            g_kv = lax.dynamic_update_slice(
                g_kv, block + g_qkv_sum[None, base : base + HEAD_DIM], at
            )
    g_kv = g_kv.astype(bf16).reshape(2, ctx, k_w, in_rows).transpose(1, 0, 2, 3)
    g_kv = g_kv.reshape(ctx, 2 * k_w, in_rows)
    g_out_rows = g_out_all.transpose(0, 2, 1).reshape(total, o_w)[: HEADS * HEAD_DIM]
    if near:
        q_task = Shift("ctx", gq_part, 1)
    else:
        q_place = lax.dynamic_update_slice(
            jnp.zeros((total, in_rows), bf16), gq_part, (me * wide, 0)
        )
        q_task = Reduce(q_place[: HEADS * HEAD_DIM].reshape(ctx, q_w, in_rows))
    kv_sum, q_got, g_out_mine, gain_all = exchange(
        7,
        Reduce(g_kv),
        q_task,
        Swap("dp", g_out_rows.reshape(dp, in_rows, o_w)),
        Gather(jnp.sum(gain_all, axis=0)),
    )
    if near:
        q_rows = jnp.concatenate([q_got, gq_part], axis=0)
        g_query = lax.dynamic_slice(
            q_rows, (wide - me * (wide - q_w), 0), (q_w, in_rows)
        ).astype(f32)
    else:
        g_query = q_got
    gain_sum = jnp.sum(gain_all, axis=0)
    return (
        out_act,
        grad_input,
        g_query.T,
        kv_sum[:k_w].T,
        kv_sum[k_w:].T,
        jnp.sum(g_out_mine.astype(f32), axis=0),
        g_gu_sum[:, :f_w],
        g_gu_sum[:, f_w:],
        g_down_sum,
        gain_sum[0],
        gain_sum[1],
    )


def solution(mesh):
    blocks = P(("dp", "ctx"), None)
    matrix = P("dp", "ctx")
    in_specs = (blocks,) * 2 + (matrix,) * 7 + (P("ctx"),) * 2
    return jax.shard_map(shards, mesh=mesh, in_specs=in_specs, out_specs=in_specs, check_vma=False)
```

```python
import functools

import jax
import jax.numpy as jnp
from jax import lax
from jax.experimental import pallas as pl
from jax.experimental.pallas import tpu as pltpu
from jax.sharding import PartitionSpec as P

HEADS = 15
KV_HEADS = 5
HEAD_DIM = 64
GROUP = HEADS // KV_HEADS

epsilon = 1e-05
rope_base = 10000.0
bf16 = jnp.bfloat16
f32 = jnp.float32


def remote(src, dst, send, recv, axis, peer):
    return pltpu.make_async_remote_copy(
        src_ref=src,
        dst_ref=dst,
        send_sem=send,
        recv_sem=recv,
        device_id={axis: peer},
        device_id_type=pl.DeviceIdType.MESH,
    )


class Gather:
    axis = "dp"

    def __init__(self, array):
        self.array = array

    def plan(self, sizes):
        self.n = sizes[self.axis]
        self.out = jax.ShapeDtypeStruct((self.n,) + self.array.shape, self.array.dtype)
        self.scratch = [pltpu.SemaphoreType.DMA((self.n,))] * 2 + [pltpu.SemaphoreType.DMA(())]

    def start(self, src, dst, send, recv, own):
        me = lax.axis_index(self.axis)
        self.local = pltpu.make_async_copy(src, dst.at[me], own)
        self.local.start()
        self.copies = []
        for k in range(1, self.n):
            peer = lax.rem(me + k, self.n)
            copy = remote(src, dst.at[me], send.at[k], recv.at[k], self.axis, peer)
            copy.start()
            self.copies.append(copy)

    def middle(self, *refs):
        pass

    def finish(self, src, dst, send, recv, own):
        me = lax.axis_index(self.axis)
        for k in range(1, self.n):
            slot = lax.rem(me + self.n - k, self.n)
            remote(src, dst.at[slot], send.at[k], recv.at[k], self.axis, slot).wait_recv()
        for copy in self.copies:
            copy.wait_send()
        self.local.wait()


class Relay:
    axis = "ctx"

    def __init__(self, array):
        self.array = array

    def plan(self, sizes):
        self.n = sizes[self.axis]
        chips = self.n // 2
        self.out = jax.ShapeDtypeStruct((self.n,) + self.array.shape, self.array.dtype)
        self.scratch = [pltpu.SemaphoreType.DMA((chips,))] * 6 + [pltpu.SemaphoreType.DMA(())]

    def at(self):
        me = lax.axis_index(self.axis)
        chip, core = me // 2, me % 2
        return me, chip, core, me + 1 - 2 * core, self.n // 2

    def start(self, src, dst, rs, rr, ls, lr, ps, pr, own):
        me, chip, core, partner, chips = self.at()

        @pl.when(chip < chips - 1)
        def _():
            remote(src, dst.at[me], rs.at[0], rr.at[0], self.axis, me + 2).start()

        @pl.when(chip > 0)
        def _():
            remote(src, dst.at[me], ls.at[0], lr.at[0], self.axis, me - 2).start()

        remote(src, dst.at[me], ps.at[chip], pr.at[chip], self.axis, partner).start()
        pltpu.make_async_copy(src, dst.at[me], own).start()

    def step(self, k, src, dst, rs, rr, ls, lr, ps, pr, own):
        me, chip, core, partner, chips = self.at()

        def arrived(slot_chip, way, send, recv):
            slot = slot_chip * 2 + core
            back = me - 2 * way
            remote(dst.at[slot], dst.at[slot], send.at[k], recv.at[k], self.axis, back).wait_recv()

            @pl.when(jnp.logical_and(chip + way >= 0, chip + way < chips))
            def _():
                remote(
                    dst.at[slot],
                    dst.at[slot],
                    send.at[k + 1],
                    recv.at[k + 1],
                    self.axis,
                    me + 2 * way,
                ).start()

            remote(
                dst.at[slot], dst.at[slot], ps.at[slot_chip], pr.at[slot_chip], self.axis, partner
            ).start()

        @pl.when(chip - 1 - k >= 0)
        def _():
            arrived(chip - 1 - k, 1, rs, rr)

        @pl.when(chip + 1 + k < chips)
        def _():
            arrived(chip + 1 + k, -1, ls, lr)

    def finish(self, src, dst, rs, rr, ls, lr, ps, pr, own):
        me, chip, core, partner, chips = self.at()
        for c in range(chips):
            slot = 2 * c + 1 - core
            remote(src, dst.at[slot], ps.at[c], pr.at[c], self.axis, partner).wait_recv()
        for c in range(chips):
            remote(src, dst.at[2 * c + core], ps.at[c], pr.at[c], self.axis, partner).wait_send()
        for k in range(chips - 1):

            @pl.when(jnp.logical_and(chip < chips - 1, k <= chip))
            def _():
                remote(src, dst.at[me], rs.at[k], rr.at[k], self.axis, me + 2).wait_send()

            @pl.when(jnp.logical_and(chip > 0, k <= chips - 1 - chip))
            def _():
                remote(src, dst.at[me], ls.at[k], lr.at[k], self.axis, me - 2).wait_send()

        pltpu.make_async_copy(src, dst.at[me], own).wait()


class Turn:
    axis = "all"

    def __init__(self, array):
        self.array = array

    def plan(self, sizes):
        self.dp, self.n = sizes["dp"], sizes["ctx"]
        self.m = self.n // self.dp
        self.out = jax.ShapeDtypeStruct(self.array.shape, self.array.dtype)
        self.scratch = [pltpu.SemaphoreType.DMA((self.m,))] * 2

    def each(self, src, dst, send, recv):
        row, col = lax.axis_index("dp"), lax.axis_index("ctx")
        put = col % self.m
        for i in range(self.m):
            to_row, to_col = col // self.m, row * self.m + i
            here = jnp.logical_and(to_row == row, to_col == col)
            far = pltpu.make_async_remote_copy(
                src_ref=src.at[i],
                dst_ref=dst.at[put],
                send_sem=send.at[i],
                recv_sem=recv.at[put],
                device_id={"dp": to_row, "ctx": to_col},
                device_id_type=pl.DeviceIdType.MESH,
            )
            local = pltpu.make_async_copy(src.at[i], dst.at[put], recv.at[put])
            yield i, here, far, local

    def start(self, *refs):
        for i, here, far, local in self.each(*refs):
            pl.when(here)(local.start)
            pl.when(jnp.logical_not(here))(far.start)

    def finish(self, src, dst, send, recv):
        row, col = lax.axis_index("dp"), lax.axis_index("ctx")
        for i, here, far, local in self.each(src, dst, send, recv):
            pl.when(jnp.logical_not(here))(far.wait_send)
        for i in range(self.m):
            own = jnp.logical_and(col // self.m == row, row * self.m + i == col)
            local = pltpu.make_async_copy(src.at[i], dst.at[i], recv.at[i])
            far = pltpu.make_async_remote_copy(
                src_ref=src.at[i],
                dst_ref=dst.at[i],
                send_sem=send.at[i],
                recv_sem=recv.at[i],
                device_id={"dp": col // self.m, "ctx": row * self.m + i},
                device_id_type=pl.DeviceIdType.MESH,
            )
            pl.when(own)(local.wait)
            pl.when(jnp.logical_not(own))(far.wait_recv)

    def middle(self, *refs):
        pass


class Swap:
    def __init__(self, axis, array):
        self.axis, self.array = axis, array

    def plan(self, sizes):
        self.n = sizes[self.axis]
        self.out = jax.ShapeDtypeStruct(self.array.shape, self.array.dtype)
        self.scratch = [pltpu.SemaphoreType.DMA((self.n,))] * 2 + [pltpu.SemaphoreType.DMA(())]

    def start(self, src, dst, send, recv, own):
        me = lax.axis_index(self.axis)
        self.local = pltpu.make_async_copy(src.at[me], dst.at[me], own)
        self.local.start()
        self.copies = []
        for k in range(1, self.n):
            peer = lax.rem(me + k, self.n)
            copy = remote(src.at[peer], dst.at[me], send.at[k], recv.at[k], self.axis, peer)
            copy.start()
            self.copies.append(copy)

    def middle(self, *refs):
        pass

    def finish(self, src, dst, send, recv, own):
        me = lax.axis_index(self.axis)
        for k in range(1, self.n):
            slot = lax.rem(me + self.n - k, self.n)
            remote(
                src.at[slot], dst.at[slot], send.at[k], recv.at[k], self.axis, slot
            ).wait_recv()
        for copy in self.copies:
            copy.wait_send()
        self.local.wait()


class Shift:
    def __init__(self, axis, array, by):
        self.axis, self.array, self.by = axis, array, by

    def plan(self, sizes):
        self.n = sizes[self.axis]
        self.out = jax.ShapeDtypeStruct(self.array.shape, self.array.dtype)
        self.scratch = [pltpu.SemaphoreType.DMA(())] * 2

    def start(self, src, dst, send, recv):
        me = lax.axis_index(self.axis)
        peer = lax.rem(me + self.n + self.by, self.n)
        self.copy = remote(src, dst, send, recv, self.axis, peer)
        self.copy.start()

    def middle(self, *refs):
        pass

    def finish(self, *refs):
        self.copy.wait_recv()
        self.copy.wait_send()


class Reduce:
    axis = "ctx"

    def __init__(self, array):
        self.array = array

    def plan(self, sizes):
        self.n = sizes[self.axis]
        block = self.array.shape[1:]
        chips = self.n // 2
        self.out = jax.ShapeDtypeStruct(block, f32)
        slots = pltpu.VMEM((chips,) + block, self.array.dtype)
        self.scratch = [pltpu.SemaphoreType.DMA((chips,))] * 4 + [slots] * 3

    def start(self, src, dst, psend, precv, send, recv, near, term, far):
        me = lax.axis_index(self.axis)
        chips = self.n // 2
        chip, core = me // 2, me % 2
        partner = me + 1 - 2 * core
        self.copies = []
        for k in list(range(1, chips)) + [0]:
            slot = lax.rem(chip + k, chips) * 2 + 1 - core
            copy = remote(
                src.at[slot], near.at[k], psend.at[k], precv.at[k], self.axis, partner
            )
            copy.start()
            self.copies.append(copy)

    def middle(self, src, dst, psend, precv, send, recv, near, term, far):
        me = lax.axis_index(self.axis)
        chips = self.n // 2
        chip, core = me // 2, me % 2
        partner = me + 1 - 2 * core
        for k in range(1, chips):
            remote(
                src.at[me], near.at[k], psend.at[k], precv.at[k], self.axis, partner
            ).wait_recv()
            peer = lax.rem(chip + k, chips) * 2 + core
            both = src[peer].astype(f32) + near[k].astype(f32)
            term[k] = both.astype(term.dtype)
            copy = remote(term.at[k], far.at[k], send.at[k], recv.at[k], self.axis, peer)
            copy.start()
            self.copies.append(copy)

    def finish(self, src, dst, psend, precv, send, recv, near, term, far):
        me = lax.axis_index(self.axis)
        chips = self.n // 2
        core = me % 2
        partner = me + 1 - 2 * core
        remote(src.at[me], near.at[0], psend.at[0], precv.at[0], self.axis, partner).wait_recv()
        dst[...] = src[me].astype(f32) + near[0].astype(f32)
        for k in range(1, chips):
            remote(
                src.at[me], far.at[k], send.at[k], recv.at[k], self.axis, partner
            ).wait_recv()
            dst[...] += far[k].astype(f32)
        for copy in self.copies:
            copy.wait_send()


def exchange(ident, *tasks):
    sizes = {axis: lax.axis_size(axis) for axis in ("dp", "ctx")}
    for task in tasks:
        task.plan(sizes)
    axes = [axis for axis in ("dp", "ctx") if any(task.axis == axis for task in tasks)]
    everyone = any(task.axis == "all" for task in tasks)
    axes = [] if everyone else axes
    count = len(tasks)

    def kernel(*refs):
        barrier = pltpu.get_barrier_semaphore()
        greeted = 0
        if everyone:
            row, col = lax.axis_index("dp"), lax.axis_index("ctx")
            for i in range(1, sizes["dp"] * sizes["ctx"]):
                other = lax.rem(row * sizes["ctx"] + col + i, sizes["dp"] * sizes["ctx"])
                pl.semaphore_signal(
                    barrier,
                    inc=1,
                    device_id={"dp": other // sizes["ctx"], "ctx": other % sizes["ctx"]},
                    device_id_type=pl.DeviceIdType.MESH,
                )
                greeted += 1
        for axis in axes:
            me, n = lax.axis_index(axis), sizes[axis]
            for k in range(1, n):
                pl.semaphore_signal(
                    barrier,
                    inc=1,
                    device_id={axis: lax.rem(me + k, n)},
                    device_id_type=pl.DeviceIdType.MESH,
                )
            greeted += n - 1
        pl.semaphore_wait(barrier, greeted)
        held, at = [], 2 * count
        for i, task in enumerate(tasks):
            held.append((refs[i], refs[count + i]) + tuple(refs[at : at + len(task.scratch)]))
            at += len(task.scratch)
        for task, own in zip(tasks, held):
            task.start(*own)
        for k in range(sizes["ctx"] // 2 - 1):
            for task, own in zip(tasks, held):
                if isinstance(task, Relay):
                    task.step(k, *own)
                elif k == 0:
                    task.middle(*own)
        for task, own in zip(tasks, held):
            task.finish(*own)

    return pl.pallas_call(
        kernel,
        out_shape=[task.out for task in tasks],
        in_specs=[pl.BlockSpec(memory_space=pltpu.VMEM)] * count,
        out_specs=[pl.BlockSpec(memory_space=pltpu.VMEM)] * count,
        scratch_shapes=[shape for task in tasks for shape in task.scratch],
        compiler_params=pltpu.CompilerParams(
            collective_id=ident, has_side_effects=True, vmem_limit_bytes=60 * 1024 * 1024
        ),
        name=f"exchange_{ident}",
    )(*[task.array for task in tasks])


def spread(axes, sizes, everyone):
    barrier = pltpu.get_barrier_semaphore()
    greeted = 0
    if everyone:
        row, col = lax.axis_index("dp"), lax.axis_index("ctx")
        total = sizes["dp"] * sizes["ctx"]

        def greet(i, carry):
            other = lax.rem(row * sizes["ctx"] + col + i, total)
            pl.semaphore_signal(
                barrier,
                inc=1,
                device_id={"dp": other // sizes["ctx"], "ctx": other % sizes["ctx"]},
                device_id_type=pl.DeviceIdType.MESH,
            )
            return carry

        lax.fori_loop(1, total, greet, 0)
        greeted = total - 1
    else:
        for axis in axes:
            me, n = lax.axis_index(axis), sizes[axis]
            for k in range(1, n):
                pl.semaphore_signal(
                    barrier,
                    inc=1,
                    device_id={axis: lax.rem(me + k, n)},
                    device_id_type=pl.DeviceIdType.MESH,
                )
            greeted += n - 1
    pl.semaphore_wait(barrier, greeted)


def entry(ident, inputs, kv_rows, q_rows, o_rows, gains, down_rows, wide, near):
    sizes = {axis: lax.axis_size(axis) for axis in ("dp", "ctx")}
    dp, ctx = sizes["dp"], sizes["ctx"]
    in_rows, o_w = o_rows.shape
    shape = jax.ShapeDtypeStruct
    x_task, gain_task = Relay(inputs), Relay(gains)
    kv_task = Relay(kv_rows)
    kv_wide = Gather(shape((ctx,) + kv_rows.shape, bf16))
    q_task = Gather(q_rows)
    q_part = shape((dp,) + q_rows.shape, bf16)
    q_more = Shift("ctx", q_part, -1) if near else Relay(q_part)
    o_task = Gather(o_rows)
    o_more = Swap("ctx", shape((ctx, wide, o_w), bf16))
    down_task = Turn(down_rows)
    tasks = [x_task, gain_task, kv_task, kv_wide, q_task, q_more, o_task, o_more, down_task]
    for task in tasks:
        task.plan(sizes)
    outs = [x_task, gain_task, kv_wide, q_task, q_more, o_more, down_task]
    steps = ctx // 2 - 1

    def kernel(*refs):
        x_in, gain_in, kv_in, q_in, o_in, down_in = refs[:6]
        x_out, gain_out, kv_out, q_out, more_out, o_out, down_out = refs[6:13]
        kv_got, o_got, o_cut = refs[13:16]
        sems, at = [], 16
        for task in tasks:
            sems.append(tuple(refs[at : at + len(task.scratch)]))
            at += len(task.scratch)
        spread(("dp", "ctx"), sizes, True)
        held = {}
        pairs = [
            (x_in, x_out),
            (gain_in, gain_out),
            (kv_in, kv_got),
            (kv_got, kv_out),
            (q_in, q_out),
            (q_out, more_out),
            (o_in, o_got),
            (o_cut, o_out),
            (down_in, down_out),
        ]
        for task, pair, sem in zip(tasks, pairs, sems):
            held[task] = pair + sem
        for task in (kv_task, q_task, gain_task, x_task, o_task, down_task):
            task.start(*held[task])
        for k in range(steps):
            kv_task.step(k, *held[kv_task])
            gain_task.step(k, *held[gain_task])
        kv_task.finish(*held[kv_task])
        kv_wide.start(*held[kv_wide])
        q_task.finish(*held[q_task])
        q_more.start(*held[q_more])
        if steps:
            x_task.step(0, *held[x_task])
        o_task.finish(*held[o_task])
        for j in range(ctx):
            for r in range(dp):
                low, high = max(r * in_rows, j * wide), min((r + 1) * in_rows, (j + 1) * wide)
                if low < high:
                    o_cut[j, low - j * wide : high - j * wide] = o_got[
                        r, low - r * in_rows : high - r * in_rows
                    ]
            used = min(max(HEADS * HEAD_DIM - j * wide, 0), wide)
            if used < wide:
                o_cut[j, used:] = jnp.zeros((wide - used, o_w), bf16)
        o_more.start(*held[o_more])
        for k in range(1, steps):
            x_task.step(k, *held[x_task])
        if not near:
            for k in range(steps):
                q_more.step(k, *held[q_more])
        for task in (gain_task, x_task, kv_wide, q_more, o_more, down_task):
            task.finish(*held[task])

    return pl.pallas_call(
        kernel,
        out_shape=[task.out for task in outs],
        in_specs=[pl.BlockSpec(memory_space=pltpu.VMEM)] * 6,
        out_specs=[pl.BlockSpec(memory_space=pltpu.VMEM)] * len(outs),
        scratch_shapes=[
            pltpu.VMEM((ctx,) + kv_rows.shape, bf16),
            pltpu.VMEM((dp, in_rows, o_w), bf16),
            pltpu.VMEM((ctx, wide, o_w), bf16),
        ]
        + [shape for task in tasks for shape in task.scratch],
        compiler_params=pltpu.CompilerParams(
            collective_id=ident, has_side_effects=True, vmem_limit_bytes=60 * 1024 * 1024
        ),
        name=f"exchange_{ident}",
    )(inputs, gains, kv_rows, q_rows, o_rows, down_rows)


def mm(a, b, dims):
    return lax.dot_general(a, b, ((dims[:1], dims[1:]), ((), ())), preferred_element_type=f32)


def nn(a, b):
    return mm(a, b, (1, 0))


def nt(a, b):
    return mm(a, b, (1, 1))


def tn(a, b):
    return mm(a, b, (0, 0))


def turned(rows):
    width = rows.shape[-1]
    parts = rows.reshape(-1, 2, HEAD_DIM // 2, width)
    return jnp.concatenate([-parts[:, 1:], parts[:, :1]], axis=1).reshape(rows.shape)


def rope_tables(row_count):
    half = HEAD_DIM // 2
    frequency = rope_base ** (-jnp.arange(half).astype(f32) * 2.0 / HEAD_DIM)
    angles = jnp.arange(row_count).astype(f32)[:, None] * frequency[None, :]
    return jnp.tile(jnp.cos(angles), (1, 2)), jnp.tile(jnp.sin(angles), (1, 2))


def norm_backward(hidden, inverse, gain_vec, upstream):
    scaled = upstream * gain_vec
    cubed = inverse * inverse * inverse
    d_hidden = (
        inverse * scaled
        - hidden
        * cubed
        * jnp.sum(scaled * hidden, axis=-1, keepdims=True)
        / hidden.shape[-1]
    )
    return d_hidden, jnp.sum(upstream * hidden * inverse, axis=0)


def inverse_rms(hidden):
    return lax.rsqrt(jnp.mean(hidden * hidden, axis=-1, keepdims=True) + epsilon)


class Line:
    axis = "ctx"

    def __init__(self, n):
        self.n, self.chips = n, n // 2
        self.scratch = [pltpu.SemaphoreType.DMA((self.chips,))] * 6

    def hold(self, dst, sems):
        self.dst = dst
        self.rs, self.rr, self.ls, self.lr, self.ps, self.pr = sems
        self.me = lax.axis_index(self.axis)
        self.chip, self.core = self.me // 2, self.me % 2
        self.partner = self.me + 1 - 2 * self.core

    def copy(self, slot, send, recv, peer):
        return remote(self.dst.at[slot], self.dst.at[slot], send, recv, self.axis, peer)

    def start(self):
        me, chip = self.me, self.chip
        pl.when(chip < self.chips - 1)(self.copy(me, self.rs.at[0], self.rr.at[0], me + 2).start)
        pl.when(chip > 0)(self.copy(me, self.ls.at[0], self.lr.at[0], me - 2).start)
        self.copy(me, self.ps.at[chip], self.pr.at[chip], self.partner).start()

    def step(self, k):
        me, chip, chips = self.me, self.chip, self.chips

        def arrived(at, way, send, recv):
            slot = at * 2 + self.core
            self.copy(slot, send.at[k], recv.at[k], me - 2 * way).wait_recv()

            @pl.when(jnp.logical_and(chip + way >= 0, chip + way < chips))
            def _():
                self.copy(slot, send.at[k + 1], recv.at[k + 1], me + 2 * way).start()

            self.copy(slot, self.ps.at[at], self.pr.at[at], self.partner).start()

        @pl.when(chip - 1 - k >= 0)
        def _():
            arrived(chip - 1 - k, 1, self.rs, self.rr)

        @pl.when(chip + 1 + k < chips)
        def _():
            arrived(chip + 1 + k, -1, self.ls, self.lr)

    def beside(self, at):
        slot = 2 * at + 1 - self.core
        self.copy(slot, self.ps.at[at], self.pr.at[at], self.partner).wait_recv()

    def each(self, body):
        self.beside(self.chip)
        body(self.chip)

        def at_step(k, carry):
            self.step(k)

            def at_side(side, inner):
                at = jnp.where(side == 0, self.chip - 1 - k, self.chip + 1 + k)

                @pl.when(jnp.logical_and(at >= 0, at < self.chips))
                def _():
                    self.beside(at)
                    body(at)

                return inner

            return lax.fori_loop(0, 2, at_side, carry)

        if self.chips > 1:
            lax.fori_loop(0, self.chips - 1, at_step, 0)

    def sent(self):
        me, chip, chips = self.me, self.chip, self.chips
        for c in range(chips):
            self.copy(2 * c + self.core, self.ps.at[c], self.pr.at[c], self.partner).wait_send()
        for k in range(chips - 1):

            @pl.when(jnp.logical_and(chip < chips - 1, k <= chip))
            def _():
                self.copy(me, self.rs.at[k], self.rr.at[k], me + 2).wait_send()

            @pl.when(jnp.logical_and(chip > 0, k <= chips - 1 - chip))
            def _():
                self.copy(me, self.ls.at[k], self.lr.at[k], me - 2).wait_send()


class Sum:
    axis = "ctx"

    def __init__(self, n):
        self.n, self.chips = n, n // 2
        self.scratch = [pltpu.SemaphoreType.DMA((self.chips,))] * 6

    def hold(self, part, near, got, sems):
        self.part, self.near, self.got = part, near, got
        self.ps, self.pr, self.rs, self.rr, self.ls, self.lr = sems
        self.me = lax.axis_index(self.axis)
        self.chip, self.core = self.me // 2, self.me % 2
        self.partner = self.me + 1 - 2 * self.core

    def beside(self, d):
        return remote(
            self.part.at[2 * d + 1 - self.core],
            self.near.at[d],
            self.ps.at[d],
            self.pr.at[d],
            self.axis,
            self.partner,
        )

    def right(self, d):
        return remote(
            self.part.at[2 * d + self.core],
            self.got.at[d],
            self.rs.at[d],
            self.rr.at[d],
            self.axis,
            self.me + 2,
        )

    def left(self, d):
        place = jnp.where(d == self.chip - 1, self.chips, d)
        return remote(
            self.part.at[2 * d + self.core],
            self.got.at[place],
            self.ls.at[d],
            self.lr.at[d],
            self.axis,
            self.me - 2,
        )

    def ready(self, d):
        self.beside(d).start()

    def order(self, k):
        return jnp.where(self.chip < self.chips // 2, self.chips - 1 - k, k)

    def pair(self, d):
        self.beside(d).wait_recv()
        return self.part[2 * d + self.core].astype(f32) + self.near[d].astype(f32)

    def step(self, t):
        chip, chips = self.chip, self.chips

        @pl.when(t >= chip)
        def _():
            d = chips - 1 - t + chip
            both = self.pair(d)

            @pl.when(chip == 0)
            def _():
                self.part[2 * d + self.core] = both.astype(bf16)

            @pl.when(chip > 0)
            def _():
                self.right(d).wait_recv()
                self.part[2 * d + self.core] = (both + self.got[d].astype(f32)).astype(bf16)

            self.right(d).start()

        @pl.when(t >= chips - 1 - chip)
        def _():
            d = t - (chips - 1 - chip)
            both = self.pair(d)

            @pl.when(chip == chips - 1)
            def _():
                self.part[2 * d + self.core] = both.astype(bf16)

            @pl.when(chip < chips - 1)
            def _():
                self.left(d).wait_recv()
                self.part[2 * d + self.core] = (both + self.got[d].astype(f32)).astype(bf16)

            self.left(d).start()

    def last(self, total):
        chip, chips = self.chip, self.chips
        total[...] = self.pair(chip)

        @pl.when(chip > 0)
        def _():
            self.right(chip).wait_recv()
            total[...] += self.got[chip].astype(f32)

        @pl.when(chip < chips - 1)
        def _():
            self.left(chip).wait_recv()
            total[...] += self.got[chips].astype(f32)

    def sent(self):
        for d in range(self.chips):
            self.beside(d).wait_send()
            pl.when(self.chip < d)(self.right(d).wait_send)
            pl.when(self.chip > d)(self.left(d).wait_send)


def mid_layer(ident, attended, wo, inputs, cotangent, cot_full, gain, w_gate, w_up, w_down_t):
    sizes = {axis: lax.axis_size(axis) for axis in ("dp", "ctx")}
    dp, n = sizes["dp"], sizes["ctx"]
    chips = n // 2
    rows, width = inputs.shape
    wide, f_w = wo.shape[0], w_gate.shape[1]
    in_rows = width // dp
    shape = jax.ShapeDtypeStruct
    lines = [Line(n), Line(n)]
    sums = [Sum(n), Sum(n)]
    swap = Swap("dp", shape((dp, in_rows, 3 * f_w), bf16))
    swap.plan(sizes)
    tasks = lines + sums + [swap]

    def kernel(*refs):
        att, wo_ref, x_ref, cot_ref, cots, gain_ref, wg, wu, wd = refs[:9]
        d_mids, d_mid, mid, out_part, g_all, g_gain = refs[9:15]
        part, near, got, n2, mixed, d_gate, d_up, grads, inv, total = refs[15:25]
        sems, at = [], 25
        for task in tasks:
            sems.append(tuple(refs[at : at + len(task.scratch)]))
            at += len(task.scratch)
        spread(("dp", "ctx"), sizes, False)
        lines[0].hold(n2, sems[0])
        lines[1].hold(d_mids, sems[1])
        sums[0].hold(part, near, got, sems[2])
        sums[1].hold(part, near, got, sems[3])
        me = lax.axis_index("ctx")

        def project(k, carry):
            d = sums[0].order(k)
            rows_of = att[pl.ds(2 * d, 2)].reshape(2 * rows, wide)
            part[pl.ds(2 * d, 2)] = nn(rows_of, wo_ref[...]).astype(bf16).reshape(2, rows, width)
            sums[0].ready(d)
            return carry

        lax.fori_loop(0, chips, project, 0)
        for t in range(chips - 1):
            sums[0].step(t)
        sums[0].last(total)
        middle = x_ref[...].astype(f32) + total[...]
        inverse = inverse_rms(middle)
        mid[...] = middle
        inv[...] = inverse
        n2[me] = (middle * inverse * gain_ref[...]).astype(bf16)
        lines[0].start()
        sums[0].sent()

        def forward(at):
            here = pl.ds(2 * at, 2)
            tokens = n2[here].reshape(2 * rows, width)
            gate_pre = nn(tokens, wg[...])
            up_pre = nn(tokens, wu[...])
            d_mixed = nn(cots[here].reshape(2 * rows, width), wd[...])
            sigma = 1.0 / (1.0 + jnp.exp(-gate_pre))
            silu_gate = gate_pre * sigma
            act = (silu_gate * up_pre).astype(bf16)
            dg = (d_mixed * up_pre * sigma * (1.0 + gate_pre * (1.0 - sigma))).astype(bf16)
            du = (d_mixed * silu_gate).astype(bf16)
            mixed[here] = act.reshape(2, rows, f_w)
            d_gate[here] = dg.reshape(2, rows, f_w)
            d_up[here] = du.reshape(2, rows, f_w)
            d_two = nt(dg, wg[...]) + nt(du, wu[...])
            part[here] = d_two.astype(bf16).reshape(2, rows, width)
            sums[1].ready(at)
            out_part[here] = nt(act, wd[...]).astype(bf16).reshape(2, rows, width)

        lines[0].each(forward)

        def gradient(i):
            left, right = ((n2, d_gate), (n2, d_up), (cots, mixed))[i]
            value = tn(
                left[...].reshape(n * rows, width), right[...].reshape(n * rows, f_w)
            ).astype(bf16)
            for r in range(dp):
                grads[r, :, i * f_w : (i + 1) * f_w] = value[r * in_rows : (r + 1) * in_rows]

        for t in range(chips - 1):
            sums[1].step(t)
            if t == 0:
                gradient(0)
                gradient(1)
            if t == min(1, chips - 2):
                gradient(2)
                swap.start(grads, g_all, *sems[4])
        sums[1].last(total)
        middle = mid[...]
        d_norm, gain_part = norm_backward(middle, inv[...], gain_ref[...], total[...])
        g_gain[...] = gain_part.reshape(1, width)
        d_middle = cot_ref[...].astype(f32) + d_norm
        d_mid[...] = d_middle
        d_mids[me] = d_middle.astype(bf16)
        lines[1].start()
        sums[1].sent()
        lines[0].sent()
        lines[1].each(lambda at: None)
        lines[1].sent()
        swap.finish(grads, g_all, *sems[4])

    whole = (n, rows, width)
    return pl.pallas_call(
        kernel,
        out_shape=[
            shape(whole, bf16),
            shape((rows, width), f32),
            shape((rows, width), f32),
            shape(whole, bf16),
            shape((dp, in_rows, 3 * f_w), bf16),
            shape((1, width), f32),
        ],
        in_specs=[pl.BlockSpec(memory_space=pltpu.VMEM)] * 9,
        out_specs=[pl.BlockSpec(memory_space=pltpu.VMEM)] * 6,
        scratch_shapes=[
            pltpu.VMEM(whole, bf16),
            pltpu.VMEM((chips, rows, width), bf16),
            pltpu.VMEM((chips + 1, rows, width), bf16),
            pltpu.VMEM(whole, bf16),
            pltpu.VMEM((n, rows, f_w), bf16),
            pltpu.VMEM((n, rows, f_w), bf16),
            pltpu.VMEM((n, rows, f_w), bf16),
            pltpu.VMEM((dp, in_rows, 3 * f_w), bf16),
            pltpu.VMEM((rows, 1), f32),
            pltpu.VMEM((rows, width), f32),
        ]
        + [item for task in tasks for item in task.scratch],
        compiler_params=pltpu.CompilerParams(
            collective_id=ident, has_side_effects=True, vmem_limit_bytes=62 * 1024 * 1024
        ),
        name=f"block_{ident}",
    )(attended, wo, inputs, cotangent, cot_full, gain, w_gate, w_up, w_down_t)


def masked_scores(queries, keys, first):
    scores = nt(queries, keys) * HEAD_DIM ** (-0.5)
    rows = first + lax.broadcasted_iota(jnp.int32, scores.shape, 0)
    return jnp.where(rows >= lax.broadcasted_iota(jnp.int32, scores.shape, 1), scores, -1e30)


def shards(
    inputs, cotangent, w_query, w_key, w_value, w_output, w_gate, w_up, w_down, gain_attn, gain_ffn
):
    dp, ctx = lax.axis_size("dp"), lax.axis_size("ctx")
    me = lax.axis_index("ctx")
    rows, width = inputs.shape
    length = rows * ctx
    q_w, k_w, o_w, f_w = w_query.shape[1], w_key.shape[1], w_output.shape[1], w_gate.shape[1]
    in_rows = w_query.shape[0]
    held = -(-HEADS // ctx)
    wide = held * HEAD_DIM
    total = ctx * wide
    near = all(wide * j >= q_w * j and wide * (j + 1) <= q_w * (j + 2) for j in range(ctx))

    each = ctx // dp
    gains = jnp.stack([gain_attn, gain_ffn])
    kv_rows = jnp.concatenate([w_key, w_value], axis=1).T
    down_rows = w_down.reshape(each, f_w, o_w).transpose(0, 2, 1)
    w_gu = lax.all_gather(jnp.concatenate([w_gate, w_up], axis=1), "dp", tiled=True)
    all_x, all_gains, kv_all, q_part, q_next, o_mine, down_rows = entry(
        0, inputs, kv_rows, w_query.T, w_output, gains, down_rows, wide, near
    )
    w_down_t = lax.all_gather(down_rows.reshape(each * o_w, f_w), "dp", tiled=True)
    cot_late, all_x = lax.optimization_barrier((cotangent, all_x))
    cot_full = lax.all_gather(cot_late, "ctx", tiled=True)
    kv_all = kv_all.transpose(1, 2, 0, 3).reshape(ctx, 2 * k_w, width)
    if near:
        q_part = q_part.transpose(1, 0, 2).reshape(q_w, width)
        q_next = q_next.transpose(1, 0, 2).reshape(q_w, width)
        q_rows = jnp.concatenate(
            [q_part, jnp.where(me == ctx - 1, jnp.zeros_like(q_next), q_next)], axis=0
        )
        q_rows = jnp.pad(q_rows, ((0, wide), (0, 0)))
        wq = lax.dynamic_slice(q_rows, (me * (wide - q_w), 0), (wide, width))
    else:
        q_next = q_next.transpose(0, 2, 1, 3)
        q_rows = jnp.pad(q_next.reshape(-1, width), ((0, total - HEADS * HEAD_DIM), (0, 0)))
        wq = lax.dynamic_slice(q_rows, (me * wide, 0), (wide, width))
    wk_all = kv_all[:, :k_w].reshape(-1, width)
    wv_all = kv_all[:, k_w:].reshape(-1, width)
    kv_head = [jnp.minimum((me * held + h) // GROUP, KV_HEADS - 1) for h in range(held)]

    def of_heads(array):
        return jnp.concatenate(
            [lax.dynamic_slice(array, (k * HEAD_DIM, 0), (HEAD_DIM, width)) for k in kv_head]
        )

    wk, wv = of_heads(wk_all), of_heads(wv_all)
    wo = o_mine.transpose(1, 0, 2).reshape(wide, ctx * o_w)
    gain_rows = all_gains.transpose(1, 0, 2).reshape(2, width).astype(f32)
    gain_one, gain_two = gain_rows[0], gain_rows[1]

    x_full = all_x.reshape(length, width)
    hid_full = x_full.astype(f32)
    normed_one = (hid_full * inverse_rms(hid_full) * gain_one).astype(bf16)
    cosine, sine = rope_tables(length)
    cosine, sine = jnp.tile(cosine, (1, held)), jnp.tile(sine, (1, held))
    projected = nt(normed_one, jnp.concatenate([wq, turned(wq), wk, turned(wk), wv]))
    q_a, q_b, k_a, k_b, v_a = [projected[:, i * wide : (i + 1) * wide] for i in range(5)]
    queries = (q_a * cosine + q_b * sine).astype(bf16)
    q_side = (q_a * sine - q_b * cosine).astype(bf16)
    keys = (k_a * cosine + k_b * sine).astype(bf16)
    k_side = (k_a * sine - k_b * cosine).astype(bf16)
    values = v_a.astype(bf16)

    def head(array, h):
        return array[:, h * HEAD_DIM : (h + 1) * HEAD_DIM]

    chunk = min(256, length)
    firsts = list(range(0, length, chunk))
    attended, logsums = [], []
    for h in range(held):
        q_h, k_h, v_h = head(queries, h), head(keys, h), head(values, h)
        outs, logs = [], []
        for first in firsts:
            last = first + chunk
            scores = masked_scores(q_h[first:last], k_h[:last], first)
            top = jnp.max(scores, axis=-1, keepdims=True)
            expo = jnp.exp(scores - top)
            weight = jnp.sum(expo, axis=-1, keepdims=True)
            outs.append(nn(expo.astype(bf16), v_h[:last]) / weight)
            logs.append(top + jnp.log(weight))
        real = me * held + h < HEADS
        attended.append(jnp.where(real, jnp.concatenate(outs), 0.0).astype(bf16))
        logsums.append(logs)
    attended_all = jnp.concatenate(attended, axis=1)

    d_mid_full, d_middle, middle, out_part, g_three, g_gain_two = mid_layer(
        2,
        attended_all.reshape(ctx, rows, wide),
        wo,
        inputs,
        cotangent,
        cot_full.reshape(ctx, rows, width),
        gain_two.reshape(1, width),
        w_gu[:, :f_w],
        w_gu[:, f_w:],
        w_down_t,
    )
    hidden = inputs.astype(f32)
    g_gain_two = g_gain_two.reshape(width)
    g_three = jnp.sum(g_three.astype(f32), axis=0)
    g_gu_sum = g_three[:, : 2 * f_w]
    g_down_part = g_three[:, 2 * f_w :].astype(bf16).reshape(each, o_w, f_w)
    out_sum = lax.psum_scatter(out_part.reshape(length, width), "ctx", tiled=True).astype(f32)
    out_act = (middle + out_sum).astype(bf16)
    d_mid_full = d_mid_full.reshape(length, width)

    g_out = tn(d_mid_full, attended_all).astype(bf16)
    d_attended = nt(d_mid_full, wo).astype(bf16)
    dq_all, dk_all, dv_all = [], [], []
    for h in range(held):
        q_h, k_h, v_h = head(queries, h), head(keys, h), head(values, h)
        q_two = jnp.concatenate([q_h, head(q_side, h)], axis=1)
        k_two = jnp.concatenate([k_h, head(k_side, h)], axis=1)
        grad_h = head(d_attended, h)
        delta = jnp.sum(grad_h.astype(f32) * attended[h].astype(f32), axis=-1, keepdims=True)
        dq_parts = []
        dk = jnp.zeros((length, 2 * HEAD_DIM), f32)
        dv = jnp.zeros((length, HEAD_DIM), f32)
        for i, first in enumerate(firsts):
            last = first + chunk
            probs = jnp.exp(masked_scores(q_h[first:last], k_h[:last], first) - logsums[h][i])
            d_probs = nt(grad_h[first:last], v_h[:last])
            d_scores = (probs * (d_probs - delta[first:last])).astype(bf16)
            dq_parts.append(nn(d_scores, k_two[:last]))
            tail = ((0, length - last), (0, 0))
            dk = dk + jnp.pad(tn(d_scores, q_two[first:last]), tail)
            dv = dv + jnp.pad(tn(probs.astype(bf16), grad_h[first:last]), tail)
        dq = jnp.concatenate(dq_parts)
        real = me * held + h < HEADS
        cos_h, sin_h = head(cosine, 0), head(sine, 0)

        def back(two):
            turned_back = two[:, :HEAD_DIM] * cos_h + two[:, HEAD_DIM:] * sin_h
            return jnp.where(real, turned_back * HEAD_DIM ** (-0.5), 0.0).astype(bf16)

        dq_all.append(back(dq))
        dk_all.append(back(dk))
        dv_all.append(jnp.where(real, dv, 0.0).astype(bf16))
    d_qkv = jnp.concatenate(dq_all + dk_all + dv_all, axis=1)
    d_one_f = nn(d_qkv, jnp.concatenate([wq, wk, wv]))
    d_one_part = d_one_f.astype(bf16)
    g_gain_one = jnp.sum(d_one_f * hid_full * inverse_rms(hid_full), axis=0)
    g_gain = jnp.stack([g_gain_one, g_gain_two]).reshape(2, ctx, -1).transpose(1, 0, 2)
    g_qkv = tn(d_qkv, normed_one).astype(bf16)
    g_qkv = g_qkv.reshape(3 * wide, dp, in_rows).transpose(1, 0, 2)

    d_norm_one, g_out_all, g_qkv_all, g_down_mine, gain_all = exchange(
        6,
        Reduce(d_one_part.reshape(ctx, rows, width)),
        Swap("ctx", g_out.reshape(ctx, o_w, wide)),
        Swap("dp", g_qkv),
        Turn(g_down_part),
        Swap("ctx", g_gain),
    )
    inv_one = inverse_rms(hidden)
    d_in_norm, _ = norm_backward(hidden, inv_one, gain_one, d_norm_one)
    grad_input = d_middle + d_in_norm
    g_down_sum = g_down_mine.astype(f32).transpose(0, 2, 1).reshape(each * f_w, o_w)
    g_qkv_sum = jnp.sum(g_qkv_all.astype(f32), axis=0)
    gq_part = g_qkv_sum[:wide].astype(bf16)
    g_kv = jnp.zeros((2, KV_HEADS * HEAD_DIM, in_rows), f32)
    for kind in range(2):
        for h in range(held):
            at = (kind, kv_head[h] * HEAD_DIM, 0)
            base = (1 + kind) * wide + h * HEAD_DIM
            block = lax.dynamic_slice(g_kv, at, (1, HEAD_DIM, in_rows))
            g_kv = lax.dynamic_update_slice(
                g_kv, block + g_qkv_sum[None, base : base + HEAD_DIM], at
            )
    g_kv = g_kv.astype(bf16).reshape(2, ctx, k_w, in_rows).transpose(1, 0, 2, 3)
    g_kv = g_kv.reshape(ctx, 2 * k_w, in_rows)
    g_out_rows = g_out_all.transpose(0, 2, 1).reshape(total, o_w)[: HEADS * HEAD_DIM]
    if near:
        q_task = Shift("ctx", gq_part, 1)
    else:
        q_place = lax.dynamic_update_slice(
            jnp.zeros((total, in_rows), bf16), gq_part, (me * wide, 0)
        )
        q_task = Reduce(q_place[: HEADS * HEAD_DIM].reshape(ctx, q_w, in_rows))
    kv_sum, q_got, g_out_mine, gain_all = exchange(
        7,
        Reduce(g_kv),
        q_task,
        Swap("dp", g_out_rows.reshape(dp, in_rows, o_w)),
        Gather(jnp.sum(gain_all, axis=0)),
    )
    if near:
        q_rows = jnp.concatenate([q_got, gq_part], axis=0)
        g_query = lax.dynamic_slice(
            q_rows, (wide - me * (wide - q_w), 0), (q_w, in_rows)
        ).astype(f32)
    else:
        g_query = q_got
    gain_sum = jnp.sum(gain_all, axis=0)
    return (
        out_act,
        grad_input,
        g_query.T,
        kv_sum[:k_w].T,
        kv_sum[k_w:].T,
        jnp.sum(g_out_mine.astype(f32), axis=0),
        g_gu_sum[:, :f_w],
        g_gu_sum[:, f_w:],
        g_down_sum,
        gain_sum[0],
        gain_sum[1],
    )


def solution(mesh):
    blocks = P(("dp", "ctx"), None)
    matrix = P("dp", "ctx")
    in_specs = (blocks,) * 2 + (matrix,) * 7 + (P("ctx"),) * 2
    return jax.shard_map(shards, mesh=mesh, in_specs=in_specs, out_specs=in_specs, check_vma=False)
```

```python
import functools

import jax
import jax.numpy as jnp
import numpy as np
from jax import lax
from jax.experimental import pallas as pl
from jax.experimental.pallas import tpu as pltpu
from jax.sharding import PartitionSpec as P

HEADS = 15
KV_HEADS = 5
HEAD_DIM = 64
GROUP = HEADS // KV_HEADS

epsilon = 1e-05
rope_base = 10000.0
bf16 = jnp.bfloat16
f32 = jnp.float32


def remote(src, dst, send, recv, axis, peer):
    return pltpu.make_async_remote_copy(
        src_ref=src,
        dst_ref=dst,
        send_sem=send,
        recv_sem=recv,
        device_id={axis: peer},
        device_id_type=pl.DeviceIdType.MESH,
    )


class Gather:
    axis = "dp"

    def __init__(self, array):
        self.array = array

    def plan(self, sizes):
        self.n = sizes[self.axis]
        self.out = jax.ShapeDtypeStruct((self.n,) + self.array.shape, self.array.dtype)
        self.scratch = [pltpu.SemaphoreType.DMA((self.n,))] * 2 + [pltpu.SemaphoreType.DMA(())]

    def start(self, src, dst, send, recv, own):
        me = lax.axis_index(self.axis)
        self.local = pltpu.make_async_copy(src, dst.at[me], own)
        self.local.start()
        self.copies = []
        for k in range(1, self.n):
            peer = lax.rem(me + k, self.n)
            copy = remote(src, dst.at[me], send.at[k], recv.at[k], self.axis, peer)
            copy.start()
            self.copies.append(copy)

    def middle(self, *refs):
        pass

    def finish(self, src, dst, send, recv, own):
        me = lax.axis_index(self.axis)
        for k in range(1, self.n):
            slot = lax.rem(me + self.n - k, self.n)
            remote(src, dst.at[slot], send.at[k], recv.at[k], self.axis, slot).wait_recv()
        for copy in self.copies:
            copy.wait_send()
        self.local.wait()


class Relay:
    axis = "ctx"

    def __init__(self, array):
        self.array = array

    def plan(self, sizes):
        self.n = sizes[self.axis]
        chips = self.n // 2
        self.out = jax.ShapeDtypeStruct((self.n,) + self.array.shape, self.array.dtype)
        self.scratch = [pltpu.SemaphoreType.DMA((chips,))] * 6 + [pltpu.SemaphoreType.DMA(())]

    def at(self):
        me = lax.axis_index(self.axis)
        chip, core = me // 2, me % 2
        return me, chip, core, me + 1 - 2 * core, self.n // 2

    def start(self, src, dst, rs, rr, ls, lr, ps, pr, own):
        me, chip, core, partner, chips = self.at()

        @pl.when(chip < chips - 1)
        def _():
            remote(src, dst.at[me], rs.at[0], rr.at[0], self.axis, me + 2).start()

        @pl.when(chip > 0)
        def _():
            remote(src, dst.at[me], ls.at[0], lr.at[0], self.axis, me - 2).start()

        remote(src, dst.at[me], ps.at[chip], pr.at[chip], self.axis, partner).start()
        pltpu.make_async_copy(src, dst.at[me], own).start()

    def step(self, k, src, dst, rs, rr, ls, lr, ps, pr, own):
        me, chip, core, partner, chips = self.at()

        def arrived(slot_chip, way, send, recv):
            slot = slot_chip * 2 + core
            back = me - 2 * way
            remote(dst.at[slot], dst.at[slot], send.at[k], recv.at[k], self.axis, back).wait_recv()

            @pl.when(jnp.logical_and(chip + way >= 0, chip + way < chips))
            def _():
                remote(
                    dst.at[slot],
                    dst.at[slot],
                    send.at[k + 1],
                    recv.at[k + 1],
                    self.axis,
                    me + 2 * way,
                ).start()

            remote(
                dst.at[slot], dst.at[slot], ps.at[slot_chip], pr.at[slot_chip], self.axis, partner
            ).start()

        @pl.when(chip - 1 - k >= 0)
        def _():
            arrived(chip - 1 - k, 1, rs, rr)

        @pl.when(chip + 1 + k < chips)
        def _():
            arrived(chip + 1 + k, -1, ls, lr)

    def finish(self, src, dst, rs, rr, ls, lr, ps, pr, own):
        me, chip, core, partner, chips = self.at()
        for c in range(chips):
            slot = 2 * c + 1 - core
            remote(src, dst.at[slot], ps.at[c], pr.at[c], self.axis, partner).wait_recv()
        for c in range(chips):
            remote(src, dst.at[2 * c + core], ps.at[c], pr.at[c], self.axis, partner).wait_send()
        for k in range(chips - 1):

            @pl.when(jnp.logical_and(chip < chips - 1, k <= chip))
            def _():
                remote(src, dst.at[me], rs.at[k], rr.at[k], self.axis, me + 2).wait_send()

            @pl.when(jnp.logical_and(chip > 0, k <= chips - 1 - chip))
            def _():
                remote(src, dst.at[me], ls.at[k], lr.at[k], self.axis, me - 2).wait_send()

        pltpu.make_async_copy(src, dst.at[me], own).wait()


class Turn:
    axis = "all"

    def __init__(self, array):
        self.array = array

    def plan(self, sizes):
        self.dp, self.n = sizes["dp"], sizes["ctx"]
        self.m = self.n // self.dp
        self.out = jax.ShapeDtypeStruct(self.array.shape, self.array.dtype)
        self.scratch = [pltpu.SemaphoreType.DMA((self.m,))] * 2

    def each(self, src, dst, send, recv):
        row, col = lax.axis_index("dp"), lax.axis_index("ctx")
        put = col % self.m
        for i in range(self.m):
            to_row, to_col = col // self.m, row * self.m + i
            here = jnp.logical_and(to_row == row, to_col == col)
            far = pltpu.make_async_remote_copy(
                src_ref=src.at[i],
                dst_ref=dst.at[put],
                send_sem=send.at[i],
                recv_sem=recv.at[put],
                device_id={"dp": to_row, "ctx": to_col},
                device_id_type=pl.DeviceIdType.MESH,
            )
            local = pltpu.make_async_copy(src.at[i], dst.at[put], recv.at[put])
            yield i, here, far, local

    def start(self, *refs):
        for i, here, far, local in self.each(*refs):
            pl.when(here)(local.start)
            pl.when(jnp.logical_not(here))(far.start)

    def finish(self, src, dst, send, recv):
        row, col = lax.axis_index("dp"), lax.axis_index("ctx")
        for i, here, far, local in self.each(src, dst, send, recv):
            pl.when(jnp.logical_not(here))(far.wait_send)
        for i in range(self.m):
            own = jnp.logical_and(col // self.m == row, row * self.m + i == col)
            local = pltpu.make_async_copy(src.at[i], dst.at[i], recv.at[i])
            far = pltpu.make_async_remote_copy(
                src_ref=src.at[i],
                dst_ref=dst.at[i],
                send_sem=send.at[i],
                recv_sem=recv.at[i],
                device_id={"dp": col // self.m, "ctx": row * self.m + i},
                device_id_type=pl.DeviceIdType.MESH,
            )
            pl.when(own)(local.wait)
            pl.when(jnp.logical_not(own))(far.wait_recv)

    def middle(self, *refs):
        pass


class Swap:
    def __init__(self, axis, array):
        self.axis, self.array = axis, array

    def plan(self, sizes):
        self.n = sizes[self.axis]
        self.out = jax.ShapeDtypeStruct(self.array.shape, self.array.dtype)
        self.scratch = [pltpu.SemaphoreType.DMA((self.n,))] * 2 + [pltpu.SemaphoreType.DMA(())]

    def start(self, src, dst, send, recv, own):
        me = lax.axis_index(self.axis)
        self.local = pltpu.make_async_copy(src.at[me], dst.at[me], own)
        self.local.start()
        self.copies = []
        for k in range(1, self.n):
            peer = lax.rem(me + k, self.n)
            copy = remote(src.at[peer], dst.at[me], send.at[k], recv.at[k], self.axis, peer)
            copy.start()
            self.copies.append(copy)

    def middle(self, *refs):
        pass

    def finish(self, src, dst, send, recv, own):
        me = lax.axis_index(self.axis)
        for k in range(1, self.n):
            slot = lax.rem(me + self.n - k, self.n)
            remote(
                src.at[slot], dst.at[slot], send.at[k], recv.at[k], self.axis, slot
            ).wait_recv()
        for copy in self.copies:
            copy.wait_send()
        self.local.wait()


class Shift:
    def __init__(self, axis, array, by):
        self.axis, self.array, self.by = axis, array, by

    def plan(self, sizes):
        self.n = sizes[self.axis]
        self.out = jax.ShapeDtypeStruct(self.array.shape, self.array.dtype)
        self.scratch = [pltpu.SemaphoreType.DMA(())] * 2

    def start(self, src, dst, send, recv):
        me = lax.axis_index(self.axis)
        peer = lax.rem(me + self.n + self.by, self.n)
        self.copy = remote(src, dst, send, recv, self.axis, peer)
        self.copy.start()

    def middle(self, *refs):
        pass

    def finish(self, *refs):
        self.copy.wait_recv()
        self.copy.wait_send()


class Reduce:
    axis = "ctx"

    def __init__(self, array):
        self.array = array

    def plan(self, sizes):
        self.n = sizes[self.axis]
        block = self.array.shape[1:]
        chips = self.n // 2
        self.out = jax.ShapeDtypeStruct(block, f32)
        slots = pltpu.VMEM((chips,) + block, self.array.dtype)
        self.scratch = [pltpu.SemaphoreType.DMA((chips,))] * 4 + [slots] * 3

    def start(self, src, dst, psend, precv, send, recv, near, term, far):
        me = lax.axis_index(self.axis)
        chips = self.n // 2
        chip, core = me // 2, me % 2
        partner = me + 1 - 2 * core
        self.copies = []
        for k in list(range(1, chips)) + [0]:
            slot = lax.rem(chip + k, chips) * 2 + 1 - core
            copy = remote(
                src.at[slot], near.at[k], psend.at[k], precv.at[k], self.axis, partner
            )
            copy.start()
            self.copies.append(copy)

    def middle(self, src, dst, psend, precv, send, recv, near, term, far):
        me = lax.axis_index(self.axis)
        chips = self.n // 2
        chip, core = me // 2, me % 2
        partner = me + 1 - 2 * core
        for k in range(1, chips):
            remote(
                src.at[me], near.at[k], psend.at[k], precv.at[k], self.axis, partner
            ).wait_recv()
            peer = lax.rem(chip + k, chips) * 2 + core
            both = src[peer].astype(f32) + near[k].astype(f32)
            term[k] = both.astype(term.dtype)
            copy = remote(term.at[k], far.at[k], send.at[k], recv.at[k], self.axis, peer)
            copy.start()
            self.copies.append(copy)

    def finish(self, src, dst, psend, precv, send, recv, near, term, far):
        me = lax.axis_index(self.axis)
        chips = self.n // 2
        core = me % 2
        partner = me + 1 - 2 * core
        remote(src.at[me], near.at[0], psend.at[0], precv.at[0], self.axis, partner).wait_recv()
        dst[...] = src[me].astype(f32) + near[0].astype(f32)
        for k in range(1, chips):
            remote(
                src.at[me], far.at[k], send.at[k], recv.at[k], self.axis, partner
            ).wait_recv()
            dst[...] += far[k].astype(f32)
        for copy in self.copies:
            copy.wait_send()


def exchange(ident, *tasks):
    sizes = {axis: lax.axis_size(axis) for axis in ("dp", "ctx")}
    for task in tasks:
        task.plan(sizes)
    axes = [axis for axis in ("dp", "ctx") if any(task.axis == axis for task in tasks)]
    everyone = any(task.axis == "all" for task in tasks)
    axes = [] if everyone else axes
    count = len(tasks)

    def kernel(*refs):
        barrier = pltpu.get_barrier_semaphore()
        greeted = 0
        if everyone:
            row, col = lax.axis_index("dp"), lax.axis_index("ctx")
            for i in range(1, sizes["dp"] * sizes["ctx"]):
                other = lax.rem(row * sizes["ctx"] + col + i, sizes["dp"] * sizes["ctx"])
                pl.semaphore_signal(
                    barrier,
                    inc=1,
                    device_id={"dp": other // sizes["ctx"], "ctx": other % sizes["ctx"]},
                    device_id_type=pl.DeviceIdType.MESH,
                )
                greeted += 1
        for axis in axes:
            me, n = lax.axis_index(axis), sizes[axis]
            for k in range(1, n):
                pl.semaphore_signal(
                    barrier,
                    inc=1,
                    device_id={axis: lax.rem(me + k, n)},
                    device_id_type=pl.DeviceIdType.MESH,
                )
            greeted += n - 1
        pl.semaphore_wait(barrier, greeted)
        held, at = [], 2 * count
        for i, task in enumerate(tasks):
            held.append((refs[i], refs[count + i]) + tuple(refs[at : at + len(task.scratch)]))
            at += len(task.scratch)
        for task, own in zip(tasks, held):
            task.start(*own)
        for k in range(sizes["ctx"] // 2 - 1):
            for task, own in zip(tasks, held):
                if isinstance(task, Relay):
                    task.step(k, *own)
                elif k == 0:
                    task.middle(*own)
        for task, own in zip(tasks, held):
            task.finish(*own)

    return pl.pallas_call(
        kernel,
        out_shape=[task.out for task in tasks],
        in_specs=[pl.BlockSpec(memory_space=pltpu.VMEM)] * count,
        out_specs=[pl.BlockSpec(memory_space=pltpu.VMEM)] * count,
        scratch_shapes=[shape for task in tasks for shape in task.scratch],
        compiler_params=pltpu.CompilerParams(
            collective_id=ident, has_side_effects=True, vmem_limit_bytes=60 * 1024 * 1024
        ),
        name=f"exchange_{ident}",
    )(*[task.array for task in tasks])


def spread(axes, sizes, everyone):
    barrier = pltpu.get_barrier_semaphore()
    greeted = 0
    if everyone:
        row, col = lax.axis_index("dp"), lax.axis_index("ctx")
        total = sizes["dp"] * sizes["ctx"]

        def greet(i, carry):
            other = lax.rem(row * sizes["ctx"] + col + i, total)
            pl.semaphore_signal(
                barrier,
                inc=1,
                device_id={"dp": other // sizes["ctx"], "ctx": other % sizes["ctx"]},
                device_id_type=pl.DeviceIdType.MESH,
            )
            return carry

        lax.fori_loop(1, total, greet, 0)
        greeted = total - 1
    else:
        for axis in axes:
            me, n = lax.axis_index(axis), sizes[axis]
            for k in range(1, n):
                pl.semaphore_signal(
                    barrier,
                    inc=1,
                    device_id={axis: lax.rem(me + k, n)},
                    device_id_type=pl.DeviceIdType.MESH,
                )
            greeted += n - 1
    pl.semaphore_wait(barrier, greeted)


def mm(a, b, dims):
    return lax.dot_general(a, b, ((dims[:1], dims[1:]), ((), ())), preferred_element_type=f32)


def nn(a, b):
    return mm(a, b, (1, 0))


def nt(a, b):
    return mm(a, b, (1, 1))


def tn(a, b):
    return mm(a, b, (0, 0))


def turned(rows):
    width = rows.shape[-1]
    parts = rows.reshape(-1, 2, HEAD_DIM // 2, width)
    return jnp.concatenate([-parts[:, 1:], parts[:, :1]], axis=1).reshape(rows.shape)


def rope_tables(row_count):
    half = HEAD_DIM // 2
    frequency = np.float32(rope_base) ** (-np.arange(half).astype(np.float32) * np.float32(2.0 / HEAD_DIM))
    angles = np.arange(row_count).astype(np.float32)[:, None] * frequency[None, :].astype(np.float32)
    return [jnp.asarray(np.tile(f(angles), (1, 2)), f32) for f in (np.cos, np.sin)]


def norm_backward(hidden, inverse, gain_vec, upstream):
    scaled = upstream * gain_vec
    cubed = inverse * inverse * inverse
    d_hidden = (
        inverse * scaled
        - hidden
        * cubed
        * jnp.sum(scaled * hidden, axis=-1, keepdims=True)
        / hidden.shape[-1]
    )
    return d_hidden, jnp.sum(upstream * hidden * inverse, axis=0)


def inverse_rms(hidden):
    return lax.rsqrt(jnp.mean(hidden * hidden, axis=-1, keepdims=True) + epsilon)


class Line:
    axis = "ctx"

    def __init__(self, n):
        self.n, self.chips = n, n // 2
        self.scratch = [pltpu.SemaphoreType.DMA((self.chips,))] * 6

    def hold(self, dst, sems):
        self.dst = dst
        self.rs, self.rr, self.ls, self.lr, self.ps, self.pr = sems
        self.me = lax.axis_index(self.axis)
        self.chip, self.core = self.me // 2, self.me % 2
        self.partner = self.me + 1 - 2 * self.core

    def copy(self, slot, send, recv, peer):
        return remote(self.dst.at[slot], self.dst.at[slot], send, recv, self.axis, peer)

    def start(self):
        me, chip = self.me, self.chip
        pl.when(chip < self.chips - 1)(self.copy(me, self.rs.at[0], self.rr.at[0], me + 2).start)
        pl.when(chip > 0)(self.copy(me, self.ls.at[0], self.lr.at[0], me - 2).start)
        self.copy(me, self.ps.at[chip], self.pr.at[chip], self.partner).start()

    def step(self, k):
        me, chip, chips = self.me, self.chip, self.chips

        def arrived(at, way, send, recv):
            slot = at * 2 + self.core
            self.copy(slot, send.at[k], recv.at[k], me - 2 * way).wait_recv()

            @pl.when(jnp.logical_and(chip + way >= 0, chip + way < chips))
            def _():
                self.copy(slot, send.at[k + 1], recv.at[k + 1], me + 2 * way).start()

            self.copy(slot, self.ps.at[at], self.pr.at[at], self.partner).start()

        @pl.when(chip - 1 - k >= 0)
        def _():
            arrived(chip - 1 - k, 1, self.rs, self.rr)

        @pl.when(chip + 1 + k < chips)
        def _():
            arrived(chip + 1 + k, -1, self.ls, self.lr)

    def beside(self, at):
        slot = 2 * at + 1 - self.core
        self.copy(slot, self.ps.at[at], self.pr.at[at], self.partner).wait_recv()

    def each(self, body):
        self.beside(self.chip)
        body(self.chip)

        def at_step(k, carry):
            self.step(k)

            def at_side(side, inner):
                at = jnp.where(side == 0, self.chip - 1 - k, self.chip + 1 + k)

                @pl.when(jnp.logical_and(at >= 0, at < self.chips))
                def _():
                    self.beside(at)
                    body(at)

                return inner

            return lax.fori_loop(0, 2, at_side, carry)

        if self.chips > 1:
            lax.fori_loop(0, self.chips - 1, at_step, 0)

    def sent(self):
        me, chip, chips = self.me, self.chip, self.chips
        for c in range(chips):
            self.copy(2 * c + self.core, self.ps.at[c], self.pr.at[c], self.partner).wait_send()
        for k in range(chips - 1):

            @pl.when(jnp.logical_and(chip < chips - 1, k <= chip))
            def _():
                self.copy(me, self.rs.at[k], self.rr.at[k], me + 2).wait_send()

            @pl.when(jnp.logical_and(chip > 0, k <= chips - 1 - chip))
            def _():
                self.copy(me, self.ls.at[k], self.lr.at[k], me - 2).wait_send()


class Sum:
    axis = "ctx"

    def __init__(self, n):
        self.n, self.chips = n, n // 2
        self.scratch = [pltpu.SemaphoreType.DMA((self.chips,))] * 6

    def hold(self, part, near, got, sems):
        self.part, self.near, self.got = part, near, got
        self.ps, self.pr, self.rs, self.rr, self.ls, self.lr = sems
        self.me = lax.axis_index(self.axis)
        self.chip, self.core = self.me // 2, self.me % 2
        self.partner = self.me + 1 - 2 * self.core

    def beside(self, d):
        return remote(
            self.part.at[2 * d + 1 - self.core],
            self.near.at[d],
            self.ps.at[d],
            self.pr.at[d],
            self.axis,
            self.partner,
        )

    def right(self, d):
        return remote(
            self.part.at[2 * d + self.core],
            self.got.at[d],
            self.rs.at[d],
            self.rr.at[d],
            self.axis,
            self.me + 2,
        )

    def left(self, d):
        place = jnp.where(d == self.chip - 1, self.chips, d)
        return remote(
            self.part.at[2 * d + self.core],
            self.got.at[place],
            self.ls.at[d],
            self.lr.at[d],
            self.axis,
            self.me - 2,
        )

    def ready(self, d):
        self.beside(d).start()

    def order(self, k):
        return jnp.where(self.chip < self.chips // 2, self.chips - 1 - k, k)

    def pair(self, d):
        self.beside(d).wait_recv()
        return self.part[2 * d + self.core].astype(f32) + self.near[d].astype(f32)

    def step(self, t):
        chip, chips = self.chip, self.chips

        @pl.when(t >= chip)
        def _():
            d = chips - 1 - t + chip
            both = self.pair(d)

            @pl.when(chip == 0)
            def _():
                self.part[2 * d + self.core] = both.astype(bf16)

            @pl.when(chip > 0)
            def _():
                self.right(d).wait_recv()
                self.part[2 * d + self.core] = (both + self.got[d].astype(f32)).astype(bf16)

            self.right(d).start()

        @pl.when(t >= chips - 1 - chip)
        def _():
            d = t - (chips - 1 - chip)
            both = self.pair(d)

            @pl.when(chip == chips - 1)
            def _():
                self.part[2 * d + self.core] = both.astype(bf16)

            @pl.when(chip < chips - 1)
            def _():
                self.left(d).wait_recv()
                self.part[2 * d + self.core] = (both + self.got[d].astype(f32)).astype(bf16)

            self.left(d).start()

    def last(self, total):
        chip, chips = self.chip, self.chips
        total[...] = self.pair(chip)

        @pl.when(chip > 0)
        def _():
            self.right(chip).wait_recv()
            total[...] += self.got[chip].astype(f32)

        @pl.when(chip < chips - 1)
        def _():
            self.left(chip).wait_recv()
            total[...] += self.got[chips].astype(f32)

    def sent(self):
        for d in range(self.chips):
            self.beside(d).wait_send()
            pl.when(self.chip < d)(self.right(d).wait_send)
            pl.when(self.chip > d)(self.left(d).wait_send)


def mid_layer(ident, attended, wo, x_own, cot_full, gains, w_gate, w_up, w_down_t):
    sizes = {axis: lax.axis_size(axis) for axis in ("dp", "ctx")}
    dp, n = sizes["dp"], sizes["ctx"]
    chips = n // 2
    rows, width = x_own.shape
    wide, f_w = wo.shape[0], w_gate.shape[1]
    in_rows = width // dp
    shape = jax.ShapeDtypeStruct
    lines = [Line(n), Line(n)]
    sums = [Sum(n), Sum(n)]
    swap = Swap("dp", shape((dp, in_rows, 3 * f_w), bf16))
    swap.plan(sizes)
    tasks = lines + sums + [swap]

    def kernel(*refs):
        att, wo_ref, x_ref, cots, gain_ref, wg, wu, wd = refs[:8]
        d_mids, d_mid, mid, out_part, g_all, g_gain = refs[8:14]
        part, near, got, n2, mixed, d_gate, d_up, grads, inv, total = refs[14:24]
        sems, at = [], 24
        for task in tasks:
            sems.append(tuple(refs[at : at + len(task.scratch)]))
            at += len(task.scratch)
        spread(("dp", "ctx"), sizes, False)
        lines[0].hold(n2, sems[0])
        lines[1].hold(d_mids, sems[1])
        sums[0].hold(part, near, got, sems[2])
        sums[1].hold(part, near, got, sems[3])
        me = lax.axis_index("ctx")

        def project(k, carry):
            d = sums[0].order(k)
            rows_of = att[pl.ds(2 * d, 2)].reshape(2 * rows, wide)
            part[pl.ds(2 * d, 2)] = nn(rows_of, wo_ref[...]).astype(bf16).reshape(2, rows, width)
            sums[0].ready(d)
            return carry

        lax.fori_loop(0, chips, project, 0)
        for t in range(chips - 1):
            sums[0].step(t)
        sums[0].last(total)
        middle = x_ref[...].astype(f32) + total[...]
        inverse = inverse_rms(middle)
        mid[...] = middle
        inv[...] = inverse
        n2[me] = (middle * inverse * gain_ref[1:2]).astype(bf16)
        lines[0].start()
        sums[0].sent()

        def forward(at):
            here = pl.ds(2 * at, 2)
            tokens = n2[here].reshape(2 * rows, width)
            gate_pre = nn(tokens, wg[...])
            up_pre = nn(tokens, wu[...])
            d_mixed = nn(cots[here].reshape(2 * rows, width), wd[...])
            sigma = 1.0 / (1.0 + jnp.exp(-gate_pre))
            silu_gate = gate_pre * sigma
            act = (silu_gate * up_pre).astype(bf16)
            dg = (d_mixed * up_pre * sigma * (1.0 + gate_pre * (1.0 - sigma))).astype(bf16)
            du = (d_mixed * silu_gate).astype(bf16)
            mixed[here] = act.reshape(2, rows, f_w)
            d_gate[here] = dg.reshape(2, rows, f_w)
            d_up[here] = du.reshape(2, rows, f_w)
            d_two = nt(dg, wg[...]) + nt(du, wu[...])
            part[here] = d_two.astype(bf16).reshape(2, rows, width)
            sums[1].ready(at)
            out_part[here] = nt(act, wd[...]).astype(bf16).reshape(2, rows, width)

        lines[0].each(forward)

        def gradient(i):
            left, right = ((n2, d_gate), (n2, d_up), (cots, mixed))[i]
            value = tn(
                left[...].reshape(n * rows, width), right[...].reshape(n * rows, f_w)
            ).astype(bf16)
            for r in range(dp):
                grads[r, :, i * f_w : (i + 1) * f_w] = value[r * in_rows : (r + 1) * in_rows]

        for t in range(chips - 1):
            sums[1].step(t)
            if t == 0:
                gradient(0)
                gradient(1)
            if t == min(1, chips - 2):
                gradient(2)
                swap.start(grads, g_all, *sems[4])
        sums[1].last(total)
        middle = mid[...]
        d_norm, gain_part = norm_backward(middle, inv[...], gain_ref[1:2], total[...])
        g_gain[...] = gain_part.reshape(1, width)
        d_middle = cots[me].astype(f32) + d_norm
        d_mid[...] = d_middle
        d_mids[me] = d_middle.astype(bf16)
        lines[1].start()
        sums[1].sent()
        lines[0].sent()
        lines[1].each(lambda at: None)
        lines[1].sent()
        swap.finish(grads, g_all, *sems[4])

    whole = (n, rows, width)
    return pl.pallas_call(
        kernel,
        out_shape=[
            shape(whole, bf16),
            shape((rows, width), f32),
            shape((rows, width), f32),
            shape(whole, bf16),
            shape((dp, in_rows, 3 * f_w), bf16),
            shape((1, width), f32),
        ],
        in_specs=[pl.BlockSpec(memory_space=pltpu.VMEM)] * 8,
        out_specs=[pl.BlockSpec(memory_space=pltpu.VMEM)] * 6,
        scratch_shapes=[
            pltpu.VMEM(whole, bf16),
            pltpu.VMEM((chips, rows, width), bf16),
            pltpu.VMEM((chips + 1, rows, width), bf16),
            pltpu.VMEM(whole, bf16),
            pltpu.VMEM((n, rows, f_w), bf16),
            pltpu.VMEM((n, rows, f_w), bf16),
            pltpu.VMEM((n, rows, f_w), bf16),
            pltpu.VMEM((dp, in_rows, 3 * f_w), bf16),
            pltpu.VMEM((rows, 1), f32),
            pltpu.VMEM((rows, width), f32),
        ]
        + [item for task in tasks for item in task.scratch],
        compiler_params=pltpu.CompilerParams(
            collective_id=ident, has_side_effects=True, vmem_limit_bytes=62 * 1024 * 1024
        ),
        name=f"block_{ident}",
    )(attended, wo, x_own, cot_full, gains, w_gate, w_up, w_down_t)


class Need:
    axis = "ctx"

    def __init__(self, n, low, high):
        self.n, self.low, self.high = n, low, high
        self.slots = max(high(d) - low(d) + 1 for d in range(n))
        self.scratch = [
            pltpu.SemaphoreType.DMA((n,)),
            pltpu.SemaphoreType.DMA((self.slots,)),
        ]

    def hold(self, src, dst, sems):
        self.src, self.dst = src, dst
        self.send, self.recv = sems
        self.me = lax.axis_index(self.axis)
        self.first, self.final = self.low(self.me), self.high(self.me)

    def each(self):
        for d in range(self.n):
            low, high = self.low(d), self.high(d)
            used = jnp.logical_and(self.me >= low, self.me <= high)
            slot = jnp.clip(self.me - low, 0, self.slots - 1)
            copy = remote(
                self.src, self.dst.at[slot], self.send.at[d], self.recv.at[slot], self.axis, d
            )
            yield jnp.logical_and(used, self.me != d), copy

    def start(self):
        for used, copy in self.each():
            pl.when(used)(copy.start)
        for t in range(self.slots):
            source = self.first + t

            @pl.when(source == self.me)
            def _():
                self.dst[t] = self.src[...]

            @pl.when(source > self.final)
            def _():
                self.dst[t] = jnp.zeros_like(self.dst[t])

    def arrive(self):
        beside = self.me + 1 - 2 * lax.rem(self.me, 2)
        for t in range(self.slots):
            source = self.first + t
            copy = remote(
                self.src, self.dst.at[t], self.send.at[0], self.recv.at[t], self.axis, beside
            )
            pl.when(jnp.logical_and(source <= self.final, source != self.me))(copy.wait_recv)

    def sent(self):
        for used, copy in self.each():
            pl.when(used)(copy.wait_send)


def least(a, b):
    return min(a, b) if isinstance(a, int) else jnp.minimum(a, b)


def over(a, b):
    return a // b if isinstance(a, int) else lax.div(a, b)


def pick(rows, first, source, sign):
    at = first + lax.broadcasted_iota(jnp.int32, (rows, source.shape[1]), 0)
    return jnp.where(at == source, sign, 0.0)


def front(ident, x_t, cot_t, w_q, kv_rows, w_o, gains, wg_t, wu_t, wd_t, held, tables):
    sizes = {axis: lax.axis_size(axis) for axis in ("dp", "ctx")}
    dp, n = sizes["dp"], sizes["ctx"]
    chips, each = n // 2, n // dp
    width, rows = x_t.shape
    in_rows, q_w = w_q.shape
    o_w, k_w, f_w = w_o.shape[1], kv_rows.shape[0] // 2, wg_t.shape[0]
    wide, total = held * HEAD_DIM, n * held * HEAD_DIM
    length, chunk = n * rows, 2 * rows
    shape = jax.ShapeDtypeStruct

    def kv_head(j):
        return least(over(j, GROUP), KV_HEADS - 1)

    q_need = Need(
        n,
        lambda d: over(least(wide * d, width - 1), q_w),
        lambda d: over(least(wide * d + wide - 1, width - 1), q_w),
    )
    kv_need = Need(
        n,
        lambda d: over(HEAD_DIM * kv_head(held * d), k_w),
        lambda d: over(HEAD_DIM * kv_head(held * d + held - 1) + HEAD_DIM - 1, k_w),
    )
    x_line, cot_line, gain_line = Line(n), Line(n), Line(n)
    q_all, kv_all, o_all = Gather(w_q), Gather(kv_rows), Gather(w_o)
    g_all, u_all = [Gather(shape((in_rows, f_w), bf16)) for _ in range(2)]
    d_turn = Turn(shape((each, o_w, f_w), bf16))
    d_all = Gather(shape((each, o_w, f_w), bf16))
    o_swap = Swap("ctx", shape((n, wide, o_w), bf16))
    planned = [q_all, kv_all, o_all, g_all, u_all, d_turn, d_all, o_swap]
    for task in planned:
        task.plan(sizes)
    tasks = [q_need, kv_need, x_line, cot_line, gain_line] + planned

    def kernel(*refs):
        xt, ct, wq_ref, kv_ref, wo_ref, gain_in, wgt, wut, wdt, cos_ref, sin_ref = refs[:11]
        att, lse, q_two, k_two, val, n1, xs, cots, wo_out, wqkv, gain_out = refs[11:22]
        wg_out, wu_out, wd_out, x_own = refs[22:26]
        gains_in, q_got, kv_got, o_got, q_in, kv_in, wall = refs[26:33]
        wg_mine, wu_mine, d_mine, d_got, o_cut, o_in = refs[33:39]
        sems, at = {}, 39
        for task in tasks:
            sems[task] = tuple(refs[at : at + len(task.scratch)])
            at += len(task.scratch)
        spread(("dp", "ctx"), sizes, True)
        me = lax.axis_index("ctx")
        x_line.hold(xs, sems[x_line])
        cot_line.hold(cots, sems[cot_line])
        gain_line.hold(gains_in, sems[gain_line])
        q_need.hold(q_got, q_in, sems[q_need])
        kv_need.hold(kv_got, kv_in, sems[kv_need])
        mine = xt[...].T
        xs[me] = mine
        x_own[...] = mine
        x_line.start()
        q_all.start(wq_ref, q_got, *sems[q_all])
        kv_all.start(kv_ref, kv_got, *sems[kv_all])
        gains_in[me] = gain_in[...]
        gain_line.start()
        cots[me] = ct[...].T
        wg_mine[...] = wgt[...].T
        wu_mine[...] = wut[...].T
        for i in range(each):
            d_mine[i] = wdt[:, i * f_w : (i + 1) * f_w]
        q_all.finish(wq_ref, q_got, *sems[q_all])
        kv_all.finish(kv_ref, kv_got, *sems[kv_all])
        q_need.start()
        kv_need.start()
        o_all.start(wo_ref, o_got, *sems[o_all])
        d_turn.start(d_mine, d_got, *sems[d_turn])
        for k in range(chips - 1):
            gain_line.step(k)
        for c in range(chips):
            gain_line.beside(c)
        gain_line.sent()
        for c in range(n):
            gain_out[:, c * o_w : (c + 1) * o_w] = gains_in[c].astype(f32)

        def turned(base, d):
            half = HEAD_DIM // 2
            return base + jnp.bitwise_and(d + half, HEAD_DIM - 1), jnp.where(d < half, -1.0, 1.0)

        def plan(heads):
            lane = lax.broadcasted_iota(jnp.int32, (1, 2 * HEAD_DIM), 1)
            d = jnp.bitwise_and(lane, HEAD_DIM - 1)
            parts = []
            for h in heads:
                parts.append((h * HEAD_DIM + d, jnp.ones((1, 2 * HEAD_DIM), f32)))
                parts.append(turned(h * HEAD_DIM, d))
            lane = lax.broadcasted_iota(jnp.int32, (1, wide), 1)
            flat = jnp.bitwise_and(lane, HEAD_DIM - 1)
            base = jnp.zeros((1, wide), jnp.int32)
            for i, h in enumerate(heads):
                inside = jnp.logical_and(lane >= i * HEAD_DIM, lane < (i + 1) * HEAD_DIM)
                base = jnp.where(inside, h * HEAD_DIM, base)
            return parts + [(base + flat, jnp.ones((1, wide), f32))]

        heads = [me * held + h for h in range(held)]
        kv_heads = [kv_head(h) for h in heads]
        q_plan, k_plan = plan(heads), plan(kv_heads)
        no = [(jnp.zeros_like(k_plan[-1][0]) - 1, k_plan[-1][1])]
        q_need.arrive()
        kv_need.arrive()
        span = 4 * held * HEAD_DIM
        for r in range(dp):
            here = slice(r * in_rows, (r + 1) * in_rows)
            value = None
            for t in range(q_need.slots):
                first = (q_need.first + t) * q_w
                take = jnp.concatenate([pick(q_w, first, *p) for p in q_plan], axis=1)
                term = nn(q_in[t, r], take.astype(bf16))
                value = term if value is None else value + term
            value = value.astype(bf16)
            wall[here, :span] = value[:, :span]
            wqkv[here, :wide] = value[:, span:]
            value = None
            for t in range(kv_need.slots):
                first = (kv_need.first + t) * k_w
                top = [pick(k_w, first, *p) for p in k_plan + no]
                zero = jnp.zeros((k_w, span + wide), f32)
                top = jnp.concatenate(top, axis=1)
                low = jnp.concatenate([zero, pick(k_w, first, *k_plan[-1])], axis=1)
                take = jnp.concatenate([top, low], axis=0).astype(bf16)
                term = tn(kv_in[t, r], take)
                value = term if value is None else value + term
            value = value.astype(bf16)
            wall[here, span:] = value[:, :span]
            wqkv[here, wide:] = value[:, span:]
        g_all.start(wg_mine, wg_out, *sems[g_all])
        u_all.start(wu_mine, wu_out, *sems[u_all])

        def project(at):
            here = pl.ds(2 * at, 2)
            tokens = xs[here].reshape(chunk, width).astype(f32)
            normed = (tokens * inverse_rms(tokens) * gain_out[0:1]).astype(bf16)
            n1[here] = normed.reshape(2, rows, width)
            both = nn(normed, wall[...])
            low = pl.multiple_of(at * chunk, chunk)
            first, second = cos_ref[pl.ds(low, chunk)], sin_ref[pl.ds(low, chunk)]
            for h in range(2 * held):
                at_h = h * 4 * HEAD_DIM
                a = both[:, at_h : at_h + 2 * HEAD_DIM]
                b = both[:, at_h + 2 * HEAD_DIM : at_h + 4 * HEAD_DIM]
                two = a * first + b * second
                if h < held:
                    q_two[h, pl.ds(low, chunk)] = (two * HEAD_DIM ** (-0.5)).astype(bf16)
                else:
                    k_two[h - held, pl.ds(low, chunk)] = two.astype(bf16)
            v = nn(normed, wqkv[:, 2 * wide :]).astype(bf16)
            for h in range(held):
                val[h, pl.ds(low, chunk)] = v[:, h * HEAD_DIM : (h + 1) * HEAD_DIM]

        x_line.each(project)
        cot_line.start()
        d_turn.finish(d_mine, d_got, *sems[d_turn])
        d_all.start(d_got, wd_out, *sems[d_all])
        o_all.finish(wo_ref, o_got, *sems[o_all])
        for j in range(n):
            for r in range(dp):
                low, high = max(r * in_rows, j * wide), min((r + 1) * in_rows, (j + 1) * wide)
                if low < high:
                    o_cut[j, low - j * wide : high - j * wide] = o_got[
                        r, low - r * in_rows : high - r * in_rows
                    ]
            used = min(max(HEADS * HEAD_DIM - j * wide, 0), wide)
            if used < wide:
                o_cut[j, used:] = jnp.zeros((wide - used, o_w), bf16)
        o_swap.start(o_cut, o_in, *sems[o_swap])
        x_line.sent()

        def attend(i):
            first, last = i * chunk, (i + 1) * chunk
            for h in range(held):
                q = q_two[h, first:last, :HEAD_DIM]
                diag = nt(q, k_two[h, first:last, :HEAD_DIM])
                row = lax.broadcasted_iota(jnp.int32, diag.shape, 0)
                col = lax.broadcasted_iota(jnp.int32, diag.shape, 1)
                diag = jnp.where(row >= col, diag, -1e30)
                top = jnp.max(diag, axis=-1, keepdims=True)
                if i:
                    off = nt(q, k_two[h, :first, :HEAD_DIM])
                    top = jnp.maximum(top, jnp.max(off, axis=-1, keepdims=True))
                expo = jnp.exp(diag - top)
                weight = jnp.sum(expo, axis=-1, keepdims=True)
                out = nn(expo.astype(bf16), val[h, first:last])
                if i:
                    expo = jnp.exp(off - top)
                    weight = weight + jnp.sum(expo, axis=-1, keepdims=True)
                    out = out + nn(expo.astype(bf16), val[h, :first])
                out = (out / weight).astype(bf16)
                lanes = slice(h * HEAD_DIM, (h + 1) * HEAD_DIM)
                att[2 * i : 2 * i + 2, :, lanes] = out.reshape(2, rows, HEAD_DIM)
                logs = jnp.broadcast_to(top + jnp.log(weight), (chunk, HEAD_DIM))
                lse[first:last, lanes] = logs

        for i in range(chips):
            attend(i)
            if i < chips - 1:
                cot_line.step(i)
        o_swap.finish(o_cut, o_in, *sems[o_swap])
        for c in range(n):
            wo_out[:, c * o_w : (c + 1) * o_w] = o_in[c]
        for c in range(chips):
            cot_line.beside(c)
        cot_line.sent()
        q_need.sent()
        kv_need.sent()
        g_all.finish(wg_mine, wg_out, *sems[g_all])
        u_all.finish(wu_mine, wu_out, *sems[u_all])
        d_all.finish(d_got, wd_out, *sems[d_all])

    whole = (n, rows, width)
    outs = [
        shape((n, rows, wide), bf16),
        shape((length, wide), f32),
        shape((held, length, 2 * HEAD_DIM), bf16),
        shape((held, length, 2 * HEAD_DIM), bf16),
        shape((held, length, HEAD_DIM), bf16),
        shape(whole, bf16),
        shape(whole, bf16),
        shape(whole, bf16),
        shape((wide, width), bf16),
        shape((width, 3 * wide), bf16),
        shape((2, width), f32),
        shape((dp, in_rows, f_w), bf16),
        shape((dp, in_rows, f_w), bf16),
        shape((dp, each, o_w, f_w), bf16),
        shape((rows, width), bf16),
    ]
    return pl.pallas_call(
        kernel,
        out_shape=outs,
        in_specs=[pl.BlockSpec(memory_space=pltpu.VMEM)] * 11,
        out_specs=[pl.BlockSpec(memory_space=pltpu.VMEM)] * len(outs),
        scratch_shapes=[
            pltpu.VMEM((n, 2, o_w), bf16),
            pltpu.VMEM((dp, in_rows, q_w), bf16),
            pltpu.VMEM((dp,) + kv_rows.shape, bf16),
            pltpu.VMEM((dp, in_rows, o_w), bf16),
            pltpu.VMEM((q_need.slots, dp, in_rows, q_w), bf16),
            pltpu.VMEM((kv_need.slots, dp) + kv_rows.shape, bf16),
            pltpu.VMEM((width, 8 * held * HEAD_DIM), bf16),
            pltpu.VMEM((in_rows, f_w), bf16),
            pltpu.VMEM((in_rows, f_w), bf16),
            pltpu.VMEM((each, o_w, f_w), bf16),
            pltpu.VMEM((each, o_w, f_w), bf16),
            pltpu.VMEM((n, wide, o_w), bf16),
            pltpu.VMEM((n, wide, o_w), bf16),
        ]
        + [item for task in tasks for item in task.scratch],
        compiler_params=pltpu.CompilerParams(
            collective_id=ident, has_side_effects=True, vmem_limit_bytes=62 * 1024 * 1024
        ),
        name=f"front_{ident}",
    )(x_t, cot_t, w_q, kv_rows, w_o, gains, wg_t, wu_t, wd_t, *tables)


def masked_scores(queries, keys, first):
    scores = nt(queries, keys)
    rows = first + lax.broadcasted_iota(jnp.int32, scores.shape, 0)
    return jnp.where(rows >= lax.broadcasted_iota(jnp.int32, scores.shape, 1), scores, -1e30)


def shards(
    inputs, cotangent, w_query, w_key, w_value, w_output, w_gate, w_up, w_down, gain_attn, gain_ffn
):
    dp, ctx = lax.axis_size("dp"), lax.axis_size("ctx")
    me = lax.axis_index("ctx")
    rows, width = inputs.shape
    length = rows * ctx
    q_w, k_w, o_w, f_w = w_query.shape[1], w_key.shape[1], w_output.shape[1], w_gate.shape[1]
    in_rows = w_query.shape[0]
    held = -(-HEADS // ctx)
    wide = held * HEAD_DIM
    total = ctx * wide
    near = all(wide * j >= q_w * j and wide * (j + 1) <= q_w * (j + 2) for j in range(ctx))

    each = ctx // dp
    gains = jnp.stack([gain_attn, gain_ffn])
    kv_rows = jnp.concatenate([w_key.T, w_value.T])
    cosine, sine = rope_tables(length)
    tables = (
        jnp.concatenate([cosine, sine], axis=1),
        jnp.concatenate([sine, -cosine], axis=1),
    )
    attended, lse, q_two, k_two, values, n1, all_x, cots, wo, wqkv, gain_rows, w_g, w_u, w_d, x_own = front(
        0,
        inputs.T,
        cotangent.T,
        w_query,
        kv_rows,
        w_output,
        gains,
        w_gate.T,
        w_up.T,
        w_down.T,
        held,
        tables,
    )
    gain_one = gain_rows[0]
    d_mid_full, d_middle, middle, out_part, g_three, g_gain_two = mid_layer(
        2,
        attended,
        wo,
        x_own,
        cots,
        gain_rows,
        w_g.reshape(width, f_w),
        w_u.reshape(width, f_w),
        w_d.reshape(width, f_w),
    )
    attended_all = attended.reshape(length, wide)
    normed_one = n1.reshape(length, width)
    hid_full = all_x.reshape(length, width).astype(f32)
    kv_head = [jnp.minimum((me * held + h) // GROUP, KV_HEADS - 1) for h in range(held)]
    chunk = min(256, length)
    firsts = list(range(0, length, chunk))

    def head(array, h):
        return array[:, h * HEAD_DIM : (h + 1) * HEAD_DIM]

    hidden = inputs.astype(f32)
    g_gain_two = g_gain_two.reshape(width)
    g_three = jnp.sum(g_three.astype(f32), axis=0)
    g_gu_sum = g_three[:, : 2 * f_w]
    g_down_part = g_three[:, 2 * f_w :].astype(bf16).reshape(each, o_w, f_w)
    out_sum = lax.psum_scatter(out_part.reshape(length, width), "ctx", tiled=True).astype(f32)
    out_act = (middle + out_sum).astype(bf16)
    d_mid_full = d_mid_full.reshape(length, width)

    g_out = tn(d_mid_full, attended_all).astype(bf16)
    d_attended = nt(d_mid_full, wo).astype(bf16)
    dq_all, dk_all, dv_all = [], [], []
    for h in range(held):
        q_h, k_h, v_h = head(q_two[h], 0), head(k_two[h], 0), values[h]
        grad_h = head(d_attended, h)
        delta = jnp.sum(
            grad_h.astype(f32) * head(attended_all, h).astype(f32), axis=-1, keepdims=True
        )
        dq_parts = []
        dk = jnp.zeros((length, 2 * HEAD_DIM), f32)
        dv = jnp.zeros((length, HEAD_DIM), f32)
        for i, first in enumerate(firsts):
            last = first + chunk
            probs = jnp.exp(masked_scores(q_h[first:last], k_h[:last], first) - head(lse, h)[first:last, :1])
            d_probs = nt(grad_h[first:last], v_h[:last])
            d_scores = (probs * (d_probs - delta[first:last])).astype(bf16)
            dq_parts.append(nn(d_scores, k_two[h][:last]))
            tail = ((0, length - last), (0, 0))
            dk = dk + jnp.pad(tn(d_scores, q_two[h][first:last]), tail)
            dv = dv + jnp.pad(tn(probs.astype(bf16), grad_h[first:last]), tail)
        dq = jnp.concatenate(dq_parts)
        real = me * held + h < HEADS
        cos_h, sin_h = head(cosine, 0), head(sine, 0)

        def back(two):
            turned_back = two[:, :HEAD_DIM] * cos_h + two[:, HEAD_DIM:] * sin_h
            return jnp.where(real, turned_back, 0.0).astype(bf16)

        dq_all.append(back(dq * HEAD_DIM ** (-0.5)))
        dk_all.append(back(dk))
        dv_all.append(jnp.where(real, dv, 0.0).astype(bf16))
    d_qkv = jnp.concatenate(dq_all + dk_all + dv_all, axis=1)
    d_one_f = nt(d_qkv, wqkv)
    d_one_part = d_one_f.astype(bf16)
    g_gain_one = jnp.sum(d_one_f * hid_full * inverse_rms(hid_full), axis=0)
    g_gain = jnp.stack([g_gain_one, g_gain_two]).reshape(2, ctx, -1).transpose(1, 0, 2)
    g_qkv = tn(d_qkv, normed_one).astype(bf16)
    g_qkv = g_qkv.reshape(3 * wide, dp, in_rows).transpose(1, 0, 2)

    d_norm_one, g_out_all, g_qkv_all, g_down_mine, gain_all = exchange(
        6,
        Reduce(d_one_part.reshape(ctx, rows, width)),
        Swap("ctx", g_out.reshape(ctx, o_w, wide)),
        Swap("dp", g_qkv),
        Turn(g_down_part),
        Swap("ctx", g_gain),
    )
    inv_one = inverse_rms(hidden)
    d_in_norm, _ = norm_backward(hidden, inv_one, gain_one, d_norm_one)
    grad_input = d_middle + d_in_norm
    g_down_sum = g_down_mine.astype(f32).transpose(0, 2, 1).reshape(each * f_w, o_w)
    g_qkv_sum = jnp.sum(g_qkv_all.astype(f32), axis=0)
    gq_part = g_qkv_sum[:wide].astype(bf16)
    g_kv = jnp.zeros((2, KV_HEADS * HEAD_DIM, in_rows), f32)
    for kind in range(2):
        for h in range(held):
            at = (kind, kv_head[h] * HEAD_DIM, 0)
            base = (1 + kind) * wide + h * HEAD_DIM
            block = lax.dynamic_slice(g_kv, at, (1, HEAD_DIM, in_rows))
            g_kv = lax.dynamic_update_slice(
                g_kv, block + g_qkv_sum[None, base : base + HEAD_DIM], at
            )
    g_kv = g_kv.astype(bf16).reshape(2, ctx, k_w, in_rows).transpose(1, 0, 2, 3)
    g_kv = g_kv.reshape(ctx, 2 * k_w, in_rows)
    g_out_rows = g_out_all.transpose(0, 2, 1).reshape(total, o_w)[: HEADS * HEAD_DIM]
    if near:
        q_task = Shift("ctx", gq_part, 1)
    else:
        q_place = lax.dynamic_update_slice(
            jnp.zeros((total, in_rows), bf16), gq_part, (me * wide, 0)
        )
        q_task = Reduce(q_place[: HEADS * HEAD_DIM].reshape(ctx, q_w, in_rows))
    kv_sum, q_got, g_out_mine, gain_all = exchange(
        7,
        Reduce(g_kv),
        q_task,
        Swap("dp", g_out_rows.reshape(dp, in_rows, o_w)),
        Gather(jnp.sum(gain_all, axis=0)),
    )
    if near:
        q_rows = jnp.concatenate([q_got, gq_part], axis=0)
        g_query = lax.dynamic_slice(
            q_rows, (wide - me * (wide - q_w), 0), (q_w, in_rows)
        ).astype(f32)
    else:
        g_query = q_got
    gain_sum = jnp.sum(gain_all, axis=0)
    return (
        out_act,
        grad_input,
        g_query.T,
        kv_sum[:k_w].T,
        kv_sum[k_w:].T,
        jnp.sum(g_out_mine.astype(f32), axis=0),
        g_gu_sum[:, :f_w],
        g_gu_sum[:, f_w:],
        g_down_sum,
        gain_sum[0],
        gain_sum[1],
    )


def solution(mesh):
    blocks = P(("dp", "ctx"), None)
    matrix = P("dp", "ctx")
    in_specs = (blocks,) * 2 + (matrix,) * 7 + (P("ctx"),) * 2
    return jax.shard_map(shards, mesh=mesh, in_specs=in_specs, out_specs=in_specs, check_vma=False)
```

```python
import functools

import jax
import jax.numpy as jnp
import numpy as np
from jax import lax
from jax.experimental import pallas as pl
from jax.experimental.pallas import tpu as pltpu
from jax.sharding import PartitionSpec as P

HEADS = 15
KV_HEADS = 5
HEAD_DIM = 64
GROUP = HEADS // KV_HEADS

epsilon = 1e-05
rope_base = 10000.0
bf16 = jnp.bfloat16
f32 = jnp.float32


def remote(src, dst, send, recv, axis, peer):
    return pltpu.make_async_remote_copy(
        src_ref=src,
        dst_ref=dst,
        send_sem=send,
        recv_sem=recv,
        device_id={axis: peer},
        device_id_type=pl.DeviceIdType.MESH,
    )


class Gather:
    axis = "dp"

    def __init__(self, array):
        self.array = array

    def plan(self, sizes):
        self.n = sizes[self.axis]
        self.out = jax.ShapeDtypeStruct((self.n,) + self.array.shape, self.array.dtype)
        self.scratch = [pltpu.SemaphoreType.DMA((self.n,))] * 2 + [pltpu.SemaphoreType.DMA(())]

    def start(self, src, dst, send, recv, own):
        me = lax.axis_index(self.axis)
        self.local = pltpu.make_async_copy(src, dst.at[me], own)
        self.local.start()
        self.copies = []
        for k in range(1, self.n):
            peer = lax.rem(me + k, self.n)
            copy = remote(src, dst.at[me], send.at[k], recv.at[k], self.axis, peer)
            copy.start()
            self.copies.append(copy)

    def middle(self, *refs):
        pass

    def finish(self, src, dst, send, recv, own):
        me = lax.axis_index(self.axis)
        for k in range(1, self.n):
            slot = lax.rem(me + self.n - k, self.n)
            remote(src, dst.at[slot], send.at[k], recv.at[k], self.axis, slot).wait_recv()
        for copy in self.copies:
            copy.wait_send()
        self.local.wait()


class Relay:
    axis = "ctx"

    def __init__(self, array):
        self.array = array

    def plan(self, sizes):
        self.n = sizes[self.axis]
        chips = self.n // 2
        self.out = jax.ShapeDtypeStruct((self.n,) + self.array.shape, self.array.dtype)
        self.scratch = [pltpu.SemaphoreType.DMA((chips,))] * 6 + [pltpu.SemaphoreType.DMA(())]

    def at(self):
        me = lax.axis_index(self.axis)
        chip, core = me // 2, me % 2
        return me, chip, core, me + 1 - 2 * core, self.n // 2

    def start(self, src, dst, rs, rr, ls, lr, ps, pr, own):
        me, chip, core, partner, chips = self.at()

        @pl.when(chip < chips - 1)
        def _():
            remote(src, dst.at[me], rs.at[0], rr.at[0], self.axis, me + 2).start()

        @pl.when(chip > 0)
        def _():
            remote(src, dst.at[me], ls.at[0], lr.at[0], self.axis, me - 2).start()

        remote(src, dst.at[me], ps.at[chip], pr.at[chip], self.axis, partner).start()
        pltpu.make_async_copy(src, dst.at[me], own).start()

    def step(self, k, src, dst, rs, rr, ls, lr, ps, pr, own):
        me, chip, core, partner, chips = self.at()

        def arrived(slot_chip, way, send, recv):
            slot = slot_chip * 2 + core
            back = me - 2 * way
            remote(dst.at[slot], dst.at[slot], send.at[k], recv.at[k], self.axis, back).wait_recv()

            @pl.when(jnp.logical_and(chip + way >= 0, chip + way < chips))
            def _():
                remote(
                    dst.at[slot],
                    dst.at[slot],
                    send.at[k + 1],
                    recv.at[k + 1],
                    self.axis,
                    me + 2 * way,
                ).start()

            remote(
                dst.at[slot], dst.at[slot], ps.at[slot_chip], pr.at[slot_chip], self.axis, partner
            ).start()

        @pl.when(chip - 1 - k >= 0)
        def _():
            arrived(chip - 1 - k, 1, rs, rr)

        @pl.when(chip + 1 + k < chips)
        def _():
            arrived(chip + 1 + k, -1, ls, lr)

    def finish(self, src, dst, rs, rr, ls, lr, ps, pr, own):
        me, chip, core, partner, chips = self.at()
        for c in range(chips):
            slot = 2 * c + 1 - core
            remote(src, dst.at[slot], ps.at[c], pr.at[c], self.axis, partner).wait_recv()
        for c in range(chips):
            remote(src, dst.at[2 * c + core], ps.at[c], pr.at[c], self.axis, partner).wait_send()
        for k in range(chips - 1):

            @pl.when(jnp.logical_and(chip < chips - 1, k <= chip))
            def _():
                remote(src, dst.at[me], rs.at[k], rr.at[k], self.axis, me + 2).wait_send()

            @pl.when(jnp.logical_and(chip > 0, k <= chips - 1 - chip))
            def _():
                remote(src, dst.at[me], ls.at[k], lr.at[k], self.axis, me - 2).wait_send()

        pltpu.make_async_copy(src, dst.at[me], own).wait()


class Turn:
    axis = "all"

    def __init__(self, array):
        self.array = array

    def plan(self, sizes):
        self.dp, self.n = sizes["dp"], sizes["ctx"]
        self.m = self.n // self.dp
        self.out = jax.ShapeDtypeStruct(self.array.shape, self.array.dtype)
        self.scratch = [pltpu.SemaphoreType.DMA((self.m,))] * 2

    def each(self, src, dst, send, recv):
        row, col = lax.axis_index("dp"), lax.axis_index("ctx")
        put = col % self.m
        for i in range(self.m):
            to_row, to_col = col // self.m, row * self.m + i
            here = jnp.logical_and(to_row == row, to_col == col)
            far = pltpu.make_async_remote_copy(
                src_ref=src.at[i],
                dst_ref=dst.at[put],
                send_sem=send.at[i],
                recv_sem=recv.at[put],
                device_id={"dp": to_row, "ctx": to_col},
                device_id_type=pl.DeviceIdType.MESH,
            )
            local = pltpu.make_async_copy(src.at[i], dst.at[put], recv.at[put])
            yield i, here, far, local

    def start(self, *refs):
        for i, here, far, local in self.each(*refs):
            pl.when(here)(local.start)
            pl.when(jnp.logical_not(here))(far.start)

    def finish(self, src, dst, send, recv):
        row, col = lax.axis_index("dp"), lax.axis_index("ctx")
        for i, here, far, local in self.each(src, dst, send, recv):
            pl.when(jnp.logical_not(here))(far.wait_send)
        for i in range(self.m):
            own = jnp.logical_and(col // self.m == row, row * self.m + i == col)
            local = pltpu.make_async_copy(src.at[i], dst.at[i], recv.at[i])
            far = pltpu.make_async_remote_copy(
                src_ref=src.at[i],
                dst_ref=dst.at[i],
                send_sem=send.at[i],
                recv_sem=recv.at[i],
                device_id={"dp": col // self.m, "ctx": row * self.m + i},
                device_id_type=pl.DeviceIdType.MESH,
            )
            pl.when(own)(local.wait)
            pl.when(jnp.logical_not(own))(far.wait_recv)

    def middle(self, *refs):
        pass


class Swap:
    def __init__(self, axis, array):
        self.axis, self.array = axis, array

    def plan(self, sizes):
        self.n = sizes[self.axis]
        self.out = jax.ShapeDtypeStruct(self.array.shape, self.array.dtype)
        self.scratch = [pltpu.SemaphoreType.DMA((self.n,))] * 2 + [pltpu.SemaphoreType.DMA(())]

    def start(self, src, dst, send, recv, own):
        me = lax.axis_index(self.axis)
        self.local = pltpu.make_async_copy(src.at[me], dst.at[me], own)
        self.local.start()
        self.copies = []
        for k in range(1, self.n):
            peer = lax.rem(me + k, self.n)
            copy = remote(src.at[peer], dst.at[me], send.at[k], recv.at[k], self.axis, peer)
            copy.start()
            self.copies.append(copy)

    def middle(self, *refs):
        pass

    def finish(self, src, dst, send, recv, own):
        me = lax.axis_index(self.axis)
        for k in range(1, self.n):
            slot = lax.rem(me + self.n - k, self.n)
            remote(
                src.at[slot], dst.at[slot], send.at[k], recv.at[k], self.axis, slot
            ).wait_recv()
        for copy in self.copies:
            copy.wait_send()
        self.local.wait()


class Shift:
    def __init__(self, axis, array, by):
        self.axis, self.array, self.by = axis, array, by

    def plan(self, sizes):
        self.n = sizes[self.axis]
        self.out = jax.ShapeDtypeStruct(self.array.shape, self.array.dtype)
        self.scratch = [pltpu.SemaphoreType.DMA(())] * 2

    def start(self, src, dst, send, recv):
        me = lax.axis_index(self.axis)
        peer = lax.rem(me + self.n + self.by, self.n)
        self.copy = remote(src, dst, send, recv, self.axis, peer)
        self.copy.start()

    def middle(self, *refs):
        pass

    def finish(self, *refs):
        self.copy.wait_recv()
        self.copy.wait_send()


class Reduce:
    axis = "ctx"

    def __init__(self, array):
        self.array = array

    def plan(self, sizes):
        self.n = sizes[self.axis]
        block = self.array.shape[1:]
        chips = self.n // 2
        self.out = jax.ShapeDtypeStruct(block, f32)
        slots = pltpu.VMEM((chips,) + block, self.array.dtype)
        self.scratch = [pltpu.SemaphoreType.DMA((chips,))] * 4 + [slots] * 3

    def start(self, src, dst, psend, precv, send, recv, near, term, far):
        me = lax.axis_index(self.axis)
        chips = self.n // 2
        chip, core = me // 2, me % 2
        partner = me + 1 - 2 * core
        self.copies = []
        for k in list(range(1, chips)) + [0]:
            slot = lax.rem(chip + k, chips) * 2 + 1 - core
            copy = remote(
                src.at[slot], near.at[k], psend.at[k], precv.at[k], self.axis, partner
            )
            copy.start()
            self.copies.append(copy)

    def middle(self, src, dst, psend, precv, send, recv, near, term, far):
        me = lax.axis_index(self.axis)
        chips = self.n // 2
        chip, core = me // 2, me % 2
        partner = me + 1 - 2 * core
        for k in range(1, chips):
            remote(
                src.at[me], near.at[k], psend.at[k], precv.at[k], self.axis, partner
            ).wait_recv()
            peer = lax.rem(chip + k, chips) * 2 + core
            both = src[peer].astype(f32) + near[k].astype(f32)
            term[k] = both.astype(term.dtype)
            copy = remote(term.at[k], far.at[k], send.at[k], recv.at[k], self.axis, peer)
            copy.start()
            self.copies.append(copy)

    def finish(self, src, dst, psend, precv, send, recv, near, term, far):
        me = lax.axis_index(self.axis)
        chips = self.n // 2
        core = me % 2
        partner = me + 1 - 2 * core
        remote(src.at[me], near.at[0], psend.at[0], precv.at[0], self.axis, partner).wait_recv()
        dst[...] = src[me].astype(f32) + near[0].astype(f32)
        for k in range(1, chips):
            remote(
                src.at[me], far.at[k], send.at[k], recv.at[k], self.axis, partner
            ).wait_recv()
            dst[...] += far[k].astype(f32)
        for copy in self.copies:
            copy.wait_send()


def exchange(ident, *tasks):
    sizes = {axis: lax.axis_size(axis) for axis in ("dp", "ctx")}
    for task in tasks:
        task.plan(sizes)
    axes = [axis for axis in ("dp", "ctx") if any(task.axis == axis for task in tasks)]
    everyone = any(task.axis == "all" for task in tasks)
    axes = [] if everyone else axes
    count = len(tasks)

    def kernel(*refs):
        barrier = pltpu.get_barrier_semaphore()
        greeted = 0
        if everyone:
            row, col = lax.axis_index("dp"), lax.axis_index("ctx")
            for i in range(1, sizes["dp"] * sizes["ctx"]):
                other = lax.rem(row * sizes["ctx"] + col + i, sizes["dp"] * sizes["ctx"])
                pl.semaphore_signal(
                    barrier,
                    inc=1,
                    device_id={"dp": other // sizes["ctx"], "ctx": other % sizes["ctx"]},
                    device_id_type=pl.DeviceIdType.MESH,
                )
                greeted += 1
        for axis in axes:
            me, n = lax.axis_index(axis), sizes[axis]
            for k in range(1, n):
                pl.semaphore_signal(
                    barrier,
                    inc=1,
                    device_id={axis: lax.rem(me + k, n)},
                    device_id_type=pl.DeviceIdType.MESH,
                )
            greeted += n - 1
        pl.semaphore_wait(barrier, greeted)
        held, at = [], 2 * count
        for i, task in enumerate(tasks):
            held.append((refs[i], refs[count + i]) + tuple(refs[at : at + len(task.scratch)]))
            at += len(task.scratch)
        for task, own in zip(tasks, held):
            task.start(*own)
        for k in range(sizes["ctx"] // 2 - 1):
            for task, own in zip(tasks, held):
                if isinstance(task, Relay):
                    task.step(k, *own)
                elif k == 0:
                    task.middle(*own)
        for task, own in zip(tasks, held):
            task.finish(*own)

    return pl.pallas_call(
        kernel,
        out_shape=[task.out for task in tasks],
        in_specs=[pl.BlockSpec(memory_space=pltpu.VMEM)] * count,
        out_specs=[pl.BlockSpec(memory_space=pltpu.VMEM)] * count,
        scratch_shapes=[shape for task in tasks for shape in task.scratch],
        compiler_params=pltpu.CompilerParams(
            collective_id=ident, has_side_effects=True, vmem_limit_bytes=60 * 1024 * 1024
        ),
        name=f"exchange_{ident}",
    )(*[task.array for task in tasks])


def spread(axes, sizes, everyone):
    barrier = pltpu.get_barrier_semaphore()
    greeted = 0
    if everyone:
        row, col = lax.axis_index("dp"), lax.axis_index("ctx")
        total = sizes["dp"] * sizes["ctx"]

        def greet(i, carry):
            other = lax.rem(row * sizes["ctx"] + col + i, total)
            pl.semaphore_signal(
                barrier,
                inc=1,
                device_id={"dp": other // sizes["ctx"], "ctx": other % sizes["ctx"]},
                device_id_type=pl.DeviceIdType.MESH,
            )
            return carry

        lax.fori_loop(1, total, greet, 0)
        greeted = total - 1
    else:
        for axis in axes:
            me, n = lax.axis_index(axis), sizes[axis]
            for k in range(1, n):
                pl.semaphore_signal(
                    barrier,
                    inc=1,
                    device_id={axis: lax.rem(me + k, n)},
                    device_id_type=pl.DeviceIdType.MESH,
                )
            greeted += n - 1
    pl.semaphore_wait(barrier, greeted)


def mm(a, b, dims):
    return lax.dot_general(a, b, ((dims[:1], dims[1:]), ((), ())), preferred_element_type=f32)


def nn(a, b):
    return mm(a, b, (1, 0))


def nt(a, b):
    return mm(a, b, (1, 1))


def tn(a, b):
    return mm(a, b, (0, 0))


def turned(rows):
    width = rows.shape[-1]
    parts = rows.reshape(-1, 2, HEAD_DIM // 2, width)
    return jnp.concatenate([-parts[:, 1:], parts[:, :1]], axis=1).reshape(rows.shape)


def rope_tables(row_count):
    half = HEAD_DIM // 2
    frequency = np.float32(rope_base) ** (-np.arange(half).astype(np.float32) * np.float32(2.0 / HEAD_DIM))
    angles = np.arange(row_count).astype(np.float32)[:, None] * frequency[None, :].astype(np.float32)
    return [jnp.asarray(np.tile(f(angles), (1, 2)), f32) for f in (np.cos, np.sin)]


def norm_backward(hidden, inverse, gain_vec, upstream):
    scaled = upstream * gain_vec
    cubed = inverse * inverse * inverse
    d_hidden = (
        inverse * scaled
        - hidden
        * cubed
        * jnp.sum(scaled * hidden, axis=-1, keepdims=True)
        / hidden.shape[-1]
    )
    return d_hidden, jnp.sum(upstream * hidden * inverse, axis=0)


def inverse_rms(hidden):
    return lax.rsqrt(jnp.mean(hidden * hidden, axis=-1, keepdims=True) + epsilon)


class Line:
    axis = "ctx"

    def __init__(self, n):
        self.n, self.chips = n, n // 2
        self.scratch = [pltpu.SemaphoreType.DMA((self.chips,))] * 6

    def hold(self, dst, sems):
        self.dst = dst
        self.rs, self.rr, self.ls, self.lr, self.ps, self.pr = sems
        self.me = lax.axis_index(self.axis)
        self.chip, self.core = self.me // 2, self.me % 2
        self.partner = self.me + 1 - 2 * self.core

    def copy(self, slot, send, recv, peer):
        return remote(self.dst.at[slot], self.dst.at[slot], send, recv, self.axis, peer)

    def start(self):
        me, chip = self.me, self.chip
        pl.when(chip < self.chips - 1)(self.copy(me, self.rs.at[0], self.rr.at[0], me + 2).start)
        pl.when(chip > 0)(self.copy(me, self.ls.at[0], self.lr.at[0], me - 2).start)
        self.copy(me, self.ps.at[chip], self.pr.at[chip], self.partner).start()

    def step(self, k):
        me, chip, chips = self.me, self.chip, self.chips

        def arrived(at, way, send, recv):
            slot = at * 2 + self.core
            self.copy(slot, send.at[k], recv.at[k], me - 2 * way).wait_recv()

            @pl.when(jnp.logical_and(chip + way >= 0, chip + way < chips))
            def _():
                self.copy(slot, send.at[k + 1], recv.at[k + 1], me + 2 * way).start()

            self.copy(slot, self.ps.at[at], self.pr.at[at], self.partner).start()

        @pl.when(chip - 1 - k >= 0)
        def _():
            arrived(chip - 1 - k, 1, self.rs, self.rr)

        @pl.when(chip + 1 + k < chips)
        def _():
            arrived(chip + 1 + k, -1, self.ls, self.lr)

    def beside(self, at):
        slot = 2 * at + 1 - self.core
        self.copy(slot, self.ps.at[at], self.pr.at[at], self.partner).wait_recv()

    def each(self, body):
        self.beside(self.chip)
        body(self.chip)

        def at_step(k, carry):
            self.step(k)

            def at_side(side, inner):
                at = jnp.where(side == 0, self.chip - 1 - k, self.chip + 1 + k)

                @pl.when(jnp.logical_and(at >= 0, at < self.chips))
                def _():
                    self.beside(at)
                    body(at)

                return inner

            return lax.fori_loop(0, 2, at_side, carry)

        if self.chips > 1:
            lax.fori_loop(0, self.chips - 1, at_step, 0)

    def sent(self):
        me, chip, chips = self.me, self.chip, self.chips
        for c in range(chips):
            self.copy(2 * c + self.core, self.ps.at[c], self.pr.at[c], self.partner).wait_send()
        for k in range(chips - 1):

            @pl.when(jnp.logical_and(chip < chips - 1, k <= chip))
            def _():
                self.copy(me, self.rs.at[k], self.rr.at[k], me + 2).wait_send()

            @pl.when(jnp.logical_and(chip > 0, k <= chips - 1 - chip))
            def _():
                self.copy(me, self.ls.at[k], self.lr.at[k], me - 2).wait_send()


class Sum:
    axis = "ctx"

    def __init__(self, n):
        self.n, self.chips = n, n // 2
        self.scratch = [pltpu.SemaphoreType.DMA((self.chips,))] * 6

    def hold(self, part, near, got, sems):
        self.part, self.near, self.got = part, near, got
        self.ps, self.pr, self.rs, self.rr, self.ls, self.lr = sems
        self.me = lax.axis_index(self.axis)
        self.chip, self.core = self.me // 2, self.me % 2
        self.partner = self.me + 1 - 2 * self.core

    def beside(self, d):
        return remote(
            self.part.at[2 * d + 1 - self.core],
            self.near.at[d],
            self.ps.at[d],
            self.pr.at[d],
            self.axis,
            self.partner,
        )

    def right(self, d):
        return remote(
            self.part.at[2 * d + self.core],
            self.got.at[d],
            self.rs.at[d],
            self.rr.at[d],
            self.axis,
            self.me + 2,
        )

    def left(self, d):
        place = jnp.where(d == self.chip - 1, self.chips, d)
        return remote(
            self.part.at[2 * d + self.core],
            self.got.at[place],
            self.ls.at[d],
            self.lr.at[d],
            self.axis,
            self.me - 2,
        )

    def ready(self, d):
        self.beside(d).start()

    def order(self, k):
        return jnp.where(self.chip < self.chips // 2, self.chips - 1 - k, k)

    def pair(self, d):
        self.beside(d).wait_recv()
        return self.part[2 * d + self.core].astype(f32) + self.near[d].astype(f32)

    def step(self, t):
        chip, chips = self.chip, self.chips

        @pl.when(t >= chip)
        def _():
            d = chips - 1 - t + chip
            both = self.pair(d)

            @pl.when(chip == 0)
            def _():
                self.part[2 * d + self.core] = both.astype(bf16)

            @pl.when(chip > 0)
            def _():
                self.right(d).wait_recv()
                self.part[2 * d + self.core] = (both + self.got[d].astype(f32)).astype(bf16)

            self.right(d).start()

        @pl.when(t >= chips - 1 - chip)
        def _():
            d = t - (chips - 1 - chip)
            both = self.pair(d)

            @pl.when(chip == chips - 1)
            def _():
                self.part[2 * d + self.core] = both.astype(bf16)

            @pl.when(chip < chips - 1)
            def _():
                self.left(d).wait_recv()
                self.part[2 * d + self.core] = (both + self.got[d].astype(f32)).astype(bf16)

            self.left(d).start()

    def last(self, total):
        chip, chips = self.chip, self.chips
        total[...] = self.pair(chip)

        @pl.when(chip > 0)
        def _():
            self.right(chip).wait_recv()
            total[...] += self.got[chip].astype(f32)

        @pl.when(chip < chips - 1)
        def _():
            self.left(chip).wait_recv()
            total[...] += self.got[chips].astype(f32)

    def sent(self):
        for d in range(self.chips):
            self.beside(d).wait_send()
            pl.when(self.chip < d)(self.right(d).wait_send)
            pl.when(self.chip > d)(self.left(d).wait_send)


def mid_layer(ident, attended, wo, x_own, cot_full, gains, w_gate, w_up, w_down_t):
    sizes = {axis: lax.axis_size(axis) for axis in ("dp", "ctx")}
    dp, n = sizes["dp"], sizes["ctx"]
    chips = n // 2
    rows, width = x_own.shape
    wide, f_w = wo.shape[0], w_gate.shape[1]
    in_rows = width // dp
    shape = jax.ShapeDtypeStruct
    lines = [Line(n), Line(n)]
    sums = [Sum(n), Sum(n)]
    swap = Swap("dp", shape((dp, in_rows, 3 * f_w), bf16))
    swap.plan(sizes)
    tasks = lines + sums + [swap]

    def kernel(*refs):
        att, wo_ref, x_ref, cots, gain_ref, wg, wu, wd = refs[:8]
        d_mids, d_mid, mid, out_part, g_all, g_gain = refs[8:14]
        part, near, got, n2, mixed, d_gate, d_up, grads, inv, total = refs[14:24]
        sems, at = [], 24
        for task in tasks:
            sems.append(tuple(refs[at : at + len(task.scratch)]))
            at += len(task.scratch)
        spread(("dp", "ctx"), sizes, False)
        lines[0].hold(n2, sems[0])
        lines[1].hold(d_mids, sems[1])
        sums[0].hold(part, near, got, sems[2])
        sums[1].hold(part, near, got, sems[3])
        me = lax.axis_index("ctx")

        def project(k, carry):
            d = sums[0].order(k)
            rows_of = att[pl.ds(2 * d, 2)].reshape(2 * rows, wide)
            part[pl.ds(2 * d, 2)] = nn(rows_of, wo_ref[...]).astype(bf16).reshape(2, rows, width)
            sums[0].ready(d)
            return carry

        lax.fori_loop(0, chips, project, 0)
        for t in range(chips - 1):
            sums[0].step(t)
        sums[0].last(total)
        middle = x_ref[...].astype(f32) + total[...]
        inverse = inverse_rms(middle)
        mid[...] = middle
        inv[...] = inverse
        n2[me] = (middle * inverse * gain_ref[1:2]).astype(bf16)
        lines[0].start()
        sums[0].sent()

        def forward(at):
            here = pl.ds(2 * at, 2)
            tokens = n2[here].reshape(2 * rows, width)
            gate_pre = nn(tokens, wg[...])
            up_pre = nn(tokens, wu[...])
            d_mixed = nn(cots[here].reshape(2 * rows, width), wd[...])
            sigma = 1.0 / (1.0 + jnp.exp(-gate_pre))
            silu_gate = gate_pre * sigma
            act = (silu_gate * up_pre).astype(bf16)
            dg = (d_mixed * up_pre * sigma * (1.0 + gate_pre * (1.0 - sigma))).astype(bf16)
            du = (d_mixed * silu_gate).astype(bf16)
            mixed[here] = act.reshape(2, rows, f_w)
            d_gate[here] = dg.reshape(2, rows, f_w)
            d_up[here] = du.reshape(2, rows, f_w)
            d_two = nt(dg, wg[...]) + nt(du, wu[...])
            part[here] = d_two.astype(bf16).reshape(2, rows, width)
            sums[1].ready(at)
            out_part[here] = nt(act, wd[...]).astype(bf16).reshape(2, rows, width)

        lines[0].each(forward)

        def gradient(i):
            left, right = ((n2, d_gate), (n2, d_up), (cots, mixed))[i]
            value = tn(
                left[...].reshape(n * rows, width), right[...].reshape(n * rows, f_w)
            ).astype(bf16)
            for r in range(dp):
                grads[r, :, i * f_w : (i + 1) * f_w] = value[r * in_rows : (r + 1) * in_rows]

        for t in range(chips - 1):
            sums[1].step(t)
            if t == 0:
                gradient(0)
                gradient(1)
            if t == min(1, chips - 2):
                gradient(2)
                swap.start(grads, g_all, *sems[4])
        sums[1].last(total)
        middle = mid[...]
        d_norm, gain_part = norm_backward(middle, inv[...], gain_ref[1:2], total[...])
        g_gain[...] = gain_part.reshape(1, width)
        d_middle = cots[me].astype(f32) + d_norm
        d_mid[...] = d_middle
        d_mids[me] = d_middle.astype(bf16)
        lines[1].start()
        sums[1].sent()
        lines[0].sent()
        lines[1].each(lambda at: None)
        lines[1].sent()
        swap.finish(grads, g_all, *sems[4])

    whole = (n, rows, width)
    return pl.pallas_call(
        kernel,
        out_shape=[
            shape(whole, bf16),
            shape((rows, width), f32),
            shape((rows, width), f32),
            shape(whole, bf16),
            shape((dp, in_rows, 3 * f_w), bf16),
            shape((1, width), f32),
        ],
        in_specs=[pl.BlockSpec(memory_space=pltpu.VMEM)] * 8,
        out_specs=[pl.BlockSpec(memory_space=pltpu.VMEM)] * 6,
        scratch_shapes=[
            pltpu.VMEM(whole, bf16),
            pltpu.VMEM((chips, rows, width), bf16),
            pltpu.VMEM((chips + 1, rows, width), bf16),
            pltpu.VMEM(whole, bf16),
            pltpu.VMEM((n, rows, f_w), bf16),
            pltpu.VMEM((n, rows, f_w), bf16),
            pltpu.VMEM((n, rows, f_w), bf16),
            pltpu.VMEM((dp, in_rows, 3 * f_w), bf16),
            pltpu.VMEM((rows, 1), f32),
            pltpu.VMEM((rows, width), f32),
        ]
        + [item for task in tasks for item in task.scratch],
        compiler_params=pltpu.CompilerParams(
            collective_id=ident, has_side_effects=True, vmem_limit_bytes=62 * 1024 * 1024
        ),
        name=f"block_{ident}",
    )(attended, wo, x_own, cot_full, gains, w_gate, w_up, w_down_t)


class Need:
    axis = "ctx"

    def __init__(self, n, low, high):
        self.n, self.low, self.high = n, low, high
        self.slots = max(high(d) - low(d) + 1 for d in range(n))
        self.scratch = [
            pltpu.SemaphoreType.DMA((n,)),
            pltpu.SemaphoreType.DMA((self.slots,)),
        ]

    def hold(self, src, dst, sems):
        self.src, self.dst = src, dst
        self.send, self.recv = sems
        self.me = lax.axis_index(self.axis)
        self.first, self.final = self.low(self.me), self.high(self.me)

    def each(self):
        for d in range(self.n):
            low, high = self.low(d), self.high(d)
            used = jnp.logical_and(self.me >= low, self.me <= high)
            slot = jnp.clip(self.me - low, 0, self.slots - 1)
            copy = remote(
                self.src, self.dst.at[slot], self.send.at[d], self.recv.at[slot], self.axis, d
            )
            yield jnp.logical_and(used, self.me != d), copy

    def start(self):
        for used, copy in self.each():
            pl.when(used)(copy.start)
        for t in range(self.slots):
            source = self.first + t

            @pl.when(source == self.me)
            def _():
                self.dst[t] = self.src[...]

            @pl.when(source > self.final)
            def _():
                self.dst[t] = jnp.zeros_like(self.dst[t])

    def arrive(self):
        beside = self.me + 1 - 2 * lax.rem(self.me, 2)
        for t in range(self.slots):
            source = self.first + t
            copy = remote(
                self.src, self.dst.at[t], self.send.at[0], self.recv.at[t], self.axis, beside
            )
            pl.when(jnp.logical_and(source <= self.final, source != self.me))(copy.wait_recv)

    def sent(self):
        for used, copy in self.each():
            pl.when(used)(copy.wait_send)


def least(a, b):
    return min(a, b) if isinstance(a, int) else jnp.minimum(a, b)


def over(a, b):
    return a // b if isinstance(a, int) else lax.div(a, b)


def pick(rows, first, source, sign):
    at = first + lax.broadcasted_iota(jnp.int32, (rows, source.shape[1]), 0)
    return jnp.where(at == source, sign, 0.0)


def kv_head(j):
    return least(over(j, GROUP), KV_HEADS - 1)


def needs(n, held, width, q_w, k_w):
    wide = held * HEAD_DIM
    q_need = Need(
        n,
        lambda d: over(least(wide * d, width - 1), q_w),
        lambda d: over(least(wide * d + wide - 1, width - 1), q_w),
    )
    kv_need = Need(
        n,
        lambda d: over(HEAD_DIM * kv_head(held * d), k_w),
        lambda d: over(HEAD_DIM * kv_head(held * d + held - 1) + HEAD_DIM - 1, k_w),
    )
    return q_need, kv_need


def front(ident, x_t, cot_t, w_q, kv_rows, w_o, gains, wg_t, wu_t, wd_t, held, tables):
    sizes = {axis: lax.axis_size(axis) for axis in ("dp", "ctx")}
    dp, n = sizes["dp"], sizes["ctx"]
    chips, each = n // 2, n // dp
    width, rows = x_t.shape
    in_rows, q_w = w_q.shape
    o_w, k_w, f_w = w_o.shape[1], kv_rows.shape[0] // 2, wg_t.shape[0]
    wide, total = held * HEAD_DIM, n * held * HEAD_DIM
    length, chunk = n * rows, 2 * rows
    shape = jax.ShapeDtypeStruct

    q_need, kv_need = needs(n, held, width, q_w, k_w)
    x_line, cot_line, gain_line = Line(n), Line(n), Line(n)
    q_all, kv_all, o_all = Gather(w_q), Gather(kv_rows), Gather(w_o)
    g_all, u_all = [Gather(shape((in_rows, f_w), bf16)) for _ in range(2)]
    d_turn = Turn(shape((each, o_w, f_w), bf16))
    d_all = Gather(shape((each, o_w, f_w), bf16))
    o_swap = Swap("ctx", shape((n, wide, o_w), bf16))
    planned = [q_all, kv_all, o_all, g_all, u_all, d_turn, d_all, o_swap]
    for task in planned:
        task.plan(sizes)
    tasks = [q_need, kv_need, x_line, cot_line, gain_line] + planned

    def kernel(*refs):
        xt, ct, wq_ref, kv_ref, wo_ref, gain_in, wgt, wut, wdt, cos_ref, sin_ref = refs[:11]
        att, lse, q_two, k_two, val, n1, cots, wo_out, wqkv, gain_out = refs[11:21]
        wg_out, wu_out, wd_out, x_own = refs[21:25]
        xs, gains_in, q_got, kv_got, o_got, q_in, kv_in, wall = refs[25:33]
        wg_mine, wu_mine, d_mine, d_got, o_cut, o_in = refs[33:39]
        sems, at = {}, 39
        for task in tasks:
            sems[task] = tuple(refs[at : at + len(task.scratch)])
            at += len(task.scratch)
        spread(("dp", "ctx"), sizes, True)
        me = lax.axis_index("ctx")
        x_line.hold(xs, sems[x_line])
        cot_line.hold(cots, sems[cot_line])
        gain_line.hold(gains_in, sems[gain_line])
        q_need.hold(q_got, q_in, sems[q_need])
        kv_need.hold(kv_got, kv_in, sems[kv_need])
        mine = xt[...].T
        xs[me] = mine
        x_own[...] = mine
        x_line.start()
        q_all.start(wq_ref, q_got, *sems[q_all])
        kv_all.start(kv_ref, kv_got, *sems[kv_all])
        gains_in[me] = gain_in[...]
        gain_line.start()
        cots[me] = ct[...].T
        wg_mine[...] = wgt[...].T
        wu_mine[...] = wut[...].T
        for i in range(each):
            d_mine[i] = wdt[:, i * f_w : (i + 1) * f_w]
        q_all.finish(wq_ref, q_got, *sems[q_all])
        kv_all.finish(kv_ref, kv_got, *sems[kv_all])
        q_need.start()
        kv_need.start()
        o_all.start(wo_ref, o_got, *sems[o_all])
        d_turn.start(d_mine, d_got, *sems[d_turn])
        for k in range(chips - 1):
            gain_line.step(k)
        for c in range(chips):
            gain_line.beside(c)
        gain_line.sent()
        for c in range(n):
            gain_out[:, c * o_w : (c + 1) * o_w] = gains_in[c].astype(f32)

        def turned(base, d):
            half = HEAD_DIM // 2
            return base + jnp.bitwise_and(d + half, HEAD_DIM - 1), jnp.where(d < half, -1.0, 1.0)

        def plan(heads):
            lane = lax.broadcasted_iota(jnp.int32, (1, 2 * HEAD_DIM), 1)
            d = jnp.bitwise_and(lane, HEAD_DIM - 1)
            parts = []
            for h in heads:
                parts.append((h * HEAD_DIM + d, jnp.ones((1, 2 * HEAD_DIM), f32)))
                parts.append(turned(h * HEAD_DIM, d))
            lane = lax.broadcasted_iota(jnp.int32, (1, wide), 1)
            flat = jnp.bitwise_and(lane, HEAD_DIM - 1)
            base = jnp.zeros((1, wide), jnp.int32)
            for i, h in enumerate(heads):
                inside = jnp.logical_and(lane >= i * HEAD_DIM, lane < (i + 1) * HEAD_DIM)
                base = jnp.where(inside, h * HEAD_DIM, base)
            return parts + [(base + flat, jnp.ones((1, wide), f32))]

        heads = [me * held + h for h in range(held)]
        kv_heads = [kv_head(h) for h in heads]
        q_plan, k_plan = plan(heads), plan(kv_heads)
        no = [(jnp.zeros_like(k_plan[-1][0]) - 1, k_plan[-1][1])]
        q_need.arrive()
        kv_need.arrive()
        span = 4 * held * HEAD_DIM
        for r in range(dp):
            here = slice(r * in_rows, (r + 1) * in_rows)
            value = None
            for t in range(q_need.slots):
                first = (q_need.first + t) * q_w
                take = jnp.concatenate([pick(q_w, first, *p) for p in q_plan], axis=1)
                term = nn(q_in[t, r], take.astype(bf16))
                value = term if value is None else value + term
            value = value.astype(bf16)
            wall[here, :span] = value[:, :span]
            wqkv[here, :wide] = value[:, span:]
            value = None
            for t in range(kv_need.slots):
                first = (kv_need.first + t) * k_w
                top = [pick(k_w, first, *p) for p in k_plan + no]
                zero = jnp.zeros((k_w, span + wide), f32)
                top = jnp.concatenate(top, axis=1)
                low = jnp.concatenate([zero, pick(k_w, first, *k_plan[-1])], axis=1)
                take = jnp.concatenate([top, low], axis=0).astype(bf16)
                term = tn(kv_in[t, r], take)
                value = term if value is None else value + term
            value = value.astype(bf16)
            wall[here, span:] = value[:, :span]
            wqkv[here, wide:] = value[:, span:]
        g_all.start(wg_mine, wg_out, *sems[g_all])
        u_all.start(wu_mine, wu_out, *sems[u_all])

        def project(at):
            here = pl.ds(2 * at, 2)
            tokens = xs[here].reshape(chunk, width).astype(f32)
            normed = (tokens * inverse_rms(tokens) * gain_out[0:1]).astype(bf16)
            n1[here] = normed.reshape(2, rows, width)
            both = nn(normed, wall[...])
            low = pl.multiple_of(at * chunk, chunk)
            first, second = cos_ref[pl.ds(low, chunk)], sin_ref[pl.ds(low, chunk)]
            for h in range(2 * held):
                at_h = h * 4 * HEAD_DIM
                a = both[:, at_h : at_h + 2 * HEAD_DIM]
                b = both[:, at_h + 2 * HEAD_DIM : at_h + 4 * HEAD_DIM]
                two = a * first + b * second
                if h < held:
                    q_two[h, pl.ds(low, chunk)] = (two * HEAD_DIM ** (-0.5)).astype(bf16)
                else:
                    k_two[h - held, pl.ds(low, chunk)] = two.astype(bf16)
            v = nn(normed, wqkv[:, 2 * wide :]).astype(bf16)
            for h in range(held):
                val[h, pl.ds(low, chunk)] = v[:, h * HEAD_DIM : (h + 1) * HEAD_DIM]

        x_line.each(project)
        cot_line.start()
        d_turn.finish(d_mine, d_got, *sems[d_turn])
        d_all.start(d_got, wd_out, *sems[d_all])
        o_all.finish(wo_ref, o_got, *sems[o_all])
        for j in range(n):
            for r in range(dp):
                low, high = max(r * in_rows, j * wide), min((r + 1) * in_rows, (j + 1) * wide)
                if low < high:
                    o_cut[j, low - j * wide : high - j * wide] = o_got[
                        r, low - r * in_rows : high - r * in_rows
                    ]
            used = min(max(HEADS * HEAD_DIM - j * wide, 0), wide)
            if used < wide:
                o_cut[j, used:] = jnp.zeros((wide - used, o_w), bf16)
        o_swap.start(o_cut, o_in, *sems[o_swap])
        x_line.sent()

        def attend(i):
            first, last = i * chunk, (i + 1) * chunk
            for h in range(held):
                q = q_two[h, first:last, :HEAD_DIM]
                diag = nt(q, k_two[h, first:last, :HEAD_DIM])
                row = lax.broadcasted_iota(jnp.int32, diag.shape, 0)
                col = lax.broadcasted_iota(jnp.int32, diag.shape, 1)
                diag = jnp.where(row >= col, diag, -1e30)
                top = jnp.max(diag, axis=-1, keepdims=True)
                if i:
                    off = nt(q, k_two[h, :first, :HEAD_DIM])
                    top = jnp.maximum(top, jnp.max(off, axis=-1, keepdims=True))
                expo = jnp.exp(diag - top)
                weight = jnp.sum(expo, axis=-1, keepdims=True)
                out = nn(expo.astype(bf16), val[h, first:last])
                if i:
                    expo = jnp.exp(off - top)
                    weight = weight + jnp.sum(expo, axis=-1, keepdims=True)
                    out = out + nn(expo.astype(bf16), val[h, :first])
                out = (out / weight).astype(bf16)
                lanes = slice(h * HEAD_DIM, (h + 1) * HEAD_DIM)
                att[2 * i : 2 * i + 2, :, lanes] = out.reshape(2, rows, HEAD_DIM)
                logs = jnp.broadcast_to(top + jnp.log(weight), (chunk, HEAD_DIM))
                lse[first:last, lanes] = logs

        for i in range(chips):
            attend(i)
            if i < chips - 1:
                cot_line.step(i)
        o_swap.finish(o_cut, o_in, *sems[o_swap])
        for c in range(n):
            wo_out[:, c * o_w : (c + 1) * o_w] = o_in[c]
        for c in range(chips):
            cot_line.beside(c)
        cot_line.sent()
        q_need.sent()
        kv_need.sent()
        g_all.finish(wg_mine, wg_out, *sems[g_all])
        u_all.finish(wu_mine, wu_out, *sems[u_all])
        d_all.finish(d_got, wd_out, *sems[d_all])

    whole = (n, rows, width)
    outs = [
        shape((n, rows, wide), bf16),
        shape((length, wide), f32),
        shape((held, length, 2 * HEAD_DIM), bf16),
        shape((held, length, 2 * HEAD_DIM), bf16),
        shape((held, length, HEAD_DIM), bf16),
        shape(whole, bf16),
        shape(whole, bf16),
        shape((wide, width), bf16),
        shape((width, 3 * wide), bf16),
        shape((2, width), f32),
        shape((dp, in_rows, f_w), bf16),
        shape((dp, in_rows, f_w), bf16),
        shape((dp, each, o_w, f_w), bf16),
        shape((rows, width), bf16),
    ]
    return pl.pallas_call(
        kernel,
        out_shape=outs,
        in_specs=[pl.BlockSpec(memory_space=pltpu.VMEM)] * 11,
        out_specs=[pl.BlockSpec(memory_space=pltpu.VMEM)] * len(outs),
        scratch_shapes=[
            pltpu.VMEM(whole, bf16),
            pltpu.VMEM((n, 2, o_w), bf16),
            pltpu.VMEM((dp, in_rows, q_w), bf16),
            pltpu.VMEM((dp,) + kv_rows.shape, bf16),
            pltpu.VMEM((dp, in_rows, o_w), bf16),
            pltpu.VMEM((q_need.slots, dp, in_rows, q_w), bf16),
            pltpu.VMEM((kv_need.slots, dp) + kv_rows.shape, bf16),
            pltpu.VMEM((width, 8 * held * HEAD_DIM), bf16),
            pltpu.VMEM((in_rows, f_w), bf16),
            pltpu.VMEM((in_rows, f_w), bf16),
            pltpu.VMEM((each, o_w, f_w), bf16),
            pltpu.VMEM((each, o_w, f_w), bf16),
            pltpu.VMEM((n, wide, o_w), bf16),
            pltpu.VMEM((n, wide, o_w), bf16),
        ]
        + [item for task in tasks for item in task.scratch],
        compiler_params=pltpu.CompilerParams(
            collective_id=ident, has_side_effects=True, vmem_limit_bytes=62 * 1024 * 1024
        ),
        name=f"front_{ident}",
    )(x_t, cot_t, w_q, kv_rows, w_o, gains, wg_t, wu_t, wd_t, *tables)


class Give:
    axis = "ctx"

    def __init__(self, need):
        self.need = need
        self.scratch = [
            pltpu.SemaphoreType.DMA((need.slots,)),
            pltpu.SemaphoreType.DMA((need.n,)),
        ]

    def hold(self, mine, got, sems):
        self.mine, self.got = mine, got
        self.send, self.recv = sems
        self.me = lax.axis_index(self.axis)
        self.first, self.final = self.need.low(self.me), self.need.high(self.me)

    def copy(self, t, owner):
        return remote(
            self.mine.at[t],
            self.got.at[self.me],
            self.send.at[t],
            self.recv.at[self.me],
            self.axis,
            owner,
        )

    def start(self, term):
        for t in range(self.need.slots):
            owner = jnp.minimum(self.first + t, self.need.n - 1)
            used = self.first + t <= self.final

            @pl.when(used)
            def _():
                self.mine[t] = term(owner)

            pl.when(jnp.logical_and(used, owner != self.me))(self.copy(t, owner).start)

            @pl.when(jnp.logical_and(used, owner == self.me))
            def _():
                self.got[self.me] = self.mine[t]

    def add(self, total):
        beside = self.me + 1 - 2 * lax.rem(self.me, 2)
        total[...] = jnp.zeros_like(total)
        for d in range(self.need.n):
            used = jnp.logical_and(self.me >= self.need.low(d), self.me <= self.need.high(d))
            copy = remote(
                self.mine.at[0], self.got.at[d], self.send.at[0], self.recv.at[d], self.axis, beside
            )
            pl.when(jnp.logical_and(used, self.me != d))(copy.wait_recv)

            @pl.when(used)
            def _():
                total[...] += self.got[d].astype(f32)

    def sent(self):
        for t in range(self.need.slots):
            owner = jnp.minimum(self.first + t, self.need.n - 1)
            used = jnp.logical_and(self.first + t <= self.final, owner != self.me)
            pl.when(used)(self.copy(t, owner).wait_send)


def back(
    ident,
    d_mids,
    att,
    wo,
    lse,
    q_two,
    k_two,
    val,
    n1,
    wqkv,
    turn,
    d_mid,
    x_own,
    gains,
    mid,
    g_three,
    g_two,
    out_part,
    q_w,
    k_w,
):
    sizes = {axis: lax.axis_size(axis) for axis in ("dp", "ctx")}
    dp, n = sizes["dp"], sizes["ctx"]
    chips, each = n // 2, n // dp
    _, rows, width = d_mids.shape
    held, length, _ = q_two.shape
    wide, chunk = held * HEAD_DIM, 2 * rows
    in_rows, f_w = g_three.shape[1], g_three.shape[2] // 3
    o_w = width // n
    shape = jax.ShapeDtypeStruct
    q_need, kv_need = needs(n, held, width, q_w, k_w)
    q_give, kv_give = Give(q_need), Give(kv_need)
    sums = [Sum(n), Sum(n)]
    o_swap = Swap("ctx", shape((n, wide, o_w), bf16))
    o_down = Swap("dp", shape((dp, in_rows, o_w), bf16))
    w_swap = Swap("dp", shape((dp, 3 * wide, in_rows), bf16))
    d_turn = Turn(shape((each, o_w, f_w), bf16))
    gain_swap = Swap("ctx", shape((n, 2, o_w), f32))
    gain_all = Gather(shape((2, o_w), f32))
    planned = [o_swap, o_down, w_swap, d_turn, gain_swap, gain_all]
    for task in planned:
        task.plan(sizes)
    tasks = [q_give, kv_give] + sums + planned

    def kernel(*refs):
        dm_in, at_ref, wo_ref, lse_ref, q2, k2, v_ref, n_in, w_ref, turn_ref = refs[:10]
        mid_ref, x_ref, gain_ref, sum_ref, three, two_gain, out_in = refs[10:17]
        out_t, in_t, gq, gk, gv, go, gg, gu, gd, g_gain = refs[17:27]
        part, near, got, near_o, got_o, datt, dk2, dv, dqkv, total = refs[27:37]
        o_src, o_got, o_cut, o_sum, w_src, w_got, d_src, d_got = refs[37:45]
        gain_src, gain_got, gain_mine, gain_sum = refs[45:49]
        q_mine, q_got, kv_mine, kv_got, kv_sum, load, dm = refs[49:56]
        sems, at = {}, 56
        for task in tasks:
            sems[task] = tuple(refs[at : at + len(task.scratch)])
            at += len(task.scratch)
        bring = pltpu.make_async_copy(out_in, part, load.at[0])
        bring.start()
        bring_d = pltpu.make_async_copy(dm_in, dm, load.at[1])
        bring_d.start()
        bring_n = pltpu.make_async_copy(n_in, dm, load.at[2])
        spread(("dp", "ctx"), sizes, True)
        me = lax.axis_index("ctx")
        sums[0].hold(part, near_o, got_o, sems[sums[0]])
        sums[1].hold(part, near, got, sems[sums[1]])
        q_give.hold(q_mine, q_got, sems[q_give])
        kv_give.hold(kv_mine, kv_got, sems[kv_give])
        bring.wait()
        for k in range(chips):
            sums[0].ready(sums[0].order(k))

        def of_dp(low, high):
            value = three[0, :, low:high].astype(f32)
            for r in range(1, dp):
                value = value + three[r, :, low:high].astype(f32)
            return value

        down = of_dp(2 * f_w, 3 * f_w).astype(bf16)
        for i in range(each):
            d_src[i] = down[i * o_w : (i + 1) * o_w]
        d_turn.start(d_src, d_got, *sems[d_turn])
        bring_d.wait()
        for i in range(chips):
            tokens = dm[2 * i : 2 * i + 2].reshape(chunk, width)
            datt[i * chunk : (i + 1) * chunk] = nt(tokens, wo_ref[...]).astype(bf16)
        value = tn(at_ref[...].reshape(length, wide), dm[...].reshape(length, width)).astype(bf16)
        bring_n.start()
        for c in range(n):
            o_src[c] = value[:, c * o_w : (c + 1) * o_w]
        o_swap.start(o_src, o_got, *sems[o_swap])

        def put(ref, h, low, high, value, first):
            if first:
                ref[h, low:high] = value
            else:
                ref[h, low:high] += value

        def folded(two, low, high):
            both = two * turn_ref[low:high]
            return both[:, :HEAD_DIM] + both[:, HEAD_DIM:]

        def attend(i):
            first, last = i * chunk, (i + 1) * chunk
            new = i == chips - 1
            for h in range(held):
                lanes = slice(h * HEAD_DIM, (h + 1) * HEAD_DIM)
                q, grad = q2[h, first:last, :HEAD_DIM], datt[first:last, lanes]
                own = at_ref[2 * i : 2 * i + 2, :, lanes].reshape(chunk, HEAD_DIM)
                delta = jnp.sum(grad.astype(f32) * own.astype(f32), axis=-1, keepdims=True)
                log = lse_ref[first:last, h * HEAD_DIM : h * HEAD_DIM + 1]
                dq = None
                for low, high in ((first, last), (0, first)):
                    if low == high:
                        continue
                    scores = nt(q, k2[h, low:high, :HEAD_DIM])
                    if low == first:
                        row = lax.broadcasted_iota(jnp.int32, scores.shape, 0)
                        col = lax.broadcasted_iota(jnp.int32, scores.shape, 1)
                        scores = jnp.where(row >= col, scores, -1e30)
                    probs = jnp.exp(scores - log)
                    d_probs = nt(grad, v_ref[h, low:high])
                    d_scores = (probs * (d_probs - delta)).astype(bf16)
                    term = nn(d_scores, k2[h, low:high])
                    dq = term if dq is None else dq + term
                    put(dk2, h, low, high, tn(d_scores, q2[h, first:last]), new)
                    put(dv, h, low, high, tn(probs.astype(bf16), grad), new)
                dq = folded(dq, first, last) * HEAD_DIM ** (-0.5)
                dqkv[first:last, lanes] = dq.astype(bf16)

        for t in range(chips):
            attend(chips - 1 - t)
            if t < chips - 1:
                sums[0].step(t)
        for i in range(chips):
            first, last = i * chunk, (i + 1) * chunk
            for h in range(held):
                base = wide + h * HEAD_DIM
                dk = folded(dk2[h, first:last], first, last)
                dqkv[first:last, base : base + HEAD_DIM] = dk.astype(bf16)
                base = base + wide
                dqkv[first:last, base : base + HEAD_DIM] = dv[h, first:last].astype(bf16)
        sums[0].last(total)
        out_t[...] = (sum_ref[...] + total[...]).T.astype(bf16)
        sums[0].sent()

        def project(k, carry):
            d = sums[1].order(k)
            low = pl.multiple_of(d * chunk, chunk)
            value = nt(dqkv[pl.ds(low, chunk)], w_ref[...]).astype(bf16)
            part[pl.ds(2 * d, 2)] = value.reshape(2, rows, width)
            sums[1].ready(d)
            return carry

        lax.fori_loop(0, chips, project, 0)
        bring_n.wait()
        value = tn(dqkv[...], dm[...].reshape(length, width)).astype(bf16)
        for t in range(min(1, chips - 1)):
            sums[1].step(t)
        for r in range(dp):
            w_src[r] = value[:, r * in_rows : (r + 1) * in_rows]
        w_swap.start(w_src, w_got, *sems[w_swap])
        o_swap.finish(o_src, o_got, *sems[o_swap])
        for j in range(n):
            for r in range(dp):
                low, high = max(r * in_rows, j * wide), min((r + 1) * in_rows, (j + 1) * wide)
                if low < high:
                    o_cut[r, low - r * in_rows : high - r * in_rows] = o_got[
                        j, low - j * wide : high - j * wide
                    ]
        o_down.start(o_cut, o_sum, *sems[o_down])
        gg[...] = of_dp(0, f_w).T
        gu[...] = of_dp(f_w, 2 * f_w).T
        for t in range(1, chips - 1):
            sums[1].step(t)
        w_swap.finish(w_src, w_got, *sems[w_swap])
        value = w_got[0].astype(f32)
        for r in range(1, dp):
            value = value + w_got[r].astype(f32)
        value = value.astype(bf16)
        heads = [me * held + h for h in range(held)]

        def columns(of):
            lane = lax.broadcasted_iota(jnp.int32, (1, wide), 1)
            base = jnp.zeros((1, wide), jnp.int32)
            for i, h in enumerate(of):
                inside = jnp.logical_and(lane >= i * HEAD_DIM, lane < (i + 1) * HEAD_DIM)
                base = jnp.where(inside, h * HEAD_DIM, base)
            return base + jnp.bitwise_and(lane, HEAD_DIM - 1)

        q_nat = value[:wide].T
        kv_part = value[wide:]
        q_cols = columns(heads)
        kv_cols = columns([least(over(h, GROUP), KV_HEADS - 1) for h in heads])
        ones = jnp.ones((1, wide), f32)

        def q_term(owner):
            return nt(q_nat, pick(q_w, owner * q_w, q_cols, ones).astype(bf16)).astype(bf16)

        def kv_term(owner):
            one = pick(k_w, owner * k_w, kv_cols, ones)
            none = jnp.zeros_like(one)
            top = jnp.concatenate([one, none], axis=1)
            low = jnp.concatenate([none, one], axis=1)
            return nn(jnp.concatenate([top, low], axis=0).astype(bf16), kv_part).astype(bf16)

        kv_give.start(kv_term)
        q_give.start(q_term)
        sums[1].last(total)
        hidden = x_ref[...].astype(f32)
        inverse = inverse_rms(hidden)
        d_norm, gain_part = norm_backward(hidden, inverse, gain_ref[0:1], total[...])
        both = jnp.concatenate([gain_part.reshape(1, width), two_gain[...]], axis=0)
        for c in range(n):
            gain_src[c] = both[:, c * o_w : (c + 1) * o_w]
        gain_swap.start(gain_src, gain_got, *sems[gain_swap])
        in_t[...] = (mid_ref[...] + d_norm).T
        d_turn.finish(d_src, d_got, *sems[d_turn])
        for i in range(each):
            gd[:, i * f_w : (i + 1) * f_w] = d_got[i].astype(f32)
        gain_swap.finish(gain_src, gain_got, *sems[gain_swap])
        gain_mine[...] = jnp.sum(gain_got[...], axis=0)
        gain_all.start(gain_mine, gain_sum, *sems[gain_all])
        o_down.finish(o_cut, o_sum, *sems[o_down])
        value = o_sum[0].astype(f32)
        for r in range(1, dp):
            value = value + o_sum[r].astype(f32)
        go[...] = value
        kv_give.add(kv_sum)
        gk[...] = kv_sum[:k_w]
        gv[...] = kv_sum[k_w:]
        q_give.add(gq)
        gain_all.finish(gain_mine, gain_sum, *sems[gain_all])
        g_gain[...] = jnp.sum(gain_sum[...], axis=0)
        q_give.sent()
        kv_give.sent()
        sums[1].sent()

    whole = (n, rows, width)
    vmem = pl.BlockSpec(memory_space=pltpu.VMEM)
    anywhere = pl.BlockSpec(memory_space=pl.ANY)
    outs = [
        shape((width, rows), bf16),
        shape((width, rows), f32),
        shape((in_rows, q_w), f32),
        shape((k_w, in_rows), f32),
        shape((k_w, in_rows), f32),
        shape((in_rows, o_w), f32),
        shape((f_w, in_rows), f32),
        shape((f_w, in_rows), f32),
        shape((o_w, each * f_w), f32),
        shape((2, o_w), f32),
    ]
    return pl.pallas_call(
        kernel,
        out_shape=outs,
        in_specs=[anywhere] + [vmem] * 6 + [anywhere] + [vmem] * 8 + [anywhere],
        out_specs=[vmem] * len(outs),
        scratch_shapes=[
            pltpu.VMEM(whole, bf16),
            pltpu.VMEM((chips, rows, width), bf16),
            pltpu.VMEM((chips + 1, rows, width), bf16),
            pltpu.VMEM((chips, rows, width), bf16),
            pltpu.VMEM((chips + 1, rows, width), bf16),
            pltpu.VMEM((length, wide), bf16),
            pltpu.VMEM((held, length, 2 * HEAD_DIM), f32),
            pltpu.VMEM((held, length, HEAD_DIM), f32),
            pltpu.VMEM((length, 3 * wide), bf16),
            pltpu.VMEM((rows, width), f32),
            pltpu.VMEM((n, wide, o_w), bf16),
            pltpu.VMEM((n, wide, o_w), bf16),
            pltpu.VMEM((dp, in_rows, o_w), bf16),
            pltpu.VMEM((dp, in_rows, o_w), bf16),
            pltpu.VMEM((dp, 3 * wide, in_rows), bf16),
            pltpu.VMEM((dp, 3 * wide, in_rows), bf16),
            pltpu.VMEM((each, o_w, f_w), bf16),
            pltpu.VMEM((each, o_w, f_w), bf16),
            pltpu.VMEM((n, 2, o_w), f32),
            pltpu.VMEM((n, 2, o_w), f32),
            pltpu.VMEM((2, o_w), f32),
            pltpu.VMEM((dp, 2, o_w), f32),
            pltpu.VMEM((q_need.slots, in_rows, q_w), bf16),
            pltpu.VMEM((n, in_rows, q_w), bf16),
            pltpu.VMEM((kv_need.slots, 2 * k_w, in_rows), bf16),
            pltpu.VMEM((n, 2 * k_w, in_rows), bf16),
            pltpu.VMEM((2 * k_w, in_rows), f32),
            pltpu.SemaphoreType.DMA((3,)),
            pltpu.VMEM(whole, bf16),
        ]
        + [item for task in tasks for item in task.scratch],
        compiler_params=pltpu.CompilerParams(
            collective_id=ident, has_side_effects=True, vmem_limit_bytes=62 * 1024 * 1024
        ),
        name=f"back_{ident}",
    )(
        d_mids,
        att,
        wo,
        lse,
        q_two,
        k_two,
        val,
        n1,
        wqkv,
        turn,
        d_mid,
        x_own,
        gains,
        mid,
        g_three,
        g_two,
        out_part,
    )


def shards(
    inputs, cotangent, w_query, w_key, w_value, w_output, w_gate, w_up, w_down, gain_attn, gain_ffn
):
    dp, ctx = lax.axis_size("dp"), lax.axis_size("ctx")
    me = lax.axis_index("ctx")
    rows, width = inputs.shape
    length = rows * ctx
    q_w, k_w, o_w, f_w = w_query.shape[1], w_key.shape[1], w_output.shape[1], w_gate.shape[1]
    in_rows = w_query.shape[0]
    held = -(-HEADS // ctx)
    wide = held * HEAD_DIM
    total = ctx * wide
    near = all(wide * j >= q_w * j and wide * (j + 1) <= q_w * (j + 2) for j in range(ctx))

    each = ctx // dp
    gains = jnp.stack([gain_attn, gain_ffn])
    kv_rows = jnp.concatenate([w_key.T, w_value.T])
    cosine, sine = rope_tables(length)
    tables = (
        jnp.concatenate([cosine, sine], axis=1),
        jnp.concatenate([sine, -cosine], axis=1),
    )
    attended, lse, q_two, k_two, values, n1, cots, wo, wqkv, gain_rows, w_g, w_u, w_d, x_own = front(
        0,
        inputs.T,
        cotangent.T,
        w_query,
        kv_rows,
        w_output,
        gains,
        w_gate.T,
        w_up.T,
        w_down.T,
        held,
        tables,
    )
    d_mid_full, d_middle, middle, out_part, g_three, g_gain_two = mid_layer(
        2,
        attended,
        wo,
        x_own,
        cots,
        gain_rows,
        w_g.reshape(width, f_w),
        w_u.reshape(width, f_w),
        w_d.reshape(width, f_w),
    )
    out, grad, g_q, g_k, g_v, g_o, g_g, g_u, g_d, g_gain = back(
        3,
        d_mid_full,
        attended,
        wo,
        lse,
        q_two,
        k_two,
        values,
        n1,
        wqkv,
        tables[0],
        d_middle,
        x_own,
        gain_rows,
        middle,
        g_three,
        g_gain_two,
        out_part,
        q_w,
        k_w,
    )
    return out.T, grad.T, g_q, g_k.T, g_v.T, g_o, g_g.T, g_u.T, g_d.T, g_gain[0], g_gain[1]


def solution(mesh):
    blocks = P(("dp", "ctx"), None)
    matrix = P("dp", "ctx")
    in_specs = (blocks,) * 2 + (matrix,) * 7 + (P("ctx"),) * 2
    return jax.shard_map(shards, mesh=mesh, in_specs=in_specs, out_specs=in_specs, check_vma=False)
```

```python
import functools

import jax
import jax.numpy as jnp
import numpy as np
from jax import lax
from jax.experimental import pallas as pl
from jax.experimental.pallas import tpu as pltpu
from jax.sharding import PartitionSpec as P

HEADS = 15
KV_HEADS = 5
HEAD_DIM = 64
GROUP = HEADS // KV_HEADS

epsilon = 1e-05
rope_base = 10000.0
bf16 = jnp.bfloat16
f32 = jnp.float32


def remote(src, dst, send, recv, axis, peer):
    return pltpu.make_async_remote_copy(
        src_ref=src,
        dst_ref=dst,
        send_sem=send,
        recv_sem=recv,
        device_id={axis: peer},
        device_id_type=pl.DeviceIdType.MESH,
    )


class Gather:
    axis = "dp"

    def __init__(self, array):
        self.array = array

    def plan(self, sizes):
        self.n = sizes[self.axis]
        self.out = jax.ShapeDtypeStruct((self.n,) + self.array.shape, self.array.dtype)
        self.scratch = [pltpu.SemaphoreType.DMA((self.n,))] * 2 + [pltpu.SemaphoreType.DMA(())]

    def start(self, src, dst, send, recv, own):
        me = lax.axis_index(self.axis)
        self.local = pltpu.make_async_copy(src, dst.at[me], own)
        self.local.start()
        self.copies = []
        for k in range(1, self.n):
            peer = lax.rem(me + k, self.n)
            copy = remote(src, dst.at[me], send.at[k], recv.at[k], self.axis, peer)
            copy.start()
            self.copies.append(copy)

    def middle(self, *refs):
        pass

    def finish(self, src, dst, send, recv, own):
        me = lax.axis_index(self.axis)
        for k in range(1, self.n):
            slot = lax.rem(me + self.n - k, self.n)
            remote(src, dst.at[slot], send.at[k], recv.at[k], self.axis, slot).wait_recv()
        for copy in self.copies:
            copy.wait_send()
        self.local.wait()


class Relay:
    axis = "ctx"

    def __init__(self, array):
        self.array = array

    def plan(self, sizes):
        self.n = sizes[self.axis]
        chips = self.n // 2
        self.out = jax.ShapeDtypeStruct((self.n,) + self.array.shape, self.array.dtype)
        self.scratch = [pltpu.SemaphoreType.DMA((chips,))] * 6 + [pltpu.SemaphoreType.DMA(())]

    def at(self):
        me = lax.axis_index(self.axis)
        chip, core = me // 2, me % 2
        return me, chip, core, me + 1 - 2 * core, self.n // 2

    def start(self, src, dst, rs, rr, ls, lr, ps, pr, own):
        me, chip, core, partner, chips = self.at()

        @pl.when(chip < chips - 1)
        def _():
            remote(src, dst.at[me], rs.at[0], rr.at[0], self.axis, me + 2).start()

        @pl.when(chip > 0)
        def _():
            remote(src, dst.at[me], ls.at[0], lr.at[0], self.axis, me - 2).start()

        remote(src, dst.at[me], ps.at[chip], pr.at[chip], self.axis, partner).start()
        pltpu.make_async_copy(src, dst.at[me], own).start()

    def step(self, k, src, dst, rs, rr, ls, lr, ps, pr, own):
        me, chip, core, partner, chips = self.at()

        def arrived(slot_chip, way, send, recv):
            slot = slot_chip * 2 + core
            back = me - 2 * way
            remote(dst.at[slot], dst.at[slot], send.at[k], recv.at[k], self.axis, back).wait_recv()

            @pl.when(jnp.logical_and(chip + way >= 0, chip + way < chips))
            def _():
                remote(
                    dst.at[slot],
                    dst.at[slot],
                    send.at[k + 1],
                    recv.at[k + 1],
                    self.axis,
                    me + 2 * way,
                ).start()

            remote(
                dst.at[slot], dst.at[slot], ps.at[slot_chip], pr.at[slot_chip], self.axis, partner
            ).start()

        @pl.when(chip - 1 - k >= 0)
        def _():
            arrived(chip - 1 - k, 1, rs, rr)

        @pl.when(chip + 1 + k < chips)
        def _():
            arrived(chip + 1 + k, -1, ls, lr)

    def finish(self, src, dst, rs, rr, ls, lr, ps, pr, own):
        me, chip, core, partner, chips = self.at()
        for c in range(chips):
            slot = 2 * c + 1 - core
            remote(src, dst.at[slot], ps.at[c], pr.at[c], self.axis, partner).wait_recv()
        for c in range(chips):
            remote(src, dst.at[2 * c + core], ps.at[c], pr.at[c], self.axis, partner).wait_send()
        for k in range(chips - 1):

            @pl.when(jnp.logical_and(chip < chips - 1, k <= chip))
            def _():
                remote(src, dst.at[me], rs.at[k], rr.at[k], self.axis, me + 2).wait_send()

            @pl.when(jnp.logical_and(chip > 0, k <= chips - 1 - chip))
            def _():
                remote(src, dst.at[me], ls.at[k], lr.at[k], self.axis, me - 2).wait_send()

        pltpu.make_async_copy(src, dst.at[me], own).wait()


class Turn:
    axis = "all"

    def __init__(self, array):
        self.array = array

    def plan(self, sizes):
        self.dp, self.n = sizes["dp"], sizes["ctx"]
        self.m = self.n // self.dp
        self.out = jax.ShapeDtypeStruct(self.array.shape, self.array.dtype)
        self.scratch = [pltpu.SemaphoreType.DMA((self.m,))] * 2

    def each(self, src, dst, send, recv):
        row, col = lax.axis_index("dp"), lax.axis_index("ctx")
        put = col % self.m
        for i in range(self.m):
            to_row, to_col = col // self.m, row * self.m + i
            here = jnp.logical_and(to_row == row, to_col == col)
            far = pltpu.make_async_remote_copy(
                src_ref=src.at[i],
                dst_ref=dst.at[put],
                send_sem=send.at[i],
                recv_sem=recv.at[put],
                device_id={"dp": to_row, "ctx": to_col},
                device_id_type=pl.DeviceIdType.MESH,
            )
            local = pltpu.make_async_copy(src.at[i], dst.at[put], recv.at[put])
            yield i, here, far, local

    def start(self, *refs):
        for i, here, far, local in self.each(*refs):
            pl.when(here)(local.start)
            pl.when(jnp.logical_not(here))(far.start)

    def finish(self, src, dst, send, recv):
        row, col = lax.axis_index("dp"), lax.axis_index("ctx")
        for i, here, far, local in self.each(src, dst, send, recv):
            pl.when(jnp.logical_not(here))(far.wait_send)
        for i in range(self.m):
            own = jnp.logical_and(col // self.m == row, row * self.m + i == col)
            local = pltpu.make_async_copy(src.at[i], dst.at[i], recv.at[i])
            far = pltpu.make_async_remote_copy(
                src_ref=src.at[i],
                dst_ref=dst.at[i],
                send_sem=send.at[i],
                recv_sem=recv.at[i],
                device_id={"dp": col // self.m, "ctx": row * self.m + i},
                device_id_type=pl.DeviceIdType.MESH,
            )
            pl.when(own)(local.wait)
            pl.when(jnp.logical_not(own))(far.wait_recv)

    def middle(self, *refs):
        pass


class Swap:
    def __init__(self, axis, array):
        self.axis, self.array = axis, array

    def plan(self, sizes):
        self.n = sizes[self.axis]
        self.out = jax.ShapeDtypeStruct(self.array.shape, self.array.dtype)
        self.scratch = [pltpu.SemaphoreType.DMA((self.n,))] * 2 + [pltpu.SemaphoreType.DMA(())]

    def start(self, src, dst, send, recv, own):
        me = lax.axis_index(self.axis)
        self.local = pltpu.make_async_copy(src.at[me], dst.at[me], own)
        self.local.start()
        self.copies = []
        for k in range(1, self.n):
            peer = lax.rem(me + k, self.n)
            copy = remote(src.at[peer], dst.at[me], send.at[k], recv.at[k], self.axis, peer)
            copy.start()
            self.copies.append(copy)

    def middle(self, *refs):
        pass

    def finish(self, src, dst, send, recv, own):
        me = lax.axis_index(self.axis)
        for k in range(1, self.n):
            slot = lax.rem(me + self.n - k, self.n)
            remote(
                src.at[slot], dst.at[slot], send.at[k], recv.at[k], self.axis, slot
            ).wait_recv()
        for copy in self.copies:
            copy.wait_send()
        self.local.wait()


class Shift:
    def __init__(self, axis, array, by):
        self.axis, self.array, self.by = axis, array, by

    def plan(self, sizes):
        self.n = sizes[self.axis]
        self.out = jax.ShapeDtypeStruct(self.array.shape, self.array.dtype)
        self.scratch = [pltpu.SemaphoreType.DMA(())] * 2

    def start(self, src, dst, send, recv):
        me = lax.axis_index(self.axis)
        peer = lax.rem(me + self.n + self.by, self.n)
        self.copy = remote(src, dst, send, recv, self.axis, peer)
        self.copy.start()

    def middle(self, *refs):
        pass

    def finish(self, *refs):
        self.copy.wait_recv()
        self.copy.wait_send()


class Reduce:
    axis = "ctx"

    def __init__(self, array):
        self.array = array

    def plan(self, sizes):
        self.n = sizes[self.axis]
        block = self.array.shape[1:]
        chips = self.n // 2
        self.out = jax.ShapeDtypeStruct(block, f32)
        slots = pltpu.VMEM((chips,) + block, self.array.dtype)
        self.scratch = [pltpu.SemaphoreType.DMA((chips,))] * 4 + [slots] * 3

    def start(self, src, dst, psend, precv, send, recv, near, term, far):
        me = lax.axis_index(self.axis)
        chips = self.n // 2
        chip, core = me // 2, me % 2
        partner = me + 1 - 2 * core
        self.copies = []
        for k in list(range(1, chips)) + [0]:
            slot = lax.rem(chip + k, chips) * 2 + 1 - core
            copy = remote(
                src.at[slot], near.at[k], psend.at[k], precv.at[k], self.axis, partner
            )
            copy.start()
            self.copies.append(copy)

    def middle(self, src, dst, psend, precv, send, recv, near, term, far):
        me = lax.axis_index(self.axis)
        chips = self.n // 2
        chip, core = me // 2, me % 2
        partner = me + 1 - 2 * core
        for k in range(1, chips):
            remote(
                src.at[me], near.at[k], psend.at[k], precv.at[k], self.axis, partner
            ).wait_recv()
            peer = lax.rem(chip + k, chips) * 2 + core
            both = src[peer].astype(f32) + near[k].astype(f32)
            term[k] = both.astype(term.dtype)
            copy = remote(term.at[k], far.at[k], send.at[k], recv.at[k], self.axis, peer)
            copy.start()
            self.copies.append(copy)

    def finish(self, src, dst, psend, precv, send, recv, near, term, far):
        me = lax.axis_index(self.axis)
        chips = self.n // 2
        core = me % 2
        partner = me + 1 - 2 * core
        remote(src.at[me], near.at[0], psend.at[0], precv.at[0], self.axis, partner).wait_recv()
        dst[...] = src[me].astype(f32) + near[0].astype(f32)
        for k in range(1, chips):
            remote(
                src.at[me], far.at[k], send.at[k], recv.at[k], self.axis, partner
            ).wait_recv()
            dst[...] += far[k].astype(f32)
        for copy in self.copies:
            copy.wait_send()


def exchange(ident, *tasks):
    sizes = {axis: lax.axis_size(axis) for axis in ("dp", "ctx")}
    for task in tasks:
        task.plan(sizes)
    axes = [axis for axis in ("dp", "ctx") if any(task.axis == axis for task in tasks)]
    everyone = any(task.axis == "all" for task in tasks)
    axes = [] if everyone else axes
    count = len(tasks)

    def kernel(*refs):
        barrier = pltpu.get_barrier_semaphore()
        greeted = 0
        if everyone:
            row, col = lax.axis_index("dp"), lax.axis_index("ctx")
            for i in range(1, sizes["dp"] * sizes["ctx"]):
                other = lax.rem(row * sizes["ctx"] + col + i, sizes["dp"] * sizes["ctx"])
                pl.semaphore_signal(
                    barrier,
                    inc=1,
                    device_id={"dp": other // sizes["ctx"], "ctx": other % sizes["ctx"]},
                    device_id_type=pl.DeviceIdType.MESH,
                )
                greeted += 1
        for axis in axes:
            me, n = lax.axis_index(axis), sizes[axis]
            for k in range(1, n):
                pl.semaphore_signal(
                    barrier,
                    inc=1,
                    device_id={axis: lax.rem(me + k, n)},
                    device_id_type=pl.DeviceIdType.MESH,
                )
            greeted += n - 1
        pl.semaphore_wait(barrier, greeted)
        held, at = [], 2 * count
        for i, task in enumerate(tasks):
            held.append((refs[i], refs[count + i]) + tuple(refs[at : at + len(task.scratch)]))
            at += len(task.scratch)
        for task, own in zip(tasks, held):
            task.start(*own)
        for k in range(sizes["ctx"] // 2 - 1):
            for task, own in zip(tasks, held):
                if isinstance(task, Relay):
                    task.step(k, *own)
                elif k == 0:
                    task.middle(*own)
        for task, own in zip(tasks, held):
            task.finish(*own)

    return pl.pallas_call(
        kernel,
        out_shape=[task.out for task in tasks],
        in_specs=[pl.BlockSpec(memory_space=pltpu.VMEM)] * count,
        out_specs=[pl.BlockSpec(memory_space=pltpu.VMEM)] * count,
        scratch_shapes=[shape for task in tasks for shape in task.scratch],
        compiler_params=pltpu.CompilerParams(
            collective_id=ident, has_side_effects=True, vmem_limit_bytes=60 * 1024 * 1024
        ),
        name=f"exchange_{ident}",
    )(*[task.array for task in tasks])


def spread(axes, sizes, everyone):
    barrier = pltpu.get_barrier_semaphore()
    greeted = 0
    if everyone:
        row, col = lax.axis_index("dp"), lax.axis_index("ctx")
        total = sizes["dp"] * sizes["ctx"]

        def greet(i, carry):
            other = lax.rem(row * sizes["ctx"] + col + i, total)
            pl.semaphore_signal(
                barrier,
                inc=1,
                device_id={"dp": other // sizes["ctx"], "ctx": other % sizes["ctx"]},
                device_id_type=pl.DeviceIdType.MESH,
            )
            return carry

        lax.fori_loop(1, total, greet, 0)
        greeted = total - 1
    else:
        for axis in axes:
            me, n = lax.axis_index(axis), sizes[axis]
            for k in range(1, n):
                pl.semaphore_signal(
                    barrier,
                    inc=1,
                    device_id={axis: lax.rem(me + k, n)},
                    device_id_type=pl.DeviceIdType.MESH,
                )
            greeted += n - 1
    pl.semaphore_wait(barrier, greeted)


def mm(a, b, dims):
    return lax.dot_general(a, b, ((dims[:1], dims[1:]), ((), ())), preferred_element_type=f32)


def nn(a, b):
    return mm(a, b, (1, 0))


def nt(a, b):
    return mm(a, b, (1, 1))


def tn(a, b):
    return mm(a, b, (0, 0))


def turned(rows):
    width = rows.shape[-1]
    parts = rows.reshape(-1, 2, HEAD_DIM // 2, width)
    return jnp.concatenate([-parts[:, 1:], parts[:, :1]], axis=1).reshape(rows.shape)


def rope_tables(row_count):
    half = HEAD_DIM // 2
    frequency = np.float32(rope_base) ** (-np.arange(half).astype(np.float32) * np.float32(2.0 / HEAD_DIM))
    angles = np.arange(row_count).astype(np.float32)[:, None] * frequency[None, :].astype(np.float32)
    return [jnp.asarray(np.tile(f(angles), (1, 2)), f32) for f in (np.cos, np.sin)]


def norm_backward(hidden, inverse, gain_vec, upstream):
    scaled = upstream * gain_vec
    cubed = inverse * inverse * inverse
    d_hidden = (
        inverse * scaled
        - hidden
        * cubed
        * jnp.sum(scaled * hidden, axis=-1, keepdims=True)
        / hidden.shape[-1]
    )
    return d_hidden, jnp.sum(upstream * hidden * inverse, axis=0)


def inverse_rms(hidden):
    return lax.rsqrt(jnp.mean(hidden * hidden, axis=-1, keepdims=True) + epsilon)


class Line:
    axis = "ctx"

    def __init__(self, n):
        self.n, self.chips = n, n // 2
        self.scratch = [pltpu.SemaphoreType.DMA((self.chips,))] * 6

    def hold(self, dst, sems):
        self.dst = dst
        self.rs, self.rr, self.ls, self.lr, self.ps, self.pr = sems
        self.me = lax.axis_index(self.axis)
        self.chip, self.core = self.me // 2, self.me % 2
        self.partner = self.me + 1 - 2 * self.core

    def copy(self, slot, send, recv, peer):
        return remote(self.dst.at[slot], self.dst.at[slot], send, recv, self.axis, peer)

    def start(self):
        me, chip = self.me, self.chip
        pl.when(chip < self.chips - 1)(self.copy(me, self.rs.at[0], self.rr.at[0], me + 2).start)
        pl.when(chip > 0)(self.copy(me, self.ls.at[0], self.lr.at[0], me - 2).start)
        self.copy(me, self.ps.at[chip], self.pr.at[chip], self.partner).start()

    def step(self, k):
        me, chip, chips = self.me, self.chip, self.chips

        def arrived(at, way, send, recv):
            slot = at * 2 + self.core
            self.copy(slot, send.at[k], recv.at[k], me - 2 * way).wait_recv()

            @pl.when(jnp.logical_and(chip + way >= 0, chip + way < chips))
            def _():
                self.copy(slot, send.at[k + 1], recv.at[k + 1], me + 2 * way).start()

            self.copy(slot, self.ps.at[at], self.pr.at[at], self.partner).start()

        @pl.when(chip - 1 - k >= 0)
        def _():
            arrived(chip - 1 - k, 1, self.rs, self.rr)

        @pl.when(chip + 1 + k < chips)
        def _():
            arrived(chip + 1 + k, -1, self.ls, self.lr)

    def beside(self, at):
        slot = 2 * at + 1 - self.core
        self.copy(slot, self.ps.at[at], self.pr.at[at], self.partner).wait_recv()

    def each(self, body):
        self.beside(self.chip)
        body(self.chip)

        def at_step(k, carry):
            self.step(k)

            def at_side(side, inner):
                at = jnp.where(side == 0, self.chip - 1 - k, self.chip + 1 + k)

                @pl.when(jnp.logical_and(at >= 0, at < self.chips))
                def _():
                    self.beside(at)
                    body(at)

                return inner

            return lax.fori_loop(0, 2, at_side, carry)

        if self.chips > 1:
            lax.fori_loop(0, self.chips - 1, at_step, 0)

    def sent(self):
        me, chip, chips = self.me, self.chip, self.chips
        for c in range(chips):
            self.copy(2 * c + self.core, self.ps.at[c], self.pr.at[c], self.partner).wait_send()
        for k in range(chips - 1):

            @pl.when(jnp.logical_and(chip < chips - 1, k <= chip))
            def _():
                self.copy(me, self.rs.at[k], self.rr.at[k], me + 2).wait_send()

            @pl.when(jnp.logical_and(chip > 0, k <= chips - 1 - chip))
            def _():
                self.copy(me, self.ls.at[k], self.lr.at[k], me - 2).wait_send()


class Sum:
    axis = "ctx"

    def __init__(self, n):
        self.n, self.chips = n, n // 2
        self.scratch = [pltpu.SemaphoreType.DMA((self.chips,))] * 6

    def hold(self, part, near, got, sems):
        self.part, self.near, self.got = part, near, got
        self.ps, self.pr, self.rs, self.rr, self.ls, self.lr = sems
        self.me = lax.axis_index(self.axis)
        self.chip, self.core = self.me // 2, self.me % 2
        self.partner = self.me + 1 - 2 * self.core

    def beside(self, d):
        return remote(
            self.part.at[2 * d + 1 - self.core],
            self.near.at[d],
            self.ps.at[d],
            self.pr.at[d],
            self.axis,
            self.partner,
        )

    def right(self, d):
        return remote(
            self.part.at[2 * d + self.core],
            self.got.at[d],
            self.rs.at[d],
            self.rr.at[d],
            self.axis,
            self.me + 2,
        )

    def left(self, d):
        place = jnp.where(d == self.chip - 1, self.chips, d)
        return remote(
            self.part.at[2 * d + self.core],
            self.got.at[place],
            self.ls.at[d],
            self.lr.at[d],
            self.axis,
            self.me - 2,
        )

    def ready(self, d):
        self.beside(d).start()

    def order(self, k):
        return jnp.where(self.chip < self.chips // 2, self.chips - 1 - k, k)

    def pair(self, d):
        self.beside(d).wait_recv()
        return self.part[2 * d + self.core].astype(f32) + self.near[d].astype(f32)

    def step(self, t):
        chip, chips = self.chip, self.chips

        @pl.when(t >= chip)
        def _():
            d = chips - 1 - t + chip
            both = self.pair(d)

            @pl.when(chip == 0)
            def _():
                self.part[2 * d + self.core] = both.astype(bf16)

            @pl.when(chip > 0)
            def _():
                self.right(d).wait_recv()
                self.part[2 * d + self.core] = (both + self.got[d].astype(f32)).astype(bf16)

            self.right(d).start()

        @pl.when(t >= chips - 1 - chip)
        def _():
            d = t - (chips - 1 - chip)
            both = self.pair(d)

            @pl.when(chip == chips - 1)
            def _():
                self.part[2 * d + self.core] = both.astype(bf16)

            @pl.when(chip < chips - 1)
            def _():
                self.left(d).wait_recv()
                self.part[2 * d + self.core] = (both + self.got[d].astype(f32)).astype(bf16)

            self.left(d).start()

    def last(self, total):
        chip, chips = self.chip, self.chips
        total[...] = self.pair(chip)

        @pl.when(chip > 0)
        def _():
            self.right(chip).wait_recv()
            total[...] += self.got[chip].astype(f32)

        @pl.when(chip < chips - 1)
        def _():
            self.left(chip).wait_recv()
            total[...] += self.got[chips].astype(f32)

    def sent(self):
        for d in range(self.chips):
            self.beside(d).wait_send()
            pl.when(self.chip < d)(self.right(d).wait_send)
            pl.when(self.chip > d)(self.left(d).wait_send)


def mid_layer(ident, attended, wo, x_own, cot_full, gains, w_gate, w_up, w_down_t):
    sizes = {axis: lax.axis_size(axis) for axis in ("dp", "ctx")}
    dp, n = sizes["dp"], sizes["ctx"]
    chips = n // 2
    rows, width = x_own.shape
    wide, f_w = wo.shape[0], w_gate.shape[1]
    in_rows = width // dp
    shape = jax.ShapeDtypeStruct
    lines = [Line(n), Line(n)]
    sums = [Sum(n), Sum(n)]
    swap = Swap("dp", shape((dp, in_rows, 3 * f_w), bf16))
    swap.plan(sizes)
    tasks = lines + sums + [swap]

    def kernel(*refs):
        att, wo_ref, x_ref, cots, gain_ref, wg, wu, wd = refs[:8]
        d_mids, d_mid, mid, out_part, g_all, g_gain = refs[8:14]
        part, near, got, n2, mixed, d_gate, d_up, grads, inv, total = refs[14:24]
        sems, at = [], 24
        for task in tasks:
            sems.append(tuple(refs[at : at + len(task.scratch)]))
            at += len(task.scratch)
        spread(("dp", "ctx"), sizes, False)
        lines[0].hold(n2, sems[0])
        lines[1].hold(d_mids, sems[1])
        sums[0].hold(part, near, got, sems[2])
        sums[1].hold(part, near, got, sems[3])
        me = lax.axis_index("ctx")

        def project(k, carry):
            d = sums[0].order(k)
            rows_of = att[pl.ds(2 * d, 2)].reshape(2 * rows, wide)
            part[pl.ds(2 * d, 2)] = nn(rows_of, wo_ref[...]).astype(bf16).reshape(2, rows, width)
            sums[0].ready(d)
            return carry

        lax.fori_loop(0, chips, project, 0)
        for t in range(chips - 1):
            sums[0].step(t)
        sums[0].last(total)
        middle = x_ref[...].astype(f32) + total[...]
        inverse = inverse_rms(middle)
        mid[...] = middle
        inv[...] = inverse
        n2[me] = (middle * inverse * gain_ref[1:2]).astype(bf16)
        lines[0].start()
        sums[0].sent()

        def forward(at):
            here = pl.ds(2 * at, 2)
            tokens = n2[here].reshape(2 * rows, width)
            gate_pre = nn(tokens, wg[...])
            up_pre = nn(tokens, wu[...])
            d_mixed = nn(cots[here].reshape(2 * rows, width), wd[...])
            sigma = 1.0 / (1.0 + jnp.exp(-gate_pre))
            silu_gate = gate_pre * sigma
            act = (silu_gate * up_pre).astype(bf16)
            dg = (d_mixed * up_pre * sigma * (1.0 + gate_pre * (1.0 - sigma))).astype(bf16)
            du = (d_mixed * silu_gate).astype(bf16)
            mixed[here] = act.reshape(2, rows, f_w)
            d_gate[here] = dg.reshape(2, rows, f_w)
            d_up[here] = du.reshape(2, rows, f_w)
            d_two = nt(dg, wg[...]) + nt(du, wu[...])
            part[here] = d_two.astype(bf16).reshape(2, rows, width)
            sums[1].ready(at)
            out_part[here] = nt(act, wd[...]).astype(bf16).reshape(2, rows, width)

        lines[0].each(forward)

        def gradient(i):
            left, right = ((n2, d_gate), (n2, d_up), (cots, mixed))[i]
            value = tn(
                left[...].reshape(n * rows, width), right[...].reshape(n * rows, f_w)
            ).astype(bf16)
            for r in range(dp):
                grads[r, :, i * f_w : (i + 1) * f_w] = value[r * in_rows : (r + 1) * in_rows]

        for t in range(chips - 1):
            sums[1].step(t)
            if t == 0:
                gradient(0)
                gradient(1)
            if t == min(1, chips - 2):
                gradient(2)
                swap.start(grads, g_all, *sems[4])
        sums[1].last(total)
        middle = mid[...]
        d_norm, gain_part = norm_backward(middle, inv[...], gain_ref[1:2], total[...])
        g_gain[...] = gain_part.reshape(1, width)
        d_middle = cots[me].astype(f32) + d_norm
        d_mid[...] = d_middle
        d_mids[me] = d_middle.astype(bf16)
        lines[1].start()
        sums[1].sent()
        lines[0].sent()
        lines[1].each(lambda at: None)
        lines[1].sent()
        swap.finish(grads, g_all, *sems[4])

    whole = (n, rows, width)
    return pl.pallas_call(
        kernel,
        out_shape=[
            shape(whole, bf16),
            shape((rows, width), f32),
            shape((rows, width), f32),
            shape(whole, bf16),
            shape((dp, in_rows, 3 * f_w), bf16),
            shape((1, width), f32),
        ],
        in_specs=[pl.BlockSpec(memory_space=pltpu.VMEM)] * 8,
        out_specs=[pl.BlockSpec(memory_space=pltpu.VMEM)] * 6,
        scratch_shapes=[
            pltpu.VMEM(whole, bf16),
            pltpu.VMEM((chips, rows, width), bf16),
            pltpu.VMEM((chips + 1, rows, width), bf16),
            pltpu.VMEM(whole, bf16),
            pltpu.VMEM((n, rows, f_w), bf16),
            pltpu.VMEM((n, rows, f_w), bf16),
            pltpu.VMEM((n, rows, f_w), bf16),
            pltpu.VMEM((dp, in_rows, 3 * f_w), bf16),
            pltpu.VMEM((rows, 1), f32),
            pltpu.VMEM((rows, width), f32),
        ]
        + [item for task in tasks for item in task.scratch],
        compiler_params=pltpu.CompilerParams(
            collective_id=ident, has_side_effects=True, vmem_limit_bytes=62 * 1024 * 1024
        ),
        name=f"block_{ident}",
    )(attended, wo, x_own, cot_full, gains, w_gate, w_up, w_down_t)


class Need:
    axis = "ctx"

    def __init__(self, n, low, high):
        self.n, self.low, self.high = n, low, high
        self.slots = max(high(d) - low(d) + 1 for d in range(n))
        self.scratch = [
            pltpu.SemaphoreType.DMA((n,)),
            pltpu.SemaphoreType.DMA((self.slots,)),
        ]

    def hold(self, src, dst, sems):
        self.src, self.dst = src, dst
        self.send, self.recv = sems
        self.me = lax.axis_index(self.axis)
        self.first, self.final = self.low(self.me), self.high(self.me)

    def each(self):
        for d in range(self.n):
            low, high = self.low(d), self.high(d)
            used = jnp.logical_and(self.me >= low, self.me <= high)
            slot = jnp.clip(self.me - low, 0, self.slots - 1)
            copy = remote(
                self.src, self.dst.at[slot], self.send.at[d], self.recv.at[slot], self.axis, d
            )
            yield jnp.logical_and(used, self.me != d), copy

    def start(self):
        for used, copy in self.each():
            pl.when(used)(copy.start)
        for t in range(self.slots):
            source = self.first + t

            @pl.when(source == self.me)
            def _():
                self.dst[t] = self.src[...]

            @pl.when(source > self.final)
            def _():
                self.dst[t] = jnp.zeros_like(self.dst[t])

    def arrive(self):
        beside = self.me + 1 - 2 * lax.rem(self.me, 2)
        for t in range(self.slots):
            source = self.first + t
            copy = remote(
                self.src, self.dst.at[t], self.send.at[0], self.recv.at[t], self.axis, beside
            )
            pl.when(jnp.logical_and(source <= self.final, source != self.me))(copy.wait_recv)

    def sent(self):
        for used, copy in self.each():
            pl.when(used)(copy.wait_send)


def least(a, b):
    return min(a, b) if isinstance(a, int) else jnp.minimum(a, b)


def over(a, b):
    return a // b if isinstance(a, int) else lax.div(a, b)


def pick(rows, first, source, sign):
    at = first + lax.broadcasted_iota(jnp.int32, (rows, source.shape[1]), 0)
    return jnp.where(at == source, sign, 0.0)


def kv_head(j):
    return least(over(j, GROUP), KV_HEADS - 1)


def needs(n, held, width, q_w, k_w):
    wide = held * HEAD_DIM
    q_need = Need(
        n,
        lambda d: over(least(wide * d, width - 1), q_w),
        lambda d: over(least(wide * d + wide - 1, width - 1), q_w),
    )
    kv_need = Need(
        n,
        lambda d: over(HEAD_DIM * kv_head(held * d), k_w),
        lambda d: over(HEAD_DIM * kv_head(held * d + held - 1) + HEAD_DIM - 1, k_w),
    )
    return q_need, kv_need


def front(
    ident, x_t, cot_t, w_q, wk_t, wv_t, w_o, gain_a, gain_b, wg_t, wu_t, wd_t, held, tables
):
    sizes = {axis: lax.axis_size(axis) for axis in ("dp", "ctx")}
    dp, n = sizes["dp"], sizes["ctx"]
    chips, each = n // 2, n // dp
    width, rows = x_t.shape
    in_rows, q_w = w_q.shape
    o_w, k_w, f_w = w_o.shape[1], wk_t.shape[0], wg_t.shape[0]
    wide, total = held * HEAD_DIM, n * held * HEAD_DIM
    length, chunk = n * rows, 2 * rows
    shape = jax.ShapeDtypeStruct
    kv_rows = shape((2 * k_w, in_rows), bf16)

    q_need, kv_need = needs(n, held, width, q_w, k_w)
    x_line, cot_line, gain_line = Line(n), Line(n), Line(n)
    q_all, kv_all, o_all = Gather(w_q), Gather(kv_rows), Gather(w_o)
    g_all, u_all = [Gather(shape((in_rows, f_w), bf16)) for _ in range(2)]
    d_turn = Turn(shape((each, o_w, f_w), bf16))
    d_all = Gather(shape((each, o_w, f_w), bf16))
    o_swap = Swap("ctx", shape((n, wide, o_w), bf16))
    planned = [q_all, kv_all, o_all, g_all, u_all, d_turn, d_all, o_swap]
    for task in planned:
        task.plan(sizes)
    tasks = [q_need, kv_need, x_line, cot_line, gain_line] + planned

    def kernel(*refs):
        xt, ct, wq_ref, wk_ref, wv_ref, wo_ref, ga_ref, gb_ref = refs[:8]
        wgt, wut, wdt, cos_ref, sin_ref = refs[8:13]
        att, lse, q_two, k_two, val, n1, cots, wo_out, wqkv, gain_out = refs[13:23]
        wg_out, wu_out, wd_out, x_own = refs[23:27]
        xs, gains_in, q_got, kv_got, o_got, q_in, kv_in, wall = refs[27:35]
        wg_mine, wu_mine, d_mine, d_got, o_cut, o_in, kv_ref = refs[35:42]
        sems, at = {}, 42
        for task in tasks:
            sems[task] = tuple(refs[at : at + len(task.scratch)])
            at += len(task.scratch)
        spread(("dp", "ctx"), sizes, True)
        me = lax.axis_index("ctx")
        x_line.hold(xs, sems[x_line])
        cot_line.hold(cots, sems[cot_line])
        gain_line.hold(gains_in, sems[gain_line])
        q_need.hold(q_got, q_in, sems[q_need])
        kv_need.hold(kv_got, kv_in, sems[kv_need])
        kv_ref[:k_w] = wk_ref[...]
        kv_ref[k_w:] = wv_ref[...]
        mine = xt[...].T
        xs[me] = mine
        x_own[...] = mine
        x_line.start()
        q_all.start(wq_ref, q_got, *sems[q_all])
        kv_all.start(kv_ref, kv_got, *sems[kv_all])
        gains_in[me] = jnp.concatenate([ga_ref[...], gb_ref[...]], axis=0)
        gain_line.start()
        cots[me] = ct[...].T
        wg_mine[...] = wgt[...].T
        wu_mine[...] = wut[...].T
        for i in range(each):
            d_mine[i] = wdt[:, i * f_w : (i + 1) * f_w]
        q_all.finish(wq_ref, q_got, *sems[q_all])
        kv_all.finish(kv_ref, kv_got, *sems[kv_all])
        q_need.start()
        kv_need.start()
        o_all.start(wo_ref, o_got, *sems[o_all])
        d_turn.start(d_mine, d_got, *sems[d_turn])
        for k in range(chips - 1):
            gain_line.step(k)
        for c in range(chips):
            gain_line.beside(c)
        gain_line.sent()
        for c in range(n):
            gain_out[:, c * o_w : (c + 1) * o_w] = gains_in[c].astype(f32)

        def turned(base, d):
            half = HEAD_DIM // 2
            return base + jnp.bitwise_and(d + half, HEAD_DIM - 1), jnp.where(d < half, -1.0, 1.0)

        def plan(heads):
            lane = lax.broadcasted_iota(jnp.int32, (1, 2 * HEAD_DIM), 1)
            d = jnp.bitwise_and(lane, HEAD_DIM - 1)
            parts = []
            for h in heads:
                parts.append((h * HEAD_DIM + d, jnp.ones((1, 2 * HEAD_DIM), f32)))
                parts.append(turned(h * HEAD_DIM, d))
            lane = lax.broadcasted_iota(jnp.int32, (1, wide), 1)
            flat = jnp.bitwise_and(lane, HEAD_DIM - 1)
            base = jnp.zeros((1, wide), jnp.int32)
            for i, h in enumerate(heads):
                inside = jnp.logical_and(lane >= i * HEAD_DIM, lane < (i + 1) * HEAD_DIM)
                base = jnp.where(inside, h * HEAD_DIM, base)
            return parts + [(base + flat, jnp.ones((1, wide), f32))]

        heads = [me * held + h for h in range(held)]
        kv_heads = [kv_head(h) for h in heads]
        q_plan, k_plan = plan(heads), plan(kv_heads)
        no = [(jnp.zeros_like(k_plan[-1][0]) - 1, k_plan[-1][1])]
        q_need.arrive()
        kv_need.arrive()
        span = 4 * held * HEAD_DIM
        for r in range(dp):
            here = slice(r * in_rows, (r + 1) * in_rows)
            value = None
            for t in range(q_need.slots):
                first = (q_need.first + t) * q_w
                take = jnp.concatenate([pick(q_w, first, *p) for p in q_plan], axis=1)
                term = nn(q_in[t, r], take.astype(bf16))
                value = term if value is None else value + term
            value = value.astype(bf16)
            wall[here, :span] = value[:, :span]
            wqkv[here, :wide] = value[:, span:]
            value = None
            for t in range(kv_need.slots):
                first = (kv_need.first + t) * k_w
                top = [pick(k_w, first, *p) for p in k_plan + no]
                zero = jnp.zeros((k_w, span + wide), f32)
                top = jnp.concatenate(top, axis=1)
                low = jnp.concatenate([zero, pick(k_w, first, *k_plan[-1])], axis=1)
                take = jnp.concatenate([top, low], axis=0).astype(bf16)
                term = tn(kv_in[t, r], take)
                value = term if value is None else value + term
            value = value.astype(bf16)
            wall[here, span:] = value[:, :span]
            wqkv[here, wide:] = value[:, span:]
        g_all.start(wg_mine, wg_out, *sems[g_all])
        u_all.start(wu_mine, wu_out, *sems[u_all])

        def project(at):
            here = pl.ds(2 * at, 2)
            tokens = xs[here].reshape(chunk, width).astype(f32)
            normed = (tokens * inverse_rms(tokens) * gain_out[0:1]).astype(bf16)
            n1[here] = normed.reshape(2, rows, width)
            both = nn(normed, wall[...])
            low = pl.multiple_of(at * chunk, chunk)
            first, second = cos_ref[pl.ds(low, chunk)], sin_ref[pl.ds(low, chunk)]
            for h in range(2 * held):
                at_h = h * 4 * HEAD_DIM
                a = both[:, at_h : at_h + 2 * HEAD_DIM]
                b = both[:, at_h + 2 * HEAD_DIM : at_h + 4 * HEAD_DIM]
                two = a * first + b * second
                if h < held:
                    q_two[h, pl.ds(low, chunk)] = (two * HEAD_DIM ** (-0.5)).astype(bf16)
                else:
                    k_two[h - held, pl.ds(low, chunk)] = two.astype(bf16)
            v = nn(normed, wqkv[:, 2 * wide :]).astype(bf16)
            for h in range(held):
                val[h, pl.ds(low, chunk)] = v[:, h * HEAD_DIM : (h + 1) * HEAD_DIM]

        x_line.each(project)
        cot_line.start()
        d_turn.finish(d_mine, d_got, *sems[d_turn])
        d_all.start(d_got, wd_out, *sems[d_all])
        o_all.finish(wo_ref, o_got, *sems[o_all])
        for j in range(n):
            for r in range(dp):
                low, high = max(r * in_rows, j * wide), min((r + 1) * in_rows, (j + 1) * wide)
                if low < high:
                    o_cut[j, low - j * wide : high - j * wide] = o_got[
                        r, low - r * in_rows : high - r * in_rows
                    ]
            used = min(max(HEADS * HEAD_DIM - j * wide, 0), wide)
            if used < wide:
                o_cut[j, used:] = jnp.zeros((wide - used, o_w), bf16)
        o_swap.start(o_cut, o_in, *sems[o_swap])
        x_line.sent()

        def attend(i):
            first, last = i * chunk, (i + 1) * chunk
            for h in range(held):
                q = q_two[h, first:last, :HEAD_DIM]
                diag = nt(q, k_two[h, first:last, :HEAD_DIM])
                row = lax.broadcasted_iota(jnp.int32, diag.shape, 0)
                col = lax.broadcasted_iota(jnp.int32, diag.shape, 1)
                diag = jnp.where(row >= col, diag, -1e30)
                top = jnp.max(diag, axis=-1, keepdims=True)
                if i:
                    off = nt(q, k_two[h, :first, :HEAD_DIM])
                    top = jnp.maximum(top, jnp.max(off, axis=-1, keepdims=True))
                expo = jnp.exp(diag - top)
                weight = jnp.sum(expo, axis=-1, keepdims=True)
                out = nn(expo.astype(bf16), val[h, first:last])
                if i:
                    expo = jnp.exp(off - top)
                    weight = weight + jnp.sum(expo, axis=-1, keepdims=True)
                    out = out + nn(expo.astype(bf16), val[h, :first])
                out = (out / weight).astype(bf16)
                lanes = slice(h * HEAD_DIM, (h + 1) * HEAD_DIM)
                att[2 * i : 2 * i + 2, :, lanes] = out.reshape(2, rows, HEAD_DIM)
                logs = jnp.broadcast_to(top + jnp.log(weight), (chunk, HEAD_DIM))
                lse[first:last, lanes] = logs

        for i in range(chips):
            attend(i)
            if i < chips - 1:
                cot_line.step(i)
        o_swap.finish(o_cut, o_in, *sems[o_swap])
        for c in range(n):
            wo_out[:, c * o_w : (c + 1) * o_w] = o_in[c]
        for c in range(chips):
            cot_line.beside(c)
        cot_line.sent()
        q_need.sent()
        kv_need.sent()
        g_all.finish(wg_mine, wg_out, *sems[g_all])
        u_all.finish(wu_mine, wu_out, *sems[u_all])
        d_all.finish(d_got, wd_out, *sems[d_all])

    whole = (n, rows, width)
    outs = [
        shape((n, rows, wide), bf16),
        shape((length, wide), f32),
        shape((held, length, 2 * HEAD_DIM), bf16),
        shape((held, length, 2 * HEAD_DIM), bf16),
        shape((held, length, HEAD_DIM), bf16),
        shape(whole, bf16),
        shape(whole, bf16),
        shape((wide, width), bf16),
        shape((width, 3 * wide), bf16),
        shape((2, width), f32),
        shape((dp, in_rows, f_w), bf16),
        shape((dp, in_rows, f_w), bf16),
        shape((dp, each, o_w, f_w), bf16),
        shape((rows, width), bf16),
    ]
    return pl.pallas_call(
        kernel,
        out_shape=outs,
        in_specs=[pl.BlockSpec(memory_space=pltpu.VMEM)] * 13,
        out_specs=[pl.BlockSpec(memory_space=pltpu.VMEM)] * len(outs),
        scratch_shapes=[
            pltpu.VMEM(whole, bf16),
            pltpu.VMEM((n, 2, o_w), bf16),
            pltpu.VMEM((dp, in_rows, q_w), bf16),
            pltpu.VMEM((dp,) + kv_rows.shape, bf16),
            pltpu.VMEM((dp, in_rows, o_w), bf16),
            pltpu.VMEM((q_need.slots, dp, in_rows, q_w), bf16),
            pltpu.VMEM((kv_need.slots, dp) + kv_rows.shape, bf16),
            pltpu.VMEM((width, 8 * held * HEAD_DIM), bf16),
            pltpu.VMEM((in_rows, f_w), bf16),
            pltpu.VMEM((in_rows, f_w), bf16),
            pltpu.VMEM((each, o_w, f_w), bf16),
            pltpu.VMEM((each, o_w, f_w), bf16),
            pltpu.VMEM((n, wide, o_w), bf16),
            pltpu.VMEM((n, wide, o_w), bf16),
            pltpu.VMEM(kv_rows.shape, bf16),
        ]
        + [item for task in tasks for item in task.scratch],
        compiler_params=pltpu.CompilerParams(
            collective_id=ident, has_side_effects=True, vmem_limit_bytes=62 * 1024 * 1024
        ),
        name=f"front_{ident}",
    )(x_t, cot_t, w_q, wk_t, wv_t, w_o, gain_a, gain_b, wg_t, wu_t, wd_t, *tables)


class Give:
    axis = "ctx"

    def __init__(self, need):
        self.need = need
        self.scratch = [
            pltpu.SemaphoreType.DMA((need.slots,)),
            pltpu.SemaphoreType.DMA((need.n,)),
        ]

    def hold(self, mine, got, sems):
        self.mine, self.got = mine, got
        self.send, self.recv = sems
        self.me = lax.axis_index(self.axis)
        self.first, self.final = self.need.low(self.me), self.need.high(self.me)

    def copy(self, t, owner):
        return remote(
            self.mine.at[t],
            self.got.at[self.me],
            self.send.at[t],
            self.recv.at[self.me],
            self.axis,
            owner,
        )

    def start(self, term):
        for t in range(self.need.slots):
            owner = jnp.minimum(self.first + t, self.need.n - 1)
            used = self.first + t <= self.final

            @pl.when(used)
            def _():
                self.mine[t] = term(owner)

            pl.when(jnp.logical_and(used, owner != self.me))(self.copy(t, owner).start)

            @pl.when(jnp.logical_and(used, owner == self.me))
            def _():
                self.got[self.me] = self.mine[t]

    def add(self, total):
        beside = self.me + 1 - 2 * lax.rem(self.me, 2)
        total[...] = jnp.zeros_like(total)
        for d in range(self.need.n):
            used = jnp.logical_and(self.me >= self.need.low(d), self.me <= self.need.high(d))
            copy = remote(
                self.mine.at[0], self.got.at[d], self.send.at[0], self.recv.at[d], self.axis, beside
            )
            pl.when(jnp.logical_and(used, self.me != d))(copy.wait_recv)

            @pl.when(used)
            def _():
                total[...] += self.got[d].astype(f32)

    def sent(self):
        for t in range(self.need.slots):
            owner = jnp.minimum(self.first + t, self.need.n - 1)
            used = jnp.logical_and(self.first + t <= self.final, owner != self.me)
            pl.when(used)(self.copy(t, owner).wait_send)


def back(
    ident,
    d_mids,
    att,
    wo,
    lse,
    q_two,
    k_two,
    val,
    n1,
    wqkv,
    turn,
    d_mid,
    x_own,
    gains,
    mid,
    g_three,
    g_two,
    out_part,
    q_w,
    k_w,
):
    sizes = {axis: lax.axis_size(axis) for axis in ("dp", "ctx")}
    dp, n = sizes["dp"], sizes["ctx"]
    chips, each = n // 2, n // dp
    _, rows, width = d_mids.shape
    held, length, _ = q_two.shape
    wide, chunk = held * HEAD_DIM, 2 * rows
    in_rows, f_w = g_three.shape[1], g_three.shape[2] // 3
    o_w = width // n
    shape = jax.ShapeDtypeStruct
    q_need, kv_need = needs(n, held, width, q_w, k_w)
    q_give, kv_give = Give(q_need), Give(kv_need)
    sums = [Sum(n), Sum(n)]
    o_swap = Swap("ctx", shape((n, wide, o_w), bf16))
    o_down = Swap("dp", shape((dp, in_rows, o_w), bf16))
    w_swap = Swap("dp", shape((dp, 3 * wide, in_rows), bf16))
    d_turn = Turn(shape((each, o_w, f_w), bf16))
    gain_swap = Swap("ctx", shape((n, 2, o_w), f32))
    gain_all = Gather(shape((2, o_w), f32))
    planned = [o_swap, o_down, w_swap, d_turn, gain_swap, gain_all]
    for task in planned:
        task.plan(sizes)
    tasks = [q_give, kv_give] + sums + planned

    def kernel(*refs):
        dm_in, at_ref, wo_ref, lse_ref, q2, k2, v_ref, n_in, w_ref, turn_ref = refs[:10]
        mid_ref, x_ref, gain_ref, sum_ref, three, two_gain, out_in = refs[10:17]
        out_t, in_t, gq, gk, gv, go, gg, gu, gd, g_one, g_last = refs[17:28]
        part, near, got, near_o, got_o, datt, dk2, dv, dqkv, total = refs[28:38]
        o_src, o_got, o_cut, o_sum, w_src, w_got, d_src, d_got = refs[38:46]
        gain_src, gain_got, gain_mine, gain_sum = refs[46:50]
        q_mine, q_got, kv_mine, kv_got, kv_sum, load, dm = refs[50:57]
        sems, at = {}, 57
        for task in tasks:
            sems[task] = tuple(refs[at : at + len(task.scratch)])
            at += len(task.scratch)
        bring = pltpu.make_async_copy(out_in, part, load.at[0])
        bring.start()
        bring_d = pltpu.make_async_copy(dm_in, dm, load.at[1])
        bring_d.start()
        bring_n = pltpu.make_async_copy(n_in, dm, load.at[2])
        spread(("dp", "ctx"), sizes, True)
        me = lax.axis_index("ctx")
        sums[0].hold(part, near_o, got_o, sems[sums[0]])
        sums[1].hold(part, near, got, sems[sums[1]])
        q_give.hold(q_mine, q_got, sems[q_give])
        kv_give.hold(kv_mine, kv_got, sems[kv_give])
        bring.wait()
        for k in range(chips):
            sums[0].ready(sums[0].order(k))

        def of_dp(low, high):
            value = three[0, :, low:high].astype(f32)
            for r in range(1, dp):
                value = value + three[r, :, low:high].astype(f32)
            return value

        down = of_dp(2 * f_w, 3 * f_w).astype(bf16)
        for i in range(each):
            d_src[i] = down[i * o_w : (i + 1) * o_w]
        d_turn.start(d_src, d_got, *sems[d_turn])
        bring_d.wait()
        for i in range(chips):
            tokens = dm[2 * i : 2 * i + 2].reshape(chunk, width)
            datt[i * chunk : (i + 1) * chunk] = nt(tokens, wo_ref[...]).astype(bf16)
        value = tn(at_ref[...].reshape(length, wide), dm[...].reshape(length, width)).astype(bf16)
        bring_n.start()
        for c in range(n):
            o_src[c] = value[:, c * o_w : (c + 1) * o_w]
        o_swap.start(o_src, o_got, *sems[o_swap])

        def put(ref, h, low, high, value, first):
            if first:
                ref[h, low:high] = value
            else:
                ref[h, low:high] += value

        def folded(two, low, high):
            both = two * turn_ref[low:high]
            return both[:, :HEAD_DIM] + both[:, HEAD_DIM:]

        def attend(i):
            first, last = i * chunk, (i + 1) * chunk
            new = i == chips - 1
            for h in range(held):
                lanes = slice(h * HEAD_DIM, (h + 1) * HEAD_DIM)
                q, grad = q2[h, first:last, :HEAD_DIM], datt[first:last, lanes]
                own = at_ref[2 * i : 2 * i + 2, :, lanes].reshape(chunk, HEAD_DIM)
                delta = jnp.sum(grad.astype(f32) * own.astype(f32), axis=-1, keepdims=True)
                log = lse_ref[first:last, h * HEAD_DIM : h * HEAD_DIM + 1]
                dq = None
                for low, high in ((first, last), (0, first)):
                    if low == high:
                        continue
                    scores = nt(q, k2[h, low:high, :HEAD_DIM])
                    if low == first:
                        row = lax.broadcasted_iota(jnp.int32, scores.shape, 0)
                        col = lax.broadcasted_iota(jnp.int32, scores.shape, 1)
                        scores = jnp.where(row >= col, scores, -1e30)
                    probs = jnp.exp(scores - log)
                    d_probs = nt(grad, v_ref[h, low:high])
                    d_scores = (probs * (d_probs - delta)).astype(bf16)
                    term = nn(d_scores, k2[h, low:high])
                    dq = term if dq is None else dq + term
                    put(dk2, h, low, high, tn(d_scores, q2[h, first:last]), new)
                    put(dv, h, low, high, tn(probs.astype(bf16), grad), new)
                dq = folded(dq, first, last) * HEAD_DIM ** (-0.5)
                dqkv[first:last, lanes] = dq.astype(bf16)

        for t in range(chips):
            attend(chips - 1 - t)
            if t < chips - 1:
                sums[0].step(t)
        for i in range(chips):
            first, last = i * chunk, (i + 1) * chunk
            for h in range(held):
                base = wide + h * HEAD_DIM
                dk = folded(dk2[h, first:last], first, last)
                dqkv[first:last, base : base + HEAD_DIM] = dk.astype(bf16)
                base = base + wide
                dqkv[first:last, base : base + HEAD_DIM] = dv[h, first:last].astype(bf16)
        sums[0].last(total)
        out_t[...] = (sum_ref[...] + total[...]).T.astype(bf16)
        sums[0].sent()

        def project(k, carry):
            d = sums[1].order(k)
            low = pl.multiple_of(d * chunk, chunk)
            value = nt(dqkv[pl.ds(low, chunk)], w_ref[...]).astype(bf16)
            part[pl.ds(2 * d, 2)] = value.reshape(2, rows, width)
            sums[1].ready(d)
            return carry

        lax.fori_loop(0, chips, project, 0)
        bring_n.wait()
        value = tn(dqkv[...], dm[...].reshape(length, width)).astype(bf16)
        for t in range(min(1, chips - 1)):
            sums[1].step(t)
        for r in range(dp):
            w_src[r] = value[:, r * in_rows : (r + 1) * in_rows]
        w_swap.start(w_src, w_got, *sems[w_swap])
        o_swap.finish(o_src, o_got, *sems[o_swap])
        for j in range(n):
            for r in range(dp):
                low, high = max(r * in_rows, j * wide), min((r + 1) * in_rows, (j + 1) * wide)
                if low < high:
                    o_cut[r, low - r * in_rows : high - r * in_rows] = o_got[
                        j, low - j * wide : high - j * wide
                    ]
        o_down.start(o_cut, o_sum, *sems[o_down])
        gg[...] = of_dp(0, f_w).T
        gu[...] = of_dp(f_w, 2 * f_w).T
        for t in range(1, chips - 1):
            sums[1].step(t)
        w_swap.finish(w_src, w_got, *sems[w_swap])
        value = w_got[0].astype(f32)
        for r in range(1, dp):
            value = value + w_got[r].astype(f32)
        value = value.astype(bf16)
        heads = [me * held + h for h in range(held)]

        def columns(of):
            lane = lax.broadcasted_iota(jnp.int32, (1, wide), 1)
            base = jnp.zeros((1, wide), jnp.int32)
            for i, h in enumerate(of):
                inside = jnp.logical_and(lane >= i * HEAD_DIM, lane < (i + 1) * HEAD_DIM)
                base = jnp.where(inside, h * HEAD_DIM, base)
            return base + jnp.bitwise_and(lane, HEAD_DIM - 1)

        q_nat = value[:wide].T
        kv_part = value[wide:]
        q_cols = columns(heads)
        kv_cols = columns([least(over(h, GROUP), KV_HEADS - 1) for h in heads])
        ones = jnp.ones((1, wide), f32)

        def q_term(owner):
            return nt(q_nat, pick(q_w, owner * q_w, q_cols, ones).astype(bf16)).astype(bf16)

        def kv_term(owner):
            one = pick(k_w, owner * k_w, kv_cols, ones)
            none = jnp.zeros_like(one)
            top = jnp.concatenate([one, none], axis=1)
            low = jnp.concatenate([none, one], axis=1)
            return nn(jnp.concatenate([top, low], axis=0).astype(bf16), kv_part).astype(bf16)

        kv_give.start(kv_term)
        q_give.start(q_term)
        sums[1].last(total)
        hidden = x_ref[...].astype(f32)
        inverse = inverse_rms(hidden)
        d_norm, gain_part = norm_backward(hidden, inverse, gain_ref[0:1], total[...])
        both = jnp.concatenate([gain_part.reshape(1, width), two_gain[...]], axis=0)
        for c in range(n):
            gain_src[c] = both[:, c * o_w : (c + 1) * o_w]
        gain_swap.start(gain_src, gain_got, *sems[gain_swap])
        in_t[...] = (mid_ref[...] + d_norm).T
        d_turn.finish(d_src, d_got, *sems[d_turn])
        for i in range(each):
            gd[:, i * f_w : (i + 1) * f_w] = d_got[i].astype(f32)
        gain_swap.finish(gain_src, gain_got, *sems[gain_swap])
        gain_mine[...] = jnp.sum(gain_got[...], axis=0)
        gain_all.start(gain_mine, gain_sum, *sems[gain_all])
        o_down.finish(o_cut, o_sum, *sems[o_down])
        value = o_sum[0].astype(f32)
        for r in range(1, dp):
            value = value + o_sum[r].astype(f32)
        go[...] = value
        kv_give.add(kv_sum)
        gk[...] = kv_sum[:k_w]
        gv[...] = kv_sum[k_w:]
        q_give.add(gq)
        gain_all.finish(gain_mine, gain_sum, *sems[gain_all])
        value = jnp.sum(gain_sum[...], axis=0)
        g_one[...] = value[0:1]
        g_last[...] = value[1:2]
        q_give.sent()
        kv_give.sent()
        sums[1].sent()

    whole = (n, rows, width)
    vmem = pl.BlockSpec(memory_space=pltpu.VMEM)
    anywhere = pl.BlockSpec(memory_space=pl.ANY)
    outs = [
        shape((width, rows), bf16),
        shape((width, rows), f32),
        shape((in_rows, q_w), f32),
        shape((k_w, in_rows), f32),
        shape((k_w, in_rows), f32),
        shape((in_rows, o_w), f32),
        shape((f_w, in_rows), f32),
        shape((f_w, in_rows), f32),
        shape((o_w, each * f_w), f32),
        shape((1, o_w), f32),
        shape((1, o_w), f32),
    ]
    return pl.pallas_call(
        kernel,
        out_shape=outs,
        in_specs=[anywhere] + [vmem] * 6 + [anywhere] + [vmem] * 8 + [anywhere],
        out_specs=[vmem] * len(outs),
        scratch_shapes=[
            pltpu.VMEM(whole, bf16),
            pltpu.VMEM((chips, rows, width), bf16),
            pltpu.VMEM((chips + 1, rows, width), bf16),
            pltpu.VMEM((chips, rows, width), bf16),
            pltpu.VMEM((chips + 1, rows, width), bf16),
            pltpu.VMEM((length, wide), bf16),
            pltpu.VMEM((held, length, 2 * HEAD_DIM), f32),
            pltpu.VMEM((held, length, HEAD_DIM), f32),
            pltpu.VMEM((length, 3 * wide), bf16),
            pltpu.VMEM((rows, width), f32),
            pltpu.VMEM((n, wide, o_w), bf16),
            pltpu.VMEM((n, wide, o_w), bf16),
            pltpu.VMEM((dp, in_rows, o_w), bf16),
            pltpu.VMEM((dp, in_rows, o_w), bf16),
            pltpu.VMEM((dp, 3 * wide, in_rows), bf16),
            pltpu.VMEM((dp, 3 * wide, in_rows), bf16),
            pltpu.VMEM((each, o_w, f_w), bf16),
            pltpu.VMEM((each, o_w, f_w), bf16),
            pltpu.VMEM((n, 2, o_w), f32),
            pltpu.VMEM((n, 2, o_w), f32),
            pltpu.VMEM((2, o_w), f32),
            pltpu.VMEM((dp, 2, o_w), f32),
            pltpu.VMEM((q_need.slots, in_rows, q_w), bf16),
            pltpu.VMEM((n, in_rows, q_w), bf16),
            pltpu.VMEM((kv_need.slots, 2 * k_w, in_rows), bf16),
            pltpu.VMEM((n, 2 * k_w, in_rows), bf16),
            pltpu.VMEM((2 * k_w, in_rows), f32),
            pltpu.SemaphoreType.DMA((3,)),
            pltpu.VMEM(whole, bf16),
        ]
        + [item for task in tasks for item in task.scratch],
        compiler_params=pltpu.CompilerParams(
            collective_id=ident, has_side_effects=True, vmem_limit_bytes=62 * 1024 * 1024
        ),
        name=f"back_{ident}",
    )(
        d_mids,
        att,
        wo,
        lse,
        q_two,
        k_two,
        val,
        n1,
        wqkv,
        turn,
        d_mid,
        x_own,
        gains,
        mid,
        g_three,
        g_two,
        out_part,
    )


def finish(arrays):
    count = len(arrays)

    def kernel(*refs):
        copies = [
            pltpu.make_async_copy(refs[i], refs[count + i], refs[2 * count].at[i])
            for i in range(count)
        ]
        for copy in copies:
            copy.start()
        for copy in copies:
            copy.wait()

    return pl.pallas_call(
        kernel,
        out_shape=[jax.ShapeDtypeStruct(array.shape, array.dtype) for array in arrays],
        in_specs=[pl.BlockSpec(memory_space=pl.ANY)] * count,
        out_specs=[pl.BlockSpec(memory_space=pl.ANY)] * count,
        scratch_shapes=[pltpu.SemaphoreType.DMA((count,))],
        name="finish",
    )(*arrays)


def shards(
    inputs, cotangent, w_query, w_key, w_value, w_output, w_gate, w_up, w_down, gain_attn, gain_ffn
):
    dp, ctx = lax.axis_size("dp"), lax.axis_size("ctx")
    me = lax.axis_index("ctx")
    rows, width = inputs.shape
    length = rows * ctx
    q_w, k_w, o_w, f_w = w_query.shape[1], w_key.shape[1], w_output.shape[1], w_gate.shape[1]
    in_rows = w_query.shape[0]
    held = -(-HEADS // ctx)
    wide = held * HEAD_DIM
    total = ctx * wide
    near = all(wide * j >= q_w * j and wide * (j + 1) <= q_w * (j + 2) for j in range(ctx))

    each = ctx // dp
    cosine, sine = rope_tables(length)
    tables = (
        jnp.concatenate([cosine, sine], axis=1),
        jnp.concatenate([sine, -cosine], axis=1),
    )
    attended, lse, q_two, k_two, values, n1, cots, wo, wqkv, gain_rows, w_g, w_u, w_d, x_own = front(
        0,
        inputs.T,
        cotangent.T,
        w_query,
        w_key.T,
        w_value.T,
        w_output,
        gain_attn.reshape(1, o_w),
        gain_ffn.reshape(1, o_w),
        w_gate.T,
        w_up.T,
        w_down.T,
        held,
        tables,
    )
    d_mid_full, d_middle, middle, out_part, g_three, g_gain_two = mid_layer(
        2,
        attended,
        wo,
        x_own,
        cots,
        gain_rows,
        w_g.reshape(width, f_w),
        w_u.reshape(width, f_w),
        w_d.reshape(width, f_w),
    )
    last = back(
        3,
        d_mid_full,
        attended,
        wo,
        lse,
        q_two,
        k_two,
        values,
        n1,
        wqkv,
        tables[0],
        d_middle,
        x_own,
        gain_rows,
        middle,
        g_three,
        g_gain_two,
        out_part,
        q_w,
        k_w,
    )
    out, grad, g_q, g_k, g_v, g_o, g_g, g_u, g_d, g_one, g_two = finish(last)
    g_one, g_two = g_one.reshape(o_w), g_two.reshape(o_w)
    return out.T, grad.T, g_q, g_k.T, g_v.T, g_o, g_g.T, g_u.T, g_d.T, g_one, g_two


def solution(mesh):
    blocks = P(("dp", "ctx"), None)
    matrix = P("dp", "ctx")
    in_specs = (blocks,) * 2 + (matrix,) * 7 + (P("ctx"),) * 2
    return jax.shard_map(shards, mesh=mesh, in_specs=in_specs, out_specs=in_specs, check_vma=False)
```

```python
import functools

import jax
import jax.numpy as jnp
import numpy as np
from jax import lax
from jax.experimental import pallas as pl
from jax.experimental.pallas import tpu as pltpu
from jax.sharding import PartitionSpec as P

HEADS = 15
KV_HEADS = 5
HEAD_DIM = 64
GROUP = HEADS // KV_HEADS

epsilon = 1e-05
rope_base = 10000.0
bf16 = jnp.bfloat16
f32 = jnp.float32


def remote(src, dst, send, recv, axis, peer):
    return pltpu.make_async_remote_copy(
        src_ref=src,
        dst_ref=dst,
        send_sem=send,
        recv_sem=recv,
        device_id={axis: peer},
        device_id_type=pl.DeviceIdType.MESH,
    )


class Gather:
    axis = "dp"

    def __init__(self, array):
        self.array = array

    def plan(self, sizes):
        self.n = sizes[self.axis]
        self.out = jax.ShapeDtypeStruct((self.n,) + self.array.shape, self.array.dtype)
        self.scratch = [pltpu.SemaphoreType.DMA((self.n,))] * 2 + [pltpu.SemaphoreType.DMA(())]

    def start(self, src, dst, send, recv, own):
        me = lax.axis_index(self.axis)
        self.local = pltpu.make_async_copy(src, dst.at[me], own)
        self.local.start()
        self.copies = []
        for k in range(1, self.n):
            peer = lax.rem(me + k, self.n)
            copy = remote(src, dst.at[me], send.at[k], recv.at[k], self.axis, peer)
            copy.start()
            self.copies.append(copy)

    def middle(self, *refs):
        pass

    def finish(self, src, dst, send, recv, own):
        me = lax.axis_index(self.axis)
        for k in range(1, self.n):
            slot = lax.rem(me + self.n - k, self.n)
            remote(src, dst.at[slot], send.at[k], recv.at[k], self.axis, slot).wait_recv()
        for copy in self.copies:
            copy.wait_send()
        self.local.wait()


class Relay:
    axis = "ctx"

    def __init__(self, array):
        self.array = array

    def plan(self, sizes):
        self.n = sizes[self.axis]
        chips = self.n // 2
        self.out = jax.ShapeDtypeStruct((self.n,) + self.array.shape, self.array.dtype)
        self.scratch = [pltpu.SemaphoreType.DMA((chips,))] * 6 + [pltpu.SemaphoreType.DMA(())]

    def at(self):
        me = lax.axis_index(self.axis)
        chip, core = me // 2, me % 2
        return me, chip, core, me + 1 - 2 * core, self.n // 2

    def start(self, src, dst, rs, rr, ls, lr, ps, pr, own):
        me, chip, core, partner, chips = self.at()

        @pl.when(chip < chips - 1)
        def _():
            remote(src, dst.at[me], rs.at[0], rr.at[0], self.axis, me + 2).start()

        @pl.when(chip > 0)
        def _():
            remote(src, dst.at[me], ls.at[0], lr.at[0], self.axis, me - 2).start()

        remote(src, dst.at[me], ps.at[chip], pr.at[chip], self.axis, partner).start()
        pltpu.make_async_copy(src, dst.at[me], own).start()

    def step(self, k, src, dst, rs, rr, ls, lr, ps, pr, own):
        me, chip, core, partner, chips = self.at()

        def arrived(slot_chip, way, send, recv):
            slot = slot_chip * 2 + core
            back = me - 2 * way
            remote(dst.at[slot], dst.at[slot], send.at[k], recv.at[k], self.axis, back).wait_recv()

            @pl.when(jnp.logical_and(chip + way >= 0, chip + way < chips))
            def _():
                remote(
                    dst.at[slot],
                    dst.at[slot],
                    send.at[k + 1],
                    recv.at[k + 1],
                    self.axis,
                    me + 2 * way,
                ).start()

            remote(
                dst.at[slot], dst.at[slot], ps.at[slot_chip], pr.at[slot_chip], self.axis, partner
            ).start()

        @pl.when(chip - 1 - k >= 0)
        def _():
            arrived(chip - 1 - k, 1, rs, rr)

        @pl.when(chip + 1 + k < chips)
        def _():
            arrived(chip + 1 + k, -1, ls, lr)

    def finish(self, src, dst, rs, rr, ls, lr, ps, pr, own):
        me, chip, core, partner, chips = self.at()
        for c in range(chips):
            slot = 2 * c + 1 - core
            remote(src, dst.at[slot], ps.at[c], pr.at[c], self.axis, partner).wait_recv()
        for c in range(chips):
            remote(src, dst.at[2 * c + core], ps.at[c], pr.at[c], self.axis, partner).wait_send()
        for k in range(chips - 1):

            @pl.when(jnp.logical_and(chip < chips - 1, k <= chip))
            def _():
                remote(src, dst.at[me], rs.at[k], rr.at[k], self.axis, me + 2).wait_send()

            @pl.when(jnp.logical_and(chip > 0, k <= chips - 1 - chip))
            def _():
                remote(src, dst.at[me], ls.at[k], lr.at[k], self.axis, me - 2).wait_send()

        pltpu.make_async_copy(src, dst.at[me], own).wait()


class Turn:
    axis = "all"

    def __init__(self, array):
        self.array = array

    def plan(self, sizes):
        self.dp, self.n = sizes["dp"], sizes["ctx"]
        self.m = self.n // self.dp
        self.out = jax.ShapeDtypeStruct(self.array.shape, self.array.dtype)
        self.scratch = [pltpu.SemaphoreType.DMA((self.m,))] * 2

    def each(self, src, dst, send, recv):
        row, col = lax.axis_index("dp"), lax.axis_index("ctx")
        put = col % self.m
        for i in range(self.m):
            to_row, to_col = col // self.m, row * self.m + i
            here = jnp.logical_and(to_row == row, to_col == col)
            far = pltpu.make_async_remote_copy(
                src_ref=src.at[i],
                dst_ref=dst.at[put],
                send_sem=send.at[i],
                recv_sem=recv.at[put],
                device_id={"dp": to_row, "ctx": to_col},
                device_id_type=pl.DeviceIdType.MESH,
            )
            local = pltpu.make_async_copy(src.at[i], dst.at[put], recv.at[put])
            yield i, here, far, local

    def start(self, *refs):
        for i, here, far, local in self.each(*refs):
            pl.when(here)(local.start)
            pl.when(jnp.logical_not(here))(far.start)

    def finish(self, src, dst, send, recv):
        row, col = lax.axis_index("dp"), lax.axis_index("ctx")
        for i, here, far, local in self.each(src, dst, send, recv):
            pl.when(jnp.logical_not(here))(far.wait_send)
        for i in range(self.m):
            own = jnp.logical_and(col // self.m == row, row * self.m + i == col)
            local = pltpu.make_async_copy(src.at[i], dst.at[i], recv.at[i])
            far = pltpu.make_async_remote_copy(
                src_ref=src.at[i],
                dst_ref=dst.at[i],
                send_sem=send.at[i],
                recv_sem=recv.at[i],
                device_id={"dp": col // self.m, "ctx": row * self.m + i},
                device_id_type=pl.DeviceIdType.MESH,
            )
            pl.when(own)(local.wait)
            pl.when(jnp.logical_not(own))(far.wait_recv)

    def middle(self, *refs):
        pass


class Swap:
    def __init__(self, axis, array):
        self.axis, self.array = axis, array

    def plan(self, sizes):
        self.n = sizes[self.axis]
        self.out = jax.ShapeDtypeStruct(self.array.shape, self.array.dtype)
        self.scratch = [pltpu.SemaphoreType.DMA((self.n,))] * 2 + [pltpu.SemaphoreType.DMA(())]

    def start(self, src, dst, send, recv, own):
        me = lax.axis_index(self.axis)
        self.local = pltpu.make_async_copy(src.at[me], dst.at[me], own)
        self.local.start()
        self.copies = []
        for k in range(1, self.n):
            peer = lax.rem(me + k, self.n)
            copy = remote(src.at[peer], dst.at[me], send.at[k], recv.at[k], self.axis, peer)
            copy.start()
            self.copies.append(copy)

    def middle(self, *refs):
        pass

    def finish(self, src, dst, send, recv, own):
        me = lax.axis_index(self.axis)
        for k in range(1, self.n):
            slot = lax.rem(me + self.n - k, self.n)
            remote(
                src.at[slot], dst.at[slot], send.at[k], recv.at[k], self.axis, slot
            ).wait_recv()
        for copy in self.copies:
            copy.wait_send()
        self.local.wait()


class Shift:
    def __init__(self, axis, array, by):
        self.axis, self.array, self.by = axis, array, by

    def plan(self, sizes):
        self.n = sizes[self.axis]
        self.out = jax.ShapeDtypeStruct(self.array.shape, self.array.dtype)
        self.scratch = [pltpu.SemaphoreType.DMA(())] * 2

    def start(self, src, dst, send, recv):
        me = lax.axis_index(self.axis)
        peer = lax.rem(me + self.n + self.by, self.n)
        self.copy = remote(src, dst, send, recv, self.axis, peer)
        self.copy.start()

    def middle(self, *refs):
        pass

    def finish(self, *refs):
        self.copy.wait_recv()
        self.copy.wait_send()


class Reduce:
    axis = "ctx"

    def __init__(self, array):
        self.array = array

    def plan(self, sizes):
        self.n = sizes[self.axis]
        block = self.array.shape[1:]
        chips = self.n // 2
        self.out = jax.ShapeDtypeStruct(block, f32)
        slots = pltpu.VMEM((chips,) + block, self.array.dtype)
        self.scratch = [pltpu.SemaphoreType.DMA((chips,))] * 4 + [slots] * 3

    def start(self, src, dst, psend, precv, send, recv, near, term, far):
        me = lax.axis_index(self.axis)
        chips = self.n // 2
        chip, core = me // 2, me % 2
        partner = me + 1 - 2 * core
        self.copies = []
        for k in list(range(1, chips)) + [0]:
            slot = lax.rem(chip + k, chips) * 2 + 1 - core
            copy = remote(
                src.at[slot], near.at[k], psend.at[k], precv.at[k], self.axis, partner
            )
            copy.start()
            self.copies.append(copy)

    def middle(self, src, dst, psend, precv, send, recv, near, term, far):
        me = lax.axis_index(self.axis)
        chips = self.n // 2
        chip, core = me // 2, me % 2
        partner = me + 1 - 2 * core
        for k in range(1, chips):
            remote(
                src.at[me], near.at[k], psend.at[k], precv.at[k], self.axis, partner
            ).wait_recv()
            peer = lax.rem(chip + k, chips) * 2 + core
            both = src[peer].astype(f32) + near[k].astype(f32)
            term[k] = both.astype(term.dtype)
            copy = remote(term.at[k], far.at[k], send.at[k], recv.at[k], self.axis, peer)
            copy.start()
            self.copies.append(copy)

    def finish(self, src, dst, psend, precv, send, recv, near, term, far):
        me = lax.axis_index(self.axis)
        chips = self.n // 2
        core = me % 2
        partner = me + 1 - 2 * core
        remote(src.at[me], near.at[0], psend.at[0], precv.at[0], self.axis, partner).wait_recv()
        dst[...] = src[me].astype(f32) + near[0].astype(f32)
        for k in range(1, chips):
            remote(
                src.at[me], far.at[k], send.at[k], recv.at[k], self.axis, partner
            ).wait_recv()
            dst[...] += far[k].astype(f32)
        for copy in self.copies:
            copy.wait_send()


def exchange(ident, *tasks):
    sizes = {axis: lax.axis_size(axis) for axis in ("dp", "ctx")}
    for task in tasks:
        task.plan(sizes)
    axes = [axis for axis in ("dp", "ctx") if any(task.axis == axis for task in tasks)]
    everyone = any(task.axis == "all" for task in tasks)
    axes = [] if everyone else axes
    count = len(tasks)

    def kernel(*refs):
        barrier = pltpu.get_barrier_semaphore()
        greeted = 0
        if everyone:
            row, col = lax.axis_index("dp"), lax.axis_index("ctx")
            for i in range(1, sizes["dp"] * sizes["ctx"]):
                other = lax.rem(row * sizes["ctx"] + col + i, sizes["dp"] * sizes["ctx"])
                pl.semaphore_signal(
                    barrier,
                    inc=1,
                    device_id={"dp": other // sizes["ctx"], "ctx": other % sizes["ctx"]},
                    device_id_type=pl.DeviceIdType.MESH,
                )
                greeted += 1
        for axis in axes:
            me, n = lax.axis_index(axis), sizes[axis]
            for k in range(1, n):
                pl.semaphore_signal(
                    barrier,
                    inc=1,
                    device_id={axis: lax.rem(me + k, n)},
                    device_id_type=pl.DeviceIdType.MESH,
                )
            greeted += n - 1
        pl.semaphore_wait(barrier, greeted)
        held, at = [], 2 * count
        for i, task in enumerate(tasks):
            held.append((refs[i], refs[count + i]) + tuple(refs[at : at + len(task.scratch)]))
            at += len(task.scratch)
        for task, own in zip(tasks, held):
            task.start(*own)
        for k in range(sizes["ctx"] // 2 - 1):
            for task, own in zip(tasks, held):
                if isinstance(task, Relay):
                    task.step(k, *own)
                elif k == 0:
                    task.middle(*own)
        for task, own in zip(tasks, held):
            task.finish(*own)

    return pl.pallas_call(
        kernel,
        out_shape=[task.out for task in tasks],
        in_specs=[pl.BlockSpec(memory_space=pltpu.VMEM)] * count,
        out_specs=[pl.BlockSpec(memory_space=pltpu.VMEM)] * count,
        scratch_shapes=[shape for task in tasks for shape in task.scratch],
        compiler_params=pltpu.CompilerParams(
            collective_id=ident, has_side_effects=True, vmem_limit_bytes=60 * 1024 * 1024
        ),
        name=f"exchange_{ident}",
    )(*[task.array for task in tasks])


def spread(axes, sizes, everyone):
    barrier = pltpu.get_barrier_semaphore()
    greeted = 0
    if everyone:
        row, col = lax.axis_index("dp"), lax.axis_index("ctx")
        total = sizes["dp"] * sizes["ctx"]

        def greet(i, carry):
            other = lax.rem(row * sizes["ctx"] + col + i, total)
            pl.semaphore_signal(
                barrier,
                inc=1,
                device_id={"dp": other // sizes["ctx"], "ctx": other % sizes["ctx"]},
                device_id_type=pl.DeviceIdType.MESH,
            )
            return carry

        lax.fori_loop(1, total, greet, 0)
        greeted = total - 1
    else:
        for axis in axes:
            me, n = lax.axis_index(axis), sizes[axis]
            for k in range(1, n):
                pl.semaphore_signal(
                    barrier,
                    inc=1,
                    device_id={axis: lax.rem(me + k, n)},
                    device_id_type=pl.DeviceIdType.MESH,
                )
            greeted += n - 1
    pl.semaphore_wait(barrier, greeted)


def mm(a, b, dims):
    return lax.dot_general(a, b, ((dims[:1], dims[1:]), ((), ())), preferred_element_type=f32)


def nn(a, b):
    return mm(a, b, (1, 0))


def nt(a, b):
    return mm(a, b, (1, 1))


def tn(a, b):
    return mm(a, b, (0, 0))


def turned(rows):
    width = rows.shape[-1]
    parts = rows.reshape(-1, 2, HEAD_DIM // 2, width)
    return jnp.concatenate([-parts[:, 1:], parts[:, :1]], axis=1).reshape(rows.shape)


def rope_tables(row_count):
    half = HEAD_DIM // 2
    frequency = np.float32(rope_base) ** (-np.arange(half).astype(np.float32) * np.float32(2.0 / HEAD_DIM))
    angles = np.arange(row_count).astype(np.float32)[:, None] * frequency[None, :].astype(np.float32)
    return [jnp.asarray(np.tile(f(angles), (1, 2)), f32) for f in (np.cos, np.sin)]


def norm_backward(hidden, inverse, gain_vec, upstream):
    scaled = upstream * gain_vec
    cubed = inverse * inverse * inverse
    d_hidden = (
        inverse * scaled
        - hidden
        * cubed
        * jnp.sum(scaled * hidden, axis=-1, keepdims=True)
        / hidden.shape[-1]
    )
    return d_hidden, jnp.sum(upstream * hidden * inverse, axis=0)


def inverse_rms(hidden):
    return lax.rsqrt(jnp.mean(hidden * hidden, axis=-1, keepdims=True) + epsilon)


class Line:
    axis = "ctx"

    def __init__(self, n, rows):
        self.n, self.chips = n, n // 2
        self.cuts = 2 if rows % 32 == 0 else 1
        self.size = rows // self.cuts
        self.scratch = [pltpu.SemaphoreType.DMA((self.chips * self.cuts,))] * 6

    def hold(self, dst, sems):
        self.dst = dst
        self.rs, self.rr, self.ls, self.lr, self.ps, self.pr = sems
        self.me = lax.axis_index(self.axis)
        self.chip, self.core = self.me // 2, self.me % 2
        self.partner = self.me + 1 - 2 * self.core

    def copy(self, slot, cut, send, recv, at, peer):
        place = self.dst.at[slot, pl.ds(cut * self.size, self.size)]
        at = at * self.cuts + cut
        return remote(place, place, send.at[at], recv.at[at], self.axis, peer)

    def right(self, slot, cut, k):
        return self.copy(slot, cut, self.rs, self.rr, k, self.me + 2)

    def left(self, slot, cut, k):
        return self.copy(slot, cut, self.ls, self.lr, k, self.me - 2)

    def share(self, slot, cut, at):
        return self.copy(slot, cut, self.ps, self.pr, at, self.partner)

    def start(self):
        me, chip = self.me, self.chip
        for cut in range(self.cuts):
            pl.when(chip < self.chips - 1)(self.right(me, cut, 0).start)
            pl.when(chip > 0)(self.left(me, cut, 0).start)
        for cut in range(self.cuts):
            self.share(me, cut, chip).start()

    def step(self, k):
        chip, chips = self.chip, self.chips
        for cut in range(self.cuts):

            @pl.when(chip - 1 - k >= 0)
            def _():
                slot = (chip - 1 - k) * 2 + self.core
                self.right(slot, cut, k).wait_recv()
                pl.when(chip + 1 < chips)(self.right(slot, cut, k + 1).start)
                self.share(slot, cut, chip - 1 - k).start()

            @pl.when(chip + 1 + k < chips)
            def _():
                slot = (chip + 1 + k) * 2 + self.core
                self.left(slot, cut, k).wait_recv()
                pl.when(chip > 0)(self.left(slot, cut, k + 1).start)
                self.share(slot, cut, chip + 1 + k).start()

    def beside(self, at):
        for cut in range(self.cuts):
            self.share(2 * at + 1 - self.core, cut, at).wait_recv()

    def each(self, body, done=0, then=None):
        self.beside(self.chip)
        body(self.chip)

        def at_step(k, carry):
            @pl.when(k >= done)
            def _():
                self.step(k)

            if then is not None:
                pl.when(k == self.chips - 2)(then)

            def at_side(side, inner):
                at = jnp.where(side == 0, self.chip - 1 - k, self.chip + 1 + k)

                @pl.when(jnp.logical_and(at >= 0, at < self.chips))
                def _():
                    self.beside(at)
                    body(at)

                return inner

            return lax.fori_loop(0, 2, at_side, carry)

        if self.chips > 1:
            lax.fori_loop(0, self.chips - 1, at_step, 0)
        elif then is not None:
            then()

    def sent(self):
        me, chip, chips = self.me, self.chip, self.chips
        for cut in range(self.cuts):
            for c in range(chips):
                self.share(2 * c + self.core, cut, c).wait_send()
            for k in range(chips - 1):
                to_right = jnp.logical_and(chip < chips - 1, k <= chip)
                pl.when(to_right)(self.right(me, cut, k).wait_send)
                to_left = jnp.logical_and(chip > 0, k <= chips - 1 - chip)
                pl.when(to_left)(self.left(me, cut, k).wait_send)


class Sum:
    axis = "ctx"

    def __init__(self, n, rows):
        self.n, self.chips = n, n // 2
        self.cuts = 2 if rows % 32 == 0 else 1
        self.size = rows // self.cuts
        self.scratch = [pltpu.SemaphoreType.DMA((self.chips,))] * 2
        self.scratch += [pltpu.SemaphoreType.DMA((self.chips * self.cuts,))] * 4

    def hold(self, part, near, got, sems):
        self.part, self.near, self.got = part, near, got
        self.ps, self.pr, self.rs, self.rr, self.ls, self.lr = sems
        self.me = lax.axis_index(self.axis)
        self.chip, self.core = self.me // 2, self.me % 2
        self.partner = self.me + 1 - 2 * self.core

    def beside(self, d):
        return remote(
            self.part.at[2 * d + 1 - self.core],
            self.near.at[d],
            self.ps.at[d],
            self.pr.at[d],
            self.axis,
            self.partner,
        )

    def rows(self, cut):
        return pl.ds(cut * self.size, self.size)

    def line(self, d, cut, place, send, recv, peer):
        at, rows = d * self.cuts + cut, self.rows(cut)
        return remote(
            self.part.at[2 * d + self.core, rows],
            self.got.at[place, rows],
            send.at[at],
            recv.at[at],
            self.axis,
            peer,
        )

    def right(self, d, cut):
        return self.line(d, cut, d, self.rs, self.rr, self.me + 2)

    def left(self, d, cut):
        place = jnp.where(d == self.chip - 1, self.chips, d)
        return self.line(d, cut, place, self.ls, self.lr, self.me - 2)

    def ready(self, d):
        self.beside(d).start()

    def order(self, k):
        return jnp.where(self.chip < self.chips // 2, self.chips - 1 - k, k)

    def pass_on(self, d, cut, edge, copy):
        if cut == 0:
            self.beside(d).wait_recv()
        rows = self.rows(cut)
        both = self.part[2 * d + self.core, rows].astype(f32) + self.near[d, rows].astype(f32)

        @pl.when(edge)
        def _():
            self.part[2 * d + self.core, rows] = both.astype(bf16)

        @pl.when(jnp.logical_not(edge))
        def _():
            copy.wait_recv()
            more = both + self.got[d, rows].astype(f32)
            self.part[2 * d + self.core, rows] = more.astype(bf16)

        copy.start()

    def step(self, t):
        chip, chips = self.chip, self.chips
        for cut in range(self.cuts):

            @pl.when(t >= chip)
            def _():
                d = chips - 1 - t + chip
                self.pass_on(d, cut, chip == 0, self.right(d, cut))

            @pl.when(t >= chips - 1 - chip)
            def _():
                d = t - (chips - 1 - chip)
                self.pass_on(d, cut, chip == chips - 1, self.left(d, cut))

    def last(self, total):
        chip, chips = self.chip, self.chips
        self.beside(chip).wait_recv()
        total[...] = self.part[self.me].astype(f32) + self.near[chip].astype(f32)
        for cut in range(self.cuts):
            rows = self.rows(cut)

            @pl.when(chip > 0)
            def _():
                self.right(chip, cut).wait_recv()
                total[rows] += self.got[chip, rows].astype(f32)

            @pl.when(chip < chips - 1)
            def _():
                self.left(chip, cut).wait_recv()
                total[rows] += self.got[chips, rows].astype(f32)

    def sent(self):
        for d in range(self.chips):
            self.beside(d).wait_send()
            for cut in range(self.cuts):
                pl.when(self.chip < d)(self.right(d, cut).wait_send)
                pl.when(self.chip > d)(self.left(d, cut).wait_send)


def mid_layer(ident, attended, wo, x_own, cot_full, gains, w_gate, w_up, w_down_t):
    sizes = {axis: lax.axis_size(axis) for axis in ("dp", "ctx")}
    dp, n = sizes["dp"], sizes["ctx"]
    chips = n // 2
    rows, width = x_own.shape
    wide, f_w = wo.shape[0], w_gate.shape[1]
    in_rows = width // dp
    shape = jax.ShapeDtypeStruct
    lines = [Line(n, rows), Line(n, rows)]
    sums = [Sum(n, rows), Sum(n, rows)]
    swap = Swap("dp", shape((dp, in_rows, 3 * f_w), bf16))
    swap.plan(sizes)
    tasks = lines + sums + [swap]

    def kernel(*refs):
        att, wo_ref, x_ref, cots, gain_ref, wg, wu, wd = refs[:8]
        d_mids, d_mid, mid, out_part, g_all, g_gain = refs[8:14]
        part, near, got, n2, mixed, d_gate, d_up, grads, inv, total = refs[14:24]
        sems, at = [], 24
        for task in tasks:
            sems.append(tuple(refs[at : at + len(task.scratch)]))
            at += len(task.scratch)
        spread(("dp", "ctx"), sizes, False)
        lines[0].hold(n2, sems[0])
        lines[1].hold(d_mids, sems[1])
        sums[0].hold(part, near, got, sems[2])
        sums[1].hold(part, near, got, sems[3])
        me = lax.axis_index("ctx")

        def project(k, carry):
            d = sums[0].order(k)
            rows_of = att[pl.ds(2 * d, 2)].reshape(2 * rows, wide)
            part[pl.ds(2 * d, 2)] = nn(rows_of, wo_ref[...]).astype(bf16).reshape(2, rows, width)
            sums[0].ready(d)
            return carry

        lax.fori_loop(0, chips, project, 0)
        for t in range(chips - 1):
            sums[0].step(t)
        sums[0].last(total)
        middle = x_ref[...].astype(f32) + total[...]
        inverse = inverse_rms(middle)
        mid[...] = middle
        inv[...] = inverse
        n2[me] = (middle * inverse * gain_ref[1:2]).astype(bf16)
        lines[0].start()
        sums[0].sent()

        def forward(at):
            here = pl.ds(2 * at, 2)
            tokens = n2[here].reshape(2 * rows, width)
            gate_pre = nn(tokens, wg[...])
            up_pre = nn(tokens, wu[...])
            d_mixed = nn(cots[here].reshape(2 * rows, width), wd[...])
            sigma = 1.0 / (1.0 + jnp.exp(-gate_pre))
            silu_gate = gate_pre * sigma
            act = (silu_gate * up_pre).astype(bf16)
            dg = (d_mixed * up_pre * sigma * (1.0 + gate_pre * (1.0 - sigma))).astype(bf16)
            du = (d_mixed * silu_gate).astype(bf16)
            mixed[here] = act.reshape(2, rows, f_w)
            d_gate[here] = dg.reshape(2, rows, f_w)
            d_up[here] = du.reshape(2, rows, f_w)
            d_two = nt(dg, wg[...]) + nt(du, wu[...])
            part[here] = d_two.astype(bf16).reshape(2, rows, width)
            sums[1].ready(at)
            out_part[here] = nt(act, wd[...]).astype(bf16).reshape(2, rows, width)

        lines[0].each(forward)

        def gradient(i):
            left, right = ((n2, d_gate), (n2, d_up), (cots, mixed))[i]
            value = tn(
                left[...].reshape(n * rows, width), right[...].reshape(n * rows, f_w)
            ).astype(bf16)
            for r in range(dp):
                grads[r, :, i * f_w : (i + 1) * f_w] = value[r * in_rows : (r + 1) * in_rows]

        for t in range(chips - 1):
            sums[1].step(t)
            if t == 0:
                gradient(0)
                gradient(1)
            if t == min(1, chips - 2):
                gradient(2)
                swap.start(grads, g_all, *sems[4])
        sums[1].last(total)
        middle = mid[...]
        d_norm, gain_part = norm_backward(middle, inv[...], gain_ref[1:2], total[...])
        g_gain[...] = gain_part.reshape(1, width)
        d_middle = cots[me].astype(f32) + d_norm
        d_mid[...] = d_middle
        d_mids[me] = d_middle.astype(bf16)
        lines[1].start()
        sums[1].sent()
        lines[0].sent()
        lines[1].each(lambda at: None)
        lines[1].sent()
        swap.finish(grads, g_all, *sems[4])

    whole = (n, rows, width)
    return pl.pallas_call(
        kernel,
        out_shape=[
            shape(whole, bf16),
            shape((rows, width), f32),
            shape((rows, width), f32),
            shape(whole, bf16),
            shape((dp, in_rows, 3 * f_w), bf16),
            shape((1, width), f32),
        ],
        in_specs=[pl.BlockSpec(memory_space=pltpu.VMEM)] * 8,
        out_specs=[pl.BlockSpec(memory_space=pltpu.VMEM)] * 6,
        scratch_shapes=[
            pltpu.VMEM(whole, bf16),
            pltpu.VMEM((chips, rows, width), bf16),
            pltpu.VMEM((chips + 1, rows, width), bf16),
            pltpu.VMEM(whole, bf16),
            pltpu.VMEM((n, rows, f_w), bf16),
            pltpu.VMEM((n, rows, f_w), bf16),
            pltpu.VMEM((n, rows, f_w), bf16),
            pltpu.VMEM((dp, in_rows, 3 * f_w), bf16),
            pltpu.VMEM((rows, 1), f32),
            pltpu.VMEM((rows, width), f32),
        ]
        + [item for task in tasks for item in task.scratch],
        compiler_params=pltpu.CompilerParams(
            collective_id=ident, has_side_effects=True, vmem_limit_bytes=62 * 1024 * 1024
        ),
        name=f"block_{ident}",
    )(attended, wo, x_own, cot_full, gains, w_gate, w_up, w_down_t)


class Need:
    axis = "ctx"

    def __init__(self, n, low, high):
        self.n, self.low, self.high = n, low, high
        self.slots = max(high(d) - low(d) + 1 for d in range(n))
        self.scratch = [
            pltpu.SemaphoreType.DMA((n,)),
            pltpu.SemaphoreType.DMA((self.slots,)),
        ]

    def hold(self, src, dst, sems):
        self.src, self.dst = src, dst
        self.send, self.recv = sems
        self.me = lax.axis_index(self.axis)
        self.first, self.final = self.low(self.me), self.high(self.me)

    def each(self):
        for d in range(self.n):
            low, high = self.low(d), self.high(d)
            used = jnp.logical_and(self.me >= low, self.me <= high)
            slot = jnp.clip(self.me - low, 0, self.slots - 1)
            copy = remote(
                self.src, self.dst.at[slot], self.send.at[d], self.recv.at[slot], self.axis, d
            )
            yield jnp.logical_and(used, self.me != d), copy

    def start(self):
        for used, copy in self.each():
            pl.when(used)(copy.start)
        for t in range(self.slots):
            source = self.first + t

            @pl.when(source == self.me)
            def _():
                self.dst[t] = self.src[...]

            @pl.when(source > self.final)
            def _():
                self.dst[t] = jnp.zeros_like(self.dst[t])

    def arrive(self):
        beside = self.me + 1 - 2 * lax.rem(self.me, 2)
        for t in range(self.slots):
            source = self.first + t
            copy = remote(
                self.src, self.dst.at[t], self.send.at[0], self.recv.at[t], self.axis, beside
            )
            pl.when(jnp.logical_and(source <= self.final, source != self.me))(copy.wait_recv)

    def sent(self):
        for used, copy in self.each():
            pl.when(used)(copy.wait_send)


def least(a, b):
    return min(a, b) if isinstance(a, int) else jnp.minimum(a, b)


def over(a, b):
    return a // b if isinstance(a, int) else lax.div(a, b)


def pick(rows, first, source, sign):
    at = first + lax.broadcasted_iota(jnp.int32, (rows, source.shape[1]), 0)
    return jnp.where(at == source, sign, 0.0)


def kv_head(j):
    return least(over(j, GROUP), KV_HEADS - 1)


def needs(n, held, width, q_w, k_w):
    wide = held * HEAD_DIM
    q_need = Need(
        n,
        lambda d: over(least(wide * d, width - 1), q_w),
        lambda d: over(least(wide * d + wide - 1, width - 1), q_w),
    )
    kv_need = Need(
        n,
        lambda d: over(HEAD_DIM * kv_head(held * d), k_w),
        lambda d: over(HEAD_DIM * kv_head(held * d + held - 1) + HEAD_DIM - 1, k_w),
    )
    return q_need, kv_need


def front(
    ident, x_t, cot_t, w_q, wk_t, wv_t, w_o, gain_a, gain_b, wg_t, wu_t, wd_t, held, tables
):
    sizes = {axis: lax.axis_size(axis) for axis in ("dp", "ctx")}
    dp, n = sizes["dp"], sizes["ctx"]
    chips, each = n // 2, n // dp
    width, rows = x_t.shape
    in_rows, q_w = w_q.shape
    o_w, k_w, f_w = w_o.shape[1], wk_t.shape[0], wg_t.shape[0]
    wide, total = held * HEAD_DIM, n * held * HEAD_DIM
    length, chunk = n * rows, 2 * rows
    shape = jax.ShapeDtypeStruct
    kv_rows = shape((2 * k_w, in_rows), bf16)

    q_need, kv_need = needs(n, held, width, q_w, k_w)
    x_line, cot_line = Line(n, rows), Line(n, rows)
    gain_all = Gather(shape((2, o_w), bf16))
    gain_all.axis = "ctx"
    q_all, kv_all, o_all = Gather(w_q), Gather(kv_rows), Gather(w_o)
    g_all, u_all = [Gather(shape((in_rows, f_w), bf16)) for _ in range(2)]
    d_turn = Turn(shape((each, o_w, f_w), bf16))
    d_all = Gather(shape((each, o_w, f_w), bf16))
    o_swap = Swap("ctx", shape((n, wide, o_w), bf16))
    planned = [q_all, kv_all, o_all, g_all, u_all, d_turn, d_all, o_swap, gain_all]
    for task in planned:
        task.plan(sizes)
    tasks = [q_need, kv_need, x_line, cot_line] + planned

    def kernel(*refs):
        xt, ct, wq_ref, wk_ref, wv_ref, wo_ref, ga_ref, gb_ref = refs[:8]
        wgt, wut, wdt, cos_ref, sin_ref = refs[8:13]
        att, lse, q_two, k_two, val, n1, cots, wo_out, wqkv, gain_out = refs[13:23]
        wg_out, wu_out, wd_out, x_own = refs[23:27]
        xs, gains_in, q_got, kv_got, o_got, q_in, kv_in, wall = refs[27:35]
        wg_mine, wu_mine, d_mine, d_got, o_cut, o_in, kv_ref, gain_mine = refs[35:43]
        sems, at = {}, 43
        for task in tasks:
            sems[task] = tuple(refs[at : at + len(task.scratch)])
            at += len(task.scratch)
        spread(("dp", "ctx"), sizes, True)
        me = lax.axis_index("ctx")
        x_line.hold(xs, sems[x_line])
        cot_line.hold(cots, sems[cot_line])
        q_need.hold(q_got, q_in, sems[q_need])
        kv_need.hold(kv_got, kv_in, sems[kv_need])
        kv_ref[:k_w] = wk_ref[...]
        kv_ref[k_w:] = wv_ref[...]
        mine = xt[...].T
        xs[me] = mine
        x_own[...] = mine
        x_line.start()
        q_all.start(wq_ref, q_got, *sems[q_all])
        kv_all.start(kv_ref, kv_got, *sems[kv_all])
        gain_mine[...] = jnp.concatenate([ga_ref[...], gb_ref[...]], axis=0)
        gain_all.start(gain_mine, gains_in, *sems[gain_all])
        cots[me] = ct[...].T
        wg_mine[...] = wgt[...].T
        wu_mine[...] = wut[...].T
        for i in range(each):
            d_mine[i] = wdt[:, i * f_w : (i + 1) * f_w]
        q_all.finish(wq_ref, q_got, *sems[q_all])
        kv_all.finish(kv_ref, kv_got, *sems[kv_all])
        q_need.start()
        kv_need.start()
        o_all.start(wo_ref, o_got, *sems[o_all])
        d_turn.start(d_mine, d_got, *sems[d_turn])
        if chips > 1:
            x_line.step(0)
        gain_all.finish(gain_mine, gains_in, *sems[gain_all])
        for c in range(n):
            gain_out[:, c * o_w : (c + 1) * o_w] = gains_in[c].astype(f32)

        def turned(base, d):
            half = HEAD_DIM // 2
            return base + jnp.bitwise_and(d + half, HEAD_DIM - 1), jnp.where(d < half, -1.0, 1.0)

        def plan(heads):
            lane = lax.broadcasted_iota(jnp.int32, (1, 2 * HEAD_DIM), 1)
            d = jnp.bitwise_and(lane, HEAD_DIM - 1)
            parts = []
            for h in heads:
                parts.append((h * HEAD_DIM + d, jnp.ones((1, 2 * HEAD_DIM), f32)))
                parts.append(turned(h * HEAD_DIM, d))
            lane = lax.broadcasted_iota(jnp.int32, (1, wide), 1)
            flat = jnp.bitwise_and(lane, HEAD_DIM - 1)
            base = jnp.zeros((1, wide), jnp.int32)
            for i, h in enumerate(heads):
                inside = jnp.logical_and(lane >= i * HEAD_DIM, lane < (i + 1) * HEAD_DIM)
                base = jnp.where(inside, h * HEAD_DIM, base)
            return parts + [(base + flat, jnp.ones((1, wide), f32))]

        heads = [me * held + h for h in range(held)]
        kv_heads = [kv_head(h) for h in heads]
        q_plan, k_plan = plan(heads), plan(kv_heads)
        no = [(jnp.zeros_like(k_plan[-1][0]) - 1, k_plan[-1][1])]
        q_need.arrive()
        kv_need.arrive()
        span = 4 * held * HEAD_DIM
        for r in range(dp):
            here = slice(r * in_rows, (r + 1) * in_rows)
            value = None
            for t in range(q_need.slots):
                first = (q_need.first + t) * q_w
                take = jnp.concatenate([pick(q_w, first, *p) for p in q_plan], axis=1)
                term = nn(q_in[t, r], take.astype(bf16))
                value = term if value is None else value + term
            value = value.astype(bf16)
            wall[here, :span] = value[:, :span]
            wqkv[here, :wide] = value[:, span:]
            value = None
            for t in range(kv_need.slots):
                first = (kv_need.first + t) * k_w
                top = [pick(k_w, first, *p) for p in k_plan + no]
                zero = jnp.zeros((k_w, span + wide), f32)
                top = jnp.concatenate(top, axis=1)
                low = jnp.concatenate([zero, pick(k_w, first, *k_plan[-1])], axis=1)
                take = jnp.concatenate([top, low], axis=0).astype(bf16)
                term = tn(kv_in[t, r], take)
                value = term if value is None else value + term
            value = value.astype(bf16)
            wall[here, span:] = value[:, :span]
            wqkv[here, wide:] = value[:, span:]
        if chips > 2:
            x_line.step(1)
        g_all.start(wg_mine, wg_out, *sems[g_all])
        u_all.start(wu_mine, wu_out, *sems[u_all])

        def project(at):
            here = pl.ds(2 * at, 2)
            tokens = xs[here].reshape(chunk, width).astype(f32)
            normed = (tokens * inverse_rms(tokens) * gain_out[0:1]).astype(bf16)
            n1[here] = normed.reshape(2, rows, width)
            both = nn(normed, wall[...])
            low = pl.multiple_of(at * chunk, chunk)
            first, second = cos_ref[pl.ds(low, chunk)], sin_ref[pl.ds(low, chunk)]
            for h in range(2 * held):
                at_h = h * 4 * HEAD_DIM
                a = both[:, at_h : at_h + 2 * HEAD_DIM]
                b = both[:, at_h + 2 * HEAD_DIM : at_h + 4 * HEAD_DIM]
                two = a * first + b * second
                if h < held:
                    q_two[h, pl.ds(low, chunk)] = (two * HEAD_DIM ** (-0.5)).astype(bf16)
                else:
                    k_two[h - held, pl.ds(low, chunk)] = two.astype(bf16)
            v = nn(normed, wqkv[:, 2 * wide :]).astype(bf16)
            for h in range(held):
                val[h, pl.ds(low, chunk)] = v[:, h * HEAD_DIM : (h + 1) * HEAD_DIM]

        x_line.each(project, min(2, chips - 1), cot_line.start)
        d_turn.finish(d_mine, d_got, *sems[d_turn])
        d_all.start(d_got, wd_out, *sems[d_all])
        o_all.finish(wo_ref, o_got, *sems[o_all])
        for j in range(n):
            for r in range(dp):
                low, high = max(r * in_rows, j * wide), min((r + 1) * in_rows, (j + 1) * wide)
                if low < high:
                    o_cut[j, low - j * wide : high - j * wide] = o_got[
                        r, low - r * in_rows : high - r * in_rows
                    ]
            used = min(max(HEADS * HEAD_DIM - j * wide, 0), wide)
            if used < wide:
                o_cut[j, used:] = jnp.zeros((wide - used, o_w), bf16)
        o_swap.start(o_cut, o_in, *sems[o_swap])
        x_line.sent()

        def attend(i):
            first, last = i * chunk, (i + 1) * chunk
            for h in range(held):
                q = q_two[h, first:last, :HEAD_DIM]
                diag = nt(q, k_two[h, first:last, :HEAD_DIM])
                row = lax.broadcasted_iota(jnp.int32, diag.shape, 0)
                col = lax.broadcasted_iota(jnp.int32, diag.shape, 1)
                diag = jnp.where(row >= col, diag, -1e30)
                top = jnp.max(diag, axis=-1, keepdims=True)
                if i:
                    off = nt(q, k_two[h, :first, :HEAD_DIM])
                    top = jnp.maximum(top, jnp.max(off, axis=-1, keepdims=True))
                expo = jnp.exp(diag - top)
                weight = jnp.sum(expo, axis=-1, keepdims=True)
                out = nn(expo.astype(bf16), val[h, first:last])
                if i:
                    expo = jnp.exp(off - top)
                    weight = weight + jnp.sum(expo, axis=-1, keepdims=True)
                    out = out + nn(expo.astype(bf16), val[h, :first])
                out = (out / weight).astype(bf16)
                lanes = slice(h * HEAD_DIM, (h + 1) * HEAD_DIM)
                att[2 * i : 2 * i + 2, :, lanes] = out.reshape(2, rows, HEAD_DIM)
                logs = jnp.broadcast_to(top + jnp.log(weight), (chunk, HEAD_DIM))
                lse[first:last, lanes] = logs

        for i in range(chips):
            attend(i)
            if i < chips - 1:
                cot_line.step(i)
        o_swap.finish(o_cut, o_in, *sems[o_swap])
        for c in range(n):
            wo_out[:, c * o_w : (c + 1) * o_w] = o_in[c]
        for c in range(chips):
            cot_line.beside(c)
        cot_line.sent()
        q_need.sent()
        kv_need.sent()
        g_all.finish(wg_mine, wg_out, *sems[g_all])
        u_all.finish(wu_mine, wu_out, *sems[u_all])
        d_all.finish(d_got, wd_out, *sems[d_all])

    whole = (n, rows, width)
    outs = [
        shape((n, rows, wide), bf16),
        shape((length, wide), f32),
        shape((held, length, 2 * HEAD_DIM), bf16),
        shape((held, length, 2 * HEAD_DIM), bf16),
        shape((held, length, HEAD_DIM), bf16),
        shape(whole, bf16),
        shape(whole, bf16),
        shape((wide, width), bf16),
        shape((width, 3 * wide), bf16),
        shape((2, width), f32),
        shape((dp, in_rows, f_w), bf16),
        shape((dp, in_rows, f_w), bf16),
        shape((dp, each, o_w, f_w), bf16),
        shape((rows, width), bf16),
    ]
    return pl.pallas_call(
        kernel,
        out_shape=outs,
        in_specs=[pl.BlockSpec(memory_space=pltpu.VMEM)] * 13,
        out_specs=[pl.BlockSpec(memory_space=pltpu.VMEM)] * len(outs),
        scratch_shapes=[
            pltpu.VMEM(whole, bf16),
            pltpu.VMEM((n, 2, o_w), bf16),
            pltpu.VMEM((dp, in_rows, q_w), bf16),
            pltpu.VMEM((dp,) + kv_rows.shape, bf16),
            pltpu.VMEM((dp, in_rows, o_w), bf16),
            pltpu.VMEM((q_need.slots, dp, in_rows, q_w), bf16),
            pltpu.VMEM((kv_need.slots, dp) + kv_rows.shape, bf16),
            pltpu.VMEM((width, 8 * held * HEAD_DIM), bf16),
            pltpu.VMEM((in_rows, f_w), bf16),
            pltpu.VMEM((in_rows, f_w), bf16),
            pltpu.VMEM((each, o_w, f_w), bf16),
            pltpu.VMEM((each, o_w, f_w), bf16),
            pltpu.VMEM((n, wide, o_w), bf16),
            pltpu.VMEM((n, wide, o_w), bf16),
            pltpu.VMEM(kv_rows.shape, bf16),
            pltpu.VMEM((2, o_w), bf16),
        ]
        + [item for task in tasks for item in task.scratch],
        compiler_params=pltpu.CompilerParams(
            collective_id=ident, has_side_effects=True, vmem_limit_bytes=62 * 1024 * 1024
        ),
        name=f"front_{ident}",
    )(x_t, cot_t, w_q, wk_t, wv_t, w_o, gain_a, gain_b, wg_t, wu_t, wd_t, *tables)


class Give:
    axis = "ctx"

    def __init__(self, need):
        self.need = need
        self.scratch = [
            pltpu.SemaphoreType.DMA((need.slots,)),
            pltpu.SemaphoreType.DMA((need.n,)),
        ]

    def hold(self, mine, got, sems):
        self.mine, self.got = mine, got
        self.send, self.recv = sems
        self.me = lax.axis_index(self.axis)
        self.first, self.final = self.need.low(self.me), self.need.high(self.me)

    def copy(self, t, owner):
        return remote(
            self.mine.at[t],
            self.got.at[self.me],
            self.send.at[t],
            self.recv.at[self.me],
            self.axis,
            owner,
        )

    def start(self, term):
        for t in range(self.need.slots):
            owner = jnp.minimum(self.first + t, self.need.n - 1)
            used = self.first + t <= self.final

            @pl.when(used)
            def _():
                self.mine[t] = term(owner)

            pl.when(jnp.logical_and(used, owner != self.me))(self.copy(t, owner).start)

            @pl.when(jnp.logical_and(used, owner == self.me))
            def _():
                self.got[self.me] = self.mine[t]

    def add(self, total):
        beside = self.me + 1 - 2 * lax.rem(self.me, 2)
        total[...] = jnp.zeros_like(total)
        for d in range(self.need.n):
            used = jnp.logical_and(self.me >= self.need.low(d), self.me <= self.need.high(d))
            copy = remote(
                self.mine.at[0], self.got.at[d], self.send.at[0], self.recv.at[d], self.axis, beside
            )
            pl.when(jnp.logical_and(used, self.me != d))(copy.wait_recv)

            @pl.when(used)
            def _():
                total[...] += self.got[d].astype(f32)

    def sent(self):
        for t in range(self.need.slots):
            owner = jnp.minimum(self.first + t, self.need.n - 1)
            used = jnp.logical_and(self.first + t <= self.final, owner != self.me)
            pl.when(used)(self.copy(t, owner).wait_send)


def back(
    ident,
    d_mids,
    att,
    wo,
    lse,
    q_two,
    k_two,
    val,
    n1,
    wqkv,
    turn,
    d_mid,
    x_own,
    gains,
    mid,
    g_three,
    g_two,
    out_part,
    q_w,
    k_w,
):
    sizes = {axis: lax.axis_size(axis) for axis in ("dp", "ctx")}
    dp, n = sizes["dp"], sizes["ctx"]
    chips, each = n // 2, n // dp
    _, rows, width = d_mids.shape
    held, length, _ = q_two.shape
    wide, chunk = held * HEAD_DIM, 2 * rows
    in_rows, f_w = g_three.shape[1], g_three.shape[2] // 3
    o_w = width // n
    shape = jax.ShapeDtypeStruct
    q_need, kv_need = needs(n, held, width, q_w, k_w)
    q_give, kv_give = Give(q_need), Give(kv_need)
    sums = [Sum(n, rows), Sum(n, rows)]
    o_swap = Swap("ctx", shape((n, wide, o_w), bf16))
    o_down = Swap("dp", shape((dp, in_rows, o_w), bf16))
    w_swap = Swap("dp", shape((dp, 3 * wide, in_rows), bf16))
    d_turn = Turn(shape((each, o_w, f_w), bf16))
    gain_swap = Swap("ctx", shape((n, 2, o_w), f32))
    gain_all = Gather(shape((2, o_w), f32))
    planned = [o_swap, o_down, w_swap, d_turn, gain_swap, gain_all]
    for task in planned:
        task.plan(sizes)
    tasks = [q_give, kv_give] + sums + planned

    def kernel(*refs):
        dm_in, at_ref, wo_ref, lse_ref, q2, k2, v_ref, n_in, w_ref, turn_ref = refs[:10]
        mid_ref, x_ref, gain_ref, sum_ref, three, two_gain, out_in = refs[10:17]
        out_t, in_t, gq, gk, gv, go, gg, gu, gd, g_one, g_last = refs[17:28]
        part, near, got, near_o, got_o, datt, dk2, dv, dqkv, total = refs[28:38]
        o_src, o_got, o_cut, o_sum, w_src, w_got, d_src, d_got = refs[38:46]
        gain_src, gain_got, gain_mine, gain_sum = refs[46:50]
        q_mine, q_got, kv_mine, kv_got, kv_sum, load, dm = refs[50:57]
        sems, at = {}, 57
        for task in tasks:
            sems[task] = tuple(refs[at : at + len(task.scratch)])
            at += len(task.scratch)
        bring = pltpu.make_async_copy(out_in, part, load.at[0])
        bring.start()
        bring_d = pltpu.make_async_copy(dm_in, dm, load.at[1])
        bring_d.start()
        bring_n = pltpu.make_async_copy(n_in, dm, load.at[2])
        spread(("dp", "ctx"), sizes, True)
        me = lax.axis_index("ctx")
        sums[0].hold(part, near_o, got_o, sems[sums[0]])
        sums[1].hold(part, near, got, sems[sums[1]])
        q_give.hold(q_mine, q_got, sems[q_give])
        kv_give.hold(kv_mine, kv_got, sems[kv_give])
        bring.wait()
        for k in range(chips):
            sums[0].ready(sums[0].order(k))

        def of_dp(low, high):
            value = three[0, :, low:high].astype(f32)
            for r in range(1, dp):
                value = value + three[r, :, low:high].astype(f32)
            return value

        down = of_dp(2 * f_w, 3 * f_w).astype(bf16)
        for i in range(each):
            d_src[i] = down[i * o_w : (i + 1) * o_w]
        d_turn.start(d_src, d_got, *sems[d_turn])
        bring_d.wait()
        for i in range(chips):
            tokens = dm[2 * i : 2 * i + 2].reshape(chunk, width)
            datt[i * chunk : (i + 1) * chunk] = nt(tokens, wo_ref[...]).astype(bf16)
        value = tn(at_ref[...].reshape(length, wide), dm[...].reshape(length, width)).astype(bf16)
        bring_n.start()
        for c in range(n):
            o_src[c] = value[:, c * o_w : (c + 1) * o_w]
        o_swap.start(o_src, o_got, *sems[o_swap])

        def put(ref, h, low, high, value, first):
            if first:
                ref[h, low:high] = value
            else:
                ref[h, low:high] += value

        def folded(two, low, high):
            both = two * turn_ref[low:high]
            return both[:, :HEAD_DIM] + both[:, HEAD_DIM:]

        def attend(i):
            first, last = i * chunk, (i + 1) * chunk
            new = i == chips - 1
            for h in range(held):
                lanes = slice(h * HEAD_DIM, (h + 1) * HEAD_DIM)
                q, grad = q2[h, first:last, :HEAD_DIM], datt[first:last, lanes]
                own = at_ref[2 * i : 2 * i + 2, :, lanes].reshape(chunk, HEAD_DIM)
                delta = jnp.sum(grad.astype(f32) * own.astype(f32), axis=-1, keepdims=True)
                log = lse_ref[first:last, h * HEAD_DIM : h * HEAD_DIM + 1]
                dq = None
                for low, high in ((first, last), (0, first)):
                    if low == high:
                        continue
                    scores = nt(q, k2[h, low:high, :HEAD_DIM])
                    if low == first:
                        row = lax.broadcasted_iota(jnp.int32, scores.shape, 0)
                        col = lax.broadcasted_iota(jnp.int32, scores.shape, 1)
                        scores = jnp.where(row >= col, scores, -1e30)
                    probs = jnp.exp(scores - log)
                    d_probs = nt(grad, v_ref[h, low:high])
                    d_scores = (probs * (d_probs - delta)).astype(bf16)
                    term = nn(d_scores, k2[h, low:high])
                    dq = term if dq is None else dq + term
                    put(dk2, h, low, high, tn(d_scores, q2[h, first:last]), new)
                    put(dv, h, low, high, tn(probs.astype(bf16), grad), new)
                dq = folded(dq, first, last) * HEAD_DIM ** (-0.5)
                dqkv[first:last, lanes] = dq.astype(bf16)

        for t in range(chips):
            attend(chips - 1 - t)
            if t < chips - 1:
                sums[0].step(t)
        for i in range(chips):
            first, last = i * chunk, (i + 1) * chunk
            for h in range(held):
                base = wide + h * HEAD_DIM
                dk = folded(dk2[h, first:last], first, last)
                dqkv[first:last, base : base + HEAD_DIM] = dk.astype(bf16)
                base = base + wide
                dqkv[first:last, base : base + HEAD_DIM] = dv[h, first:last].astype(bf16)
        sums[0].last(total)
        out_t[...] = (sum_ref[...] + total[...]).T.astype(bf16)
        sums[0].sent()

        def project(k, carry):
            d = sums[1].order(k)
            low = pl.multiple_of(d * chunk, chunk)
            value = nt(dqkv[pl.ds(low, chunk)], w_ref[...]).astype(bf16)
            part[pl.ds(2 * d, 2)] = value.reshape(2, rows, width)
            sums[1].ready(d)
            return carry

        lax.fori_loop(0, chips, project, 0)
        bring_n.wait()
        value = tn(dqkv[...], dm[...].reshape(length, width)).astype(bf16)
        for t in range(min(1, chips - 1)):
            sums[1].step(t)
        for r in range(dp):
            w_src[r] = value[:, r * in_rows : (r + 1) * in_rows]
        w_swap.start(w_src, w_got, *sems[w_swap])
        o_swap.finish(o_src, o_got, *sems[o_swap])
        for j in range(n):
            for r in range(dp):
                low, high = max(r * in_rows, j * wide), min((r + 1) * in_rows, (j + 1) * wide)
                if low < high:
                    o_cut[r, low - r * in_rows : high - r * in_rows] = o_got[
                        j, low - j * wide : high - j * wide
                    ]
        o_down.start(o_cut, o_sum, *sems[o_down])
        gg[...] = of_dp(0, f_w).T
        gu[...] = of_dp(f_w, 2 * f_w).T
        for t in range(1, chips - 1):
            sums[1].step(t)
        w_swap.finish(w_src, w_got, *sems[w_swap])
        value = w_got[0].astype(f32)
        for r in range(1, dp):
            value = value + w_got[r].astype(f32)
        value = value.astype(bf16)
        heads = [me * held + h for h in range(held)]

        def columns(of):
            lane = lax.broadcasted_iota(jnp.int32, (1, wide), 1)
            base = jnp.zeros((1, wide), jnp.int32)
            for i, h in enumerate(of):
                inside = jnp.logical_and(lane >= i * HEAD_DIM, lane < (i + 1) * HEAD_DIM)
                base = jnp.where(inside, h * HEAD_DIM, base)
            return base + jnp.bitwise_and(lane, HEAD_DIM - 1)

        q_nat = value[:wide].T
        kv_part = value[wide:]
        q_cols = columns(heads)
        kv_cols = columns([least(over(h, GROUP), KV_HEADS - 1) for h in heads])
        ones = jnp.ones((1, wide), f32)

        def q_term(owner):
            return nt(q_nat, pick(q_w, owner * q_w, q_cols, ones).astype(bf16)).astype(bf16)

        def kv_term(owner):
            one = pick(k_w, owner * k_w, kv_cols, ones)
            none = jnp.zeros_like(one)
            top = jnp.concatenate([one, none], axis=1)
            low = jnp.concatenate([none, one], axis=1)
            return nn(jnp.concatenate([top, low], axis=0).astype(bf16), kv_part).astype(bf16)

        kv_give.start(kv_term)
        q_give.start(q_term)
        sums[1].last(total)
        hidden = x_ref[...].astype(f32)
        inverse = inverse_rms(hidden)
        d_norm, gain_part = norm_backward(hidden, inverse, gain_ref[0:1], total[...])
        both = jnp.concatenate([gain_part.reshape(1, width), two_gain[...]], axis=0)
        for c in range(n):
            gain_src[c] = both[:, c * o_w : (c + 1) * o_w]
        gain_swap.start(gain_src, gain_got, *sems[gain_swap])
        in_t[...] = (mid_ref[...] + d_norm).T
        d_turn.finish(d_src, d_got, *sems[d_turn])
        for i in range(each):
            gd[:, i * f_w : (i + 1) * f_w] = d_got[i].astype(f32)
        gain_swap.finish(gain_src, gain_got, *sems[gain_swap])
        gain_mine[...] = jnp.sum(gain_got[...], axis=0)
        gain_all.start(gain_mine, gain_sum, *sems[gain_all])
        o_down.finish(o_cut, o_sum, *sems[o_down])
        value = o_sum[0].astype(f32)
        for r in range(1, dp):
            value = value + o_sum[r].astype(f32)
        go[...] = value
        kv_give.add(kv_sum)
        gk[...] = kv_sum[:k_w]
        gv[...] = kv_sum[k_w:]
        q_give.add(gq)
        gain_all.finish(gain_mine, gain_sum, *sems[gain_all])
        value = jnp.sum(gain_sum[...], axis=0)
        g_one[...] = value[0:1]
        g_last[...] = value[1:2]
        q_give.sent()
        kv_give.sent()
        sums[1].sent()

    whole = (n, rows, width)
    vmem = pl.BlockSpec(memory_space=pltpu.VMEM)
    anywhere = pl.BlockSpec(memory_space=pl.ANY)
    outs = [
        shape((width, rows), bf16),
        shape((width, rows), f32),
        shape((in_rows, q_w), f32),
        shape((k_w, in_rows), f32),
        shape((k_w, in_rows), f32),
        shape((in_rows, o_w), f32),
        shape((f_w, in_rows), f32),
        shape((f_w, in_rows), f32),
        shape((o_w, each * f_w), f32),
        shape((1, o_w), f32),
        shape((1, o_w), f32),
    ]
    return pl.pallas_call(
        kernel,
        out_shape=outs,
        in_specs=[anywhere] + [vmem] * 6 + [anywhere] + [vmem] * 8 + [anywhere],
        out_specs=[vmem] * len(outs),
        scratch_shapes=[
            pltpu.VMEM(whole, bf16),
            pltpu.VMEM((chips, rows, width), bf16),
            pltpu.VMEM((chips + 1, rows, width), bf16),
            pltpu.VMEM((chips, rows, width), bf16),
            pltpu.VMEM((chips + 1, rows, width), bf16),
            pltpu.VMEM((length, wide), bf16),
            pltpu.VMEM((held, length, 2 * HEAD_DIM), f32),
            pltpu.VMEM((held, length, HEAD_DIM), f32),
            pltpu.VMEM((length, 3 * wide), bf16),
            pltpu.VMEM((rows, width), f32),
            pltpu.VMEM((n, wide, o_w), bf16),
            pltpu.VMEM((n, wide, o_w), bf16),
            pltpu.VMEM((dp, in_rows, o_w), bf16),
            pltpu.VMEM((dp, in_rows, o_w), bf16),
            pltpu.VMEM((dp, 3 * wide, in_rows), bf16),
            pltpu.VMEM((dp, 3 * wide, in_rows), bf16),
            pltpu.VMEM((each, o_w, f_w), bf16),
            pltpu.VMEM((each, o_w, f_w), bf16),
            pltpu.VMEM((n, 2, o_w), f32),
            pltpu.VMEM((n, 2, o_w), f32),
            pltpu.VMEM((2, o_w), f32),
            pltpu.VMEM((dp, 2, o_w), f32),
            pltpu.VMEM((q_need.slots, in_rows, q_w), bf16),
            pltpu.VMEM((n, in_rows, q_w), bf16),
            pltpu.VMEM((kv_need.slots, 2 * k_w, in_rows), bf16),
            pltpu.VMEM((n, 2 * k_w, in_rows), bf16),
            pltpu.VMEM((2 * k_w, in_rows), f32),
            pltpu.SemaphoreType.DMA((3,)),
            pltpu.VMEM(whole, bf16),
        ]
        + [item for task in tasks for item in task.scratch],
        compiler_params=pltpu.CompilerParams(
            collective_id=ident, has_side_effects=True, vmem_limit_bytes=62 * 1024 * 1024
        ),
        name=f"back_{ident}",
    )(
        d_mids,
        att,
        wo,
        lse,
        q_two,
        k_two,
        val,
        n1,
        wqkv,
        turn,
        d_mid,
        x_own,
        gains,
        mid,
        g_three,
        g_two,
        out_part,
    )


def finish(arrays):
    count = len(arrays)

    def kernel(*refs):
        for i in range(count):
            refs[count + i][...] = refs[i][...]

    return pl.pallas_call(
        kernel,
        out_shape=[jax.ShapeDtypeStruct(array.shape, array.dtype) for array in arrays],
        in_specs=[pl.BlockSpec(memory_space=pltpu.VMEM)] * count,
        out_specs=[pl.BlockSpec(memory_space=pltpu.VMEM)] * count,
        name="finish",
    )(*arrays)


def shards(
    inputs, cotangent, w_query, w_key, w_value, w_output, w_gate, w_up, w_down, gain_attn, gain_ffn
):
    dp, ctx = lax.axis_size("dp"), lax.axis_size("ctx")
    me = lax.axis_index("ctx")
    rows, width = inputs.shape
    length = rows * ctx
    q_w, k_w, o_w, f_w = w_query.shape[1], w_key.shape[1], w_output.shape[1], w_gate.shape[1]
    in_rows = w_query.shape[0]
    held = -(-HEADS // ctx)
    wide = held * HEAD_DIM
    total = ctx * wide
    near = all(wide * j >= q_w * j and wide * (j + 1) <= q_w * (j + 2) for j in range(ctx))

    each = ctx // dp
    cosine, sine = rope_tables(length)
    tables = (
        jnp.concatenate([cosine, sine], axis=1),
        jnp.concatenate([sine, -cosine], axis=1),
    )
    attended, lse, q_two, k_two, values, n1, cots, wo, wqkv, gain_rows, w_g, w_u, w_d, x_own = front(
        0,
        inputs.T,
        cotangent.T,
        w_query,
        w_key.T,
        w_value.T,
        w_output,
        gain_attn.reshape(1, o_w),
        gain_ffn.reshape(1, o_w),
        w_gate.T,
        w_up.T,
        w_down.T,
        held,
        tables,
    )
    d_mid_full, d_middle, middle, out_part, g_three, g_gain_two = mid_layer(
        2,
        attended,
        wo,
        x_own,
        cots,
        gain_rows,
        w_g.reshape(width, f_w),
        w_u.reshape(width, f_w),
        w_d.reshape(width, f_w),
    )
    last = back(
        3,
        d_mid_full,
        attended,
        wo,
        lse,
        q_two,
        k_two,
        values,
        n1,
        wqkv,
        tables[0],
        d_middle,
        x_own,
        gain_rows,
        middle,
        g_three,
        g_gain_two,
        out_part,
        q_w,
        k_w,
    )
    out, grad, g_q, g_k, g_v, g_o, g_g, g_u, g_d, g_one, g_two = finish(last)
    g_one, g_two = g_one.reshape(o_w), g_two.reshape(o_w)
    return out.T, grad.T, g_q, g_k.T, g_v.T, g_o, g_g.T, g_u.T, g_d.T, g_one, g_two


def solution(mesh):
    blocks = P(("dp", "ctx"), None)
    matrix = P("dp", "ctx")
    in_specs = (blocks,) * 2 + (matrix,) * 7 + (P("ctx"),) * 2
    return jax.shard_map(shards, mesh=mesh, in_specs=in_specs, out_specs=in_specs, check_vma=False)
```

```python
import functools

import jax
import jax.numpy as jnp
import numpy as np
from jax import lax
from jax.experimental import pallas as pl
from jax.experimental.pallas import tpu as pltpu
from jax.sharding import PartitionSpec as P

HEADS = 15
KV_HEADS = 5
HEAD_DIM = 64
GROUP = HEADS // KV_HEADS

epsilon = 1e-05
rope_base = 10000.0
bf16 = jnp.bfloat16
f32 = jnp.float32


def remote(src, dst, send, recv, axis, peer):
    return pltpu.make_async_remote_copy(
        src_ref=src,
        dst_ref=dst,
        send_sem=send,
        recv_sem=recv,
        device_id={axis: peer},
        device_id_type=pl.DeviceIdType.MESH,
    )


class Gather:
    axis = "dp"

    def __init__(self, array):
        self.array = array

    def plan(self, sizes):
        self.n = sizes[self.axis]
        self.out = jax.ShapeDtypeStruct((self.n,) + self.array.shape, self.array.dtype)
        self.scratch = [pltpu.SemaphoreType.DMA((self.n,))] * 2 + [pltpu.SemaphoreType.DMA(())]

    def start(self, src, dst, send, recv, own):
        me = lax.axis_index(self.axis)
        self.local = pltpu.make_async_copy(src, dst.at[me], own)
        self.local.start()
        self.copies = []
        for k in range(1, self.n):
            peer = lax.rem(me + k, self.n)
            copy = remote(src, dst.at[me], send.at[k], recv.at[k], self.axis, peer)
            copy.start()
            self.copies.append(copy)

    def middle(self, *refs):
        pass

    def finish(self, src, dst, send, recv, own):
        me = lax.axis_index(self.axis)
        for k in range(1, self.n):
            slot = lax.rem(me + self.n - k, self.n)
            remote(src, dst.at[slot], send.at[k], recv.at[k], self.axis, slot).wait_recv()
        for copy in self.copies:
            copy.wait_send()
        self.local.wait()


class Relay:
    axis = "ctx"

    def __init__(self, array):
        self.array = array

    def plan(self, sizes):
        self.n = sizes[self.axis]
        chips = self.n // 2
        self.out = jax.ShapeDtypeStruct((self.n,) + self.array.shape, self.array.dtype)
        self.scratch = [pltpu.SemaphoreType.DMA((chips,))] * 6 + [pltpu.SemaphoreType.DMA(())]

    def at(self):
        me = lax.axis_index(self.axis)
        chip, core = me // 2, me % 2
        return me, chip, core, me + 1 - 2 * core, self.n // 2

    def start(self, src, dst, rs, rr, ls, lr, ps, pr, own):
        me, chip, core, partner, chips = self.at()

        @pl.when(chip < chips - 1)
        def _():
            remote(src, dst.at[me], rs.at[0], rr.at[0], self.axis, me + 2).start()

        @pl.when(chip > 0)
        def _():
            remote(src, dst.at[me], ls.at[0], lr.at[0], self.axis, me - 2).start()

        remote(src, dst.at[me], ps.at[chip], pr.at[chip], self.axis, partner).start()
        pltpu.make_async_copy(src, dst.at[me], own).start()

    def step(self, k, src, dst, rs, rr, ls, lr, ps, pr, own):
        me, chip, core, partner, chips = self.at()

        def arrived(slot_chip, way, send, recv):
            slot = slot_chip * 2 + core
            back = me - 2 * way
            remote(dst.at[slot], dst.at[slot], send.at[k], recv.at[k], self.axis, back).wait_recv()

            @pl.when(jnp.logical_and(chip + way >= 0, chip + way < chips))
            def _():
                remote(
                    dst.at[slot],
                    dst.at[slot],
                    send.at[k + 1],
                    recv.at[k + 1],
                    self.axis,
                    me + 2 * way,
                ).start()

            remote(
                dst.at[slot], dst.at[slot], ps.at[slot_chip], pr.at[slot_chip], self.axis, partner
            ).start()

        @pl.when(chip - 1 - k >= 0)
        def _():
            arrived(chip - 1 - k, 1, rs, rr)

        @pl.when(chip + 1 + k < chips)
        def _():
            arrived(chip + 1 + k, -1, ls, lr)

    def finish(self, src, dst, rs, rr, ls, lr, ps, pr, own):
        me, chip, core, partner, chips = self.at()
        for c in range(chips):
            slot = 2 * c + 1 - core
            remote(src, dst.at[slot], ps.at[c], pr.at[c], self.axis, partner).wait_recv()
        for c in range(chips):
            remote(src, dst.at[2 * c + core], ps.at[c], pr.at[c], self.axis, partner).wait_send()
        for k in range(chips - 1):

            @pl.when(jnp.logical_and(chip < chips - 1, k <= chip))
            def _():
                remote(src, dst.at[me], rs.at[k], rr.at[k], self.axis, me + 2).wait_send()

            @pl.when(jnp.logical_and(chip > 0, k <= chips - 1 - chip))
            def _():
                remote(src, dst.at[me], ls.at[k], lr.at[k], self.axis, me - 2).wait_send()

        pltpu.make_async_copy(src, dst.at[me], own).wait()


class Turn:
    axis = "all"

    def __init__(self, array):
        self.array = array

    def plan(self, sizes):
        self.dp, self.n = sizes["dp"], sizes["ctx"]
        self.m = self.n // self.dp
        self.out = jax.ShapeDtypeStruct(self.array.shape, self.array.dtype)
        self.scratch = [pltpu.SemaphoreType.DMA((self.m,))] * 2

    def each(self, src, dst, send, recv):
        row, col = lax.axis_index("dp"), lax.axis_index("ctx")
        put = col % self.m
        for i in range(self.m):
            to_row, to_col = col // self.m, row * self.m + i
            here = jnp.logical_and(to_row == row, to_col == col)
            far = pltpu.make_async_remote_copy(
                src_ref=src.at[i],
                dst_ref=dst.at[put],
                send_sem=send.at[i],
                recv_sem=recv.at[put],
                device_id={"dp": to_row, "ctx": to_col},
                device_id_type=pl.DeviceIdType.MESH,
            )
            local = pltpu.make_async_copy(src.at[i], dst.at[put], recv.at[put])
            yield i, here, far, local

    def start(self, *refs):
        for i, here, far, local in self.each(*refs):
            pl.when(here)(local.start)
            pl.when(jnp.logical_not(here))(far.start)

    def finish(self, src, dst, send, recv):
        row, col = lax.axis_index("dp"), lax.axis_index("ctx")
        for i, here, far, local in self.each(src, dst, send, recv):
            pl.when(jnp.logical_not(here))(far.wait_send)
        for i in range(self.m):
            own = jnp.logical_and(col // self.m == row, row * self.m + i == col)
            local = pltpu.make_async_copy(src.at[i], dst.at[i], recv.at[i])
            far = pltpu.make_async_remote_copy(
                src_ref=src.at[i],
                dst_ref=dst.at[i],
                send_sem=send.at[i],
                recv_sem=recv.at[i],
                device_id={"dp": col // self.m, "ctx": row * self.m + i},
                device_id_type=pl.DeviceIdType.MESH,
            )
            pl.when(own)(local.wait)
            pl.when(jnp.logical_not(own))(far.wait_recv)

    def middle(self, *refs):
        pass


class Swap:
    def __init__(self, axis, array):
        self.axis, self.array = axis, array

    def plan(self, sizes):
        self.n = sizes[self.axis]
        self.out = jax.ShapeDtypeStruct(self.array.shape, self.array.dtype)
        self.scratch = [pltpu.SemaphoreType.DMA((self.n,))] * 2 + [pltpu.SemaphoreType.DMA(())]

    def start(self, src, dst, send, recv, own):
        me = lax.axis_index(self.axis)
        self.local = pltpu.make_async_copy(src.at[me], dst.at[me], own)
        self.local.start()
        self.copies = []
        for k in range(1, self.n):
            peer = lax.rem(me + k, self.n)
            copy = remote(src.at[peer], dst.at[me], send.at[k], recv.at[k], self.axis, peer)
            copy.start()
            self.copies.append(copy)

    def middle(self, *refs):
        pass

    def finish(self, src, dst, send, recv, own):
        me = lax.axis_index(self.axis)
        for k in range(1, self.n):
            slot = lax.rem(me + self.n - k, self.n)
            remote(
                src.at[slot], dst.at[slot], send.at[k], recv.at[k], self.axis, slot
            ).wait_recv()
        for copy in self.copies:
            copy.wait_send()
        self.local.wait()


class Shift:
    def __init__(self, axis, array, by):
        self.axis, self.array, self.by = axis, array, by

    def plan(self, sizes):
        self.n = sizes[self.axis]
        self.out = jax.ShapeDtypeStruct(self.array.shape, self.array.dtype)
        self.scratch = [pltpu.SemaphoreType.DMA(())] * 2

    def start(self, src, dst, send, recv):
        me = lax.axis_index(self.axis)
        peer = lax.rem(me + self.n + self.by, self.n)
        self.copy = remote(src, dst, send, recv, self.axis, peer)
        self.copy.start()

    def middle(self, *refs):
        pass

    def finish(self, *refs):
        self.copy.wait_recv()
        self.copy.wait_send()


class Reduce:
    axis = "ctx"

    def __init__(self, array):
        self.array = array

    def plan(self, sizes):
        self.n = sizes[self.axis]
        block = self.array.shape[1:]
        chips = self.n // 2
        self.out = jax.ShapeDtypeStruct(block, f32)
        slots = pltpu.VMEM((chips,) + block, self.array.dtype)
        self.scratch = [pltpu.SemaphoreType.DMA((chips,))] * 4 + [slots] * 3

    def start(self, src, dst, psend, precv, send, recv, near, term, far):
        me = lax.axis_index(self.axis)
        chips = self.n // 2
        chip, core = me // 2, me % 2
        partner = me + 1 - 2 * core
        self.copies = []
        for k in list(range(1, chips)) + [0]:
            slot = lax.rem(chip + k, chips) * 2 + 1 - core
            copy = remote(
                src.at[slot], near.at[k], psend.at[k], precv.at[k], self.axis, partner
            )
            copy.start()
            self.copies.append(copy)

    def middle(self, src, dst, psend, precv, send, recv, near, term, far):
        me = lax.axis_index(self.axis)
        chips = self.n // 2
        chip, core = me // 2, me % 2
        partner = me + 1 - 2 * core
        for k in range(1, chips):
            remote(
                src.at[me], near.at[k], psend.at[k], precv.at[k], self.axis, partner
            ).wait_recv()
            peer = lax.rem(chip + k, chips) * 2 + core
            both = src[peer].astype(f32) + near[k].astype(f32)
            term[k] = both.astype(term.dtype)
            copy = remote(term.at[k], far.at[k], send.at[k], recv.at[k], self.axis, peer)
            copy.start()
            self.copies.append(copy)

    def finish(self, src, dst, psend, precv, send, recv, near, term, far):
        me = lax.axis_index(self.axis)
        chips = self.n // 2
        core = me % 2
        partner = me + 1 - 2 * core
        remote(src.at[me], near.at[0], psend.at[0], precv.at[0], self.axis, partner).wait_recv()
        dst[...] = src[me].astype(f32) + near[0].astype(f32)
        for k in range(1, chips):
            remote(
                src.at[me], far.at[k], send.at[k], recv.at[k], self.axis, partner
            ).wait_recv()
            dst[...] += far[k].astype(f32)
        for copy in self.copies:
            copy.wait_send()


def exchange(ident, *tasks):
    sizes = {axis: lax.axis_size(axis) for axis in ("dp", "ctx")}
    for task in tasks:
        task.plan(sizes)
    axes = [axis for axis in ("dp", "ctx") if any(task.axis == axis for task in tasks)]
    everyone = any(task.axis == "all" for task in tasks)
    axes = [] if everyone else axes
    count = len(tasks)

    def kernel(*refs):
        barrier = pltpu.get_barrier_semaphore()
        greeted = 0
        if everyone:
            row, col = lax.axis_index("dp"), lax.axis_index("ctx")
            for i in range(1, sizes["dp"] * sizes["ctx"]):
                other = lax.rem(row * sizes["ctx"] + col + i, sizes["dp"] * sizes["ctx"])
                pl.semaphore_signal(
                    barrier,
                    inc=1,
                    device_id={"dp": other // sizes["ctx"], "ctx": other % sizes["ctx"]},
                    device_id_type=pl.DeviceIdType.MESH,
                )
                greeted += 1
        for axis in axes:
            me, n = lax.axis_index(axis), sizes[axis]
            for k in range(1, n):
                pl.semaphore_signal(
                    barrier,
                    inc=1,
                    device_id={axis: lax.rem(me + k, n)},
                    device_id_type=pl.DeviceIdType.MESH,
                )
            greeted += n - 1
        pl.semaphore_wait(barrier, greeted)
        held, at = [], 2 * count
        for i, task in enumerate(tasks):
            held.append((refs[i], refs[count + i]) + tuple(refs[at : at + len(task.scratch)]))
            at += len(task.scratch)
        for task, own in zip(tasks, held):
            task.start(*own)
        for k in range(sizes["ctx"] // 2 - 1):
            for task, own in zip(tasks, held):
                if isinstance(task, Relay):
                    task.step(k, *own)
                elif k == 0:
                    task.middle(*own)
        for task, own in zip(tasks, held):
            task.finish(*own)

    return pl.pallas_call(
        kernel,
        out_shape=[task.out for task in tasks],
        in_specs=[pl.BlockSpec(memory_space=pltpu.VMEM)] * count,
        out_specs=[pl.BlockSpec(memory_space=pltpu.VMEM)] * count,
        scratch_shapes=[shape for task in tasks for shape in task.scratch],
        compiler_params=pltpu.CompilerParams(
            collective_id=ident, has_side_effects=True, vmem_limit_bytes=60 * 1024 * 1024
        ),
        name=f"exchange_{ident}",
    )(*[task.array for task in tasks])


def spread(axes, sizes, everyone):
    barrier = pltpu.get_barrier_semaphore()
    greeted = 0
    if everyone:
        row, col = lax.axis_index("dp"), lax.axis_index("ctx")
        total = sizes["dp"] * sizes["ctx"]

        def greet(i, carry):
            other = lax.rem(row * sizes["ctx"] + col + i, total)
            pl.semaphore_signal(
                barrier,
                inc=1,
                device_id={"dp": other // sizes["ctx"], "ctx": other % sizes["ctx"]},
                device_id_type=pl.DeviceIdType.MESH,
            )
            return carry

        lax.fori_loop(1, total, greet, 0)
        greeted = total - 1
    else:
        for axis in axes:
            me, n = lax.axis_index(axis), sizes[axis]
            for k in range(1, n):
                pl.semaphore_signal(
                    barrier,
                    inc=1,
                    device_id={axis: lax.rem(me + k, n)},
                    device_id_type=pl.DeviceIdType.MESH,
                )
            greeted += n - 1
    pl.semaphore_wait(barrier, greeted)


def mm(a, b, dims):
    return lax.dot_general(a, b, ((dims[:1], dims[1:]), ((), ())), preferred_element_type=f32)


def nn(a, b):
    return mm(a, b, (1, 0))


def nt(a, b):
    return mm(a, b, (1, 1))


def tn(a, b):
    return mm(a, b, (0, 0))


def turned(rows):
    width = rows.shape[-1]
    parts = rows.reshape(-1, 2, HEAD_DIM // 2, width)
    return jnp.concatenate([-parts[:, 1:], parts[:, :1]], axis=1).reshape(rows.shape)


def rope_tables(row_count):
    half = HEAD_DIM // 2
    frequency = np.float32(rope_base) ** (-np.arange(half).astype(np.float32) * np.float32(2.0 / HEAD_DIM))
    angles = np.arange(row_count).astype(np.float32)[:, None] * frequency[None, :].astype(np.float32)
    return [jnp.asarray(np.tile(f(angles), (1, 2)), f32) for f in (np.cos, np.sin)]


def norm_backward(hidden, inverse, gain_vec, upstream):
    scaled = upstream * gain_vec
    cubed = inverse * inverse * inverse
    d_hidden = (
        inverse * scaled
        - hidden
        * cubed
        * jnp.sum(scaled * hidden, axis=-1, keepdims=True)
        / hidden.shape[-1]
    )
    return d_hidden, jnp.sum(upstream * hidden * inverse, axis=0)


def inverse_rms(hidden):
    return lax.rsqrt(jnp.mean(hidden * hidden, axis=-1, keepdims=True) + epsilon)


class Line:
    axis = "ctx"

    def __init__(self, n, rows):
        self.n, self.chips = n, n // 2
        self.cuts = 2 if rows % 32 == 0 else 1
        self.size = rows // self.cuts
        self.scratch = [pltpu.SemaphoreType.DMA((self.chips * self.cuts,))] * 6

    def hold(self, dst, sems):
        self.dst = dst
        self.rs, self.rr, self.ls, self.lr, self.ps, self.pr = sems
        self.me = lax.axis_index(self.axis)
        self.chip, self.core = self.me // 2, self.me % 2
        self.partner = self.me + 1 - 2 * self.core

    def copy(self, slot, cut, send, recv, at, peer):
        place = self.dst.at[slot, pl.ds(cut * self.size, self.size)]
        at = at * self.cuts + cut
        return remote(place, place, send.at[at], recv.at[at], self.axis, peer)

    def right(self, slot, cut, k):
        return self.copy(slot, cut, self.rs, self.rr, k, self.me + 2)

    def left(self, slot, cut, k):
        return self.copy(slot, cut, self.ls, self.lr, k, self.me - 2)

    def share(self, slot, cut, at):
        return self.copy(slot, cut, self.ps, self.pr, at, self.partner)

    def start(self):
        me, chip = self.me, self.chip
        for cut in range(self.cuts):
            pl.when(chip < self.chips - 1)(self.right(me, cut, 0).start)
            pl.when(chip > 0)(self.left(me, cut, 0).start)
        for cut in range(self.cuts):
            self.share(me, cut, chip).start()

    def step(self, k):
        chip, chips = self.chip, self.chips
        for cut in range(self.cuts):

            @pl.when(chip - 1 - k >= 0)
            def _():
                slot = (chip - 1 - k) * 2 + self.core
                self.right(slot, cut, k).wait_recv()
                pl.when(chip + 1 < chips)(self.right(slot, cut, k + 1).start)
                self.share(slot, cut, chip - 1 - k).start()

            @pl.when(chip + 1 + k < chips)
            def _():
                slot = (chip + 1 + k) * 2 + self.core
                self.left(slot, cut, k).wait_recv()
                pl.when(chip > 0)(self.left(slot, cut, k + 1).start)
                self.share(slot, cut, chip + 1 + k).start()

    def beside(self, at):
        for cut in range(self.cuts):
            self.share(2 * at + 1 - self.core, cut, at).wait_recv()

    def each(self, body, done=0, then=None):
        self.beside(self.chip)
        body(self.chip)

        def at_step(k, carry):
            @pl.when(k >= done)
            def _():
                self.step(k)

            if then is not None:
                pl.when(k == self.chips - 2)(then)

            def at_side(side, inner):
                at = jnp.where(side == 0, self.chip - 1 - k, self.chip + 1 + k)

                @pl.when(jnp.logical_and(at >= 0, at < self.chips))
                def _():
                    self.beside(at)
                    body(at)

                return inner

            return lax.fori_loop(0, 2, at_side, carry)

        if self.chips > 1:
            lax.fori_loop(0, self.chips - 1, at_step, 0)
        elif then is not None:
            then()

    def sent(self):
        me, chip, chips = self.me, self.chip, self.chips
        for cut in range(self.cuts):
            for c in range(chips):
                self.share(2 * c + self.core, cut, c).wait_send()
            for k in range(chips - 1):
                to_right = jnp.logical_and(chip < chips - 1, k <= chip)
                pl.when(to_right)(self.right(me, cut, k).wait_send)
                to_left = jnp.logical_and(chip > 0, k <= chips - 1 - chip)
                pl.when(to_left)(self.left(me, cut, k).wait_send)


class Sum:
    axis = "ctx"

    def __init__(self, n, rows):
        self.n, self.chips = n, n // 2
        self.cuts = 2 if rows % 32 == 0 else 1
        self.size = rows // self.cuts
        self.scratch = [pltpu.SemaphoreType.DMA((self.chips,))] * 2
        self.scratch += [pltpu.SemaphoreType.DMA((self.chips * self.cuts,))] * 4

    def hold(self, part, near, got, sems):
        self.part, self.near, self.got = part, near, got
        self.ps, self.pr, self.rs, self.rr, self.ls, self.lr = sems
        self.me = lax.axis_index(self.axis)
        self.chip, self.core = self.me // 2, self.me % 2
        self.partner = self.me + 1 - 2 * self.core

    def beside(self, d):
        return remote(
            self.part.at[2 * d + 1 - self.core],
            self.near.at[d],
            self.ps.at[d],
            self.pr.at[d],
            self.axis,
            self.partner,
        )

    def rows(self, cut):
        return pl.ds(cut * self.size, self.size)

    def line(self, d, cut, place, send, recv, peer):
        at, rows = d * self.cuts + cut, self.rows(cut)
        return remote(
            self.part.at[2 * d + self.core, rows],
            self.got.at[place, rows],
            send.at[at],
            recv.at[at],
            self.axis,
            peer,
        )

    def right(self, d, cut):
        return self.line(d, cut, d, self.rs, self.rr, self.me + 2)

    def left(self, d, cut):
        place = jnp.where(d == self.chip - 1, self.chips, d)
        return self.line(d, cut, place, self.ls, self.lr, self.me - 2)

    def ready(self, d):
        self.beside(d).start()

    def order(self, k):
        return jnp.where(self.chip < self.chips // 2, self.chips - 1 - k, k)

    def pass_on(self, d, cut, edge, copy):
        if cut == 0:
            self.beside(d).wait_recv()
        rows = self.rows(cut)
        both = self.part[2 * d + self.core, rows].astype(f32) + self.near[d, rows].astype(f32)

        @pl.when(edge)
        def _():
            self.part[2 * d + self.core, rows] = both.astype(bf16)

        @pl.when(jnp.logical_not(edge))
        def _():
            copy.wait_recv()
            more = both + self.got[d, rows].astype(f32)
            self.part[2 * d + self.core, rows] = more.astype(bf16)

        copy.start()

    def step(self, t):
        chip, chips = self.chip, self.chips
        for cut in range(self.cuts):

            @pl.when(t >= chip)
            def _():
                d = chips - 1 - t + chip
                self.pass_on(d, cut, chip == 0, self.right(d, cut))

            @pl.when(t >= chips - 1 - chip)
            def _():
                d = t - (chips - 1 - chip)
                self.pass_on(d, cut, chip == chips - 1, self.left(d, cut))

    def last(self, total):
        chip, chips = self.chip, self.chips
        self.beside(chip).wait_recv()
        total[...] = self.part[self.me].astype(f32) + self.near[chip].astype(f32)
        for cut in range(self.cuts):
            rows = self.rows(cut)

            @pl.when(chip > 0)
            def _():
                self.right(chip, cut).wait_recv()
                total[rows] += self.got[chip, rows].astype(f32)

            @pl.when(chip < chips - 1)
            def _():
                self.left(chip, cut).wait_recv()
                total[rows] += self.got[chips, rows].astype(f32)

    def sent(self):
        for d in range(self.chips):
            self.beside(d).wait_send()
            for cut in range(self.cuts):
                pl.when(self.chip < d)(self.right(d, cut).wait_send)
                pl.when(self.chip > d)(self.left(d, cut).wait_send)


def mid_layer(ident, attended, wo, x_own, cot_full, gains, w_gate, w_up, w_down_t):
    sizes = {axis: lax.axis_size(axis) for axis in ("dp", "ctx")}
    dp, n = sizes["dp"], sizes["ctx"]
    chips = n // 2
    rows, width = x_own.shape
    wide, f_w = attended.shape[2], w_gate.shape[1]
    in_rows = width // dp
    shape = jax.ShapeDtypeStruct
    lines = [Line(n, rows), Line(n, rows)]
    sums = [Sum(n, rows)]
    att_swap = Swap("ctx", attended)
    att_swap.plan(sizes)
    swap = Swap("dp", shape((dp, in_rows, 3 * f_w), bf16))
    swap.plan(sizes)
    tasks = lines + sums + [att_swap, swap]

    def kernel(*refs):
        att, wo_ref, x_ref, cots, gain_ref, wg, wu, wd = refs[:8]
        d_mids, d_mid, mid, out_part, g_all, g_gain = refs[8:14]
        part, near, got, n2, mixed, d_gate, d_up, grads, inv, total = refs[14:24]
        att_got, load = refs[24:26]
        sems, at = [], 26
        for task in tasks:
            sems.append(tuple(refs[at : at + len(task.scratch)]))
            at += len(task.scratch)
        bring = pltpu.make_async_copy(wo_ref, part.at[pl.ds(0, wo.shape[0])], load)
        bring.start()
        spread(("dp", "ctx"), sizes, False)
        att_swap.start(att, att_got, *sems[3])
        lines[0].hold(n2, sems[0])
        lines[1].hold(d_mids, sems[1])
        sums[0].hold(part, near, got, sems[2])
        me = lax.axis_index("ctx")

        bring.wait()
        att_swap.finish(att, att_got, *sems[3])
        value = None
        for j in range(n):
            low = j * wide
            term = nn(att_got[j], part[low // rows, low % rows : low % rows + wide])
            value = term if value is None else value + term
        total[...] = value
        middle = x_ref[...].astype(f32) + total[...]
        inverse = inverse_rms(middle)
        mid[...] = middle
        inv[...] = inverse
        n2[me] = (middle * inverse * gain_ref[1:2]).astype(bf16)
        lines[0].start()

        def forward(at):
            here = pl.ds(2 * at, 2)
            tokens = n2[here].reshape(2 * rows, width)
            gate_pre = nn(tokens, wg[...])
            up_pre = nn(tokens, wu[...])
            d_mixed = nn(cots[here].reshape(2 * rows, width), wd[...])
            sigma = 1.0 / (1.0 + jnp.exp(-gate_pre))
            silu_gate = gate_pre * sigma
            act = (silu_gate * up_pre).astype(bf16)
            dg = (d_mixed * up_pre * sigma * (1.0 + gate_pre * (1.0 - sigma))).astype(bf16)
            du = (d_mixed * silu_gate).astype(bf16)
            mixed[here] = act.reshape(2, rows, f_w)
            d_gate[here] = dg.reshape(2, rows, f_w)
            d_up[here] = du.reshape(2, rows, f_w)
            d_two = nt(dg, wg[...]) + nt(du, wu[...])
            part[here] = d_two.astype(bf16).reshape(2, rows, width)
            sums[0].ready(at)
            out_part[here] = nt(act, wd[...]).astype(bf16).reshape(2, rows, width)

        lines[0].each(forward)

        def gradient(i):
            left, right = ((n2, d_gate), (n2, d_up), (cots, mixed))[i]
            value = tn(
                left[...].reshape(n * rows, width), right[...].reshape(n * rows, f_w)
            ).astype(bf16)
            for r in range(dp):
                grads[r, :, i * f_w : (i + 1) * f_w] = value[r * in_rows : (r + 1) * in_rows]

        for t in range(chips - 1):
            sums[0].step(t)
            if t == 0:
                gradient(0)
                gradient(1)
            if t == min(1, chips - 2):
                gradient(2)
                swap.start(grads, g_all, *sems[4])
        sums[0].last(total)
        middle = mid[...]
        d_norm, gain_part = norm_backward(middle, inv[...], gain_ref[1:2], total[...])
        g_gain[...] = gain_part.reshape(1, width)
        d_middle = cots[me].astype(f32) + d_norm
        d_mid[...] = d_middle
        d_mids[me] = d_middle.astype(bf16)
        lines[1].start()
        sums[0].sent()
        lines[0].sent()
        lines[1].each(lambda at: None)
        lines[1].sent()
        swap.finish(grads, g_all, *sems[4])

    whole = (n, rows, width)
    vmem = pl.BlockSpec(memory_space=pltpu.VMEM)
    return pl.pallas_call(
        kernel,
        out_shape=[
            shape(whole, bf16),
            shape((rows, width), f32),
            shape((rows, width), f32),
            shape(whole, bf16),
            shape((dp, in_rows, 3 * f_w), bf16),
            shape((1, width), f32),
        ],
        in_specs=[vmem, pl.BlockSpec(memory_space=pl.ANY)] + [vmem] * 6,
        out_specs=[pl.BlockSpec(memory_space=pltpu.VMEM)] * 6,
        scratch_shapes=[
            pltpu.VMEM(whole, bf16),
            pltpu.VMEM((chips, rows, width), bf16),
            pltpu.VMEM((chips + 1, rows, width), bf16),
            pltpu.VMEM(whole, bf16),
            pltpu.VMEM((n, rows, f_w), bf16),
            pltpu.VMEM((n, rows, f_w), bf16),
            pltpu.VMEM((n, rows, f_w), bf16),
            pltpu.VMEM((dp, in_rows, 3 * f_w), bf16),
            pltpu.VMEM((rows, 1), f32),
            pltpu.VMEM((rows, width), f32),
            pltpu.VMEM(attended.shape, bf16),
            pltpu.SemaphoreType.DMA(()),
        ]
        + [item for task in tasks for item in task.scratch],
        compiler_params=pltpu.CompilerParams(
            collective_id=ident, has_side_effects=True, vmem_limit_bytes=62 * 1024 * 1024
        ),
        name=f"block_{ident}",
    )(attended, wo, x_own, cot_full, gains, w_gate, w_up, w_down_t)


class Need:
    axis = "ctx"

    def __init__(self, n, low, high):
        self.n, self.low, self.high = n, low, high
        self.slots = max(high(d) - low(d) + 1 for d in range(n))
        self.scratch = [
            pltpu.SemaphoreType.DMA((n,)),
            pltpu.SemaphoreType.DMA((self.slots,)),
        ]

    def hold(self, src, dst, sems):
        self.src, self.dst = src, dst
        self.send, self.recv = sems
        self.me = lax.axis_index(self.axis)
        self.first, self.final = self.low(self.me), self.high(self.me)

    def each(self):
        for d in range(self.n):
            low, high = self.low(d), self.high(d)
            used = jnp.logical_and(self.me >= low, self.me <= high)
            slot = jnp.clip(self.me - low, 0, self.slots - 1)
            copy = remote(
                self.src, self.dst.at[slot], self.send.at[d], self.recv.at[slot], self.axis, d
            )
            yield jnp.logical_and(used, self.me != d), copy

    def start(self):
        for used, copy in self.each():
            pl.when(used)(copy.start)
        for t in range(self.slots):
            source = self.first + t

            @pl.when(source == self.me)
            def _():
                self.dst[t] = self.src[...]

            @pl.when(source > self.final)
            def _():
                self.dst[t] = jnp.zeros_like(self.dst[t])

    def arrive(self):
        beside = self.me + 1 - 2 * lax.rem(self.me, 2)
        for t in range(self.slots):
            source = self.first + t
            copy = remote(
                self.src, self.dst.at[t], self.send.at[0], self.recv.at[t], self.axis, beside
            )
            pl.when(jnp.logical_and(source <= self.final, source != self.me))(copy.wait_recv)

    def sent(self):
        for used, copy in self.each():
            pl.when(used)(copy.wait_send)


def least(a, b):
    return min(a, b) if isinstance(a, int) else jnp.minimum(a, b)


def over(a, b):
    return a // b if isinstance(a, int) else lax.div(a, b)


def pick(rows, first, source, sign):
    at = first + lax.broadcasted_iota(jnp.int32, (rows, source.shape[1]), 0)
    return jnp.where(at == source, sign, 0.0)


def kv_head(j):
    return least(over(j, GROUP), KV_HEADS - 1)


def needs(n, held, width, q_w, k_w):
    wide = held * HEAD_DIM
    q_need = Need(
        n,
        lambda d: over(least(wide * d, width - 1), q_w),
        lambda d: over(least(wide * d + wide - 1, width - 1), q_w),
    )
    kv_need = Need(
        n,
        lambda d: over(HEAD_DIM * kv_head(held * d), k_w),
        lambda d: over(HEAD_DIM * kv_head(held * d + held - 1) + HEAD_DIM - 1, k_w),
    )
    return q_need, kv_need


def front(
    ident, x_t, cot_t, w_q, wk_t, wv_t, w_o, gain_a, gain_b, wg_t, wu_t, wd_t, held, tables
):
    sizes = {axis: lax.axis_size(axis) for axis in ("dp", "ctx")}
    dp, n = sizes["dp"], sizes["ctx"]
    chips, each = n // 2, n // dp
    width, rows = x_t.shape
    in_rows, q_w = w_q.shape
    o_w, k_w, f_w = w_o.shape[1], wk_t.shape[0], wg_t.shape[0]
    wide, total = held * HEAD_DIM, n * held * HEAD_DIM
    length, chunk = n * rows, 2 * rows
    shape = jax.ShapeDtypeStruct
    kv_rows = shape((2 * k_w, in_rows), bf16)

    q_need, kv_need = needs(n, held, width, q_w, k_w)
    x_line, cot_line = Line(n, rows), Line(n, rows)
    gain_all = Gather(shape((2, o_w), bf16))
    gain_all.axis = "ctx"
    q_all, kv_all = Gather(w_q), Gather(kv_rows)
    o_line, o_all = Line(n, in_rows), Gather(shape((chips, in_rows, o_w), bf16))
    g_all, u_all = [Gather(shape((in_rows, f_w), bf16)) for _ in range(2)]
    d_turn = Turn(shape((each, o_w, f_w), bf16))
    d_all = Gather(shape((each, o_w, f_w), bf16))
    planned = [q_all, kv_all, o_all, g_all, u_all, d_turn, d_all, gain_all]
    for task in planned:
        task.plan(sizes)
    tasks = [q_need, kv_need, x_line, cot_line, o_line] + planned

    def kernel(*refs):
        xt, ct, wq_ref, wk_ref, wv_ref, wo_ref, ga_ref, gb_ref = refs[:8]
        wgt, wut, wdt, cos_ref, sin_ref = refs[8:13]
        att, lse, q_two, k_two, val, n1, cots, wo_out, wqkv, gain_out = refs[13:23]
        wg_out, wu_out, wd_out, x_own, wo_all = refs[23:28]
        xs, gains_in, q_got, kv_got, o_got, q_in, kv_in, wall = refs[28:36]
        wg_mine, wu_mine, d_mine, d_got, o_side, kv_ref, gain_mine = refs[36:43]
        o_half, o_more, pair = refs[43:46]
        sems, at = {}, 46
        for task in tasks:
            sems[task] = tuple(refs[at : at + len(task.scratch)])
            at += len(task.scratch)
        spread(("dp", "ctx"), sizes, True)
        me = lax.axis_index("ctx")
        core = lax.rem(me, 2)
        x_line.hold(xs, sems[x_line])
        cot_line.hold(cots, sems[cot_line])
        o_line.hold(o_side, sems[o_line])
        q_need.hold(q_got, q_in, sems[q_need])
        kv_need.hold(kv_got, kv_in, sems[kv_need])
        kv_ref[:k_w] = wk_ref[...]
        kv_ref[k_w:] = wv_ref[...]
        mine = xt[...].T
        xs[me] = mine
        x_own[...] = mine
        x_line.start()
        q_all.start(wq_ref, q_got, *sems[q_all])
        kv_all.start(kv_ref, kv_got, *sems[kv_all])
        o_side[me] = wo_ref[...]
        gain_mine[...] = jnp.concatenate([ga_ref[...], gb_ref[...]], axis=0)
        gain_all.start(gain_mine, gains_in, *sems[gain_all])
        cots[me] = ct[...].T
        wg_mine[...] = wgt[...].T
        wu_mine[...] = wut[...].T
        for i in range(each):
            d_mine[i] = wdt[:, i * f_w : (i + 1) * f_w]
        q_all.finish(wq_ref, q_got, *sems[q_all])
        kv_all.finish(kv_ref, kv_got, *sems[kv_all])
        q_need.start()
        kv_need.start()
        d_turn.start(d_mine, d_got, *sems[d_turn])
        if chips > 1:
            x_line.step(0)
        gain_all.finish(gain_mine, gains_in, *sems[gain_all])
        for c in range(n):
            gain_out[:, c * o_w : (c + 1) * o_w] = gains_in[c].astype(f32)

        def turned(base, d):
            half = HEAD_DIM // 2
            return base + jnp.bitwise_and(d + half, HEAD_DIM - 1), jnp.where(d < half, -1.0, 1.0)

        def plan(heads):
            lane = lax.broadcasted_iota(jnp.int32, (1, 2 * HEAD_DIM), 1)
            d = jnp.bitwise_and(lane, HEAD_DIM - 1)
            parts = []
            for h in heads:
                parts.append((h * HEAD_DIM + d, jnp.ones((1, 2 * HEAD_DIM), f32)))
                parts.append(turned(h * HEAD_DIM, d))
            lane = lax.broadcasted_iota(jnp.int32, (1, wide), 1)
            flat = jnp.bitwise_and(lane, HEAD_DIM - 1)
            base = jnp.zeros((1, wide), jnp.int32)
            for i, h in enumerate(heads):
                inside = jnp.logical_and(lane >= i * HEAD_DIM, lane < (i + 1) * HEAD_DIM)
                base = jnp.where(inside, h * HEAD_DIM, base)
            return parts + [(base + flat, jnp.ones((1, wide), f32))]

        heads = [me * held + h for h in range(held)]
        kv_heads = [kv_head(h) for h in heads]
        q_plan, k_plan = plan(heads), plan(kv_heads)
        no = [(jnp.zeros_like(k_plan[-1][0]) - 1, k_plan[-1][1])]
        q_need.arrive()
        kv_need.arrive()
        span = 4 * held * HEAD_DIM
        for r in range(dp):
            here = slice(r * in_rows, (r + 1) * in_rows)
            value = None
            for t in range(q_need.slots):
                first = (q_need.first + t) * q_w
                take = jnp.concatenate([pick(q_w, first, *p) for p in q_plan], axis=1)
                term = nn(q_in[t, r], take.astype(bf16))
                value = term if value is None else value + term
            value = value.astype(bf16)
            wall[here, :span] = value[:, :span]
            wqkv[here, :wide] = value[:, span:]
            value = None
            for t in range(kv_need.slots):
                first = (kv_need.first + t) * k_w
                top = [pick(k_w, first, *p) for p in k_plan + no]
                zero = jnp.zeros((k_w, span + wide), f32)
                top = jnp.concatenate(top, axis=1)
                low = jnp.concatenate([zero, pick(k_w, first, *k_plan[-1])], axis=1)
                take = jnp.concatenate([top, low], axis=0).astype(bf16)
                term = tn(kv_in[t, r], take)
                value = term if value is None else value + term
            value = value.astype(bf16)
            wall[here, span:] = value[:, :span]
            wqkv[here, wide:] = value[:, span:]
        if chips > 2:
            x_line.step(1)
        g_all.start(wg_mine, wg_out, *sems[g_all])
        u_all.start(wu_mine, wu_out, *sems[u_all])

        def project(at):
            here = pl.ds(2 * at, 2)
            tokens = xs[here].reshape(chunk, width).astype(f32)
            normed = (tokens * inverse_rms(tokens) * gain_out[0:1]).astype(bf16)
            n1[here] = normed.reshape(2, rows, width)
            both = nn(normed, wall[...])
            low = pl.multiple_of(at * chunk, chunk)
            first, second = cos_ref[pl.ds(low, chunk)], sin_ref[pl.ds(low, chunk)]
            for h in range(2 * held):
                at_h = h * 4 * HEAD_DIM
                a = both[:, at_h : at_h + 2 * HEAD_DIM]
                b = both[:, at_h + 2 * HEAD_DIM : at_h + 4 * HEAD_DIM]
                two = a * first + b * second
                if h < held:
                    q_two[h, pl.ds(low, chunk)] = (two * HEAD_DIM ** (-0.5)).astype(bf16)
                else:
                    k_two[h - held, pl.ds(low, chunk)] = two.astype(bf16)
            v = nn(normed, wqkv[:, 2 * wide :]).astype(bf16)
            for h in range(held):
                val[h, pl.ds(low, chunk)] = v[:, h * HEAD_DIM : (h + 1) * HEAD_DIM]

        def begin():
            o_line.start()
            cot_line.start()

        x_line.each(project, min(2, chips - 1), begin)
        for k in range(chips - 1):
            o_line.step(k)
        for c in range(chips):
            o_line.beside(c)
        for c in range(chips):
            o_half[c] = o_side[2 * c + core]
        o_all.start(o_half, o_got, *sems[o_all])
        d_turn.finish(d_mine, d_got, *sems[d_turn])
        d_all.start(d_got, wd_out, *sems[d_all])
        x_line.sent()

        def attend(i):
            first, last = i * chunk, (i + 1) * chunk
            for h in range(held):
                q = q_two[h, first:last, :HEAD_DIM]
                diag = nt(q, k_two[h, first:last, :HEAD_DIM])
                row = lax.broadcasted_iota(jnp.int32, diag.shape, 0)
                col = lax.broadcasted_iota(jnp.int32, diag.shape, 1)
                diag = jnp.where(row >= col, diag, -1e30)
                top = jnp.max(diag, axis=-1, keepdims=True)
                if i:
                    off = nt(q, k_two[h, :first, :HEAD_DIM])
                    top = jnp.maximum(top, jnp.max(off, axis=-1, keepdims=True))
                expo = jnp.exp(diag - top)
                weight = jnp.sum(expo, axis=-1, keepdims=True)
                out = nn(expo.astype(bf16), val[h, first:last])
                if i:
                    expo = jnp.exp(off - top)
                    weight = weight + jnp.sum(expo, axis=-1, keepdims=True)
                    out = out + nn(expo.astype(bf16), val[h, :first])
                out = (out / weight).astype(bf16)
                lanes = slice(h * HEAD_DIM, (h + 1) * HEAD_DIM)
                att[2 * i : 2 * i + 2, :, lanes] = out.reshape(2, rows, HEAD_DIM)
                logs = jnp.broadcast_to(top + jnp.log(weight), (chunk, HEAD_DIM))
                lse[first:last, lanes] = logs

        for i in range(chips):
            attend(i)
            if i < chips - 1:
                cot_line.step(i)
        o_line.sent()
        o_all.finish(o_half, o_got, *sems[o_all])
        trade = remote(o_got, o_more, pair.at[0], pair.at[1], "ctx", me + 1 - 2 * core)
        trade.start()
        for c in range(chips):
            cot_line.beside(c)
        cot_line.sent()
        q_need.sent()
        kv_need.sent()
        g_all.finish(wg_mine, wg_out, *sems[g_all])
        u_all.finish(wu_mine, wu_out, *sems[u_all])
        d_all.finish(d_got, wd_out, *sems[d_all])
        trade.wait()
        for r in range(dp):
            pieces = []
            for c in range(n):
                mine, more = o_got[r, c // 2], o_more[r, c // 2]
                pieces.append(jnp.where(core == c % 2, mine, more))
            value = jnp.concatenate(pieces, axis=1)
            for j in range(total // rows):
                low, high = max(r * in_rows, j * rows), min((r + 1) * in_rows, (j + 1) * rows)
                if low < high:
                    wo_all[j, low - j * rows : high - j * rows] = value[
                        low - r * in_rows : high - r * in_rows
                    ]
        for j in range(total // rows):
            used = min(max(width - j * rows, 0), rows)
            if used < rows:
                wo_all[j, used:] = jnp.zeros((rows - used, width), bf16)
        offset = pl.multiple_of(lax.rem(me * wide, rows), wide)
        wo_out[...] = wo_all[lax.div(me * wide, rows), pl.ds(offset, wide)]

    whole = (n, rows, width)
    outs = [
        shape((n, rows, wide), bf16),
        shape((length, wide), f32),
        shape((held, length, 2 * HEAD_DIM), bf16),
        shape((held, length, 2 * HEAD_DIM), bf16),
        shape((held, length, HEAD_DIM), bf16),
        shape(whole, bf16),
        shape(whole, bf16),
        shape((wide, width), bf16),
        shape((width, 3 * wide), bf16),
        shape((2, width), f32),
        shape((dp, in_rows, f_w), bf16),
        shape((dp, in_rows, f_w), bf16),
        shape((dp, each, o_w, f_w), bf16),
        shape((rows, width), bf16),
        shape((total // rows, rows, width), bf16),
    ]
    return pl.pallas_call(
        kernel,
        out_shape=outs,
        in_specs=[pl.BlockSpec(memory_space=pltpu.VMEM)] * 13,
        out_specs=[pl.BlockSpec(memory_space=pltpu.VMEM)] * len(outs),
        scratch_shapes=[
            pltpu.VMEM(whole, bf16),
            pltpu.VMEM((n, 2, o_w), bf16),
            pltpu.VMEM((dp, in_rows, q_w), bf16),
            pltpu.VMEM((dp,) + kv_rows.shape, bf16),
            pltpu.VMEM((dp, chips, in_rows, o_w), bf16),
            pltpu.VMEM((q_need.slots, dp, in_rows, q_w), bf16),
            pltpu.VMEM((kv_need.slots, dp) + kv_rows.shape, bf16),
            pltpu.VMEM((width, 8 * held * HEAD_DIM), bf16),
            pltpu.VMEM((in_rows, f_w), bf16),
            pltpu.VMEM((in_rows, f_w), bf16),
            pltpu.VMEM((each, o_w, f_w), bf16),
            pltpu.VMEM((each, o_w, f_w), bf16),
            pltpu.VMEM((n, in_rows, o_w), bf16),
            pltpu.VMEM(kv_rows.shape, bf16),
            pltpu.VMEM((2, o_w), bf16),
            pltpu.VMEM((chips, in_rows, o_w), bf16),
            pltpu.VMEM((dp, chips, in_rows, o_w), bf16),
            pltpu.SemaphoreType.DMA((2,)),
        ]
        + [item for task in tasks for item in task.scratch],
        compiler_params=pltpu.CompilerParams(
            collective_id=ident, has_side_effects=True, vmem_limit_bytes=62 * 1024 * 1024
        ),
        name=f"front_{ident}",
    )(x_t, cot_t, w_q, wk_t, wv_t, w_o, gain_a, gain_b, wg_t, wu_t, wd_t, *tables)


class Give:
    axis = "ctx"

    def __init__(self, need):
        self.need = need
        self.scratch = [
            pltpu.SemaphoreType.DMA((need.slots,)),
            pltpu.SemaphoreType.DMA((need.n,)),
        ]

    def hold(self, mine, got, sems):
        self.mine, self.got = mine, got
        self.send, self.recv = sems
        self.me = lax.axis_index(self.axis)
        self.first, self.final = self.need.low(self.me), self.need.high(self.me)

    def copy(self, t, owner):
        return remote(
            self.mine.at[t],
            self.got.at[self.me],
            self.send.at[t],
            self.recv.at[self.me],
            self.axis,
            owner,
        )

    def start(self, term):
        for t in range(self.need.slots):
            owner = jnp.minimum(self.first + t, self.need.n - 1)
            used = self.first + t <= self.final

            @pl.when(used)
            def _():
                self.mine[t] = term(owner)

            pl.when(jnp.logical_and(used, owner != self.me))(self.copy(t, owner).start)

            @pl.when(jnp.logical_and(used, owner == self.me))
            def _():
                self.got[self.me] = self.mine[t]

    def add(self, total):
        beside = self.me + 1 - 2 * lax.rem(self.me, 2)
        total[...] = jnp.zeros_like(total)
        for d in range(self.need.n):
            used = jnp.logical_and(self.me >= self.need.low(d), self.me <= self.need.high(d))
            copy = remote(
                self.mine.at[0], self.got.at[d], self.send.at[0], self.recv.at[d], self.axis, beside
            )
            pl.when(jnp.logical_and(used, self.me != d))(copy.wait_recv)

            @pl.when(used)
            def _():
                total[...] += self.got[d].astype(f32)

    def sent(self):
        for t in range(self.need.slots):
            owner = jnp.minimum(self.first + t, self.need.n - 1)
            used = jnp.logical_and(self.first + t <= self.final, owner != self.me)
            pl.when(used)(self.copy(t, owner).wait_send)


def back(
    ident,
    d_mids,
    att,
    wo,
    lse,
    q_two,
    k_two,
    val,
    n1,
    wqkv,
    turn,
    d_mid,
    x_own,
    gains,
    mid,
    g_three,
    g_two,
    out_part,
    q_w,
    k_w,
):
    sizes = {axis: lax.axis_size(axis) for axis in ("dp", "ctx")}
    dp, n = sizes["dp"], sizes["ctx"]
    chips, each = n // 2, n // dp
    _, rows, width = d_mids.shape
    held, length, _ = q_two.shape
    wide, chunk = held * HEAD_DIM, 2 * rows
    in_rows, f_w = g_three.shape[1], g_three.shape[2] // 3
    o_w = width // n
    shape = jax.ShapeDtypeStruct
    q_need, kv_need = needs(n, held, width, q_w, k_w)
    q_give, kv_give = Give(q_need), Give(kv_need)
    sums = [Sum(n, rows), Sum(n, rows)]
    o_swap = Swap("ctx", shape((n, wide, o_w), bf16))
    o_down = Swap("dp", shape((dp, in_rows, o_w), bf16))
    w_swap = Swap("dp", shape((dp, 3 * wide, in_rows), bf16))
    d_turn = Turn(shape((each, o_w, f_w), bf16))
    gain_swap = Swap("ctx", shape((n, 2, o_w), f32))
    gain_all = Gather(shape((2, o_w), f32))
    planned = [o_swap, o_down, w_swap, d_turn, gain_swap, gain_all]
    for task in planned:
        task.plan(sizes)
    tasks = [q_give, kv_give] + sums + planned

    def kernel(*refs):
        dm_in, at_ref, wo_ref, lse_ref, q2, k2, v_ref, n_in, w_ref, turn_ref = refs[:10]
        mid_ref, x_ref, gain_ref, sum_ref, three, two_gain, out_in = refs[10:17]
        out_t, in_t, gq, gk, gv, go, gg, gu, gd, g_one, g_last = refs[17:28]
        part, near, got, near_o, got_o, datt, dk2, dv, dqkv, total = refs[28:38]
        o_src, o_got, o_cut, o_sum, w_src, w_got, d_src, d_got = refs[38:46]
        gain_src, gain_got, gain_mine, gain_sum = refs[46:50]
        q_mine, q_got, kv_mine, kv_got, kv_sum, load, dm = refs[50:57]
        sems, at = {}, 57
        for task in tasks:
            sems[task] = tuple(refs[at : at + len(task.scratch)])
            at += len(task.scratch)
        bring = pltpu.make_async_copy(out_in, part, load.at[0])
        bring.start()
        bring_d = pltpu.make_async_copy(dm_in, dm, load.at[1])
        bring_d.start()
        bring_n = pltpu.make_async_copy(n_in, dm, load.at[2])
        spread(("dp", "ctx"), sizes, True)
        me = lax.axis_index("ctx")
        sums[0].hold(part, near_o, got_o, sems[sums[0]])
        sums[1].hold(part, near, got, sems[sums[1]])
        q_give.hold(q_mine, q_got, sems[q_give])
        kv_give.hold(kv_mine, kv_got, sems[kv_give])
        bring.wait()
        for k in range(chips):
            sums[0].ready(sums[0].order(k))

        def of_dp(low, high):
            value = three[0, :, low:high].astype(f32)
            for r in range(1, dp):
                value = value + three[r, :, low:high].astype(f32)
            return value

        down = of_dp(2 * f_w, 3 * f_w).astype(bf16)
        for i in range(each):
            d_src[i] = down[i * o_w : (i + 1) * o_w]
        d_turn.start(d_src, d_got, *sems[d_turn])
        bring_d.wait()
        for i in range(chips):
            tokens = dm[2 * i : 2 * i + 2].reshape(chunk, width)
            datt[i * chunk : (i + 1) * chunk] = nt(tokens, wo_ref[...]).astype(bf16)
        value = tn(at_ref[...].reshape(length, wide), dm[...].reshape(length, width)).astype(bf16)
        bring_n.start()
        for c in range(n):
            o_src[c] = value[:, c * o_w : (c + 1) * o_w]
        o_swap.start(o_src, o_got, *sems[o_swap])

        def put(ref, h, low, high, value, first):
            if first:
                ref[h, low:high] = value
            else:
                ref[h, low:high] += value

        def folded(two, low, high):
            both = two * turn_ref[low:high]
            return both[:, :HEAD_DIM] + both[:, HEAD_DIM:]

        def attend(i):
            first, last = i * chunk, (i + 1) * chunk
            new = i == chips - 1
            for h in range(held):
                lanes = slice(h * HEAD_DIM, (h + 1) * HEAD_DIM)
                q, grad = q2[h, first:last, :HEAD_DIM], datt[first:last, lanes]
                own = at_ref[2 * i : 2 * i + 2, :, lanes].reshape(chunk, HEAD_DIM)
                delta = jnp.sum(grad.astype(f32) * own.astype(f32), axis=-1, keepdims=True)
                log = lse_ref[first:last, h * HEAD_DIM : h * HEAD_DIM + 1]
                dq = None
                for low, high in ((first, last), (0, first)):
                    if low == high:
                        continue
                    scores = nt(q, k2[h, low:high, :HEAD_DIM])
                    if low == first:
                        row = lax.broadcasted_iota(jnp.int32, scores.shape, 0)
                        col = lax.broadcasted_iota(jnp.int32, scores.shape, 1)
                        scores = jnp.where(row >= col, scores, -1e30)
                    probs = jnp.exp(scores - log)
                    d_probs = nt(grad, v_ref[h, low:high])
                    d_scores = (probs * (d_probs - delta)).astype(bf16)
                    term = nn(d_scores, k2[h, low:high])
                    dq = term if dq is None else dq + term
                    put(dk2, h, low, high, tn(d_scores, q2[h, first:last]), new)
                    put(dv, h, low, high, tn(probs.astype(bf16), grad), new)
                dq = folded(dq, first, last) * HEAD_DIM ** (-0.5)
                dqkv[first:last, lanes] = dq.astype(bf16)

        for t in range(chips):
            attend(chips - 1 - t)
            if t < chips - 1:
                sums[0].step(t)
        for i in range(chips):
            first, last = i * chunk, (i + 1) * chunk
            for h in range(held):
                base = wide + h * HEAD_DIM
                dk = folded(dk2[h, first:last], first, last)
                dqkv[first:last, base : base + HEAD_DIM] = dk.astype(bf16)
                base = base + wide
                dqkv[first:last, base : base + HEAD_DIM] = dv[h, first:last].astype(bf16)
        sums[0].last(total)
        out_t[...] = (sum_ref[...] + total[...]).T.astype(bf16)
        sums[0].sent()

        def project(k, carry):
            d = sums[1].order(k)
            low = pl.multiple_of(d * chunk, chunk)
            value = nt(dqkv[pl.ds(low, chunk)], w_ref[...]).astype(bf16)
            part[pl.ds(2 * d, 2)] = value.reshape(2, rows, width)
            sums[1].ready(d)
            return carry

        lax.fori_loop(0, chips, project, 0)
        bring_n.wait()
        value = tn(dqkv[...], dm[...].reshape(length, width)).astype(bf16)
        for t in range(min(1, chips - 1)):
            sums[1].step(t)
        for r in range(dp):
            w_src[r] = value[:, r * in_rows : (r + 1) * in_rows]
        w_swap.start(w_src, w_got, *sems[w_swap])
        o_swap.finish(o_src, o_got, *sems[o_swap])
        for j in range(n):
            for r in range(dp):
                low, high = max(r * in_rows, j * wide), min((r + 1) * in_rows, (j + 1) * wide)
                if low < high:
                    o_cut[r, low - r * in_rows : high - r * in_rows] = o_got[
                        j, low - j * wide : high - j * wide
                    ]
        o_down.start(o_cut, o_sum, *sems[o_down])
        gg[...] = of_dp(0, f_w).T
        gu[...] = of_dp(f_w, 2 * f_w).T
        for t in range(1, chips - 1):
            sums[1].step(t)
        w_swap.finish(w_src, w_got, *sems[w_swap])
        value = w_got[0].astype(f32)
        for r in range(1, dp):
            value = value + w_got[r].astype(f32)
        value = value.astype(bf16)
        heads = [me * held + h for h in range(held)]

        def columns(of):
            lane = lax.broadcasted_iota(jnp.int32, (1, wide), 1)
            base = jnp.zeros((1, wide), jnp.int32)
            for i, h in enumerate(of):
                inside = jnp.logical_and(lane >= i * HEAD_DIM, lane < (i + 1) * HEAD_DIM)
                base = jnp.where(inside, h * HEAD_DIM, base)
            return base + jnp.bitwise_and(lane, HEAD_DIM - 1)

        q_nat = value[:wide].T
        kv_part = value[wide:]
        q_cols = columns(heads)
        kv_cols = columns([least(over(h, GROUP), KV_HEADS - 1) for h in heads])
        ones = jnp.ones((1, wide), f32)

        def q_term(owner):
            return nt(q_nat, pick(q_w, owner * q_w, q_cols, ones).astype(bf16)).astype(bf16)

        def kv_term(owner):
            one = pick(k_w, owner * k_w, kv_cols, ones)
            none = jnp.zeros_like(one)
            top = jnp.concatenate([one, none], axis=1)
            low = jnp.concatenate([none, one], axis=1)
            return nn(jnp.concatenate([top, low], axis=0).astype(bf16), kv_part).astype(bf16)

        kv_give.start(kv_term)
        q_give.start(q_term)
        sums[1].last(total)
        hidden = x_ref[...].astype(f32)
        inverse = inverse_rms(hidden)
        d_norm, gain_part = norm_backward(hidden, inverse, gain_ref[0:1], total[...])
        both = jnp.concatenate([gain_part.reshape(1, width), two_gain[...]], axis=0)
        for c in range(n):
            gain_src[c] = both[:, c * o_w : (c + 1) * o_w]
        gain_swap.start(gain_src, gain_got, *sems[gain_swap])
        in_t[...] = (mid_ref[...] + d_norm).T
        d_turn.finish(d_src, d_got, *sems[d_turn])
        for i in range(each):
            gd[:, i * f_w : (i + 1) * f_w] = d_got[i].astype(f32)
        gain_swap.finish(gain_src, gain_got, *sems[gain_swap])
        gain_mine[...] = jnp.sum(gain_got[...], axis=0)
        gain_all.start(gain_mine, gain_sum, *sems[gain_all])
        o_down.finish(o_cut, o_sum, *sems[o_down])
        value = o_sum[0].astype(f32)
        for r in range(1, dp):
            value = value + o_sum[r].astype(f32)
        go[...] = value
        kv_give.add(kv_sum)
        gk[...] = kv_sum[:k_w]
        gv[...] = kv_sum[k_w:]
        q_give.add(gq)
        gain_all.finish(gain_mine, gain_sum, *sems[gain_all])
        value = jnp.sum(gain_sum[...], axis=0)
        g_one[...] = value[0:1]
        g_last[...] = value[1:2]
        q_give.sent()
        kv_give.sent()
        sums[1].sent()

    whole = (n, rows, width)
    vmem = pl.BlockSpec(memory_space=pltpu.VMEM)
    anywhere = pl.BlockSpec(memory_space=pl.ANY)
    outs = [
        shape((width, rows), bf16),
        shape((width, rows), f32),
        shape((in_rows, q_w), f32),
        shape((k_w, in_rows), f32),
        shape((k_w, in_rows), f32),
        shape((in_rows, o_w), f32),
        shape((f_w, in_rows), f32),
        shape((f_w, in_rows), f32),
        shape((o_w, each * f_w), f32),
        shape((1, o_w), f32),
        shape((1, o_w), f32),
    ]
    return pl.pallas_call(
        kernel,
        out_shape=outs,
        in_specs=[anywhere] + [vmem] * 6 + [anywhere] + [vmem] * 8 + [anywhere],
        out_specs=[vmem] * len(outs),
        scratch_shapes=[
            pltpu.VMEM(whole, bf16),
            pltpu.VMEM((chips, rows, width), bf16),
            pltpu.VMEM((chips + 1, rows, width), bf16),
            pltpu.VMEM((chips, rows, width), bf16),
            pltpu.VMEM((chips + 1, rows, width), bf16),
            pltpu.VMEM((length, wide), bf16),
            pltpu.VMEM((held, length, 2 * HEAD_DIM), f32),
            pltpu.VMEM((held, length, HEAD_DIM), f32),
            pltpu.VMEM((length, 3 * wide), bf16),
            pltpu.VMEM((rows, width), f32),
            pltpu.VMEM((n, wide, o_w), bf16),
            pltpu.VMEM((n, wide, o_w), bf16),
            pltpu.VMEM((dp, in_rows, o_w), bf16),
            pltpu.VMEM((dp, in_rows, o_w), bf16),
            pltpu.VMEM((dp, 3 * wide, in_rows), bf16),
            pltpu.VMEM((dp, 3 * wide, in_rows), bf16),
            pltpu.VMEM((each, o_w, f_w), bf16),
            pltpu.VMEM((each, o_w, f_w), bf16),
            pltpu.VMEM((n, 2, o_w), f32),
            pltpu.VMEM((n, 2, o_w), f32),
            pltpu.VMEM((2, o_w), f32),
            pltpu.VMEM((dp, 2, o_w), f32),
            pltpu.VMEM((q_need.slots, in_rows, q_w), bf16),
            pltpu.VMEM((n, in_rows, q_w), bf16),
            pltpu.VMEM((kv_need.slots, 2 * k_w, in_rows), bf16),
            pltpu.VMEM((n, 2 * k_w, in_rows), bf16),
            pltpu.VMEM((2 * k_w, in_rows), f32),
            pltpu.SemaphoreType.DMA((3,)),
            pltpu.VMEM(whole, bf16),
        ]
        + [item for task in tasks for item in task.scratch],
        compiler_params=pltpu.CompilerParams(
            collective_id=ident, has_side_effects=True, vmem_limit_bytes=62 * 1024 * 1024
        ),
        name=f"back_{ident}",
    )(
        d_mids,
        att,
        wo,
        lse,
        q_two,
        k_two,
        val,
        n1,
        wqkv,
        turn,
        d_mid,
        x_own,
        gains,
        mid,
        g_three,
        g_two,
        out_part,
    )


def finish(arrays):
    count = len(arrays)

    def kernel(*refs):
        for i in range(count):
            refs[count + i][...] = refs[i][...]

    return pl.pallas_call(
        kernel,
        out_shape=[jax.ShapeDtypeStruct(array.shape, array.dtype) for array in arrays],
        in_specs=[pl.BlockSpec(memory_space=pltpu.VMEM)] * count,
        out_specs=[pl.BlockSpec(memory_space=pltpu.VMEM)] * count,
        name="finish",
    )(*arrays)


def shards(
    inputs, cotangent, w_query, w_key, w_value, w_output, w_gate, w_up, w_down, gain_attn, gain_ffn
):
    dp, ctx = lax.axis_size("dp"), lax.axis_size("ctx")
    me = lax.axis_index("ctx")
    rows, width = inputs.shape
    length = rows * ctx
    q_w, k_w, o_w, f_w = w_query.shape[1], w_key.shape[1], w_output.shape[1], w_gate.shape[1]
    in_rows = w_query.shape[0]
    held = -(-HEADS // ctx)
    wide = held * HEAD_DIM
    total = ctx * wide
    near = all(wide * j >= q_w * j and wide * (j + 1) <= q_w * (j + 2) for j in range(ctx))

    each = ctx // dp
    cosine, sine = rope_tables(length)
    tables = (
        jnp.concatenate([cosine, sine], axis=1),
        jnp.concatenate([sine, -cosine], axis=1),
    )
    attended, lse, q_two, k_two, values, n1, cots, wo, wqkv, gain_rows, w_g, w_u, w_d, x_own, wo_all = front(
        0,
        inputs.T,
        cotangent.T,
        w_query,
        w_key.T,
        w_value.T,
        w_output,
        gain_attn.reshape(1, o_w),
        gain_ffn.reshape(1, o_w),
        w_gate.T,
        w_up.T,
        w_down.T,
        held,
        tables,
    )
    d_mid_full, d_middle, middle, out_part, g_three, g_gain_two = mid_layer(
        2,
        attended,
        wo_all,
        x_own,
        cots,
        gain_rows,
        w_g.reshape(width, f_w),
        w_u.reshape(width, f_w),
        w_d.reshape(width, f_w),
    )
    last = back(
        3,
        d_mid_full,
        attended,
        wo,
        lse,
        q_two,
        k_two,
        values,
        n1,
        wqkv,
        tables[0],
        d_middle,
        x_own,
        gain_rows,
        middle,
        g_three,
        g_gain_two,
        out_part,
        q_w,
        k_w,
    )
    out, grad, g_q, g_k, g_v, g_o, g_g, g_u, g_d, g_one, g_two = finish(last)
    g_one, g_two = g_one.reshape(o_w), g_two.reshape(o_w)
    return out.T, grad.T, g_q, g_k.T, g_v.T, g_o, g_g.T, g_u.T, g_d.T, g_one, g_two


def solution(mesh):
    blocks = P(("dp", "ctx"), None)
    matrix = P("dp", "ctx")
    in_specs = (blocks,) * 2 + (matrix,) * 7 + (P("ctx"),) * 2
    return jax.shard_map(shards, mesh=mesh, in_specs=in_specs, out_specs=in_specs, check_vma=False)
```

```python
import functools

import jax
import jax.numpy as jnp
import numpy as np
from jax import lax
from jax.experimental import pallas as pl
from jax.experimental.pallas import tpu as pltpu
from jax.sharding import PartitionSpec as P

HEADS = 15
KV_HEADS = 5
HEAD_DIM = 64
GROUP = HEADS // KV_HEADS

epsilon = 1e-05
rope_base = 10000.0
bf16 = jnp.bfloat16
f32 = jnp.float32


def remote(src, dst, send, recv, axis, peer):
    return pltpu.make_async_remote_copy(
        src_ref=src,
        dst_ref=dst,
        send_sem=send,
        recv_sem=recv,
        device_id={axis: peer},
        device_id_type=pl.DeviceIdType.MESH,
    )


class Gather:
    axis = "dp"

    def __init__(self, array):
        self.array = array

    def plan(self, sizes):
        self.n = sizes[self.axis]
        self.out = jax.ShapeDtypeStruct((self.n,) + self.array.shape, self.array.dtype)
        self.scratch = [pltpu.SemaphoreType.DMA((self.n,))] * 2 + [pltpu.SemaphoreType.DMA(())]

    def start(self, src, dst, send, recv, own):
        me = lax.axis_index(self.axis)
        self.local = pltpu.make_async_copy(src, dst.at[me], own)
        self.local.start()
        self.copies = []
        for k in range(1, self.n):
            peer = lax.rem(me + k, self.n)
            copy = remote(src, dst.at[me], send.at[k], recv.at[k], self.axis, peer)
            copy.start()
            self.copies.append(copy)

    def middle(self, *refs):
        pass

    def finish(self, src, dst, send, recv, own):
        me = lax.axis_index(self.axis)
        for k in range(1, self.n):
            slot = lax.rem(me + self.n - k, self.n)
            remote(src, dst.at[slot], send.at[k], recv.at[k], self.axis, slot).wait_recv()
        for copy in self.copies:
            copy.wait_send()
        self.local.wait()


class Relay:
    axis = "ctx"

    def __init__(self, array):
        self.array = array

    def plan(self, sizes):
        self.n = sizes[self.axis]
        chips = self.n // 2
        self.out = jax.ShapeDtypeStruct((self.n,) + self.array.shape, self.array.dtype)
        self.scratch = [pltpu.SemaphoreType.DMA((chips,))] * 6 + [pltpu.SemaphoreType.DMA(())]

    def at(self):
        me = lax.axis_index(self.axis)
        chip, core = me // 2, me % 2
        return me, chip, core, me + 1 - 2 * core, self.n // 2

    def start(self, src, dst, rs, rr, ls, lr, ps, pr, own):
        me, chip, core, partner, chips = self.at()

        @pl.when(chip < chips - 1)
        def _():
            remote(src, dst.at[me], rs.at[0], rr.at[0], self.axis, me + 2).start()

        @pl.when(chip > 0)
        def _():
            remote(src, dst.at[me], ls.at[0], lr.at[0], self.axis, me - 2).start()

        remote(src, dst.at[me], ps.at[chip], pr.at[chip], self.axis, partner).start()
        pltpu.make_async_copy(src, dst.at[me], own).start()

    def step(self, k, src, dst, rs, rr, ls, lr, ps, pr, own):
        me, chip, core, partner, chips = self.at()

        def arrived(slot_chip, way, send, recv):
            slot = slot_chip * 2 + core
            back = me - 2 * way
            remote(dst.at[slot], dst.at[slot], send.at[k], recv.at[k], self.axis, back).wait_recv()

            @pl.when(jnp.logical_and(chip + way >= 0, chip + way < chips))
            def _():
                remote(
                    dst.at[slot],
                    dst.at[slot],
                    send.at[k + 1],
                    recv.at[k + 1],
                    self.axis,
                    me + 2 * way,
                ).start()

            remote(
                dst.at[slot], dst.at[slot], ps.at[slot_chip], pr.at[slot_chip], self.axis, partner
            ).start()

        @pl.when(chip - 1 - k >= 0)
        def _():
            arrived(chip - 1 - k, 1, rs, rr)

        @pl.when(chip + 1 + k < chips)
        def _():
            arrived(chip + 1 + k, -1, ls, lr)

    def finish(self, src, dst, rs, rr, ls, lr, ps, pr, own):
        me, chip, core, partner, chips = self.at()
        for c in range(chips):
            slot = 2 * c + 1 - core
            remote(src, dst.at[slot], ps.at[c], pr.at[c], self.axis, partner).wait_recv()
        for c in range(chips):
            remote(src, dst.at[2 * c + core], ps.at[c], pr.at[c], self.axis, partner).wait_send()
        for k in range(chips - 1):

            @pl.when(jnp.logical_and(chip < chips - 1, k <= chip))
            def _():
                remote(src, dst.at[me], rs.at[k], rr.at[k], self.axis, me + 2).wait_send()

            @pl.when(jnp.logical_and(chip > 0, k <= chips - 1 - chip))
            def _():
                remote(src, dst.at[me], ls.at[k], lr.at[k], self.axis, me - 2).wait_send()

        pltpu.make_async_copy(src, dst.at[me], own).wait()


class Turn:
    axis = "all"

    def __init__(self, array):
        self.array = array

    def plan(self, sizes):
        self.dp, self.n = sizes["dp"], sizes["ctx"]
        self.m = self.n // self.dp
        self.out = jax.ShapeDtypeStruct(self.array.shape, self.array.dtype)
        self.scratch = [pltpu.SemaphoreType.DMA((self.m,))] * 2

    def each(self, src, dst, send, recv):
        row, col = lax.axis_index("dp"), lax.axis_index("ctx")
        put = col % self.m
        for i in range(self.m):
            to_row, to_col = col // self.m, row * self.m + i
            here = jnp.logical_and(to_row == row, to_col == col)
            far = pltpu.make_async_remote_copy(
                src_ref=src.at[i],
                dst_ref=dst.at[put],
                send_sem=send.at[i],
                recv_sem=recv.at[put],
                device_id={"dp": to_row, "ctx": to_col},
                device_id_type=pl.DeviceIdType.MESH,
            )
            local = pltpu.make_async_copy(src.at[i], dst.at[put], recv.at[put])
            yield i, here, far, local

    def start(self, *refs):
        for i, here, far, local in self.each(*refs):
            pl.when(here)(local.start)
            pl.when(jnp.logical_not(here))(far.start)

    def finish(self, src, dst, send, recv):
        row, col = lax.axis_index("dp"), lax.axis_index("ctx")
        for i, here, far, local in self.each(src, dst, send, recv):
            pl.when(jnp.logical_not(here))(far.wait_send)
        for i in range(self.m):
            own = jnp.logical_and(col // self.m == row, row * self.m + i == col)
            local = pltpu.make_async_copy(src.at[i], dst.at[i], recv.at[i])
            far = pltpu.make_async_remote_copy(
                src_ref=src.at[i],
                dst_ref=dst.at[i],
                send_sem=send.at[i],
                recv_sem=recv.at[i],
                device_id={"dp": col // self.m, "ctx": row * self.m + i},
                device_id_type=pl.DeviceIdType.MESH,
            )
            pl.when(own)(local.wait)
            pl.when(jnp.logical_not(own))(far.wait_recv)

    def middle(self, *refs):
        pass


class Swap:
    def __init__(self, axis, array):
        self.axis, self.array = axis, array

    def plan(self, sizes):
        self.n = sizes[self.axis]
        self.out = jax.ShapeDtypeStruct(self.array.shape, self.array.dtype)
        self.scratch = [pltpu.SemaphoreType.DMA((self.n,))] * 2 + [pltpu.SemaphoreType.DMA(())]

    def start(self, src, dst, send, recv, own):
        me = lax.axis_index(self.axis)
        self.local = pltpu.make_async_copy(src.at[me], dst.at[me], own)
        self.local.start()
        self.copies = []
        for k in range(1, self.n):
            peer = lax.rem(me + k, self.n)
            copy = remote(src.at[peer], dst.at[me], send.at[k], recv.at[k], self.axis, peer)
            copy.start()
            self.copies.append(copy)

    def middle(self, *refs):
        pass

    def finish(self, src, dst, send, recv, own):
        me = lax.axis_index(self.axis)
        for k in range(1, self.n):
            slot = lax.rem(me + self.n - k, self.n)
            remote(
                src.at[slot], dst.at[slot], send.at[k], recv.at[k], self.axis, slot
            ).wait_recv()
        for copy in self.copies:
            copy.wait_send()
        self.local.wait()


class Shift:
    def __init__(self, axis, array, by):
        self.axis, self.array, self.by = axis, array, by

    def plan(self, sizes):
        self.n = sizes[self.axis]
        self.out = jax.ShapeDtypeStruct(self.array.shape, self.array.dtype)
        self.scratch = [pltpu.SemaphoreType.DMA(())] * 2

    def start(self, src, dst, send, recv):
        me = lax.axis_index(self.axis)
        peer = lax.rem(me + self.n + self.by, self.n)
        self.copy = remote(src, dst, send, recv, self.axis, peer)
        self.copy.start()

    def middle(self, *refs):
        pass

    def finish(self, *refs):
        self.copy.wait_recv()
        self.copy.wait_send()


class Reduce:
    axis = "ctx"

    def __init__(self, array):
        self.array = array

    def plan(self, sizes):
        self.n = sizes[self.axis]
        block = self.array.shape[1:]
        chips = self.n // 2
        self.out = jax.ShapeDtypeStruct(block, f32)
        slots = pltpu.VMEM((chips,) + block, self.array.dtype)
        self.scratch = [pltpu.SemaphoreType.DMA((chips,))] * 4 + [slots] * 3

    def start(self, src, dst, psend, precv, send, recv, near, term, far):
        me = lax.axis_index(self.axis)
        chips = self.n // 2
        chip, core = me // 2, me % 2
        partner = me + 1 - 2 * core
        self.copies = []
        for k in list(range(1, chips)) + [0]:
            slot = lax.rem(chip + k, chips) * 2 + 1 - core
            copy = remote(
                src.at[slot], near.at[k], psend.at[k], precv.at[k], self.axis, partner
            )
            copy.start()
            self.copies.append(copy)

    def middle(self, src, dst, psend, precv, send, recv, near, term, far):
        me = lax.axis_index(self.axis)
        chips = self.n // 2
        chip, core = me // 2, me % 2
        partner = me + 1 - 2 * core
        for k in range(1, chips):
            remote(
                src.at[me], near.at[k], psend.at[k], precv.at[k], self.axis, partner
            ).wait_recv()
            peer = lax.rem(chip + k, chips) * 2 + core
            both = src[peer].astype(f32) + near[k].astype(f32)
            term[k] = both.astype(term.dtype)
            copy = remote(term.at[k], far.at[k], send.at[k], recv.at[k], self.axis, peer)
            copy.start()
            self.copies.append(copy)

    def finish(self, src, dst, psend, precv, send, recv, near, term, far):
        me = lax.axis_index(self.axis)
        chips = self.n // 2
        core = me % 2
        partner = me + 1 - 2 * core
        remote(src.at[me], near.at[0], psend.at[0], precv.at[0], self.axis, partner).wait_recv()
        dst[...] = src[me].astype(f32) + near[0].astype(f32)
        for k in range(1, chips):
            remote(
                src.at[me], far.at[k], send.at[k], recv.at[k], self.axis, partner
            ).wait_recv()
            dst[...] += far[k].astype(f32)
        for copy in self.copies:
            copy.wait_send()


def exchange(ident, *tasks):
    sizes = {axis: lax.axis_size(axis) for axis in ("dp", "ctx")}
    for task in tasks:
        task.plan(sizes)
    axes = [axis for axis in ("dp", "ctx") if any(task.axis == axis for task in tasks)]
    everyone = any(task.axis == "all" for task in tasks)
    axes = [] if everyone else axes
    count = len(tasks)

    def kernel(*refs):
        barrier = pltpu.get_barrier_semaphore()
        greeted = 0
        if everyone:
            row, col = lax.axis_index("dp"), lax.axis_index("ctx")
            for i in range(1, sizes["dp"] * sizes["ctx"]):
                other = lax.rem(row * sizes["ctx"] + col + i, sizes["dp"] * sizes["ctx"])
                pl.semaphore_signal(
                    barrier,
                    inc=1,
                    device_id={"dp": other // sizes["ctx"], "ctx": other % sizes["ctx"]},
                    device_id_type=pl.DeviceIdType.MESH,
                )
                greeted += 1
        for axis in axes:
            me, n = lax.axis_index(axis), sizes[axis]
            for k in range(1, n):
                pl.semaphore_signal(
                    barrier,
                    inc=1,
                    device_id={axis: lax.rem(me + k, n)},
                    device_id_type=pl.DeviceIdType.MESH,
                )
            greeted += n - 1
        pl.semaphore_wait(barrier, greeted)
        held, at = [], 2 * count
        for i, task in enumerate(tasks):
            held.append((refs[i], refs[count + i]) + tuple(refs[at : at + len(task.scratch)]))
            at += len(task.scratch)
        for task, own in zip(tasks, held):
            task.start(*own)
        for k in range(sizes["ctx"] // 2 - 1):
            for task, own in zip(tasks, held):
                if isinstance(task, Relay):
                    task.step(k, *own)
                elif k == 0:
                    task.middle(*own)
        for task, own in zip(tasks, held):
            task.finish(*own)

    return pl.pallas_call(
        kernel,
        out_shape=[task.out for task in tasks],
        in_specs=[pl.BlockSpec(memory_space=pltpu.VMEM)] * count,
        out_specs=[pl.BlockSpec(memory_space=pltpu.VMEM)] * count,
        scratch_shapes=[shape for task in tasks for shape in task.scratch],
        compiler_params=pltpu.CompilerParams(
            collective_id=ident, has_side_effects=True, vmem_limit_bytes=60 * 1024 * 1024
        ),
        name=f"exchange_{ident}",
    )(*[task.array for task in tasks])


def spread(axes, sizes, everyone):
    barrier = pltpu.get_barrier_semaphore()
    greeted = 0
    if everyone:
        row, col = lax.axis_index("dp"), lax.axis_index("ctx")
        total = sizes["dp"] * sizes["ctx"]

        def greet(i, carry):
            other = lax.rem(row * sizes["ctx"] + col + i, total)
            pl.semaphore_signal(
                barrier,
                inc=1,
                device_id={"dp": other // sizes["ctx"], "ctx": other % sizes["ctx"]},
                device_id_type=pl.DeviceIdType.MESH,
            )
            return carry

        lax.fori_loop(1, total, greet, 0)
        greeted = total - 1
    else:
        for axis in axes:
            me, n = lax.axis_index(axis), sizes[axis]
            for k in range(1, n):
                pl.semaphore_signal(
                    barrier,
                    inc=1,
                    device_id={axis: lax.rem(me + k, n)},
                    device_id_type=pl.DeviceIdType.MESH,
                )
            greeted += n - 1
    pl.semaphore_wait(barrier, greeted)


def mm(a, b, dims):
    return lax.dot_general(a, b, ((dims[:1], dims[1:]), ((), ())), preferred_element_type=f32)


def nn(a, b):
    return mm(a, b, (1, 0))


def nt(a, b):
    return mm(a, b, (1, 1))


def tn(a, b):
    return mm(a, b, (0, 0))


def turned(rows):
    width = rows.shape[-1]
    parts = rows.reshape(-1, 2, HEAD_DIM // 2, width)
    return jnp.concatenate([-parts[:, 1:], parts[:, :1]], axis=1).reshape(rows.shape)


def rope_tables(row_count):
    half = HEAD_DIM // 2
    frequency = np.float32(rope_base) ** (-np.arange(half).astype(np.float32) * np.float32(2.0 / HEAD_DIM))
    angles = np.arange(row_count).astype(np.float32)[:, None] * frequency[None, :].astype(np.float32)
    return [jnp.asarray(np.tile(f(angles), (1, 2)), f32) for f in (np.cos, np.sin)]


def norm_backward(hidden, inverse, gain_vec, upstream):
    scaled = upstream * gain_vec
    cubed = inverse * inverse * inverse
    d_hidden = (
        inverse * scaled
        - hidden
        * cubed
        * jnp.sum(scaled * hidden, axis=-1, keepdims=True)
        / hidden.shape[-1]
    )
    return d_hidden, jnp.sum(upstream * hidden * inverse, axis=0)


def inverse_rms(hidden):
    return lax.rsqrt(jnp.mean(hidden * hidden, axis=-1, keepdims=True) + epsilon)


class Line:
    axis = "ctx"

    def __init__(self, n, rows):
        self.n, self.chips = n, n // 2
        self.cuts = 2 if rows % 32 == 0 else 1
        self.size = rows // self.cuts
        self.scratch = [pltpu.SemaphoreType.DMA((self.chips * self.cuts,))] * 6

    def hold(self, dst, sems):
        self.dst = dst
        self.rs, self.rr, self.ls, self.lr, self.ps, self.pr = sems
        self.me = lax.axis_index(self.axis)
        self.chip, self.core = self.me // 2, self.me % 2
        self.partner = self.me + 1 - 2 * self.core

    def copy(self, slot, cut, send, recv, at, peer):
        place = self.dst.at[slot, pl.ds(cut * self.size, self.size)]
        at = at * self.cuts + cut
        return remote(place, place, send.at[at], recv.at[at], self.axis, peer)

    def right(self, slot, cut, k):
        return self.copy(slot, cut, self.rs, self.rr, k, self.me + 2)

    def left(self, slot, cut, k):
        return self.copy(slot, cut, self.ls, self.lr, k, self.me - 2)

    def share(self, slot, cut, at):
        return self.copy(slot, cut, self.ps, self.pr, at, self.partner)

    def start(self):
        me, chip = self.me, self.chip
        for cut in range(self.cuts):
            pl.when(chip < self.chips - 1)(self.right(me, cut, 0).start)
            pl.when(chip > 0)(self.left(me, cut, 0).start)
        for cut in range(self.cuts):
            self.share(me, cut, chip).start()

    def step(self, k):
        chip, chips = self.chip, self.chips
        for cut in range(self.cuts):

            @pl.when(chip - 1 - k >= 0)
            def _():
                slot = (chip - 1 - k) * 2 + self.core
                self.right(slot, cut, k).wait_recv()
                pl.when(chip + 1 < chips)(self.right(slot, cut, k + 1).start)
                self.share(slot, cut, chip - 1 - k).start()

            @pl.when(chip + 1 + k < chips)
            def _():
                slot = (chip + 1 + k) * 2 + self.core
                self.left(slot, cut, k).wait_recv()
                pl.when(chip > 0)(self.left(slot, cut, k + 1).start)
                self.share(slot, cut, chip + 1 + k).start()

    def beside(self, at):
        for cut in range(self.cuts):
            self.share(2 * at + 1 - self.core, cut, at).wait_recv()

    def each(self, body, done=0, then=None):
        self.beside(self.chip)
        body(self.chip)

        def at_step(k, carry):
            @pl.when(k >= done)
            def _():
                self.step(k)

            if then is not None:
                pl.when(k == self.chips - 2)(then)

            def at_side(side, inner):
                at = jnp.where(side == 0, self.chip - 1 - k, self.chip + 1 + k)

                @pl.when(jnp.logical_and(at >= 0, at < self.chips))
                def _():
                    self.beside(at)
                    body(at)

                return inner

            return lax.fori_loop(0, 2, at_side, carry)

        if self.chips > 1:
            lax.fori_loop(0, self.chips - 1, at_step, 0)
        elif then is not None:
            then()

    def sent(self):
        me, chip, chips = self.me, self.chip, self.chips
        for cut in range(self.cuts):
            for c in range(chips):
                self.share(2 * c + self.core, cut, c).wait_send()
            for k in range(chips - 1):
                to_right = jnp.logical_and(chip < chips - 1, k <= chip)
                pl.when(to_right)(self.right(me, cut, k).wait_send)
                to_left = jnp.logical_and(chip > 0, k <= chips - 1 - chip)
                pl.when(to_left)(self.left(me, cut, k).wait_send)


class Sum:
    axis = "ctx"

    def __init__(self, n, rows):
        self.n, self.chips = n, n // 2
        self.cuts = 2 if rows % 32 == 0 else 1
        self.size = rows // self.cuts
        self.scratch = [pltpu.SemaphoreType.DMA((self.chips,))] * 2
        self.scratch += [pltpu.SemaphoreType.DMA((self.chips * self.cuts,))] * 4

    def hold(self, part, near, got, sems):
        self.part, self.near, self.got = part, near, got
        self.ps, self.pr, self.rs, self.rr, self.ls, self.lr = sems
        self.me = lax.axis_index(self.axis)
        self.chip, self.core = self.me // 2, self.me % 2
        self.partner = self.me + 1 - 2 * self.core

    def beside(self, d):
        return remote(
            self.part.at[2 * d + 1 - self.core],
            self.near.at[d],
            self.ps.at[d],
            self.pr.at[d],
            self.axis,
            self.partner,
        )

    def rows(self, cut):
        return pl.ds(cut * self.size, self.size)

    def line(self, d, cut, place, send, recv, peer):
        at, rows = d * self.cuts + cut, self.rows(cut)
        return remote(
            self.part.at[2 * d + self.core, rows],
            self.got.at[place, rows],
            send.at[at],
            recv.at[at],
            self.axis,
            peer,
        )

    def right(self, d, cut):
        return self.line(d, cut, d, self.rs, self.rr, self.me + 2)

    def left(self, d, cut):
        place = jnp.where(d == self.chip - 1, self.chips, d)
        return self.line(d, cut, place, self.ls, self.lr, self.me - 2)

    def ready(self, d):
        self.beside(d).start()

    def order(self, k):
        return jnp.where(self.chip < self.chips // 2, self.chips - 1 - k, k)

    def pass_on(self, d, cut, edge, copy):
        if cut == 0:
            self.beside(d).wait_recv()
        rows = self.rows(cut)
        both = self.part[2 * d + self.core, rows].astype(f32) + self.near[d, rows].astype(f32)

        @pl.when(edge)
        def _():
            self.part[2 * d + self.core, rows] = both.astype(bf16)

        @pl.when(jnp.logical_not(edge))
        def _():
            copy.wait_recv()
            more = both + self.got[d, rows].astype(f32)
            self.part[2 * d + self.core, rows] = more.astype(bf16)

        copy.start()

    def step(self, t):
        chip, chips = self.chip, self.chips
        for cut in range(self.cuts):

            @pl.when(t >= chip)
            def _():
                d = chips - 1 - t + chip
                self.pass_on(d, cut, chip == 0, self.right(d, cut))

            @pl.when(t >= chips - 1 - chip)
            def _():
                d = t - (chips - 1 - chip)
                self.pass_on(d, cut, chip == chips - 1, self.left(d, cut))

    def last(self, total):
        chip, chips = self.chip, self.chips
        self.beside(chip).wait_recv()
        total[...] = self.part[self.me].astype(f32) + self.near[chip].astype(f32)
        for cut in range(self.cuts):
            rows = self.rows(cut)

            @pl.when(chip > 0)
            def _():
                self.right(chip, cut).wait_recv()
                total[rows] += self.got[chip, rows].astype(f32)

            @pl.when(chip < chips - 1)
            def _():
                self.left(chip, cut).wait_recv()
                total[rows] += self.got[chips, rows].astype(f32)

    def sent(self):
        for d in range(self.chips):
            self.beside(d).wait_send()
            for cut in range(self.cuts):
                pl.when(self.chip < d)(self.right(d, cut).wait_send)
                pl.when(self.chip > d)(self.left(d, cut).wait_send)


def mid_layer(ident, attended, wo, x_own, cot_full, gains, w_both, w_down_t):
    sizes = {axis: lax.axis_size(axis) for axis in ("dp", "ctx")}
    dp, n = sizes["dp"], sizes["ctx"]
    chips = n // 2
    rows, width = x_own.shape
    wide, f_w = attended.shape[2], w_down_t.shape[1]
    in_rows = width // dp
    shape = jax.ShapeDtypeStruct
    lines = [Line(n, rows), Line(n, rows)]
    sums = [Sum(n, rows)]
    att_swap = Swap("ctx", attended)
    att_swap.plan(sizes)
    swap = Swap("dp", shape((dp, in_rows, 3 * f_w), bf16))
    swap.plan(sizes)
    tasks = lines + sums + [att_swap, swap]

    def kernel(*refs):
        att, wo_ref, x_ref, cots, gain_ref, wgu, wd = refs[:7]
        d_mids, d_mid, mid, out_part, g_all, g_gain = refs[7:13]
        part, near, got, n2, mixed, d_gate, d_up, grads, inv, total = refs[13:23]
        att_got, load = refs[23:25]
        sems, at = [], 25
        for task in tasks:
            sems.append(tuple(refs[at : at + len(task.scratch)]))
            at += len(task.scratch)
        bring = pltpu.make_async_copy(wo_ref, part.at[pl.ds(0, wo.shape[0])], load)
        bring.start()
        spread(("dp", "ctx"), sizes, False)
        att_swap.start(att, att_got, *sems[3])
        lines[0].hold(n2, sems[0])
        lines[1].hold(d_mids, sems[1])
        sums[0].hold(part, near, got, sems[2])
        me = lax.axis_index("ctx")

        bring.wait()
        att_swap.finish(att, att_got, *sems[3])
        value = None
        for j in range(n):
            low = j * wide
            term = nn(att_got[j], part[low // rows, low % rows : low % rows + wide])
            value = term if value is None else value + term
        total[...] = value
        middle = x_ref[...].astype(f32) + total[...]
        inverse = inverse_rms(middle)
        mid[...] = middle
        inv[...] = inverse
        n2[me] = (middle * inverse * gain_ref[1:2]).astype(bf16)
        lines[0].start()

        def forward(at):
            here = pl.ds(2 * at, 2)
            tokens = n2[here].reshape(2 * rows, width)
            both = nn(tokens, wgu[...])
            gate_pre, up_pre = both[:, :f_w], both[:, f_w:]
            d_mixed = nn(cots[here].reshape(2 * rows, width), wd[...])
            sigma = 1.0 / (1.0 + jnp.exp(-gate_pre))
            silu_gate = gate_pre * sigma
            act = (silu_gate * up_pre).astype(bf16)
            dg = (d_mixed * up_pre * sigma * (1.0 + gate_pre * (1.0 - sigma))).astype(bf16)
            du = (d_mixed * silu_gate).astype(bf16)
            mixed[here] = act.reshape(2, rows, f_w)
            d_gate[here] = dg.reshape(2, rows, f_w)
            d_up[here] = du.reshape(2, rows, f_w)
            d_two = nt(jnp.concatenate([dg, du], axis=1), wgu[...])
            part[here] = d_two.astype(bf16).reshape(2, rows, width)
            sums[0].ready(at)
            out_part[here] = nt(act, wd[...]).astype(bf16).reshape(2, rows, width)

        lines[0].each(forward)

        def gradient(i):
            left, right = ((n2, d_gate), (n2, d_up), (cots, mixed))[i]
            value = tn(
                left[...].reshape(n * rows, width), right[...].reshape(n * rows, f_w)
            ).astype(bf16)
            for r in range(dp):
                grads[r, :, i * f_w : (i + 1) * f_w] = value[r * in_rows : (r + 1) * in_rows]

        for t in range(chips - 1):
            sums[0].step(t)
            if t == 0:
                gradient(0)
                gradient(1)
            if t == min(1, chips - 2):
                gradient(2)
                swap.start(grads, g_all, *sems[4])
        sums[0].last(total)
        middle = mid[...]
        d_norm, gain_part = norm_backward(middle, inv[...], gain_ref[1:2], total[...])
        g_gain[...] = gain_part.reshape(1, width)
        d_middle = cots[me].astype(f32) + d_norm
        d_mid[...] = d_middle
        d_mids[me] = d_middle.astype(bf16)
        lines[1].start()
        sums[0].sent()
        lines[0].sent()
        lines[1].each(lambda at: None)
        lines[1].sent()
        swap.finish(grads, g_all, *sems[4])

    whole = (n, rows, width)
    vmem = pl.BlockSpec(memory_space=pltpu.VMEM)
    return pl.pallas_call(
        kernel,
        out_shape=[
            shape(whole, bf16),
            shape((rows, width), f32),
            shape((rows, width), f32),
            shape(whole, bf16),
            shape((dp, in_rows, 3 * f_w), bf16),
            shape((1, width), f32),
        ],
        in_specs=[vmem, pl.BlockSpec(memory_space=pl.ANY)] + [vmem] * 5,
        out_specs=[pl.BlockSpec(memory_space=pltpu.VMEM)] * 6,
        scratch_shapes=[
            pltpu.VMEM(whole, bf16),
            pltpu.VMEM((chips, rows, width), bf16),
            pltpu.VMEM((chips + 1, rows, width), bf16),
            pltpu.VMEM(whole, bf16),
            pltpu.VMEM((n, rows, f_w), bf16),
            pltpu.VMEM((n, rows, f_w), bf16),
            pltpu.VMEM((n, rows, f_w), bf16),
            pltpu.VMEM((dp, in_rows, 3 * f_w), bf16),
            pltpu.VMEM((rows, 1), f32),
            pltpu.VMEM((rows, width), f32),
            pltpu.VMEM(attended.shape, bf16),
            pltpu.SemaphoreType.DMA(()),
        ]
        + [item for task in tasks for item in task.scratch],
        compiler_params=pltpu.CompilerParams(
            collective_id=ident, has_side_effects=True, vmem_limit_bytes=62 * 1024 * 1024
        ),
        name=f"block_{ident}",
    )(attended, wo, x_own, cot_full, gains, w_both, w_down_t)


class Need:
    axis = "ctx"

    def __init__(self, n, low, high):
        self.n, self.low, self.high = n, low, high
        self.slots = max(high(d) - low(d) + 1 for d in range(n))
        self.scratch = [
            pltpu.SemaphoreType.DMA((n,)),
            pltpu.SemaphoreType.DMA((self.slots,)),
        ]

    def hold(self, src, dst, sems):
        self.src, self.dst = src, dst
        self.send, self.recv = sems
        self.me = lax.axis_index(self.axis)
        self.first, self.final = self.low(self.me), self.high(self.me)

    def each(self):
        for d in range(self.n):
            low, high = self.low(d), self.high(d)
            used = jnp.logical_and(self.me >= low, self.me <= high)
            slot = jnp.clip(self.me - low, 0, self.slots - 1)
            copy = remote(
                self.src, self.dst.at[slot], self.send.at[d], self.recv.at[slot], self.axis, d
            )
            yield jnp.logical_and(used, self.me != d), copy

    def start(self):
        for used, copy in self.each():
            pl.when(used)(copy.start)
        for t in range(self.slots):
            source = self.first + t

            @pl.when(source == self.me)
            def _():
                self.dst[t] = self.src[...]

            @pl.when(source > self.final)
            def _():
                self.dst[t] = jnp.zeros_like(self.dst[t])

    def arrive(self):
        beside = self.me + 1 - 2 * lax.rem(self.me, 2)
        for t in range(self.slots):
            source = self.first + t
            copy = remote(
                self.src, self.dst.at[t], self.send.at[0], self.recv.at[t], self.axis, beside
            )
            pl.when(jnp.logical_and(source <= self.final, source != self.me))(copy.wait_recv)

    def sent(self):
        for used, copy in self.each():
            pl.when(used)(copy.wait_send)


def least(a, b):
    return min(a, b) if isinstance(a, int) else jnp.minimum(a, b)


def over(a, b):
    return a // b if isinstance(a, int) else lax.div(a, b)


def pick(rows, first, source, sign):
    at = first + lax.broadcasted_iota(jnp.int32, (rows, source.shape[1]), 0)
    return jnp.where(at == source, sign, 0.0)


def kv_head(j):
    return least(over(j, GROUP), KV_HEADS - 1)


def needs(n, held, width, q_w, k_w):
    wide = held * HEAD_DIM
    q_need = Need(
        n,
        lambda d: over(least(wide * d, width - 1), q_w),
        lambda d: over(least(wide * d + wide - 1, width - 1), q_w),
    )
    kv_need = Need(
        n,
        lambda d: over(HEAD_DIM * kv_head(held * d), k_w),
        lambda d: over(HEAD_DIM * kv_head(held * d + held - 1) + HEAD_DIM - 1, k_w),
    )
    return q_need, kv_need


def front(
    ident, x_t, cot_t, w_q, wk_t, wv_t, w_o, gain_a, gain_b, wg_t, wu_t, wd_t, held, tables
):
    sizes = {axis: lax.axis_size(axis) for axis in ("dp", "ctx")}
    dp, n = sizes["dp"], sizes["ctx"]
    chips, each = n // 2, n // dp
    width, rows = x_t.shape
    in_rows, q_w = w_q.shape
    o_w, k_w, f_w = w_o.shape[1], wk_t.shape[0], wg_t.shape[0]
    wide, total = held * HEAD_DIM, n * held * HEAD_DIM
    length, chunk = n * rows, 2 * rows
    shape = jax.ShapeDtypeStruct
    kv_rows = shape((2 * k_w, in_rows), bf16)

    q_need, kv_need = needs(n, held, width, q_w, k_w)
    x_line, cot_line = Line(n, rows), Line(n, rows)
    gain_all = Gather(shape((2, o_w), bf16))
    gain_all.axis = "ctx"
    q_all, kv_all = Gather(w_q), Gather(kv_rows)
    o_line, o_all = Line(n, in_rows), Gather(shape((chips, in_rows, o_w), bf16))
    g_all = Gather(shape((in_rows, 2 * f_w), bf16))
    d_turn = Turn(shape((each, o_w, f_w), bf16))
    d_all = Gather(shape((each, o_w, f_w), bf16))
    planned = [q_all, kv_all, o_all, g_all, d_turn, d_all, gain_all]
    for task in planned:
        task.plan(sizes)
    tasks = [q_need, kv_need, x_line, cot_line, o_line] + planned

    def kernel(*refs):
        xt, ct, wq_ref, wk_ref, wv_ref, wo_ref, ga_ref, gb_ref = refs[:8]
        wgt, wut, wdt, cos_ref, sin_ref = refs[8:13]
        att, lse, q_two, k_two, val, n1, cots, wo_out, wqkv, gain_out = refs[13:23]
        wg_out, wd_out, x_own, wo_all = refs[23:27]
        xs, gains_in, q_got, kv_got, o_got, q_in, kv_in, wall = refs[27:35]
        wg_mine, d_mine, d_got, o_side, kv_ref, gain_mine = refs[35:41]
        o_half, o_more, pair = refs[41:44]
        sems, at = {}, 44
        for task in tasks:
            sems[task] = tuple(refs[at : at + len(task.scratch)])
            at += len(task.scratch)
        spread(("dp", "ctx"), sizes, True)
        me = lax.axis_index("ctx")
        core = lax.rem(me, 2)
        x_line.hold(xs, sems[x_line])
        cot_line.hold(cots, sems[cot_line])
        o_line.hold(o_side, sems[o_line])
        q_need.hold(q_got, q_in, sems[q_need])
        kv_need.hold(kv_got, kv_in, sems[kv_need])
        kv_ref[:k_w] = wk_ref[...]
        kv_ref[k_w:] = wv_ref[...]
        mine = xt[...].T
        xs[me] = mine
        x_own[...] = mine
        x_line.start()
        q_all.start(wq_ref, q_got, *sems[q_all])
        kv_all.start(kv_ref, kv_got, *sems[kv_all])
        o_side[me] = wo_ref[...]
        gain_mine[...] = jnp.concatenate([ga_ref[...], gb_ref[...]], axis=0)
        gain_all.start(gain_mine, gains_in, *sems[gain_all])
        cots[me] = ct[...].T
        wg_mine[:, :f_w] = wgt[...].T
        wg_mine[:, f_w:] = wut[...].T
        for i in range(each):
            d_mine[i] = wdt[:, i * f_w : (i + 1) * f_w]
        q_all.finish(wq_ref, q_got, *sems[q_all])
        kv_all.finish(kv_ref, kv_got, *sems[kv_all])
        q_need.start()
        kv_need.start()
        d_turn.start(d_mine, d_got, *sems[d_turn])
        if chips > 1:
            x_line.step(0)
        gain_all.finish(gain_mine, gains_in, *sems[gain_all])
        for c in range(n):
            gain_out[:, c * o_w : (c + 1) * o_w] = gains_in[c].astype(f32)

        def turned(base, d):
            half = HEAD_DIM // 2
            return base + jnp.bitwise_and(d + half, HEAD_DIM - 1), jnp.where(d < half, -1.0, 1.0)

        def plan(heads):
            lane = lax.broadcasted_iota(jnp.int32, (1, 2 * HEAD_DIM), 1)
            d = jnp.bitwise_and(lane, HEAD_DIM - 1)
            parts = []
            for h in heads:
                parts.append((h * HEAD_DIM + d, jnp.ones((1, 2 * HEAD_DIM), f32)))
                parts.append(turned(h * HEAD_DIM, d))
            lane = lax.broadcasted_iota(jnp.int32, (1, wide), 1)
            flat = jnp.bitwise_and(lane, HEAD_DIM - 1)
            base = jnp.zeros((1, wide), jnp.int32)
            for i, h in enumerate(heads):
                inside = jnp.logical_and(lane >= i * HEAD_DIM, lane < (i + 1) * HEAD_DIM)
                base = jnp.where(inside, h * HEAD_DIM, base)
            return parts + [(base + flat, jnp.ones((1, wide), f32))]

        heads = [me * held + h for h in range(held)]
        kv_heads = [kv_head(h) for h in heads]
        q_plan, k_plan = plan(heads), plan(kv_heads)
        no = [(jnp.zeros_like(k_plan[-1][0]) - 1, k_plan[-1][1])]
        q_need.arrive()
        kv_need.arrive()
        span = 4 * held * HEAD_DIM
        for r in range(dp):
            here = slice(r * in_rows, (r + 1) * in_rows)
            value = None
            for t in range(q_need.slots):
                first = (q_need.first + t) * q_w
                take = jnp.concatenate([pick(q_w, first, *p) for p in q_plan], axis=1)
                term = nn(q_in[t, r], take.astype(bf16))
                value = term if value is None else value + term
            value = value.astype(bf16)
            wall[here, :span] = value[:, :span]
            wqkv[here, :wide] = value[:, span:]
            value = None
            for t in range(kv_need.slots):
                first = (kv_need.first + t) * k_w
                top = [pick(k_w, first, *p) for p in k_plan + no]
                zero = jnp.zeros((k_w, span + wide), f32)
                top = jnp.concatenate(top, axis=1)
                low = jnp.concatenate([zero, pick(k_w, first, *k_plan[-1])], axis=1)
                take = jnp.concatenate([top, low], axis=0).astype(bf16)
                term = tn(kv_in[t, r], take)
                value = term if value is None else value + term
            value = value.astype(bf16)
            wall[here, span:] = value[:, :span]
            wqkv[here, wide:] = value[:, span:]
        if chips > 2:
            x_line.step(1)
        o_line.start()
        g_all.start(wg_mine, wg_out, *sems[g_all])

        def project(at):
            here = pl.ds(2 * at, 2)
            tokens = xs[here].reshape(chunk, width).astype(f32)
            normed = (tokens * inverse_rms(tokens) * gain_out[0:1]).astype(bf16)
            n1[here] = normed.reshape(2, rows, width)
            both = nn(normed, wall[...])
            low = pl.multiple_of(at * chunk, chunk)
            first, second = cos_ref[pl.ds(low, chunk)], sin_ref[pl.ds(low, chunk)]
            for h in range(2 * held):
                at_h = h * 4 * HEAD_DIM
                a = both[:, at_h : at_h + 2 * HEAD_DIM]
                b = both[:, at_h + 2 * HEAD_DIM : at_h + 4 * HEAD_DIM]
                two = a * first + b * second
                if h < held:
                    q_two[h, pl.ds(low, chunk)] = (two * HEAD_DIM ** (-0.5)).astype(bf16)
                else:
                    k_two[h - held, pl.ds(low, chunk)] = two.astype(bf16)
            v = nn(normed, wqkv[:, 2 * wide :]).astype(bf16)
            for h in range(held):
                val[h, pl.ds(low, chunk)] = v[:, h * HEAD_DIM : (h + 1) * HEAD_DIM]

        x_line.each(project, min(2, chips - 1), cot_line.start)
        for k in range(chips - 1):
            o_line.step(k)
        for c in range(chips):
            o_line.beside(c)
        for c in range(chips):
            o_half[c] = o_side[2 * c + core]
        o_all.start(o_half, o_got, *sems[o_all])
        d_turn.finish(d_mine, d_got, *sems[d_turn])
        d_all.start(d_got, wd_out, *sems[d_all])
        x_line.sent()

        def attend(i):
            first, last = i * chunk, (i + 1) * chunk
            for h in range(held):
                q = q_two[h, first:last, :HEAD_DIM]
                diag = nt(q, k_two[h, first:last, :HEAD_DIM])
                row = lax.broadcasted_iota(jnp.int32, diag.shape, 0)
                col = lax.broadcasted_iota(jnp.int32, diag.shape, 1)
                diag = jnp.where(row >= col, diag, -1e30)
                top = jnp.max(diag, axis=-1, keepdims=True)
                if i:
                    off = nt(q, k_two[h, :first, :HEAD_DIM])
                    top = jnp.maximum(top, jnp.max(off, axis=-1, keepdims=True))
                expo = jnp.exp(diag - top)
                weight = jnp.sum(expo, axis=-1, keepdims=True)
                out = nn(expo.astype(bf16), val[h, first:last])
                if i:
                    expo = jnp.exp(off - top)
                    weight = weight + jnp.sum(expo, axis=-1, keepdims=True)
                    out = out + nn(expo.astype(bf16), val[h, :first])
                out = (out / weight).astype(bf16)
                lanes = slice(h * HEAD_DIM, (h + 1) * HEAD_DIM)
                att[2 * i : 2 * i + 2, :, lanes] = out.reshape(2, rows, HEAD_DIM)
                logs = jnp.broadcast_to(top + jnp.log(weight), (chunk, HEAD_DIM))
                lse[first:last, lanes] = logs

        for i in range(chips):
            attend(i)
            if i < chips - 1:
                cot_line.step(i)
        o_line.sent()
        o_all.finish(o_half, o_got, *sems[o_all])
        trade = remote(o_got, o_more, pair.at[0], pair.at[1], "ctx", me + 1 - 2 * core)
        trade.start()
        for c in range(chips):
            cot_line.beside(c)
        cot_line.sent()
        q_need.sent()
        kv_need.sent()
        g_all.finish(wg_mine, wg_out, *sems[g_all])
        d_all.finish(d_got, wd_out, *sems[d_all])
        trade.wait()
        for r in range(dp):
            pieces = []
            for c in range(n):
                mine, more = o_got[r, c // 2], o_more[r, c // 2]
                pieces.append(jnp.where(core == c % 2, mine, more))
            value = jnp.concatenate(pieces, axis=1)
            for j in range(total // rows):
                low, high = max(r * in_rows, j * rows), min((r + 1) * in_rows, (j + 1) * rows)
                if low < high:
                    wo_all[j, low - j * rows : high - j * rows] = value[
                        low - r * in_rows : high - r * in_rows
                    ]
        for j in range(total // rows):
            used = min(max(width - j * rows, 0), rows)
            if used < rows:
                wo_all[j, used:] = jnp.zeros((rows - used, width), bf16)
        offset = pl.multiple_of(lax.rem(me * wide, rows), wide)
        wo_out[...] = wo_all[lax.div(me * wide, rows), pl.ds(offset, wide)]

    whole = (n, rows, width)
    outs = [
        shape((n, rows, wide), bf16),
        shape((length, wide), f32),
        shape((held, length, 2 * HEAD_DIM), bf16),
        shape((held, length, 2 * HEAD_DIM), bf16),
        shape((held, length, HEAD_DIM), bf16),
        shape(whole, bf16),
        shape(whole, bf16),
        shape((wide, width), bf16),
        shape((width, 3 * wide), bf16),
        shape((2, width), f32),
        shape((dp, in_rows, 2 * f_w), bf16),
        shape((dp, each, o_w, f_w), bf16),
        shape((rows, width), bf16),
        shape((total // rows, rows, width), bf16),
    ]
    return pl.pallas_call(
        kernel,
        out_shape=outs,
        in_specs=[pl.BlockSpec(memory_space=pltpu.VMEM)] * 13,
        out_specs=[pl.BlockSpec(memory_space=pltpu.VMEM)] * len(outs),
        scratch_shapes=[
            pltpu.VMEM(whole, bf16),
            pltpu.VMEM((n, 2, o_w), bf16),
            pltpu.VMEM((dp, in_rows, q_w), bf16),
            pltpu.VMEM((dp,) + kv_rows.shape, bf16),
            pltpu.VMEM((dp, chips, in_rows, o_w), bf16),
            pltpu.VMEM((q_need.slots, dp, in_rows, q_w), bf16),
            pltpu.VMEM((kv_need.slots, dp) + kv_rows.shape, bf16),
            pltpu.VMEM((width, 8 * held * HEAD_DIM), bf16),
            pltpu.VMEM((in_rows, 2 * f_w), bf16),
            pltpu.VMEM((each, o_w, f_w), bf16),
            pltpu.VMEM((each, o_w, f_w), bf16),
            pltpu.VMEM((n, in_rows, o_w), bf16),
            pltpu.VMEM(kv_rows.shape, bf16),
            pltpu.VMEM((2, o_w), bf16),
            pltpu.VMEM((chips, in_rows, o_w), bf16),
            pltpu.VMEM((dp, chips, in_rows, o_w), bf16),
            pltpu.SemaphoreType.DMA((2,)),
        ]
        + [item for task in tasks for item in task.scratch],
        compiler_params=pltpu.CompilerParams(
            collective_id=ident, has_side_effects=True, vmem_limit_bytes=62 * 1024 * 1024
        ),
        name=f"front_{ident}",
    )(x_t, cot_t, w_q, wk_t, wv_t, w_o, gain_a, gain_b, wg_t, wu_t, wd_t, *tables)


class Give:
    axis = "ctx"

    def __init__(self, need):
        self.need = need
        self.scratch = [
            pltpu.SemaphoreType.DMA((need.slots,)),
            pltpu.SemaphoreType.DMA((need.n,)),
        ]

    def hold(self, mine, got, sems):
        self.mine, self.got = mine, got
        self.send, self.recv = sems
        self.me = lax.axis_index(self.axis)
        self.first, self.final = self.need.low(self.me), self.need.high(self.me)

    def copy(self, t, owner):
        return remote(
            self.mine.at[t],
            self.got.at[self.me],
            self.send.at[t],
            self.recv.at[self.me],
            self.axis,
            owner,
        )

    def start(self, term):
        for t in range(self.need.slots):
            owner = jnp.minimum(self.first + t, self.need.n - 1)
            used = self.first + t <= self.final

            @pl.when(used)
            def _():
                self.mine[t] = term(owner)

            pl.when(jnp.logical_and(used, owner != self.me))(self.copy(t, owner).start)

            @pl.when(jnp.logical_and(used, owner == self.me))
            def _():
                self.got[self.me] = self.mine[t]

    def add(self, total):
        beside = self.me + 1 - 2 * lax.rem(self.me, 2)
        total[...] = jnp.zeros_like(total)
        for d in range(self.need.n):
            used = jnp.logical_and(self.me >= self.need.low(d), self.me <= self.need.high(d))
            copy = remote(
                self.mine.at[0], self.got.at[d], self.send.at[0], self.recv.at[d], self.axis, beside
            )
            pl.when(jnp.logical_and(used, self.me != d))(copy.wait_recv)

            @pl.when(used)
            def _():
                total[...] += self.got[d].astype(f32)

    def sent(self):
        for t in range(self.need.slots):
            owner = jnp.minimum(self.first + t, self.need.n - 1)
            used = jnp.logical_and(self.first + t <= self.final, owner != self.me)
            pl.when(used)(self.copy(t, owner).wait_send)


def back(
    ident,
    d_mids,
    att,
    wo,
    lse,
    q_two,
    k_two,
    val,
    n1,
    wqkv,
    turn,
    d_mid,
    x_own,
    gains,
    mid,
    g_three,
    g_two,
    out_part,
    q_w,
    k_w,
):
    sizes = {axis: lax.axis_size(axis) for axis in ("dp", "ctx")}
    dp, n = sizes["dp"], sizes["ctx"]
    chips, each = n // 2, n // dp
    _, rows, width = d_mids.shape
    held, length, _ = q_two.shape
    wide, chunk = held * HEAD_DIM, 2 * rows
    in_rows, f_w = g_three.shape[1], g_three.shape[2] // 3
    o_w = width // n
    shape = jax.ShapeDtypeStruct
    q_need, kv_need = needs(n, held, width, q_w, k_w)
    q_give, kv_give = Give(q_need), Give(kv_need)
    sums = [Sum(n, rows), Sum(n, rows)]
    o_swap = Swap("ctx", shape((n, wide, o_w), bf16))
    o_down = Swap("dp", shape((dp, in_rows, o_w), bf16))
    w_swap = Swap("dp", shape((dp, 3 * wide, in_rows), bf16))
    d_turn = Turn(shape((each, o_w, f_w), bf16))
    gain_swap = Swap("ctx", shape((n, 2, o_w), f32))
    gain_all = Gather(shape((2, o_w), f32))
    planned = [o_swap, o_down, w_swap, d_turn, gain_swap, gain_all]
    for task in planned:
        task.plan(sizes)
    tasks = [q_give, kv_give] + sums + planned

    def kernel(*refs):
        dm_in, at_ref, wo_ref, lse_ref, q2, k2, v_ref, n_in, w_ref, turn_ref = refs[:10]
        mid_ref, x_ref, gain_ref, sum_ref, three, two_gain, out_in = refs[10:17]
        out_t, in_t, gq, gk, gv, go, gg, gu, gd, g_one, g_last = refs[17:28]
        part, near, got, near_o, got_o, datt, dk2, dv, dqkv, total = refs[28:38]
        o_src, o_got, o_cut, o_sum, w_src, w_got, d_src, d_got = refs[38:46]
        gain_src, gain_got, gain_mine, gain_sum = refs[46:50]
        q_mine, q_got, kv_mine, kv_got, kv_sum, load, dm = refs[50:57]
        sems, at = {}, 57
        for task in tasks:
            sems[task] = tuple(refs[at : at + len(task.scratch)])
            at += len(task.scratch)
        bring = pltpu.make_async_copy(out_in, part, load.at[0])
        bring.start()
        bring_d = pltpu.make_async_copy(dm_in, dm, load.at[1])
        bring_d.start()
        bring_n = pltpu.make_async_copy(n_in, dm, load.at[2])
        spread(("dp", "ctx"), sizes, True)
        me = lax.axis_index("ctx")
        sums[0].hold(part, near_o, got_o, sems[sums[0]])
        sums[1].hold(part, near, got, sems[sums[1]])
        q_give.hold(q_mine, q_got, sems[q_give])
        kv_give.hold(kv_mine, kv_got, sems[kv_give])
        bring.wait()
        for k in range(chips):
            sums[0].ready(sums[0].order(k))

        def of_dp(low, high):
            value = three[0, :, low:high].astype(f32)
            for r in range(1, dp):
                value = value + three[r, :, low:high].astype(f32)
            return value

        down = of_dp(2 * f_w, 3 * f_w).astype(bf16)
        for i in range(each):
            d_src[i] = down[i * o_w : (i + 1) * o_w]
        d_turn.start(d_src, d_got, *sems[d_turn])
        bring_d.wait()
        for i in range(chips):
            tokens = dm[2 * i : 2 * i + 2].reshape(chunk, width)
            datt[i * chunk : (i + 1) * chunk] = nt(tokens, wo_ref[...]).astype(bf16)
        value = tn(at_ref[...].reshape(length, wide), dm[...].reshape(length, width)).astype(bf16)
        bring_n.start()
        for c in range(n):
            o_src[c] = value[:, c * o_w : (c + 1) * o_w]
        o_swap.start(o_src, o_got, *sems[o_swap])

        def put(ref, h, low, high, value, first):
            if first:
                ref[h, low:high] = value
            else:
                ref[h, low:high] += value

        def folded(two, low, high):
            both = two * turn_ref[low:high]
            return both[:, :HEAD_DIM] + both[:, HEAD_DIM:]

        def attend(i):
            first, last = i * chunk, (i + 1) * chunk
            new = i == chips - 1
            for h in range(held):
                lanes = slice(h * HEAD_DIM, (h + 1) * HEAD_DIM)
                q, grad = q2[h, first:last, :HEAD_DIM], datt[first:last, lanes]
                own = at_ref[2 * i : 2 * i + 2, :, lanes].reshape(chunk, HEAD_DIM)
                delta = jnp.sum(grad.astype(f32) * own.astype(f32), axis=-1, keepdims=True)
                log = lse_ref[first:last, h * HEAD_DIM : h * HEAD_DIM + 1]
                dq = None
                for low, high in ((first, last), (0, first)):
                    if low == high:
                        continue
                    scores = nt(q, k2[h, low:high, :HEAD_DIM])
                    if low == first:
                        row = lax.broadcasted_iota(jnp.int32, scores.shape, 0)
                        col = lax.broadcasted_iota(jnp.int32, scores.shape, 1)
                        scores = jnp.where(row >= col, scores, -1e30)
                    probs = jnp.exp(scores - log)
                    d_probs = nt(grad, v_ref[h, low:high])
                    d_scores = (probs * (d_probs - delta)).astype(bf16)
                    term = nn(d_scores, k2[h, low:high])
                    dq = term if dq is None else dq + term
                    put(dk2, h, low, high, tn(d_scores, q2[h, first:last]), new)
                    put(dv, h, low, high, tn(probs.astype(bf16), grad), new)
                dq = folded(dq, first, last) * HEAD_DIM ** (-0.5)
                dqkv[first:last, lanes] = dq.astype(bf16)

        for t in range(chips):
            attend(chips - 1 - t)
            if t < chips - 1:
                sums[0].step(t)
        for i in range(chips):
            first, last = i * chunk, (i + 1) * chunk
            for h in range(held):
                base = wide + h * HEAD_DIM
                dk = folded(dk2[h, first:last], first, last)
                dqkv[first:last, base : base + HEAD_DIM] = dk.astype(bf16)
                base = base + wide
                dqkv[first:last, base : base + HEAD_DIM] = dv[h, first:last].astype(bf16)
        sums[0].last(total)
        out_t[...] = (sum_ref[...] + total[...]).T.astype(bf16)
        sums[0].sent()

        def project(k, carry):
            d = sums[1].order(k)
            low = pl.multiple_of(d * chunk, chunk)
            value = nt(dqkv[pl.ds(low, chunk)], w_ref[...]).astype(bf16)
            part[pl.ds(2 * d, 2)] = value.reshape(2, rows, width)
            sums[1].ready(d)
            return carry

        lax.fori_loop(0, chips, project, 0)
        bring_n.wait()
        value = tn(dqkv[...], dm[...].reshape(length, width)).astype(bf16)
        for t in range(min(1, chips - 1)):
            sums[1].step(t)
        for r in range(dp):
            w_src[r] = value[:, r * in_rows : (r + 1) * in_rows]
        w_swap.start(w_src, w_got, *sems[w_swap])
        o_swap.finish(o_src, o_got, *sems[o_swap])
        for j in range(n):
            for r in range(dp):
                low, high = max(r * in_rows, j * wide), min((r + 1) * in_rows, (j + 1) * wide)
                if low < high:
                    o_cut[r, low - r * in_rows : high - r * in_rows] = o_got[
                        j, low - j * wide : high - j * wide
                    ]
        o_down.start(o_cut, o_sum, *sems[o_down])
        gg[...] = of_dp(0, f_w).T
        gu[...] = of_dp(f_w, 2 * f_w).T
        for t in range(1, chips - 1):
            sums[1].step(t)
        w_swap.finish(w_src, w_got, *sems[w_swap])
        value = w_got[0].astype(f32)
        for r in range(1, dp):
            value = value + w_got[r].astype(f32)
        value = value.astype(bf16)
        heads = [me * held + h for h in range(held)]

        def columns(of):
            lane = lax.broadcasted_iota(jnp.int32, (1, wide), 1)
            base = jnp.zeros((1, wide), jnp.int32)
            for i, h in enumerate(of):
                inside = jnp.logical_and(lane >= i * HEAD_DIM, lane < (i + 1) * HEAD_DIM)
                base = jnp.where(inside, h * HEAD_DIM, base)
            return base + jnp.bitwise_and(lane, HEAD_DIM - 1)

        q_nat = value[:wide].T
        kv_part = value[wide:]
        q_cols = columns(heads)
        kv_cols = columns([least(over(h, GROUP), KV_HEADS - 1) for h in heads])
        ones = jnp.ones((1, wide), f32)

        def q_term(owner):
            return nt(q_nat, pick(q_w, owner * q_w, q_cols, ones).astype(bf16)).astype(bf16)

        def kv_term(owner):
            one = pick(k_w, owner * k_w, kv_cols, ones)
            none = jnp.zeros_like(one)
            top = jnp.concatenate([one, none], axis=1)
            low = jnp.concatenate([none, one], axis=1)
            return nn(jnp.concatenate([top, low], axis=0).astype(bf16), kv_part).astype(bf16)

        kv_give.start(kv_term)
        q_give.start(q_term)
        sums[1].last(total)
        hidden = x_ref[...].astype(f32)
        inverse = inverse_rms(hidden)
        d_norm, gain_part = norm_backward(hidden, inverse, gain_ref[0:1], total[...])
        both = jnp.concatenate([gain_part.reshape(1, width), two_gain[...]], axis=0)
        for c in range(n):
            gain_src[c] = both[:, c * o_w : (c + 1) * o_w]
        gain_swap.start(gain_src, gain_got, *sems[gain_swap])
        in_t[...] = (mid_ref[...] + d_norm).T
        d_turn.finish(d_src, d_got, *sems[d_turn])
        for i in range(each):
            gd[:, i * f_w : (i + 1) * f_w] = d_got[i].astype(f32)
        gain_swap.finish(gain_src, gain_got, *sems[gain_swap])
        gain_mine[...] = jnp.sum(gain_got[...], axis=0)
        gain_all.start(gain_mine, gain_sum, *sems[gain_all])
        o_down.finish(o_cut, o_sum, *sems[o_down])
        value = o_sum[0].astype(f32)
        for r in range(1, dp):
            value = value + o_sum[r].astype(f32)
        go[...] = value
        kv_give.add(kv_sum)
        gk[...] = kv_sum[:k_w]
        gv[...] = kv_sum[k_w:]
        q_give.add(gq)
        gain_all.finish(gain_mine, gain_sum, *sems[gain_all])
        value = jnp.sum(gain_sum[...], axis=0)
        g_one[...] = value[0:1]
        g_last[...] = value[1:2]
        q_give.sent()
        kv_give.sent()
        sums[1].sent()

    whole = (n, rows, width)
    vmem = pl.BlockSpec(memory_space=pltpu.VMEM)
    anywhere = pl.BlockSpec(memory_space=pl.ANY)
    outs = [
        shape((width, rows), bf16),
        shape((width, rows), f32),
        shape((in_rows, q_w), f32),
        shape((k_w, in_rows), f32),
        shape((k_w, in_rows), f32),
        shape((in_rows, o_w), f32),
        shape((f_w, in_rows), f32),
        shape((f_w, in_rows), f32),
        shape((o_w, each * f_w), f32),
        shape((1, o_w), f32),
        shape((1, o_w), f32),
    ]
    return pl.pallas_call(
        kernel,
        out_shape=outs,
        in_specs=[anywhere] + [vmem] * 6 + [anywhere] + [vmem] * 8 + [anywhere],
        out_specs=[vmem] * len(outs),
        scratch_shapes=[
            pltpu.VMEM(whole, bf16),
            pltpu.VMEM((chips, rows, width), bf16),
            pltpu.VMEM((chips + 1, rows, width), bf16),
            pltpu.VMEM((chips, rows, width), bf16),
            pltpu.VMEM((chips + 1, rows, width), bf16),
            pltpu.VMEM((length, wide), bf16),
            pltpu.VMEM((held, length, 2 * HEAD_DIM), f32),
            pltpu.VMEM((held, length, HEAD_DIM), f32),
            pltpu.VMEM((length, 3 * wide), bf16),
            pltpu.VMEM((rows, width), f32),
            pltpu.VMEM((n, wide, o_w), bf16),
            pltpu.VMEM((n, wide, o_w), bf16),
            pltpu.VMEM((dp, in_rows, o_w), bf16),
            pltpu.VMEM((dp, in_rows, o_w), bf16),
            pltpu.VMEM((dp, 3 * wide, in_rows), bf16),
            pltpu.VMEM((dp, 3 * wide, in_rows), bf16),
            pltpu.VMEM((each, o_w, f_w), bf16),
            pltpu.VMEM((each, o_w, f_w), bf16),
            pltpu.VMEM((n, 2, o_w), f32),
            pltpu.VMEM((n, 2, o_w), f32),
            pltpu.VMEM((2, o_w), f32),
            pltpu.VMEM((dp, 2, o_w), f32),
            pltpu.VMEM((q_need.slots, in_rows, q_w), bf16),
            pltpu.VMEM((n, in_rows, q_w), bf16),
            pltpu.VMEM((kv_need.slots, 2 * k_w, in_rows), bf16),
            pltpu.VMEM((n, 2 * k_w, in_rows), bf16),
            pltpu.VMEM((2 * k_w, in_rows), f32),
            pltpu.SemaphoreType.DMA((3,)),
            pltpu.VMEM(whole, bf16),
        ]
        + [item for task in tasks for item in task.scratch],
        compiler_params=pltpu.CompilerParams(
            collective_id=ident, has_side_effects=True, vmem_limit_bytes=62 * 1024 * 1024
        ),
        name=f"back_{ident}",
    )(
        d_mids,
        att,
        wo,
        lse,
        q_two,
        k_two,
        val,
        n1,
        wqkv,
        turn,
        d_mid,
        x_own,
        gains,
        mid,
        g_three,
        g_two,
        out_part,
    )


def finish(arrays):
    count = len(arrays)

    def kernel(*refs):
        for i in range(count):
            refs[count + i][...] = refs[i][...]

    return pl.pallas_call(
        kernel,
        out_shape=[jax.ShapeDtypeStruct(array.shape, array.dtype) for array in arrays],
        in_specs=[pl.BlockSpec(memory_space=pltpu.VMEM)] * count,
        out_specs=[pl.BlockSpec(memory_space=pltpu.VMEM)] * count,
        name="finish",
    )(*arrays)


def shards(
    inputs, cotangent, w_query, w_key, w_value, w_output, w_gate, w_up, w_down, gain_attn, gain_ffn
):
    dp, ctx = lax.axis_size("dp"), lax.axis_size("ctx")
    me = lax.axis_index("ctx")
    rows, width = inputs.shape
    length = rows * ctx
    q_w, k_w, o_w, f_w = w_query.shape[1], w_key.shape[1], w_output.shape[1], w_gate.shape[1]
    in_rows = w_query.shape[0]
    held = -(-HEADS // ctx)
    wide = held * HEAD_DIM
    total = ctx * wide
    near = all(wide * j >= q_w * j and wide * (j + 1) <= q_w * (j + 2) for j in range(ctx))

    each = ctx // dp
    cosine, sine = rope_tables(length)
    tables = (
        jnp.concatenate([cosine, sine], axis=1),
        jnp.concatenate([sine, -cosine], axis=1),
    )
    attended, lse, q_two, k_two, values, n1, cots, wo, wqkv, gain_rows, w_gu, w_d, x_own, wo_all = front(
        0,
        inputs.T,
        cotangent.T,
        w_query,
        w_key.T,
        w_value.T,
        w_output,
        gain_attn.reshape(1, o_w),
        gain_ffn.reshape(1, o_w),
        w_gate.T,
        w_up.T,
        w_down.T,
        held,
        tables,
    )
    d_mid_full, d_middle, middle, out_part, g_three, g_gain_two = mid_layer(
        2,
        attended,
        wo_all,
        x_own,
        cots,
        gain_rows,
        w_gu.reshape(width, 2 * f_w),
        w_d.reshape(width, f_w),
    )
    last = back(
        3,
        d_mid_full,
        attended,
        wo,
        lse,
        q_two,
        k_two,
        values,
        n1,
        wqkv,
        tables[0],
        d_middle,
        x_own,
        gain_rows,
        middle,
        g_three,
        g_gain_two,
        out_part,
        q_w,
        k_w,
    )
    out, grad, g_q, g_k, g_v, g_o, g_g, g_u, g_d, g_one, g_two = finish(last)
    g_one, g_two = g_one.reshape(o_w), g_two.reshape(o_w)
    return out.T, grad.T, g_q, g_k.T, g_v.T, g_o, g_g.T, g_u.T, g_d.T, g_one, g_two


def solution(mesh):
    blocks = P(("dp", "ctx"), None)
    matrix = P("dp", "ctx")
    in_specs = (blocks,) * 2 + (matrix,) * 7 + (P("ctx"),) * 2
    return jax.shard_map(shards, mesh=mesh, in_specs=in_specs, out_specs=in_specs, check_vma=False)
```
